32 devices in a mesh: dp: 8 (over z, x), shard: 4 (over y, core).
Axes of the slice: x: 2, y: 2, z: 4, core: 2. Of those that a mesh axis runs over, the one named last changes fastest.
Arguments:
- noisy: float32 [128, 256, 16], P(('dp', 'shard')), may hold values from -6 to 6
- velocity: float32 [128, 256, 16], P(('dp', 'shard')), may hold values from -6 to 6
- tstep_idx: int32 [128], P(('dp', 'shard')), may hold values from 0 to 999
- class_ids: int32 [128], P(('dp', 'shard')), may hold values from 0 to 1000
- time_weight: float32 [128], P(('dp', 'shard')), may hold values from 0.3 to 3
- dino: bfloat16 [128, 256, 768], P(('dp', 'shard')), may hold values from -6 to 6
- owner_map: int32 [12], replicated, may hold values from 0 to 11, each once
- adam_flat: float32 [2129920], P(('dp', 'shard')), may hold values from -4 to 4
- adam_m: float32 [2129920], P(('dp', 'shard')), may hold values from -0.015625 to 0.015625
- adam_v: float32 [2129920], P(('dp', 'shard')), may hold values from 1e-06 to 0.0001
- blocks_w: float32 [12, 384, 384], P('shard'), may hold values from -0.3125 to 0.3125
- stat_left: float32 [12, 384, 384], P('shard'), may hold values from -0.005 to 0.01, as said below
- stat_right: float32 [12, 384, 384], P('shard'), may hold values from -0.005 to 0.01, as said below
- root_left: float32 [12, 384, 384], P('shard'), may hold values from -3 to 3, as said below
- root_right: float32 [12, 384, 384], P('shard'), may hold values from -3 to 3, as said below
Outputs:
- loss: float32 [], replicated
- block_update: float32 [12, 384, 384], P('shard')
- stat_left_new: float32 [12, 384, 384], P('shard')
- stat_right_new: float32 [12, 384, 384], P('shard')
- adam_update: float32 [2129920], P(('dp', 'shard'))
- adam_m_new: float32 [2129920], P(('dp', 'shard'))
- adam_v_new: float32 [2129920], P(('dp', 'shard'))
The draws below stay inside these ranges and needn't reach their ends.
Inputs may be any that keep to these rules, and one draw needn't show every extreme that they name: `owner_map`: each block number appears once. `stat_left`: each slot is symmetric positive definite. `stat_right`: each slot is symmetric positive definite. `root_left`: each slot is symmetric positive definite. `root_right`: each slot is symmetric positive definite.
All inputs are finite; a program needn't handle non-finite values.
Results may differ from the reference program's by a relative error of at most 0.0097.
Values may be sent and summed in bfloat16 or wider, within the bound.
No kernel may reach another device: no remote copies, remote signals or barrier semaphores. Data moves between devices by JAX's collectives and lax.ppermute only.
A program may use at most 192 MiB of HBM per device.

```python
import math
import jax
import jax.numpy as jnp
from jax import lax

D = 384
HEADS = 6
HDIM = 64
F = 1536
PD = 16
GRID = 16
SEQ = 256
FREQ = 256
NCLS = 1001
DINO = 768
TSTEPS = 1000
STEP = 10
NBLK = 12
ADAM_LEN = 2125072
ADAM_PAD = 2129920
TOTAL_IMG = 128


def segment_spreads():
    return [(PD * D, PD ** (-0.5)), (D, 0.1), (FREQ * D, FREQ ** (-0.5)), (D, 0.1), (D * D, D ** (-0.5)), (D, 0.1), (NCLS * D, 1.0), (6 * D * D, D ** (-0.5)), (6 * D, 0.3), (D, 0.1), (D, 0.1), (D, 0.1), (F, 0.1), (D, 0.1), (2 * D * D, D ** (-0.5)), (2 * D, 0.3), (D * PD, D ** (-0.5)), (PD, 0.1), (D * DINO, D ** (-0.5)), (DINO, 0.1)]


def draw_adam_flat(key, part):
    key = jax.random.fold_in(key, 5)
    spreads = jnp.concatenate([jnp.full((length_of,), spread_of, jnp.float32) for length_of, spread_of in segment_spreads()] + [jnp.full((ADAM_PAD - ADAM_LEN,), 0.1, jnp.float32)])
    unit_draw = jnp.clip(jax.random.normal(key, (ADAM_PAD,), jnp.float32), -4.0, 4.0)
    return unit_draw * spreads


def definite_draw(key, low_diag, high_diag, off_weight):
    key_diag, key_off = jax.random.split(key)
    diag_vals = jnp.exp(jax.random.uniform(key_diag, (NBLK, D), jnp.float32, math.log(low_diag), math.log(high_diag)))
    raw_normal = jnp.clip(jax.random.normal(key_off, (NBLK, D, D), jnp.float32), -4.0, 4.0)
    symmetric = (raw_normal + jnp.swapaxes(raw_normal, 1, 2)) * 0.5
    root_diag = jnp.sqrt(diag_vals)
    off_part = symmetric * root_diag[:, :, None] * root_diag[:, None, :] * (off_weight / math.sqrt(D))
    identity_mat = jnp.eye(D, dtype=jnp.float32)
    return off_part * (1.0 - identity_mat) + identity_mat * diag_vals[:, :, None]


def draw_stat_left(key, part):
    return definite_draw(jax.random.fold_in(key, 1), 0.001, 0.01, 0.6)


def draw_stat_right(key, part):
    return definite_draw(jax.random.fold_in(key, 2), 0.001, 0.01, 0.6)


def draw_root_left(key, part):
    return definite_draw(jax.random.fold_in(key, 3), 0.5, 2.0, 0.6)


def draw_root_right(key, part):
    return definite_draw(jax.random.fold_in(key, 4), 0.5, 2.0, 0.6)


def plant(values, own_key, low, top_value):
    dims = values.shape
    spot = [jax.random.randint(jax.random.fold_in(own_key, axis), (), 0, dims[axis]) for axis in range(len(dims))]
    values = values.at[tuple(spot)].set(low)
    longest = dims.index(max(dims))
    spot[longest] = (spot[longest] + 1) % dims[longest]
    return values.at[tuple(spot)].set(top_value)


def levels(key, shape, cuts, low, largest):
    factor_of = 1.0
    for axis_at, blocks in cuts:
        heights = jax.random.uniform(jax.random.fold_in(jax.random.fold_in(key, 6), axis_at), (blocks,), jnp.float32, low / len(cuts), largest / len(cuts))
        factor_of = factor_of * jnp.repeat(jnp.exp(heights), shape[axis_at] // blocks).reshape((-1,) + (1,) * (len(shape) - 1 - axis_at))
    return factor_of


def noise(key, shape, width, reach, cuts=(), kind=jnp.bfloat16):
    entries = jax.random.normal(key, shape, jnp.float32) * width
    if len(cuts) > 0:
        entries = levels(key, shape, cuts, -0.22, 0.18) * entries
    return jnp.clip(entries, min=-reach, max=reach).astype(kind)


def setup_inputs(seed: int = 0) -> dict:
    keys = jax.random.split(jax.random.key(seed), 16)
    return {
        "noisy": noise(keys[0], (TOTAL_IMG, SEQ, PD), 1.0, 6.0, ((0, 32),), jnp.float32),
        "velocity": noise(keys[1], (TOTAL_IMG, SEQ, PD), 1.0, 6.0, ((0, 32),), jnp.float32),
        "tstep_idx": plant(jax.random.randint(keys[2], (TOTAL_IMG,), 0, TSTEPS), jax.random.fold_in(keys[2], 1), 0, TSTEPS - 1).astype(jnp.int32),
        "class_ids": plant(jax.random.randint(keys[3], (TOTAL_IMG,), 0, NCLS), jax.random.fold_in(keys[3], 1), 0, NCLS - 1).astype(jnp.int32),
        "time_weight": jnp.clip(jnp.exp(math.log(3.0) - 2.3025851 * jax.random.uniform(keys[4], (TOTAL_IMG,), jnp.float32) ** levels(keys[4], (TOTAL_IMG,), ((0, 32),), -0.2, 0.2)), 0.3, 3.0),
        "dino": noise(keys[5], (TOTAL_IMG, SEQ, DINO), 1.0, 6.0, ((0, 32),)),
        "owner_map": jax.random.permutation(keys[6], NBLK).astype(jnp.int32),
        "adam_flat": draw_adam_flat(jax.random.fold_in(keys[15], 71), 0),
        "adam_m": noise(keys[8], (ADAM_PAD,), 0.001, 0.015625, ((0, 32),), jnp.float32),
        "adam_v": jnp.clip(jnp.exp(math.log(0.0001) - 4.6051702 * jax.random.uniform(keys[9], (ADAM_PAD,), jnp.float32) ** levels(keys[9], (ADAM_PAD,), ((0, 32),), -0.2, 0.2)), 9.999999974752427e-07, 0.0001),
        "blocks_w": noise(keys[10], (NBLK, D, D), D ** -0.5, 0.3125, ((0, 4),), jnp.float32),
        "stat_left": draw_stat_left(jax.random.fold_in(keys[15], 71), 0),
        "stat_right": draw_stat_right(jax.random.fold_in(keys[15], 71), 0),
        "root_left": draw_root_left(jax.random.fold_in(keys[15], 71), 0),
        "root_right": draw_root_right(jax.random.fold_in(keys[15], 71), 0),
    }


@jax.custom_vjp
def low(v):
    return lax.optimization_barrier(v.astype(jnp.bfloat16)).astype(jnp.float32)

@jax.custom_vjp
def low_back(v):
    return v

def low_keep(v):
    return (low(v), None)

def low_pass(kept, grad):
    return (grad,)

def back_keep(v):
    return (v, None)

def back_low(kept, grad):
    return (low(grad),)
low.defvjp(low_keep, low_pass)
low_back.defvjp(back_keep, back_low)
HIGHEST = lax.Precision.HIGHEST
BETA_ONE = 0.9
BETA_TWO = 0.95
ADAM_EPS = 1e-08
ADAM_RATE = 0.01
DECAY_RATE = 0.1
STAT_BETA = 0.9
SHAMPOO_RATE = 0.02
RMS_EPS = 1e-08
REPA_WEIGHT = 0.5
NORM_EPS = 1e-06

def segment_shapes():
    return [(PD, D), (D,), (FREQ, D), (D,), (D, D), (D,), (NCLS, D), (D, 6 * D), (6 * D,), (D,), (D,), (D,), (F,), (D,), (D, 2 * D), (2 * D,), (D, PD), (PD,), (D, DINO), (DINO,)]

def unflatten(flat):
    pieces = []
    offset = 0
    for seg_dims in segment_shapes():
        length = math.prod(seg_dims)
        pieces.append(flat[offset:offset + length].reshape(seg_dims))
        offset += length
    return pieces

def position_table():
    quarter = D // 4
    frequencies = 1.0 / 10000.0 ** (jnp.arange(quarter, dtype=jnp.float32) / quarter)
    cell_ids = jnp.arange(SEQ, dtype=jnp.int32)
    row_arg = (cell_ids // GRID).astype(jnp.float32)[:, None] * frequencies[None, :]
    col_arg = (cell_ids % GRID).astype(jnp.float32)[:, None] * frequencies[None, :]
    return jnp.concatenate([jnp.sin(col_arg), jnp.cos(col_arg), jnp.sin(row_arg), jnp.cos(row_arg)], axis=1)

def time_features(tstep_idx):
    half_freq = FREQ // 2
    frequencies = jnp.exp(-math.log(10000.0) * jnp.arange(half_freq, dtype=jnp.float32) / half_freq)
    angles = (tstep_idx.astype(jnp.float32) + 0.5)[:, None] * frequencies[None, :]
    return jnp.concatenate([jnp.cos(angles), jnp.sin(angles)], axis=1)

def layer_norm(values):
    centered = values - lax.optimization_barrier(jnp.mean(values, axis=-1, keepdims=True))
    return centered * lax.rsqrt(lax.optimization_barrier(jnp.mean(centered * centered, axis=-1, keepdims=True)) + NORM_EPS)

def group_loss(flat, model_blocks, noisy, velocity, tstep_idx, class_ids, time_weight, dino_f, total_img):
    patch_weight, patch_bias, time_in_weight, time_in_bias, time_out_weight, time_out_bias, class_table, mod_weight, mod_bias, query_bias, value_bias, proj_bias, hidden_bias, down_bias, final_mod_weight, final_mod_bias, final_weight, final_bias, align_weight, align_bias = unflatten(low(flat))
    blocks = low(model_blocks)
    fc_ratio = F // D
    w_qkv = jnp.concatenate([blocks[0], blocks[1], blocks[2]], axis=1)
    w_proj = blocks[3]
    w_up = jnp.concatenate([blocks[4 + which] for which in range(fc_ratio)], axis=1)
    w_down = blocks[4 + fc_ratio:].reshape(F, D)
    features = time_features(tstep_idx)
    time_hidden = jax.nn.silu(jnp.dot(features, time_in_weight, precision=HIGHEST) + time_in_bias)
    condition = jnp.dot(time_hidden, time_out_weight, precision=HIGHEST) + time_out_bias + class_table[class_ids]
    cond_act = jax.nn.silu(condition)
    modulation = jnp.dot(cond_act, mod_weight, precision=HIGHEST) + mod_bias
    final_mods = jnp.dot(cond_act, final_mod_weight, precision=HIGHEST) + final_mod_bias
    shift_one, scale_one, gate_one, shift_two, scale_two, gate_two = [modulation[:, None, which * D:(which + 1) * D] for which in range(6)]
    final_shift = final_mods[:, None, :D]
    final_scale = final_mods[:, None, D:]
    groups = noisy.shape[0]
    seq = noisy.shape[1]
    hidden0 = low_back(jnp.einsum('gsp,pd->gsd', low(noisy), patch_weight, precision=HIGHEST) + patch_bias) + position_table()
    act_one = low(layer_norm(hidden0) * (1.0 + scale_one) + shift_one)
    qkv_bias = jnp.concatenate([query_bias, jnp.zeros((D,), jnp.float32), value_bias])
    projected = low_back(jnp.einsum('gsd,de->gse', act_one, w_qkv, precision=HIGHEST) + qkv_bias)
    queries = low(projected[..., :D]).reshape(groups, seq, HEADS, HDIM)
    key_part = low(projected[..., D:2 * D]).reshape(groups, seq, HEADS, HDIM)
    values = low(projected[..., 2 * D:]).reshape(groups, seq, HEADS, HDIM)
    scores = low_back(jnp.einsum('gqhe,gkhe->ghqk', queries, key_part, precision=HIGHEST) * HDIM ** (-0.5))
    probs = low(jax.nn.softmax(scores, axis=-1))
    attended = low(low_back(jnp.einsum('ghqk,gkhe->gqhe', probs, values, precision=HIGHEST).reshape(groups, seq, D)))
    branch_one = low_back(jnp.einsum('gsd,de->gse', attended, w_proj, precision=HIGHEST) + proj_bias)
    hidden1 = hidden0 + gate_one * branch_one
    act_two = low(layer_norm(hidden1) * (1.0 + scale_two) + shift_two)
    inner_pre = low_back(jnp.einsum('gsd,de->gse', act_two, w_up, precision=HIGHEST) + hidden_bias)
    gelu_out = low(jax.nn.gelu(inner_pre, approximate=True))
    branch_two = low_back(jnp.einsum('gse,ed->gsd', gelu_out, w_down, precision=HIGHEST) + down_bias)
    hidden2 = hidden1 + gate_two * branch_two
    act_three = low(layer_norm(hidden2) * (1.0 + final_scale) + final_shift)
    output = low_back(jnp.einsum('gsd,dp->gsp', act_three, final_weight, precision=HIGHEST) + final_bias)
    errors = output - velocity
    main_term = jnp.sum(time_weight[:, None, None] * errors * errors) / (total_img * SEQ * PD)
    aligned = low_back(jnp.einsum('gsd,de->gse', low(hidden1), align_weight, precision=HIGHEST) + align_bias)
    cosine = lax.optimization_barrier(jnp.sum(aligned * dino_f, axis=-1)) * lax.rsqrt(lax.optimization_barrier(jnp.sum(aligned * aligned, axis=-1)) + NORM_EPS) * lax.rsqrt(lax.optimization_barrier(jnp.sum(dino_f * dino_f, axis=-1)) + NORM_EPS)
    return main_term - REPA_WEIGHT * jnp.sum(cosine) / (total_img * SEQ)

def reference(noisy, velocity, tstep_idx, class_ids, time_weight, dino, owner_map, adam_flat, adam_m, adam_v, blocks_w, stat_left, stat_right, root_left, root_right):
    total_img = noisy.shape[0]
    block_ids = jnp.arange(NBLK, dtype=jnp.int32)
    slot_of = lax.optimization_barrier(jnp.sum(block_ids[:, None] * (owner_map[:, None] == block_ids[None, :]).astype(jnp.int32), axis=0)).astype(jnp.int32)
    model_blocks = blocks_w[slot_of]
    group = math.gcd(total_img, max(1, 4096 // SEQ))

    def grouped(array):
        return array.reshape((total_img // group, group) + array.shape[1:])
    batches = (grouped(noisy), grouped(velocity), grouped(tstep_idx), grouped(class_ids), grouped(time_weight), grouped(dino.astype(jnp.float32)))

    def step_fn(carry, batch):
        loss_acc, flat_acc, block_acc = carry

        def local_loss(flat, blocks):
            return group_loss(flat, blocks, batch[0], batch[1], batch[2], batch[3], batch[4], batch[5], total_img)
        value, pullback = jax.vjp(local_loss, adam_flat, model_blocks)
        flat_grad, block_grad = pullback(jnp.ones_like(value))
        return ((loss_acc + value, flat_acc + flat_grad, block_acc + block_grad), None)
    start = (jnp.zeros((), jnp.float32), jnp.zeros_like(adam_flat), jnp.zeros_like(model_blocks))
    (loss_total, flat_total, block_total), unused = lax.scan(step_fn, start, batches)
    grads_slot = block_total[owner_map]
    new_left = STAT_BETA * stat_left + (1.0 - STAT_BETA) * jnp.einsum('bij,bkj->bik', grads_slot, grads_slot, precision=HIGHEST)
    new_right = STAT_BETA * stat_right + (1.0 - STAT_BETA) * jnp.einsum('bji,bjk->bik', grads_slot, grads_slot, precision=HIGHEST)
    left_applied = jnp.einsum('bij,bjk->bik', root_left, grads_slot, precision=HIGHEST)
    direction = jnp.einsum('bij,bjk->bik', left_applied, root_right, precision=HIGHEST)
    root_mean = jnp.sqrt(lax.optimization_barrier(jnp.mean(direction * direction, axis=(1, 2), keepdims=True)))
    block_update = -SHAMPOO_RATE * (direction / (root_mean + RMS_EPS) + DECAY_RATE * blocks_w)
    new_m = BETA_ONE * adam_m + (1.0 - BETA_ONE) * flat_total
    new_v = BETA_TWO * adam_v + (1.0 - BETA_TWO) * flat_total * flat_total
    corrected_m = new_m / (1.0 - BETA_ONE ** STEP)
    corrected_v = new_v / (1.0 - BETA_TWO ** STEP)
    adam_update = -ADAM_RATE * (corrected_m / (jnp.sqrt(corrected_v) + ADAM_EPS) + DECAY_RATE * adam_flat)
    return (loss_total, block_update, new_left, new_right, adam_update, new_m, new_v)
```

```python
import functools
import math

import jax
import jax.numpy as jnp
from jax import lax
from jax.experimental import pallas as pl
from jax.experimental.pallas import tpu as pltpu
from jax.sharding import PartitionSpec as P

D = 384
HEADS = 6
HDIM = 64
F = 1536
PD = 16
GRID = 16
SEQ = 256
FREQ = 256
NCLS = 1001
DINO = 768
STEP = 10
NBLK = 12
ADAM_LEN = 2125072
ADAM_PAD = 2129920

BETA_ONE = 0.9
BETA_TWO = 0.95
ADAM_EPS = 1e-08
ADAM_RATE = 0.01
DECAY_RATE = 0.1
STAT_BETA = 0.9
SHAMPOO_RATE = 0.02
RMS_EPS = 1e-08
REPA_WEIGHT = 0.5
NORM_EPS = 1e-06
QK_SCALE = HDIM ** (-0.5)

AXES = ("dp", "shard")
BF = jnp.bfloat16
F32 = jnp.float32
VM = pl.BlockSpec(memory_space=pltpu.VMEM)
SM = pl.BlockSpec(memory_space=pltpu.SMEM)

FLAT_ROWS = ADAM_PAD // 128
R_PATCH = 0
R_PATCH_B = 48
R_TIME_IN = 51
R_TIME_IN_B = 819
R_TIME_OUT = 822
R_TIME_OUT_B = 1974
R_CLASS = 1977
R_MOD = 4980
R_MOD_B = 11892
R_QUERY_B = 11910
R_VALUE_B = 11913
R_PROJ_B = 11916
R_HIDDEN_B = 11919
R_DOWN_B = 11931
R_FMOD = 11934
R_FMOD_B = 14238
R_FINAL = 14244
R_FINAL_B = 14292
ALIGN_ROWS = 2310

MISC = 256
PAY = 56


def shape(dims, kind=F32):
    return jax.ShapeDtypeStruct(dims, kind)


def mm(left, right):
    return jnp.dot(left, right, preferred_element_type=F32)


def mm_nt(left, right):
    return lax.dot_general(left, right, (((1,), (1,)), ((), ())), preferred_element_type=F32)


def mm_tn(left, right):
    return lax.dot_general(left, right, (((0,), (0,)), ((), ())), preferred_element_type=F32)


def silu(v):
    return v / (1.0 + jnp.exp(-v))


def silu_slope(v):
    s = 1.0 / (1.0 + jnp.exp(-v))
    return s * (1.0 + v * (1.0 - s))


def split3(v):
    one = v.astype(BF)
    rest = v - one.astype(F32)
    two = rest.astype(BF)
    return one, two, (rest - two.astype(F32)).astype(BF)


def stack3(v):
    one, two, three = split3(v)
    return jnp.concatenate([one.astype(F32), two.astype(F32), three.astype(F32)], axis=0).astype(BF)


def fold3(v):
    third = v.shape[0] // 3
    return v[:third] + v[third : 2 * third] + v[2 * third :]


def place_of(z, x, y, c):
    return ((z * 2 + x) * 2 + y) * 2 + c


def permutation(move):
    pairs = []
    for z in range(4):
        for x in range(2):
            for y in range(2):
                for c in range(2):
                    pairs.append((place_of(z, x, y, c), place_of(*move(z, x, y, c))))
    return pairs


TO_C = permutation(lambda z, x, y, c: (z, x, y, 1 - c))
TO_Y = permutation(lambda z, x, y, c: (z, x, 1 - y, c))
TO_X = permutation(lambda z, x, y, c: (z, 1 - x, y, c))
TO_Z = [permutation(lambda z, x, y, c, d=d: ((z + d) % 4, x, y, c)) for d in range(4)]


def send(value, pairs):
    return lax.ppermute(value, AXES, pairs)


def coordinates():
    dp = lax.axis_index("dp")
    sh = lax.axis_index("shard")
    return dp // 2, dp % 2, sh // 2, sh % 2


def pick(array, start, size):
    return lax.dynamic_slice_in_dim(array, start, size, 0)


def gather_all(piece, cut):
    turned = [piece] + [send(piece, TO_Z[d]) for d in (1, 2, 3)]
    first = jnp.stack([t[:cut] for t in turned])
    second = jnp.stack([t[cut:] for t in turned])
    first_x = send(first, TO_X)
    second_y = send(second, TO_Y)
    first = jnp.concatenate([first, first_x])
    second = jnp.concatenate([second, second_y])
    parts = [first, second, send(first, TO_Y), send(second, TO_X)]
    return parts + [send(p, TO_C) for p in parts]


def flip(value, bit):
    return 1 - value if bit else value


def gather_places(cut):
    def maker(dc, kind):
        def entry(i, at):
            z, x, y, c = at
            dz, far = i % 4, i // 4
            dx, dy = {0: (far, 0), 1: (0, far), 2: (far, 1), 3: (1, far)}[kind]
            return place_of(lax.rem(z + 4 - dz, 4), flip(x, dx), flip(y, dy), flip(c, dc))
        return entry

    offsets = [0, cut, 0, cut]
    return [(offsets[k], maker(dc, k)) for dc in (0, 1) for k in range(4)]


def read_coordinates(ref):
    return ref[0], ref[1], ref[2], ref[3]


def cond_kernel(places, rows, at_ref, cls_ref, feat_ref, *refs):
    count = len(places)
    pieces = refs[:count]
    (mods_ref, pre_ref, th_ref, cond_ref, modw_ref, fmodw_ref, tout_ref, align_ref, bias_ref,
     patch_ref, final_ref, flat, rolled) = refs[count:]
    at = read_coordinates(at_ref)
    for ref, (offset, entry) in zip(pieces, places):
        for i in range(ref.shape[0]):
            start = pl.multiple_of(entry(i, at) * rows + offset, 8)
            flat[pl.ds(start, ref.shape[1]), :] = ref[i].astype(F32)

    def row(first, count):
        return jnp.concatenate([flat[first + l : first + l + 1, :] for l in range(count)], axis=1)

    def columns(first, depth, count, which):
        return flat[pl.ds(first + which, depth, stride=count), :].astype(BF)

    def wide(v, first, depth, count, keep=None):
        stacked = stack3(v)
        out = []
        for j in range(count):
            w = columns(first, depth, count, j)
            if keep is not None:
                keep[:, 128 * j : 128 * j + 128] = w
            out.append(fold3(mm(stacked, w)))
        return jnp.concatenate(out, axis=1)

    pre = wide(feat_ref[...], R_TIME_IN, FREQ, 3) + row(R_TIME_IN_B, 3)
    th = silu(pre)
    picked = []
    for m in range(4):
        r = R_CLASS + 3 * cls_ref[m]
        picked.append(jnp.concatenate([flat[pl.ds(r + l, 1), :] for l in range(3)], axis=1))
    picked = jnp.concatenate(picked + [jnp.zeros((4, D), F32)], axis=0)
    cond = wide(th, R_TIME_OUT, D, 3, tout_ref) + row(R_TIME_OUT_B, 3) + picked
    act = silu(cond)
    pre_ref[...] = pre
    th_ref[...] = th
    cond_ref[...] = cond
    mods_ref[:, : 6 * D] = wide(act, R_MOD, D, 18, modw_ref) + row(R_MOD_B, 18)
    mods_ref[:, 6 * D :] = wide(act, R_FMOD, D, 6, fmodw_ref) + row(R_FMOD_B, 6)

    spot = lax.broadcasted_iota(jnp.int32, (ALIGN_ROWS, 128), 1)
    here = pltpu.roll(flat[R_FINAL_B : R_FINAL_B + ALIGN_ROWS, :], 112, 1)
    after = pltpu.roll(flat[R_FINAL_B + 1 : R_FINAL_B + 1 + ALIGN_ROWS, :], 112, 1)
    rolled[...] = jnp.where(spot < 112, here, after)
    for j in range(6):
        align_ref[:, 128 * j : 128 * j + 128] = rolled[pl.ds(j, D, stride=6), :].astype(BF)

    bias_ref[...] = jnp.zeros_like(bias_ref)
    for at_row, first in ((0, R_PATCH_B), (1, R_QUERY_B), (2, R_VALUE_B), (3, R_PROJ_B),
                          (4, R_HIDDEN_B), (5, R_HIDDEN_B + 3), (6, R_HIDDEN_B + 6),
                          (7, R_HIDDEN_B + 9), (8, R_DOWN_B)):
        bias_ref[at_row : at_row + 1, :] = row(first, 3)
    for half in range(2):
        bias_ref[9 + half : 10 + half, :] = jnp.concatenate(
            [rolled[2304 + 3 * half + l : 2305 + 3 * half + l, :] for l in range(3)], axis=1)
    lane = lax.broadcasted_iota(jnp.int32, (1, 128), 1)
    bias_ref[11:12, :128] = jnp.where(lane < PD, flat[R_FINAL_B : R_FINAL_B + 1, :], 0.0)
    patch = [flat[pl.ds(R_PATCH + l, PD, stride=3), :] for l in range(3)]
    patch_ref[...] = jnp.concatenate(patch, axis=1).astype(BF)
    spread = (lax.broadcasted_iota(jnp.int32, (D, 48), 0) // 8
              == lax.broadcasted_iota(jnp.int32, (D, 48), 1)).astype(F32).astype(BF)
    wide_rows = mm(spread, flat[R_FINAL : R_FINAL + 48, :].astype(BF))
    keep = (lax.broadcasted_iota(jnp.int32, (D, 128), 1) // PD
            == lax.broadcasted_iota(jnp.int32, (D, 128), 0) % 8)
    fold = (lax.broadcasted_iota(jnp.int32, (128, 128), 0) % PD
            == lax.broadcasted_iota(jnp.int32, (128, 128), 1)).astype(F32).astype(BF)
    final_ref[...] = mm(jnp.where(keep, wide_rows, 0.0).astype(BF), fold).astype(BF)


def conditioning(at, classes, features, pieces, places, rows):
    kernel = functools.partial(cond_kernel, places, rows)
    return pl.pallas_call(
        kernel,
        name="conditioning",
        out_shape=(shape((8, 8 * D)), shape((8, D)), shape((8, D)), shape((8, D)),
                   shape((D, 6 * D), BF), shape((D, 2 * D), BF), shape((D, D), BF),
                   shape((D, DINO), BF), shape((16, D)), shape((PD, D), BF), shape((D, 128), BF)),
        in_specs=[SM, SM, VM] + [VM] * len(pieces),
        out_specs=[VM] * 11,
        scratch_shapes=[pltpu.VMEM((FLAT_ROWS + 8, 128), F32), pltpu.VMEM((ALIGN_ROWS, 128), F32)],
        cost_estimate=pl.CostEstimate(flops=10**9, bytes_accessed=10**7, transcendentals=0),
    )(at, classes, features, *pieces)


def blocks_kernel(at_ref, own_ref, mine_ref, pair_ref, near_ref, far_ref, near_c_ref, far_c_ref, out_ref):
    z, x, y, c = read_coordinates(at_ref)
    for t in range(3):
        out_ref[own_ref[3 * (2 * y + c) + t]] = mine_ref[t]
        out_ref[own_ref[3 * (2 * y + 1 - c) + t]] = pair_ref[t]
        over = own_ref[3 * (2 * (1 - y) + c) + t]
        over_c = own_ref[3 * (2 * (1 - y) + 1 - c) + t]
        for side in range(2):
            @pl.when(x == side)
            def _():
                low, high = 192 * side, 192 * (1 - side)
                out_ref[over, low : low + 192, :] = near_ref[t]
                out_ref[over, high : high + 192, :] = far_ref[t]
                out_ref[over_c, low : low + 192, :] = near_c_ref[t]
                out_ref[over_c, high : high + 192, :] = far_c_ref[t]


def gather_blocks(at, owner_map, mine):
    x = lax.rem(lax.axis_index("dp"), 2)
    half = lax.dynamic_slice_in_dim(mine, 192 * x, 192, 1)
    near = send(half, TO_Y)
    far = send(near, TO_X)
    pair = send(mine, TO_C)
    near_c = send(near, TO_C)
    far_c = send(far, TO_C)
    return pl.pallas_call(
        blocks_kernel,
        name="gather_blocks",
        out_shape=shape((NBLK, D, D), BF),
        in_specs=[SM, SM] + [VM] * 6,
        out_specs=VM,
        cost_estimate=pl.CostEstimate(flops=0, bytes_accessed=7 * 10**6, transcendentals=0),
    )(at, owner_map, mine, pair, near, far, near_c, far_c)


UNIT = 24
CHIP_ROWS = 7 * UNIT + 8


def unit_of(z, x, y):
    return jnp.where(z < 2, x * 4 + y * 2 + z, 6 + y * 4 + x * 2 + z)


def add_low(left, right):
    return (left.astype(F32) + right.astype(F32)).astype(BF)


def reduce_units(units):
    z, x, y, c = coordinates()
    got = send(pick(units, 1 - c, 1)[0], TO_C)
    both = add_low(pick(units, c, 1)[0], got)
    first, second = both[:8], both[8:]
    got_x = send(pick(first, 4 * (1 - x), 4), TO_X)
    got_y = send(pick(second, 4 * (1 - y), 4), TO_Y)
    first = add_low(pick(first, 4 * x, 4), got_x)
    second = add_low(pick(second, 4 * y, 4), got_y)
    got_y = send(pick(first, 2 * (1 - y), 2), TO_Y)
    got_x = send(pick(second, 2 * (1 - x), 2), TO_X)
    quarter = jnp.concatenate(
        [add_low(pick(first, 2 * y, 2), got_y), add_low(pick(second, 2 * x, 2), got_x)])
    got = [send(pick(quarter, (z + d) % 4, 1)[0], TO_Z[d]) for d in (1, 2, 3)]
    total = pick(quarter, z, 1)[0].astype(F32)
    for g in got:
        total = total + g.astype(F32)
    return total.astype(BF)


def gather_owned(mine, owner_map):
    z, x, y, c = coordinates()
    pair = send(mine, TO_C)
    whole = jnp.where(c == 0, jnp.concatenate([mine, pair]), jnp.concatenate([pair, mine]))
    slots = jnp.take(whole, owner_map, axis=0).reshape(2, 2, 3, UNIT, D)
    slots = lax.dynamic_index_in_dim(slots, c, 1, keepdims=False)
    near = send(lax.dynamic_index_in_dim(slots, 1 - y, 0, keepdims=False), TO_Y)
    both = jnp.stack([lax.dynamic_index_in_dim(slots, y, 0, keepdims=False), near])
    column = jnp.stack([both] + [send(both, TO_Z[d]) for d in (1, 2, 3)])
    return column, send(column, TO_X)


def place_kernel(places, at_ref, *refs):
    pieces = refs[: len(places)]
    pay_ref, align_ref, misc_ref = refs[len(places) :]
    at = read_coordinates(at_ref)
    for ref, (offset, entry) in zip(pieces, places):
        for i in range(ref.shape[0]):
            dev = entry(i, at)
            z, x, y, c = dev // 8, (dev // 4) % 2, (dev // 2) % 2, dev % 2
            unit = unit_of(z, x, y)
            value = ref[i].astype(F32)
            if offset == 0:
                pay_ref[dev, 0:48, :] = value
            else:
                pay_ref[dev, 48:PAY, :] = value[0:8]
                align_ref[c, pl.ds(pl.multiple_of(unit * UNIT, 8), UNIT), :] = value[8:32]
                misc_ref[pl.ds(pl.multiple_of(c * 128 + unit * 8, 8), 8), :] = value[32:40]


def adam_kernel(local, pay_ref, align_ref, misc_ref, *refs):
    if local:
        at_ref, w_ref, m_ref, v_ref, loss_ref, upd_ref, new_m_ref, new_v_ref, flat, rolled = refs
    else:
        loss_ref, flat, rolled = refs
    rows = 8 * pay_ref.shape[0]

    def tile(j):
        return pay_ref[:, 8 * j : 8 * j + 8, :].reshape(rows, D)

    upper = lax.broadcasted_iota(jnp.int32, (rows, 1), 0) % 8 < 4

    def first(v):
        return jnp.where(upper, v, 0.0)

    def second(v):
        return jnp.where(upper, 0.0, v)

    def put_row(v, row):
        for l in range(v.shape[1] // 128):
            flat[row + l : row + l + 1, :] = v[:, 128 * l : 128 * l + 128]

    def put_matrix(v, row, count, which, height):
        for l in range(v.shape[1] // 128):
            flat[pl.ds(row + which + l, height, stride=count), :] = v[:, 128 * l : 128 * l + 128]

    def total(v):
        return jnp.sum(v, axis=0, keepdims=True)

    last = tile(6)
    ids = second(last[:, 2 * 128 :])
    numbers = (ids[:, 0:1] * 256.0 + ids[:, 1:2]).astype(jnp.int32)
    loss_ref[...] = total(ids[:, 2:3]) + total(ids[:, 3:4]) + total(ids[:, 4:5])

    g_pre = second(tile(5))
    put_matrix(mm_tn(last[:, :FREQ].astype(BF), g_pre.astype(BF)), R_TIME_IN, 3, 0, FREQ)
    put_row(total(g_pre), R_TIME_IN_B)
    g_cond = second(tile(4))
    g_cond_low = g_cond.astype(BF)
    put_matrix(mm_tn(tile(3).astype(BF), g_cond_low), R_TIME_OUT, 3, 0, D)
    put_row(total(g_cond), R_TIME_OUT_B)
    for part in range(3):
        height = 336 if part < 2 else 329
        marks = lax.broadcasted_iota(jnp.int32, (rows, 336), 1) + 336 * part
        hits = second(jnp.where(marks == numbers, 1.0, 0.0)).astype(BF)
        put_matrix(mm_tn(hits, g_cond_low)[:height], R_CLASS + 3 * 336 * part, 3, 0, height)
    act = tile(0)
    act_first = first(act).astype(BF)
    act_second = second(act).astype(BF)
    for t in range(6):
        g = tile(1 + t)
        put_matrix(mm_tn(act_first, g.astype(BF)), R_MOD, 18, 3 * t, D)
        put_row(total(first(g)), R_MOD_B + 3 * t)
    for t in range(2):
        g = tile(1 + t)
        put_matrix(mm_tn(act_second, g.astype(BF)), R_FMOD, 6, 3 * t, D)
        put_row(total(second(g)), R_FMOD_B + 3 * t)

    for l in range(3):
        lanes = slice(128 * l, 128 * l + 128)
        flat[pl.ds(R_PATCH + l, PD, stride=3), :] = misc_ref[0:PD, lanes]
        flat[pl.ds(R_FINAL + l, PD, stride=3), :] = misc_ref[32:48, lanes]
    for at_row, row in ((16, R_PATCH_B), (17, R_QUERY_B), (18, R_VALUE_B), (19, R_PROJ_B),
                        (20, R_HIDDEN_B), (21, R_HIDDEN_B + 3), (22, R_HIDDEN_B + 6),
                        (23, R_HIDDEN_B + 9), (24, R_DOWN_B)):
        put_row(misc_ref[at_row : at_row + 1, :], row)
    rolled[0:8, :] = jnp.zeros((8, 128), F32)
    rolled[8 + ALIGN_ROWS :, :] = jnp.zeros_like(rolled[8 + ALIGN_ROWS :, :])
    rolled[7:8, :] = pltpu.roll(misc_ref[27:28, 0:128], 112, 1)
    for half in range(2):
        for l in range(3):
            rolled[pl.ds(8 + 3 * half + l, D, stride=6), :] = align_ref[half, :, 128 * l : 128 * l + 128]
            r = 8 + 2304 + 3 * half + l
            rolled[r : r + 1, :] = misc_ref[25 + half : 26 + half, 128 * l : 128 * l + 128]
    count = FLAT_ROWS - R_FINAL_B
    spot = lax.broadcasted_iota(jnp.int32, (count, 128), 1)
    here = pltpu.roll(rolled[8 : 8 + count, :], 16, 1)
    before = pltpu.roll(rolled[7 : 7 + count, :], 16, 1)
    flat[R_FINAL_B:FLAT_ROWS, :] = jnp.where(spot < 16, before, here)

    if local:
        z, x, y, c = read_coordinates(at_ref)
        size = w_ref.shape[0]
        start = pl.multiple_of(place_of(z, x, y, c) * size, 8)
        adam_step(flat[pl.ds(start, size), :], w_ref, m_ref, v_ref, upd_ref, new_m_ref, new_v_ref)


def adam_step(grad, w_ref, m_ref, v_ref, upd_ref, new_m_ref, new_v_ref):
    new_m = BETA_ONE * m_ref[...] + (1.0 - BETA_ONE) * grad
    new_v = BETA_TWO * v_ref[...] + (1.0 - BETA_TWO) * grad * grad
    new_m_ref[...] = new_m
    new_v_ref[...] = new_v
    right_m = new_m / (1.0 - BETA_ONE**STEP)
    right_v = new_v / (1.0 - BETA_TWO**STEP)
    upd_ref[...] = -ADAM_RATE * (right_m / (jnp.sqrt(right_v) + ADAM_EPS) + DECAY_RATE * w_ref[...])


ROLL_ROWS = 8 + FLAT_ROWS - R_FINAL_B + 8


def adam_near(at, parts, flat_w, m, v):
    places = gather_places(48)
    pay, align, misc = pl.pallas_call(
        functools.partial(place_kernel, places),
        name="place_gradients",
        out_shape=(shape((32, PAY, D)), shape((2, D, D)), shape((MISC, D))),
        in_specs=[SM] + [VM] * len(parts),
        out_specs=[VM] * 3,
    )(at, *parts)
    size = flat_w.shape
    loss, upd, new_m, new_v = pl.pallas_call(
        functools.partial(adam_kernel, True),
        name="adam",
        out_shape=(shape((1, 1)), shape(size), shape(size), shape(size)),
        in_specs=[VM, VM, VM, SM, VM, VM, VM],
        out_specs=[VM] * 4,
        scratch_shapes=[pltpu.VMEM((FLAT_ROWS, 128), F32), pltpu.VMEM((ROLL_ROWS, 128), F32)],
        cost_estimate=pl.CostEstimate(flops=10**9, bytes_accessed=10**7, transcendentals=0),
    )(pay, align, misc, at, flat_w, m, v)
    return loss[0, 0], upd, new_m, new_v


def adam_wide(pay, align, misc, flat_w, m, v):
    loss, flat = pl.pallas_call(
        functools.partial(adam_kernel, False),
        name="adam_gradient",
        out_shape=(shape((1, 1)), shape((FLAT_ROWS, 128))),
        in_specs=[VM] * 3,
        out_specs=[VM] * 2,
        scratch_shapes=[pltpu.VMEM((ROLL_ROWS, 128), F32)],
    )(pay, align, misc)
    size = flat_w.shape[0]
    place = lax.axis_index("dp") * lax.axis_size("shard") + lax.axis_index("shard")
    grad = lax.dynamic_slice_in_dim(flat, place * size, size, 0)
    upd, new_m, new_v = pl.pallas_call(
        lambda g, *refs: adam_step(g[...], *refs),
        name="adam",
        out_shape=(shape(flat_w.shape),) * 3,
        in_specs=[VM] * 4,
        out_specs=[VM] * 3,
    )(grad, flat_w, m, v)
    return loss[0, 0], upd, new_m, new_v


def shampoo_kernel(near, at_ref, *refs):
    if near:
        column_ref, far_ref, w_ref, sl_ref, sr_ref, rl_ref, rr_ref, upd_ref, nl_ref, nr_ref, grad = refs
        z, x, y, c = read_coordinates(at_ref)
        t = pl.program_id(0)
        for dx in range(2):
            ref = (column_ref, far_ref)[dx]
            for dz in range(4):
                for dy in range(2):
                    unit = unit_of(lax.rem(z + 4 - dz, 4), flip(x, dx), flip(y, dy))
                    rows = pl.ds(pl.multiple_of(unit * UNIT, 8), UNIT)
                    grad[rows, :] = ref[dz, dy, t].astype(F32)
        g = grad[...].astype(BF)
    else:
        grad_ref, w_ref, sl_ref, sr_ref, rl_ref, rr_ref, upd_ref, nl_ref, nr_ref = refs
        g = grad_ref[0]
    nl_ref[0] = STAT_BETA * sl_ref[0] + (1.0 - STAT_BETA) * mm_nt(g, g)
    nr_ref[0] = STAT_BETA * sr_ref[0] + (1.0 - STAT_BETA) * mm_tn(g, g)
    one, two, three = split3(rl_ref[0])
    left = mm(one, g) + (mm(two, g) + mm(three, g))
    l_one, l_two, l_three = split3(left)
    r_one, r_two, r_three = split3(rr_ref[0])
    p = mm(l_one, r_one) + (mm(l_one, r_two) + mm(l_two, r_one)) + (
        mm(l_two, r_two) + mm(l_one, r_three) + mm(l_three, r_one))
    mean = jnp.sum(jnp.sum(p * p, axis=1, keepdims=True), axis=0, keepdims=True) * (1.0 / (D * D))
    root = jnp.sqrt(mean)
    upd_ref[0] = -SHAMPOO_RATE * (p / (root + RMS_EPS) + DECAY_RATE * w_ref[0])


def shampoo(at, grads, blocks_w, stat_left, stat_right, root_left, root_right):
    near = len(grads) == 2
    slots = blocks_w.shape[0]
    one = pl.BlockSpec((1, D, D), lambda t: (t, 0, 0))
    return pl.pallas_call(
        functools.partial(shampoo_kernel, near),
        name="shampoo",
        grid=(slots,),
        out_shape=(shape((slots, D, D)),) * 3,
        in_specs=[SM] + ([VM, VM] if near else [one]) + [one] * 5,
        out_specs=[one] * 3,
        scratch_shapes=[pltpu.VMEM((D, D), F32)] if near else [],
        cost_estimate=pl.CostEstimate(flops=3 * 10**9, bytes_accessed=15 * 10**6, transcendentals=0),
    )(at, *grads, blocks_w, stat_left, stat_right, root_left, root_right)


def position_table():
    quarter = D // 4
    frequencies = 1.0 / 10000.0 ** (jnp.arange(quarter, dtype=jnp.float32) / quarter)
    cell_ids = jnp.arange(SEQ, dtype=jnp.int32)
    row_arg = (cell_ids // GRID).astype(jnp.float32)[:, None] * frequencies[None, :]
    col_arg = (cell_ids % GRID).astype(jnp.float32)[:, None] * frequencies[None, :]
    return jnp.concatenate(
        [jnp.sin(col_arg), jnp.cos(col_arg), jnp.sin(row_arg), jnp.cos(row_arg)], axis=1
    )


def time_features(tstep_idx):
    half_freq = FREQ // 2
    frequencies = jnp.exp(-math.log(10000.0) * jnp.arange(half_freq, dtype=jnp.float32) / half_freq)
    angles = (tstep_idx.astype(jnp.float32) + 0.5)[:, None] * frequencies[None, :]
    return jnp.concatenate([jnp.cos(angles), jnp.sin(angles)], axis=1)


def normalize(values):
    centered = values - jnp.mean(values, axis=-1, keepdims=True)
    inv_dev = lax.rsqrt(jnp.mean(centered * centered, axis=-1, keepdims=True) + NORM_EPS)
    return (centered * inv_dev, inv_dev)


def normalize_back(grad_in, normed, inv_dev):
    return inv_dev * (
        grad_in
        - jnp.mean(grad_in, axis=-1, keepdims=True)
        - normed * jnp.mean(grad_in * normed, axis=-1, keepdims=True)
    )


def cosine_total(aligned, dino_f):
    products = jnp.sum(aligned * dino_f, axis=-1)
    return jnp.sum(
        products
        * lax.rsqrt(jnp.sum(aligned * aligned, axis=-1) + NORM_EPS)
        * lax.rsqrt(jnp.sum(dino_f * dino_f, axis=-1) + NORM_EPS), axis=-1
    )


def row_total(rounded):
    return jnp.sum(rounded.astype(jnp.float32), axis=0)


matmul = mm


def tokens(total_img, noisy, velocity, time_weight, dino, mods, weights, blocks):
    images, seq = noisy.shape[:2]
    rows = images * seq
    bias, patch_low, final_low, align_low = weights
    patch_bias, query_bias, value_bias, proj_bias = bias[0], bias[1], bias[2], bias[3]
    hidden_bias = bias[4:8].reshape(F)
    down_bias = bias[8]
    align_bias = bias[9:11].reshape(DINO)
    final_bias = bias[11, :PD]
    final_low = final_low[:, :PD]
    w_qkv = jnp.concatenate([blocks[0], blocks[1], blocks[2]], axis=1)
    w_proj = blocks[3]
    w_up = jnp.concatenate([blocks[4], blocks[5], blocks[6], blocks[7]], axis=1)
    w_down = blocks[8:].reshape(F, D)
    (shift_one, scale_one, gate_one, shift_two, scale_two, gate_two, final_shift, final_scale) = [
        mods[:, None, which * D : (which + 1) * D] for which in range(8)
    ]
    noisy_low = noisy.astype(jnp.bfloat16).reshape(rows, PD)
    hidden0 = (matmul(noisy_low, patch_low) + patch_bias).reshape(images, seq, D) + position_table()
    norm_one, inv_one = normalize(hidden0)
    act_one = (norm_one * (1.0 + scale_one) + shift_one).astype(jnp.bfloat16).reshape(rows, D)
    qkv_bias = jnp.concatenate([query_bias, jnp.zeros((D,), jnp.float32), value_bias])
    projected = (
        (matmul(act_one, w_qkv) + qkv_bias)
        .astype(jnp.bfloat16)
        .reshape(images, seq, 3, HEADS, HDIM)
    )
    queries = projected[:, :, 0]
    key_part = projected[:, :, 1]
    values = projected[:, :, 2]
    scale_qk = HDIM ** (-0.5)
    scores = (
        jnp.einsum("gqhe,gkhe->ghqk", queries, key_part, preferred_element_type=jnp.float32)
        * scale_qk
    )
    row_max = jnp.max(scores, axis=-1, keepdims=True)
    log_total = row_max + jnp.log(jnp.sum(jnp.exp(scores - row_max), axis=-1, keepdims=True))
    probs_low = jnp.exp(scores - log_total).astype(jnp.bfloat16)
    attended = (
        jnp.einsum("ghqk,gkhe->gqhe", probs_low, values, preferred_element_type=jnp.float32)
        .reshape(rows, D)
        .astype(jnp.bfloat16)
    )
    branch_one = (matmul(attended, w_proj) + proj_bias).reshape(images, seq, D)
    hidden1 = hidden0 + gate_one * branch_one
    norm_two, inv_two = normalize(hidden1)
    act_two = (norm_two * (1.0 + scale_two) + shift_two).astype(jnp.bfloat16).reshape(rows, D)
    inner_pre = matmul(act_two, w_up) + hidden_bias
    gelu_out, gelu_back = jax.vjp(functools.partial(jax.nn.gelu, approximate=True), inner_pre)
    gelu_low = gelu_out.astype(jnp.bfloat16)
    branch_two = (matmul(gelu_low, w_down) + down_bias).reshape(images, seq, D)
    hidden2 = hidden1 + gate_two * branch_two
    norm_three, inv_three = normalize(hidden2)
    act_three = (
        (norm_three * (1.0 + final_scale) + final_shift).astype(jnp.bfloat16).reshape(rows, D)
    )
    output = (matmul(act_three, final_low) + final_bias).reshape(images, seq, PD)
    errors = output - velocity
    main_term = jnp.sum(time_weight[:, None, None] * errors * errors, axis=(1, 2)) / (total_img * SEQ * PD)
    hidden1_low = hidden1.astype(jnp.bfloat16).reshape(rows, D)
    aligned = (matmul(hidden1_low, align_low) + align_bias).reshape(images, seq, DINO)
    dino_f = dino.astype(jnp.float32)
    cosine_sum, cosine_back = jax.vjp(functools.partial(cosine_total, dino_f=dino_f), aligned)
    align_scale = REPA_WEIGHT / (total_img * SEQ)
    loss_local = main_term - align_scale * cosine_sum
    back_output = (
        (2.0 * time_weight[:, None, None] * errors / (total_img * SEQ * PD))
        .reshape(rows, PD)
        .astype(jnp.bfloat16)
    )
    grad_final = matmul(act_three.T, back_output)
    grad_final_bias = row_total(back_output)
    back_three = matmul(back_output, final_low.T).reshape(images, seq, D)
    grad_final_shift = jnp.sum(back_three, axis=1)
    grad_final_scale = jnp.sum(back_three * norm_three, axis=1)
    back_hidden2 = normalize_back(back_three * (1.0 + final_scale), norm_three, inv_three)
    back_branch_two = (back_hidden2 * gate_two).reshape(rows, D).astype(jnp.bfloat16)
    grad_gate_two = jnp.sum(back_hidden2 * branch_two, axis=1)
    grad_down = matmul(gelu_low.T, back_branch_two)
    grad_down_bias = row_total(back_branch_two)
    back_inner = gelu_back(matmul(back_branch_two, w_down.T))[0].astype(jnp.bfloat16)
    grad_up = matmul(act_two.T, back_inner)
    grad_hidden_bias = row_total(back_inner)
    back_two = matmul(back_inner, w_up.T).reshape(images, seq, D)
    grad_shift_two = jnp.sum(back_two, axis=1)
    grad_scale_two = jnp.sum(back_two * norm_two, axis=1)
    back_aligned = cosine_back(jnp.full((images,), -align_scale, jnp.float32))[0].astype(jnp.bfloat16).reshape(rows, DINO)
    grad_align = matmul(hidden1_low.T, back_aligned)
    grad_align_bias = row_total(back_aligned)
    back_hidden1 = (
        back_hidden2
        + normalize_back(back_two * (1.0 + scale_two), norm_two, inv_two)
        + matmul(back_aligned, align_low.T).reshape(images, seq, D)
    )
    back_branch_one = (back_hidden1 * gate_one).reshape(rows, D).astype(jnp.bfloat16)
    grad_gate_one = jnp.sum(back_hidden1 * branch_one, axis=1)
    grad_proj = matmul(attended.T, back_branch_one)
    grad_proj_bias = row_total(back_branch_one)
    back_attended = (
        matmul(back_branch_one, w_proj.T).astype(jnp.bfloat16).reshape(images, seq, HEADS, HDIM)
    )
    back_probs = jnp.einsum(
        "gqhe,gkhe->ghqk", back_attended, values, preferred_element_type=jnp.float32
    )
    grad_values = jnp.einsum(
        "ghqk,gqhe->gkhe", probs_low, back_attended, preferred_element_type=jnp.float32
    )
    scores_again = (
        jnp.einsum("gqhe,gkhe->ghqk", queries, key_part, preferred_element_type=jnp.float32)
        * scale_qk
    )
    probs_again = jnp.exp(scores_again - log_total)
    back_scores = (
        probs_again * (back_probs - jnp.sum(back_probs * probs_again, axis=-1, keepdims=True))
    ).astype(jnp.bfloat16)
    grad_queries = (
        jnp.einsum("ghqk,gkhe->gqhe", back_scores, key_part, preferred_element_type=jnp.float32)
        * scale_qk
    )
    grad_keys = (
        jnp.einsum("ghqk,gqhe->gkhe", back_scores, queries, preferred_element_type=jnp.float32)
        * scale_qk
    )
    back_projected = (
        jnp.stack([grad_queries, grad_keys, grad_values], axis=2)
        .reshape(rows, 3 * D)
        .astype(jnp.bfloat16)
    )
    grad_qkv = matmul(act_one.T, back_projected)
    grad_qkv_bias = row_total(back_projected)
    back_one = matmul(back_projected, w_qkv.T).reshape(images, seq, D)
    grad_shift_one = jnp.sum(back_one, axis=1)
    grad_scale_one = jnp.sum(back_one * norm_one, axis=1)
    back_hidden0 = (
        (back_hidden1 + normalize_back(back_one * (1.0 + scale_one), norm_one, inv_one))
        .reshape(rows, D)
        .astype(jnp.bfloat16)
    )
    grad_patch = matmul(noisy_low.T, back_hidden0)
    grad_patch_bias = row_total(back_hidden0)
    grad_mods = jnp.concatenate(
        [
            grad_shift_one,
            grad_scale_one,
            grad_gate_one,
            grad_shift_two,
            grad_scale_two,
            grad_gate_two,
            grad_final_shift,
            grad_final_scale,
        ],
        axis=1,
    )
    fc_ratio = F // D
    grad_model = jnp.concatenate(
        [
            grad_qkv.reshape(D, 3, D).transpose(1, 0, 2),
            grad_proj[None],
            grad_up.reshape(D, fc_ratio, D).transpose(1, 0, 2),
            grad_down.reshape(fc_ratio, D, D),
        ],
        axis=0,
    ).astype(BF)
    grad_align = grad_align.reshape(D, 2, D).transpose(1, 0, 2).astype(BF)
    zero = jnp.zeros((D,), F32)
    misc = jnp.concatenate([
        grad_patch,
        jnp.stack([grad_patch_bias, grad_qkv_bias[:D], grad_qkv_bias[2 * D :], grad_proj_bias]),
        grad_hidden_bias.reshape(4, D),
        grad_down_bias[None],
        grad_align_bias.reshape(2, D),
        jnp.pad(grad_final_bias, (0, D - PD))[None],
        jnp.zeros((4, D), F32),
        grad_final.reshape(PD, D),
        jnp.zeros((MISC - 48, D), F32),
    ]).astype(BF)
    return loss_local, grad_model, grad_align, misc, grad_mods


def payload(cond_act, th, features, grad_mods, g_cond, g_pre, class_ids, losses):
    images = cond_act.shape[0]
    one, two, three = split3(losses)
    ids = jnp.stack([(class_ids // 256).astype(F32), (class_ids % 256).astype(F32),
                     one.astype(F32), two.astype(F32), three.astype(F32)], axis=1)
    ids = jnp.pad(ids, ((0, 0), (0, 123)))
    first = jnp.concatenate([cond_act, grad_mods[:, : 6 * D]], axis=1)
    second = jnp.concatenate(
        [cond_act, grad_mods[:, 6 * D :], th, g_cond, g_pre, features, ids], axis=1)
    both = jnp.concatenate([first, second], axis=0)
    return both.reshape(2 * images, 7, D).transpose(1, 0, 2).reshape(PAY, D).astype(BF)


def body(
    noisy,
    velocity,
    tstep_idx,
    class_ids,
    time_weight,
    dino,
    owner_map,
    adam_flat,
    adam_m,
    adam_v,
    blocks_w,
    stat_left,
    stat_right,
    root_left,
    root_right,
):
    dp, group = lax.axis_size("dp"), lax.axis_size("shard")
    near = (dp, group) == (8, 4)
    images = noisy.shape[0]
    total_img = images * dp * group
    at = jnp.stack([jnp.asarray(v, jnp.int32) for v in coordinates()])
    flat_w = adam_flat.reshape(-1, 128)
    flat_m = adam_m.reshape(-1, 128)
    flat_v = adam_v.reshape(-1, 128)
    mine = flat_w.astype(BF)
    features = time_features(tstep_idx)
    rows = flat_w.shape[0]
    if near:
        cut = rows // 16 * 8 + 8 if rows // 8 % 2 else rows // 2
        pieces = gather_all(mine, cut)
        places = gather_places(cut)
        blocks = gather_blocks(at, owner_map, blocks_w.astype(BF))
    else:
        pieces = [lax.all_gather(mine, AXES, axis=0, tiled=True)[None]]
        places = [(0, lambda i, at: 0)]
        slot_low = lax.all_gather(blocks_w.astype(BF), "shard", axis=0, tiled=True)
        block_ids = jnp.arange(NBLK, dtype=jnp.int32)
        slot_of = jnp.sum(
            block_ids[:, None] * (owner_map[:, None] == block_ids[None, :]).astype(jnp.int32), axis=0
        )
        blocks = jnp.take(slot_low, slot_of, axis=0)
    (mods, pre, th, cond, mod_w, fmod_w, tout_w, align_low, bias, patch_low, final_low) = conditioning(
        at, class_ids, jnp.pad(features, ((0, 4), (0, 0))), pieces, places, rows)
    mods, pre, th, cond = mods[:images], pre[:images], th[:images], cond[:images]
    losses, grad_model, grad_align, misc, grad_mods = tokens(
        total_img, noisy, velocity, time_weight, dino, mods,
        (bias, patch_low, final_low, align_low), blocks)
    high = lax.Precision.HIGHEST
    g_act = jnp.dot(grad_mods[:, : 6 * D], mod_w.T.astype(F32), precision=high) + jnp.dot(
        grad_mods[:, 6 * D :], fmod_w.T.astype(F32), precision=high)
    g_cond = g_act * silu_slope(cond)
    g_pre = jnp.dot(g_cond, tout_w.T.astype(F32), precision=high) * silu_slope(pre)
    pay = payload(silu(cond), th, features, grad_mods, g_cond, g_pre, class_ids, losses)
    if near:
        units = jnp.concatenate([
            jnp.concatenate([grad_model.reshape(2, 6, D, D), grad_align[:, None]], axis=1)
            .reshape(2, 7, 16, UNIT, D).transpose(0, 2, 1, 3, 4).reshape(2, 16, 7 * UNIT, D),
            misc.reshape(2, 16, 8, D)], axis=2)
        owned = reduce_units(units)
        grads = gather_owned(owned[: 6 * UNIT].reshape(6, UNIT, D), owner_map)
        parts = gather_all(jnp.concatenate([pay, owned[6 * UNIT :]]), 48)
        loss, upd, new_m, new_v = adam_near(at, parts, flat_w, flat_m, flat_v)
    else:
        pays = lax.all_gather(pay, AXES, axis=0, tiled=True).reshape(dp * group, PAY, D).astype(F32)
        align_sum = lax.psum(grad_align.astype(F32), AXES)
        misc_sum = lax.psum(misc.astype(F32), AXES)
        loss, upd, new_m, new_v = adam_wide(pays, align_sum, misc_sum, flat_w, flat_m, flat_v)
        slots = jnp.take(grad_model, owner_map, axis=0)
        owned = lax.psum_scatter(slots, "shard", scatter_dimension=0, tiled=True)
        grads = [lax.psum(owned.astype(F32), "dp").astype(BF)]
    block_update, new_left, new_right = shampoo(
        at, grads, blocks_w, stat_left, stat_right, root_left, root_right)
    return (loss, block_update, new_left, new_right,
            upd.reshape(-1), new_m.reshape(-1), new_v.reshape(-1))


def solution(mesh):
    return jax.shard_map(
        body,
        mesh=mesh,
        in_specs=(
            P(("dp", "shard"), None, None),
            P(("dp", "shard"), None, None),
            P(("dp", "shard")),
            P(("dp", "shard")),
            P(("dp", "shard")),
            P(("dp", "shard"), None, None),
            P(),
            P(("dp", "shard")),
            P(("dp", "shard")),
            P(("dp", "shard")),
            P("shard", None, None),
            P("shard", None, None),
            P("shard", None, None),
            P("shard", None, None),
            P("shard", None, None),
        ),
        out_specs=(
            P(),
            P("shard", None, None),
            P("shard", None, None),
            P("shard", None, None),
            P(("dp", "shard")),
            P(("dp", "shard")),
            P(("dp", "shard")),
        ),
        check_vma=False,
    )
```

```python
import functools
import math

import jax
import jax.numpy as jnp
from jax import lax
from jax.experimental import pallas as pl
from jax.experimental.pallas import tpu as pltpu
from jax.sharding import PartitionSpec as P

D = 384
HEADS = 6
HDIM = 64
F = 1536
PD = 16
GRID = 16
SEQ = 256
FREQ = 256
NCLS = 1001
DINO = 768
STEP = 10
NBLK = 12
ADAM_LEN = 2125072
ADAM_PAD = 2129920

BETA_ONE = 0.9
BETA_TWO = 0.95
ADAM_EPS = 1e-08
ADAM_RATE = 0.01
DECAY_RATE = 0.1
STAT_BETA = 0.9
SHAMPOO_RATE = 0.02
RMS_EPS = 1e-08
REPA_WEIGHT = 0.5
NORM_EPS = 1e-06
QK_SCALE = HDIM ** (-0.5)

AXES = ("dp", "shard")
BF = jnp.bfloat16
F32 = jnp.float32
VM = pl.BlockSpec(memory_space=pltpu.VMEM)
SM = pl.BlockSpec(memory_space=pltpu.SMEM)

FLAT_ROWS = ADAM_PAD // 128
R_PATCH = 0
R_PATCH_B = 48
R_TIME_IN = 51
R_TIME_IN_B = 819
R_TIME_OUT = 822
R_TIME_OUT_B = 1974
R_CLASS = 1977
R_MOD = 4980
R_MOD_B = 11892
R_QUERY_B = 11910
R_VALUE_B = 11913
R_PROJ_B = 11916
R_HIDDEN_B = 11919
R_DOWN_B = 11931
R_FMOD = 11934
R_FMOD_B = 14238
R_FINAL = 14244
R_FINAL_B = 14292
ALIGN_ROWS = 2310

PAY = 104
PAY_CUT = 64


def shape(dims, kind=F32):
    return jax.ShapeDtypeStruct(dims, kind)


def mm(left, right):
    return jnp.dot(left, right, preferred_element_type=F32)


def mm_nt(left, right):
    return lax.dot_general(left, right, (((1,), (1,)), ((), ())), preferred_element_type=F32)


def mm_tn(left, right):
    return lax.dot_general(left, right, (((0,), (0,)), ((), ())), preferred_element_type=F32)


def silu(v):
    return v / (1.0 + jnp.exp(-v))


def silu_slope(v):
    s = 1.0 / (1.0 + jnp.exp(-v))
    return s * (1.0 + v * (1.0 - s))


def split3(v):
    one = v.astype(BF)
    rest = v - one.astype(F32)
    two = rest.astype(BF)
    return one, two, (rest - two.astype(F32)).astype(BF)


def stack3(v):
    one, two, three = split3(v)
    return jnp.concatenate([one.astype(F32), two.astype(F32), three.astype(F32)], axis=0).astype(BF)


def fold3(v):
    third = v.shape[0] // 3
    return v[:third] + v[third : 2 * third] + v[2 * third :]


def place_of(z, x, y, c):
    return ((z * 2 + x) * 2 + y) * 2 + c


def permutation(move):
    pairs = []
    for z in range(4):
        for x in range(2):
            for y in range(2):
                for c in range(2):
                    pairs.append((place_of(z, x, y, c), place_of(*move(z, x, y, c))))
    return pairs


TO_C = permutation(lambda z, x, y, c: (z, x, y, 1 - c))
TO_Y = permutation(lambda z, x, y, c: (z, x, 1 - y, c))
TO_X = permutation(lambda z, x, y, c: (z, 1 - x, y, c))
TO_Z = [permutation(lambda z, x, y, c, d=d: ((z + d) % 4, x, y, c)) for d in range(4)]


def send(value, pairs):
    return lax.ppermute(value, AXES, pairs)


def coordinates():
    dp = lax.axis_index("dp")
    sh = lax.axis_index("shard")
    return dp // 2, dp % 2, sh // 2, sh % 2


def pick(array, start, size):
    return lax.dynamic_slice_in_dim(array, start, size, 0)


def gather_all(piece, cut):
    turned = [piece] + [send(piece, TO_Z[d]) for d in (1, 2, 3)]
    first = jnp.stack([t[:cut] for t in turned])
    second = jnp.stack([t[cut:] for t in turned])
    first_x = send(first, TO_X)
    second_y = send(second, TO_Y)
    first = jnp.concatenate([first, first_x])
    second = jnp.concatenate([second, second_y])
    parts = [first, second, send(first, TO_Y), send(second, TO_X)]
    return parts + [send(p, TO_C) for p in parts]


def flip(value, bit):
    return 1 - value if bit else value


def gather_places(cut):
    def maker(dc, kind):
        def entry(i, at):
            z, x, y, c = at
            dz, far = i % 4, i // 4
            dx, dy = {0: (far, 0), 1: (0, far), 2: (far, 1), 3: (1, far)}[kind]
            return place_of(lax.rem(z + 4 - dz, 4), flip(x, dx), flip(y, dy), flip(c, dc))
        return entry

    offsets = [0, cut, 0, cut]
    return [(offsets[k], maker(dc, k)) for dc in (0, 1) for k in range(4)]


def read_coordinates(ref):
    return ref[0], ref[1], ref[2], ref[3]


def cond_kernel(places, rows, at_ref, cls_ref, feat_ref, *refs):
    count = len(places)
    pieces = refs[:count]
    (mods_ref, pre_ref, th_ref, cond_ref, modw_ref, fmodw_ref, tout_ref, align_ref, bias_ref,
     patch_ref, final_ref, flat, rolled) = refs[count:]
    at = read_coordinates(at_ref)
    for ref, (offset, entry) in zip(pieces, places):
        for i in range(ref.shape[0]):
            start = pl.multiple_of(entry(i, at) * rows + offset, 8)
            flat[pl.ds(start, ref.shape[1]), :] = ref[i].astype(F32)

    def row(first, count):
        return jnp.concatenate([flat[first + l : first + l + 1, :] for l in range(count)], axis=1)

    def columns(first, depth, count, which):
        return flat[pl.ds(first + which, depth, stride=count), :].astype(BF)

    def wide(v, first, depth, count, keep=None):
        stacked = stack3(v)
        out = []
        for j in range(count):
            w = columns(first, depth, count, j)
            if keep is not None:
                keep[:, 128 * j : 128 * j + 128] = w
            out.append(fold3(mm(stacked, w)))
        return jnp.concatenate(out, axis=1)

    pre = wide(feat_ref[...], R_TIME_IN, FREQ, 3) + row(R_TIME_IN_B, 3)
    th = silu(pre)
    picked = []
    for m in range(4):
        r = R_CLASS + 3 * cls_ref[m]
        picked.append(jnp.concatenate([flat[pl.ds(r + l, 1), :] for l in range(3)], axis=1))
    picked = jnp.concatenate(picked + [jnp.zeros((4, D), F32)], axis=0)
    cond = wide(th, R_TIME_OUT, D, 3, tout_ref) + row(R_TIME_OUT_B, 3) + picked
    act = silu(cond)
    pre_ref[...] = pre
    th_ref[...] = th
    cond_ref[...] = cond
    mods_ref[:, : 6 * D] = wide(act, R_MOD, D, 18, modw_ref) + row(R_MOD_B, 18)
    mods_ref[:, 6 * D :] = wide(act, R_FMOD, D, 6, fmodw_ref) + row(R_FMOD_B, 6)

    spot = lax.broadcasted_iota(jnp.int32, (ALIGN_ROWS, 128), 1)
    here = pltpu.roll(flat[R_FINAL_B : R_FINAL_B + ALIGN_ROWS, :], 112, 1)
    after = pltpu.roll(flat[R_FINAL_B + 1 : R_FINAL_B + 1 + ALIGN_ROWS, :], 112, 1)
    rolled[...] = jnp.where(spot < 112, here, after)
    for j in range(6):
        align_ref[:, 128 * j : 128 * j + 128] = rolled[pl.ds(j, D, stride=6), :].astype(BF)

    bias_ref[...] = jnp.zeros_like(bias_ref)
    for at_row, first in ((0, R_PATCH_B), (1, R_QUERY_B), (2, R_VALUE_B), (3, R_PROJ_B),
                          (4, R_HIDDEN_B), (5, R_HIDDEN_B + 3), (6, R_HIDDEN_B + 6),
                          (7, R_HIDDEN_B + 9), (8, R_DOWN_B)):
        bias_ref[at_row : at_row + 1, :] = row(first, 3)
    for half in range(2):
        bias_ref[9 + half : 10 + half, :] = jnp.concatenate(
            [rolled[2304 + 3 * half + l : 2305 + 3 * half + l, :] for l in range(3)], axis=1)
    lane = lax.broadcasted_iota(jnp.int32, (1, 128), 1)
    bias_ref[11:12, :128] = jnp.where(lane < PD, flat[R_FINAL_B : R_FINAL_B + 1, :], 0.0)
    patch = [flat[pl.ds(R_PATCH + l, PD, stride=3), :] for l in range(3)]
    patch_ref[...] = jnp.concatenate(patch, axis=1).astype(BF)
    spread = (lax.broadcasted_iota(jnp.int32, (D, 48), 0) // 8
              == lax.broadcasted_iota(jnp.int32, (D, 48), 1)).astype(F32).astype(BF)
    wide_rows = mm(spread, flat[R_FINAL : R_FINAL + 48, :].astype(BF))
    keep = (lax.broadcasted_iota(jnp.int32, (D, 128), 1) // PD
            == lax.broadcasted_iota(jnp.int32, (D, 128), 0) % 8)
    fold = (lax.broadcasted_iota(jnp.int32, (128, 128), 0) % PD
            == lax.broadcasted_iota(jnp.int32, (128, 128), 1)).astype(F32).astype(BF)
    final_ref[...] = mm(jnp.where(keep, wide_rows, 0.0).astype(BF), fold).astype(BF)


def conditioning(at, classes, features, pieces, places, rows):
    kernel = functools.partial(cond_kernel, places, rows)
    return pl.pallas_call(
        kernel,
        name="conditioning",
        out_shape=(shape((8, 8 * D)), shape((8, D)), shape((8, D)), shape((8, D)),
                   shape((D, 6 * D), BF), shape((D, 2 * D), BF), shape((D, D), BF),
                   shape((D, DINO), BF), shape((16, D)), shape((PD, D), BF), shape((D, 128), BF)),
        in_specs=[SM, SM, VM] + [VM] * len(pieces),
        out_specs=[VM] * 11,
        scratch_shapes=[pltpu.VMEM((FLAT_ROWS + 8, 128), F32), pltpu.VMEM((ALIGN_ROWS, 128), F32)],
        cost_estimate=pl.CostEstimate(flops=10**9, bytes_accessed=10**7, transcendentals=0),
    )(at, classes, features, *pieces)


def blocks_kernel(at_ref, own_ref, mine_ref, pair_ref, near_ref, far_ref, near_c_ref, far_c_ref, out_ref):
    z, x, y, c = read_coordinates(at_ref)
    for t in range(3):
        out_ref[own_ref[3 * (2 * y + c) + t]] = mine_ref[t]
        out_ref[own_ref[3 * (2 * y + 1 - c) + t]] = pair_ref[t]
        over = own_ref[3 * (2 * (1 - y) + c) + t]
        over_c = own_ref[3 * (2 * (1 - y) + 1 - c) + t]
        for side in range(2):
            @pl.when(x == side)
            def _():
                low, high = 192 * side, 192 * (1 - side)
                out_ref[over, low : low + 192, :] = near_ref[t]
                out_ref[over, high : high + 192, :] = far_ref[t]
                out_ref[over_c, low : low + 192, :] = near_c_ref[t]
                out_ref[over_c, high : high + 192, :] = far_c_ref[t]


def gather_blocks(at, owner_map, mine):
    x = lax.rem(lax.axis_index("dp"), 2)
    half = lax.dynamic_slice_in_dim(mine, 192 * x, 192, 1)
    near = send(half, TO_Y)
    far = send(near, TO_X)
    pair = send(mine, TO_C)
    near_c = send(near, TO_C)
    far_c = send(far, TO_C)
    return pl.pallas_call(
        blocks_kernel,
        name="gather_blocks",
        out_shape=shape((NBLK, D, D), BF),
        in_specs=[SM, SM] + [VM] * 6,
        out_specs=VM,
        cost_estimate=pl.CostEstimate(flops=0, bytes_accessed=7 * 10**6, transcendentals=0),
    )(at, owner_map, mine, pair, near, far, near_c, far_c)


UNIT = 24


def unit_of(z, x, y):
    return jnp.where(z < 2, x * 4 + y * 2 + z, 6 + y * 4 + x * 2 + z)


def add_low(left, right):
    return (left.astype(F32) + right.astype(F32)).astype(BF)


def reduce_units(units):
    z, x, y, c = coordinates()
    got = send(pick(units, 1 - c, 1)[0], TO_C)
    both = add_low(pick(units, c, 1)[0], got)
    first, second = both[:8], both[8:]
    got_x = send(pick(first, 4 * (1 - x), 4), TO_X)
    got_y = send(pick(second, 4 * (1 - y), 4), TO_Y)
    first = add_low(pick(first, 4 * x, 4), got_x)
    second = add_low(pick(second, 4 * y, 4), got_y)
    got_y = send(pick(first, 2 * (1 - y), 2), TO_Y)
    got_x = send(pick(second, 2 * (1 - x), 2), TO_X)
    quarter = jnp.concatenate(
        [add_low(pick(first, 2 * y, 2), got_y), add_low(pick(second, 2 * x, 2), got_x)])
    got = [send(pick(quarter, (z + d) % 4, 1)[0], TO_Z[d]) for d in (1, 2, 3)]
    total = pick(quarter, z, 1)[0].astype(F32)
    for g in got:
        total = total + g.astype(F32)
    return total.astype(BF)


def gather_owned(late, early, owner_map):
    z, x, y, c = coordinates()
    mine = jnp.concatenate([late, early]).reshape(6, UNIT, D)
    pair = send(mine, TO_C)
    one = jnp.where(c == 0, mine, pair)
    two = jnp.where(c == 0, pair, mine)
    whole = jnp.concatenate([one[:2], two[:2], one[2:], two[2:]])
    slots = jnp.take(whole, owner_map, axis=0).reshape(2, 2, 3, UNIT, D)
    slots = lax.dynamic_index_in_dim(slots, c, 1, keepdims=False)
    near = send(lax.dynamic_index_in_dim(slots, 1 - y, 0, keepdims=False), TO_Y)
    both = jnp.stack([lax.dynamic_index_in_dim(slots, y, 0, keepdims=False), near])
    column = jnp.stack([both] + [send(both, TO_Z[d]) for d in (1, 2, 3)])
    return column, send(column, TO_X)


def place_kernel(places, at_ref, *refs):
    pieces = refs[: len(places)]
    pay_ref, align_ref = refs[len(places) :]
    at = read_coordinates(at_ref)
    for ref, (offset, entry) in zip(pieces, places):
        for i in range(ref.shape[0]):
            dev = entry(i, at)
            z, x, y, c = dev // 8, (dev // 4) % 2, (dev // 2) % 2, dev % 2
            unit = unit_of(z, x, y)
            value = ref[i].astype(F32)
            if offset == 0:
                pay_ref[dev, 0:PAY_CUT, :] = value
            else:
                pay_ref[dev, PAY_CUT:PAY, :] = value[: PAY - PAY_CUT]
                align_ref[c, pl.ds(pl.multiple_of(unit * UNIT, 8), UNIT), :] = value[PAY - PAY_CUT :]


def adam_kernel(local, pay_ref, align_ref, *refs):
    if local:
        at_ref, w_ref, m_ref, v_ref, loss_ref, upd_ref, new_m_ref, new_v_ref, flat, rolled = refs
    else:
        loss_ref, flat, rolled = refs
    rows = 8 * pay_ref.shape[0]

    def tile(j):
        return pay_ref[:, 8 * j : 8 * j + 8, :].astype(F32).reshape(rows, D)

    upper = lax.broadcasted_iota(jnp.int32, (rows, 1), 0) % 8 < 4

    def first(v):
        return jnp.where(upper, v, 0.0)

    def second(v):
        return jnp.where(upper, 0.0, v)

    def put_row(v, row):
        for l in range(v.shape[1] // 128):
            flat[row + l : row + l + 1, :] = v[:, 128 * l : 128 * l + 128]

    def put_matrix(v, row, count, which, height):
        for l in range(v.shape[1] // 128):
            flat[pl.ds(row + which + l, height, stride=count), :] = v[:, 128 * l : 128 * l + 128]

    def total(v):
        return jnp.sum(v, axis=0, keepdims=True)

    last = tile(6)
    ids = second(last[:, 2 * 128 :])
    numbers = (ids[:, 0:1] * 256.0 + ids[:, 1:2]).astype(jnp.int32)
    loss_ref[...] = total(ids[:, 2:3]) + total(ids[:, 3:4]) + total(ids[:, 4:5])

    g_pre = second(tile(5))
    put_matrix(mm_tn(last[:, :FREQ].astype(BF), g_pre.astype(BF)), R_TIME_IN, 3, 0, FREQ)
    put_row(total(g_pre), R_TIME_IN_B)
    g_cond = second(tile(4))
    g_cond_low = g_cond.astype(BF)
    put_matrix(mm_tn(tile(3).astype(BF), g_cond_low), R_TIME_OUT, 3, 0, D)
    put_row(total(g_cond), R_TIME_OUT_B)
    for part in range(3):
        height = 336 if part < 2 else 329
        marks = lax.broadcasted_iota(jnp.int32, (rows, 336), 1) + 336 * part
        hits = second(jnp.where(marks == numbers, 1.0, 0.0)).astype(BF)
        put_matrix(mm_tn(hits, g_cond_low)[:height], R_CLASS + 3 * 336 * part, 3, 0, height)
    act = tile(0)
    act_first = first(act).astype(BF)
    act_second = second(act).astype(BF)
    for t in range(6):
        g = tile(1 + t)
        put_matrix(mm_tn(act_first, g.astype(BF)), R_MOD, 18, 3 * t, D)
        put_row(total(first(g)), R_MOD_B + 3 * t)
    for t in range(2):
        g = tile(1 + t)
        put_matrix(mm_tn(act_second, g.astype(BF)), R_FMOD, 6, 3 * t, D)
        put_row(total(second(g)), R_FMOD_B + 3 * t)

    sums = jnp.sum(pay_ref[:, 56:PAY, :].astype(F32), axis=0)
    for l in range(3):
        lanes = slice(128 * l, 128 * l + 128)
        flat[pl.ds(R_PATCH + l, PD, stride=3), :] = sums[24:40, lanes]
        flat[R_FINAL + 16 * l : R_FINAL + 16 * l + 16, :] = sums[0:16, lanes]
    for at_row, row in ((40, R_PATCH_B), (41, R_QUERY_B), (42, R_VALUE_B), (43, R_PROJ_B),
                        (16, R_HIDDEN_B), (17, R_HIDDEN_B + 3), (18, R_HIDDEN_B + 6),
                        (19, R_HIDDEN_B + 9), (20, R_DOWN_B)):
        put_row(sums[at_row : at_row + 1, :], row)
    rolled[0:8, :] = jnp.zeros((8, 128), F32)
    rolled[8 + ALIGN_ROWS :, :] = jnp.zeros_like(rolled[8 + ALIGN_ROWS :, :])
    rolled[7:8, :] = pltpu.roll(sums[23:24, 0:128], 112, 1)
    for half in range(2):
        for l in range(3):
            lanes = slice(128 * l, 128 * l + 128)
            rolled[pl.ds(8 + 3 * half + l, D, stride=6), :] = align_ref[half, :, lanes].astype(F32)
            r = 8 + 2304 + 3 * half + l
            rolled[r : r + 1, :] = sums[21 + half : 22 + half, lanes]
    count = FLAT_ROWS - R_FINAL_B
    spot = lax.broadcasted_iota(jnp.int32, (count, 128), 1)
    here = pltpu.roll(rolled[8 : 8 + count, :], 16, 1)
    before = pltpu.roll(rolled[7 : 7 + count, :], 16, 1)
    flat[R_FINAL_B:FLAT_ROWS, :] = jnp.where(spot < 16, before, here)

    if local:
        z, x, y, c = read_coordinates(at_ref)
        size = w_ref.shape[0]
        start = pl.multiple_of(place_of(z, x, y, c) * size, 8)
        adam_step(flat[pl.ds(start, size), :], w_ref, m_ref, v_ref, upd_ref, new_m_ref, new_v_ref)


def adam_step(grad, w_ref, m_ref, v_ref, upd_ref, new_m_ref, new_v_ref):
    new_m = BETA_ONE * m_ref[...] + (1.0 - BETA_ONE) * grad
    new_v = BETA_TWO * v_ref[...] + (1.0 - BETA_TWO) * grad * grad
    new_m_ref[...] = new_m
    new_v_ref[...] = new_v
    right_m = new_m / (1.0 - BETA_ONE**STEP)
    right_v = new_v / (1.0 - BETA_TWO**STEP)
    upd_ref[...] = -ADAM_RATE * (right_m / (jnp.sqrt(right_v) + ADAM_EPS) + DECAY_RATE * w_ref[...])


ROLL_ROWS = 8 + FLAT_ROWS - R_FINAL_B + 8


def adam_near(at, parts, flat_w, m, v):
    places = gather_places(PAY_CUT)
    pay, align = pl.pallas_call(
        functools.partial(place_kernel, places),
        name="place_gradients",
        out_shape=(shape((32, PAY, D)), shape((2, D, D))),
        in_specs=[SM] + [VM] * len(parts),
        out_specs=[VM] * 2,
    )(at, *parts)
    size = flat_w.shape
    loss, upd, new_m, new_v = pl.pallas_call(
        functools.partial(adam_kernel, True),
        name="adam",
        out_shape=(shape((1, 1)), shape(size), shape(size), shape(size)),
        in_specs=[VM, VM, SM, VM, VM, VM],
        out_specs=[VM] * 4,
        scratch_shapes=[pltpu.VMEM((FLAT_ROWS, 128), F32), pltpu.VMEM((ROLL_ROWS, 128), F32)],
        cost_estimate=pl.CostEstimate(flops=10**9, bytes_accessed=10**7, transcendentals=0),
    )(pay, align, at, flat_w, m, v)
    return loss[0, 0], upd, new_m, new_v


def adam_wide(pay, align, flat_w, m, v):
    loss, flat = pl.pallas_call(
        functools.partial(adam_kernel, False),
        name="adam_gradient",
        out_shape=(shape((1, 1)), shape((FLAT_ROWS, 128))),
        in_specs=[VM] * 2,
        out_specs=[VM] * 2,
        scratch_shapes=[pltpu.VMEM((ROLL_ROWS, 128), F32)],
    )(pay, align)
    size = flat_w.shape[0]
    place = lax.axis_index("dp") * lax.axis_size("shard") + lax.axis_index("shard")
    grad = lax.dynamic_slice_in_dim(flat, place * size, size, 0)
    upd, new_m, new_v = pl.pallas_call(
        lambda g, *refs: adam_step(g[...], *refs),
        name="adam",
        out_shape=(shape(flat_w.shape),) * 3,
        in_specs=[VM] * 4,
        out_specs=[VM] * 3,
    )(grad, flat_w, m, v)
    return loss[0, 0], upd, new_m, new_v


def shampoo_kernel(near, at_ref, *refs):
    if near:
        column_ref, far_ref, w_ref, sl_ref, sr_ref, rl_ref, rr_ref, upd_ref, nl_ref, nr_ref, grad = refs
        z, x, y, c = read_coordinates(at_ref)
        t = pl.program_id(0)
        for dx in range(2):
            ref = (column_ref, far_ref)[dx]
            for dz in range(4):
                for dy in range(2):
                    unit = unit_of(lax.rem(z + 4 - dz, 4), flip(x, dx), flip(y, dy))
                    rows = pl.ds(pl.multiple_of(unit * UNIT, 8), UNIT)
                    grad[rows, :] = ref[dz, dy, t].astype(F32)
        g = grad[...].astype(BF)
    else:
        grad_ref, w_ref, sl_ref, sr_ref, rl_ref, rr_ref, upd_ref, nl_ref, nr_ref = refs
        g = grad_ref[0]
    nl_ref[0] = STAT_BETA * sl_ref[0] + (1.0 - STAT_BETA) * mm_nt(g, g)
    nr_ref[0] = STAT_BETA * sr_ref[0] + (1.0 - STAT_BETA) * mm_tn(g, g)
    one, two, three = split3(rl_ref[0])
    left = mm(one, g) + (mm(two, g) + mm(three, g))
    l_one, l_two, l_three = split3(left)
    r_one, r_two, r_three = split3(rr_ref[0])
    p = mm(l_one, r_one) + (mm(l_one, r_two) + mm(l_two, r_one)) + (
        mm(l_two, r_two) + mm(l_one, r_three) + mm(l_three, r_one))
    mean = jnp.sum(jnp.sum(p * p, axis=1, keepdims=True), axis=0, keepdims=True) * (1.0 / (D * D))
    root = jnp.sqrt(mean)
    upd_ref[0] = -SHAMPOO_RATE * (p / (root + RMS_EPS) + DECAY_RATE * w_ref[0])


def shampoo(at, grads, blocks_w, stat_left, stat_right, root_left, root_right):
    near = len(grads) == 2
    slots = blocks_w.shape[0]
    one = pl.BlockSpec((1, D, D), lambda t: (t, 0, 0))
    return pl.pallas_call(
        functools.partial(shampoo_kernel, near),
        name="shampoo",
        grid=(slots,),
        out_shape=(shape((slots, D, D)),) * 3,
        in_specs=[SM] + ([VM, VM] if near else [one]) + [one] * 5,
        out_specs=[one] * 3,
        scratch_shapes=[pltpu.VMEM((D, D), F32)] if near else [],
        cost_estimate=pl.CostEstimate(flops=3 * 10**9, bytes_accessed=15 * 10**6, transcendentals=0),
    )(at, *grads, blocks_w, stat_left, stat_right, root_left, root_right)


GELU_C = math.sqrt(2.0 / math.pi)
GELU_D = 0.044715
EARLY = 5 * 24
LATE = 2 * 24
SUMS_MLP = 24
SUMS_ATT = 24


def norm_stats(v):
    centered = v - jnp.sum(v, axis=-1, keepdims=True) * (1.0 / D)
    inv = lax.rsqrt(jnp.sum(centered * centered, axis=-1, keepdims=True) * (1.0 / D) + NORM_EPS)
    return centered * inv, inv


def norm_back(g, normed, inv):
    mean_g = jnp.sum(g, axis=-1, keepdims=True) * (1.0 / D)
    mean_gn = jnp.sum(g * normed, axis=-1, keepdims=True) * (1.0 / D)
    return inv * (g - mean_g - normed * mean_gn)


def column_sum(v):
    return jnp.sum(v, axis=0, keepdims=True)


def head(v, h):
    return v[:, HDIM * h : HDIM * h + HDIM]


def front_kernel(noisy_ref, mods_ref, bias_ref, patch_ref, pos_ref, w_ref,
                 h0_ref, qkv_ref, att_ref, h1_ref):
    i = pl.program_id(0)

    def mod(t):
        return mods_ref[pl.ds(i, 1), D * t : D * t + D]

    h0 = mm(noisy_ref[0].astype(BF), patch_ref[...]) + bias_ref[0:1, :] + pos_ref[...]
    h0_ref[0] = h0
    normed, _ = norm_stats(h0)
    act = (normed * (1.0 + mod(1)) + mod(0)).astype(BF)
    q = (mm(act, w_ref[0]) + bias_ref[1:2, :]).astype(BF)
    k = mm(act, w_ref[1]).astype(BF)
    v = (mm(act, w_ref[2]) + bias_ref[2:3, :]).astype(BF)
    qkv_ref[0, :, 0:D] = q
    qkv_ref[0, :, D : 2 * D] = k
    qkv_ref[0, :, 2 * D :] = v
    outs = []
    for h in range(HEADS):
        s = mm_nt(head(q, h), head(k, h)) * QK_SCALE
        e = jnp.exp(s - jnp.max(s, axis=-1, keepdims=True))
        p = e * (1.0 / jnp.sum(e, axis=-1, keepdims=True))
        outs.append(mm(p.astype(BF), head(v, h)))
    att = jnp.concatenate(outs, axis=1).astype(BF)
    att_ref[0] = att
    h1_ref[0] = h0 + mod(2) * (mm(att, w_ref[3]) + bias_ref[3:4, :])


def middle_kernel(images, total_img, tw_ref, h1_ref, vel_ref, dino_ref, mods_ref, bias_ref, w_ref, aw_ref, fw_ref,
                  bh1_ref, gm_ref, units_ref, sums_ref,
                  act2_s, gelu_s, slope_s, bi_s, bb2_s, h1_s, ba_s, act3_s, bo_s):
    i = pl.program_id(0)
    rows = pl.ds(pl.multiple_of(i * SEQ, SEQ), SEQ)

    def mod(t):
        return mods_ref[pl.ds(i, 1), D * t : D * t + D]

    @pl.when(i == 0)
    def _():
        sums_ref[...] = jnp.zeros_like(sums_ref)

    h1 = h1_ref[0]
    n2, inv2 = norm_stats(h1)
    act2 = (n2 * (1.0 + mod(4)) + mod(3)).astype(BF)
    act2_s[rows, :] = act2
    branch = jnp.zeros((SEQ, D), F32) + bias_ref[8:9, :]
    for j in range(4):
        lanes = slice(D * j, D * j + D)
        x = mm(act2, w_ref[4 + j]) + bias_ref[4 + j : 5 + j, :]
        xx = x * x
        t = jnp.tanh(x * (GELU_C + (GELU_C * GELU_D) * xx))
        half = 0.5 + 0.5 * t
        g = (x * half).astype(BF)
        slope_s[:, lanes] = half + (0.5 * x) * (1.0 - t * t) * (GELU_C + (3.0 * GELU_C * GELU_D) * xx)
        gelu_s[rows, lanes] = g
        branch = branch + mm(g, w_ref[8 + j])
    h2 = h1 + mod(5) * branch
    n3, inv3 = norm_stats(h2)
    act3 = (n3 * (1.0 + mod(7)) + mod(6)).astype(BF)
    act3_s[rows, :] = act3
    out = mm(act3, fw_ref[...]) + bias_ref[11:12, 0:128]
    err = out[:, :PD] - vel_ref[0]
    weight = tw_ref[i]
    loss = jnp.sum(column_sum(err * err), axis=1, keepdims=True) * (weight / (total_img * SEQ * PD))
    bo = jnp.concatenate([err * (2.0 * weight / (total_img * SEQ * PD)), jnp.zeros((SEQ, 128 - PD), F32)],
                         axis=1).astype(BF)
    bo_s[rows, :] = bo

    h1_low = h1.astype(BF)
    h1_s[rows, :] = h1_low
    aligned = mm(h1_low, aw_ref[...]) + jnp.concatenate([bias_ref[9:10, :], bias_ref[10:11, :]], axis=1)
    dino = dino_ref[0].astype(F32)
    dot = jnp.sum(aligned * dino, axis=-1, keepdims=True)
    ra = lax.rsqrt(jnp.sum(aligned * aligned, axis=-1, keepdims=True) + NORM_EPS)
    rd = lax.rsqrt(jnp.sum(dino * dino, axis=-1, keepdims=True) + NORM_EPS)
    scale = REPA_WEIGHT / (total_img * SEQ)
    both = ra * rd
    cosine = dot * both
    loss = loss - column_sum(cosine) * scale
    ba = (dino * (both * -scale) + aligned * (cosine * (ra * ra) * scale)).astype(BF)
    ba_s[rows, :] = ba
    through = mm_nt(ba, aw_ref[...])

    b3 = mm_nt(bo, fw_ref[...])
    bh2 = norm_back(b3 * (1.0 + mod(7)), n3, inv3)
    bb2 = (bh2 * mod(5)).astype(BF)
    bb2_s[rows, :] = bb2
    b2 = jnp.zeros((SEQ, D), F32)
    for j in range(4):
        lanes = slice(D * j, D * j + D)
        bi = (mm_nt(bb2, w_ref[8 + j]) * slope_s[:, lanes]).astype(BF)
        bi_s[rows, lanes] = bi
        sums_ref[16 + j : 17 + j, :] += column_sum(bi.astype(F32))
        b2 = b2 + mm_nt(bi, w_ref[4 + j])
    sums_ref[20:21, :] += column_sum(bb2.astype(F32))
    ba_sum = column_sum(ba.astype(F32))
    sums_ref[21:22, :] += ba_sum[:, :D]
    sums_ref[22:23, :] += ba_sum[:, D:]
    sums_ref[23:24, 0:128] += column_sum(bo.astype(F32))
    bh1_ref[0] = bh2 + norm_back(b2 * (1.0 + mod(4)), n2, inv2) + through
    gm_ref[0, 0:1, :] = column_sum(b2)
    gm_ref[0, 1:2, :] = column_sum(b2 * n2)
    gm_ref[0, 2:3, :] = column_sum(bh2 * branch)
    gm_ref[0, 3:4, :] = column_sum(b3)
    gm_ref[0, 4:5, :] = column_sum(b3 * n3)
    gm_ref[0, 5:6, :] = jnp.broadcast_to(loss, (1, D))
    gm_ref[0, 6:8, :] = jnp.zeros((2, D), F32)

    @pl.when(i == images - 1)
    def _():
        def put(part, j, g):
            g = g.astype(BF)
            for u in range(16):
                units_ref[part, u, 24 * j : 24 * j + 24, :] = g[24 * u : 24 * u + 24, :]

        for j in range(4):
            lanes = slice(D * j, D * j + D)
            put(0, j, mm_tn(act2_s[...], bi_s[:, lanes]))
            put(1, j, mm_tn(gelu_s[:, lanes], bb2_s[...]))
        for p in range(2):
            put(p, 4, mm_tn(h1_s[...], ba_s[:, D * p : D * p + D]))
        g = mm_tn(act3_s[...], bo_s[...]).astype(BF)
        spread = (lax.broadcasted_iota(jnp.int32, (128, 128), 1) % PD
                  == lax.broadcasted_iota(jnp.int32, (128, 128), 0)).astype(F32).astype(BF)
        keep = (lax.broadcasted_iota(jnp.int32, (D, 128), 1) // PD
                == lax.broadcasted_iota(jnp.int32, (D, 128), 0) % 8)
        fold = (lax.broadcasted_iota(jnp.int32, (48, D), 1) // 8
                == lax.broadcasted_iota(jnp.int32, (48, D), 0)).astype(F32).astype(BF)
        flat = mm(fold, jnp.where(keep, mm(g, spread), 0.0).astype(BF))
        for l in range(3):
            sums_ref[0:16, 128 * l : 128 * l + 128] = flat[16 * l : 16 * l + 16, :]


def back_kernel(bh1_ref, h0_ref, qkv_ref, att_ref, mods_ref, bias_ref, w_ref, first,
                bb1_ref, bp_ref, act_ref, bh0_ref, gm_ref):
    i = pl.program_id(0) + first

    def mod(t):
        return mods_ref[pl.ds(i, 1), D * t : D * t + D]

    bh1 = bh1_ref[0]
    att = att_ref[0]
    bb1 = (bh1 * mod(2)).astype(BF)
    bb1_ref[0] = bb1
    gm_ref[0, 2:3, :] = column_sum(bh1 * (mm(att, w_ref[3]) + bias_ref[3:4, :]))
    batt = mm_nt(bb1, w_ref[3]).astype(BF)
    q, k, v = qkv_ref[0, :, 0:D], qkv_ref[0, :, D : 2 * D], qkv_ref[0, :, 2 * D :]
    gq, gk, gv = [], [], []
    for h in range(HEADS):
        qh, kh, vh, bh = head(q, h), head(k, h), head(v, h), head(batt, h)
        s = mm_nt(kh, qh) * QK_SCALE
        e = jnp.exp(s - jnp.max(s, axis=0, keepdims=True))
        p = e * (1.0 / column_sum(e))
        dp = mm_nt(vh, bh)
        ds = (p * (dp - column_sum(dp * p))).astype(BF)
        gv.append(mm(p.astype(BF), bh))
        gk.append(mm(ds, qh))
        gq.append(mm_tn(ds, kh))
    bq = (jnp.concatenate(gq, axis=1) * QK_SCALE).astype(BF)
    bk = (jnp.concatenate(gk, axis=1) * QK_SCALE).astype(BF)
    bv = jnp.concatenate(gv, axis=1).astype(BF)
    bp_ref[0, :, 0:D] = bq
    bp_ref[0, :, D : 2 * D] = bk
    bp_ref[0, :, 2 * D :] = bv
    b1 = mm_nt(bq, w_ref[0]) + mm_nt(bk, w_ref[1]) + mm_nt(bv, w_ref[2])
    n1, inv1 = norm_stats(h0_ref[0])
    act_ref[0] = (n1 * (1.0 + mod(1)) + mod(0)).astype(BF)
    gm_ref[0, 0:1, :] = column_sum(b1)
    gm_ref[0, 1:2, :] = column_sum(b1 * n1)
    bh0 = (bh1 + norm_back(b1 * (1.0 + mod(1)), n1, inv1)).astype(BF)
    bh0_ref[0] = bh0
    gm_ref[0, 3:4, :] = column_sum(bh0.astype(F32))
    gm_ref[0, 4:5, :] = column_sum(bq.astype(F32))
    gm_ref[0, 5:6, :] = column_sum(bv.astype(F32))
    gm_ref[0, 6:7, :] = column_sum(bb1.astype(F32))
    gm_ref[0, 7:8, :] = jnp.zeros((1, D), F32)


def last_kernel(act_ref, bp_ref, att_ref, bb1_ref, noisy_ref, bh0_ref, units_ref, patch_ref):
    def put(part, j, g):
        g = g.astype(BF)
        for u in range(16):
            units_ref[part, u, 24 * j : 24 * j + 24, :] = g[24 * u : 24 * u + 24, :]

    act = act_ref[...]
    put(0, 0, mm_tn(act, bp_ref[:, 0:D]))
    put(0, 1, mm_tn(act, bp_ref[:, D : 2 * D]))
    put(1, 0, mm_tn(act, bp_ref[:, 2 * D :]))
    put(1, 1, mm_tn(att_ref[...], bb1_ref[...]))
    patch_ref[...] = mm_tn(noisy_ref[...].astype(BF), bh0_ref[...])


def cond_back_kernel(images, cls_ref, gm2_ref, gm3_ref, pre_ref, th_ref, cond_ref, feat_ref, modw_ref, fmodw_ref,
                     tout_ref, sums_ref, patch_ref, pay_ref):
    none = jnp.zeros((4, D), F32)

    def rows_of(ref, r):
        return jnp.concatenate([ref[m, r : r + 1, :] for m in range(images)] + [none], axis=0)

    tiles = [rows_of(gm3_ref, 0), rows_of(gm3_ref, 1), rows_of(gm3_ref, 2),
             rows_of(gm2_ref, 0), rows_of(gm2_ref, 1), rows_of(gm2_ref, 2)]
    finals = [rows_of(gm2_ref, 3), rows_of(gm2_ref, 4)]
    g_act = jnp.zeros((24, D), F32)
    for t in range(6):
        g_act = g_act + mm_nt(stack3(tiles[t]), modw_ref[:, D * t : D * t + D])
    for t in range(2):
        g_act = g_act + mm_nt(stack3(finals[t]), fmodw_ref[:, D * t : D * t + D])
    cond = cond_ref[...]
    g_cond = fold3(g_act) * silu_slope(cond)
    g_pre = fold3(mm_nt(stack3(g_cond), tout_ref[...])) * silu_slope(pre_ref[...])
    act = silu(cond)
    lane = lax.broadcasted_iota(jnp.int32, (1, 128), 1)
    ids = []
    for m in range(images):
        one, two, three = split3(gm2_ref[m, 5:6, 0:128])
        number = cls_ref[m]
        row = jnp.where(lane == 0, (number // 256).astype(F32), 0.0)
        row = jnp.where(lane == 1, (number % 256).astype(F32), row)
        row = jnp.where(lane == 2, one.astype(F32), row)
        row = jnp.where(lane == 3, two.astype(F32), row)
        ids.append(jnp.where(lane == 4, three.astype(F32), row))
    ids = jnp.concatenate(ids, axis=0)
    first = [act] + tiles
    second = [act] + finals + [th_ref[...], g_cond, g_pre]
    for j in range(6):
        pay_ref[8 * j : 8 * j + 8, :] = jnp.concatenate([first[j][:4], second[j][:4]], axis=0).astype(BF)
    tail = jnp.concatenate([feat_ref[0:4, :], ids], axis=1)
    pay_ref[48:56, :] = jnp.concatenate([first[6][:4], tail], axis=0).astype(BF)
    pay_ref[56:80, :] = sums_ref[...].astype(BF)
    pay_ref[80:96, :] = patch_ref[...].astype(BF)

    def over(r):
        total = gm3_ref[0, r : r + 1, :]
        for m in range(1, images):
            total = total + gm3_ref[m, r : r + 1, :]
        return total

    rest = [over(3), over(4), over(5), over(6), jnp.zeros((4, D), F32)]
    pay_ref[96:104, :] = jnp.concatenate(rest, axis=0).astype(BF)


def cost(flops, moved):
    return pl.CostEstimate(flops=int(flops), bytes_accessed=int(moved), transcendentals=0)


def tokens(total_img, noisy, velocity, time_weight, dino, mods, weights, blocks):
    images = noisy.shape[0]
    bias, patch_low, final_low, align_low = weights
    each = lambda *dims: pl.BlockSpec((1,) + dims, lambda i: (i,) + (0,) * len(dims))
    pos = position_table()
    h0, qkv, att, h1 = pl.pallas_call(
        front_kernel,
        name="front",
        grid=(images,),
        out_shape=(shape((images, SEQ, D)), shape((images, SEQ, 3 * D), BF),
                   shape((images, SEQ, D), BF), shape((images, SEQ, D))),
        in_specs=[each(SEQ, PD), VM, VM, VM, VM, VM],
        out_specs=[each(SEQ, D), each(SEQ, 3 * D), each(SEQ, D), each(SEQ, D)],
        cost_estimate=cost(2.2e9, 1.2e7),
    )(noisy, mods, bias, patch_low, pos, blocks)
    full = lambda lanes, kind=BF: pltpu.VMEM((images * SEQ, lanes), kind)
    bh1, gm2, early, sums = pl.pallas_call(
        functools.partial(middle_kernel, images, total_img),
        name="middle",
        grid=(images,),
        out_shape=(shape((images, SEQ, D)), shape((images, 8, D)),
                   shape((2, 16, EARLY, D), BF), shape((SUMS_MLP, D))),
        in_specs=[SM, each(SEQ, D), each(SEQ, PD), each(SEQ, DINO), VM, VM, VM, VM, VM],
        out_specs=[each(SEQ, D), each(8, D), VM, VM],
        scratch_shapes=[full(D), full(F), pltpu.VMEM((SEQ, F), F32), full(F), full(D), full(D),
                        full(DINO), full(D), full(128)],
        cost_estimate=cost(9e9, 1.4e7),
    )(time_weight, h1, velocity, dino, mods, bias, blocks, align_low, final_low)
    return h0, qkv, att, bh1, gm2, early, sums


def attention_back(images, first, count, bh1, h0, qkv, att, mods, bias, blocks):
    each = lambda *dims: pl.BlockSpec((1,) + dims, lambda i: (i + first,) + (0,) * len(dims))
    out = lambda *dims: pl.BlockSpec((1,) + dims, lambda i: (i,) + (0,) * len(dims))

    def kernel(*refs):
        back_kernel(*refs[:7], first, *refs[7:])

    return pl.pallas_call(
        kernel,
        name="attention_back",
        grid=(count,),
        out_shape=(shape((count, SEQ, D), BF), shape((count, SEQ, 3 * D), BF), shape((count, SEQ, D), BF),
                   shape((count, SEQ, D), BF), shape((count, 8, D))),
        in_specs=[each(SEQ, D), each(SEQ, D), each(SEQ, 3 * D), each(SEQ, D), VM, VM, VM],
        out_specs=[out(SEQ, D), out(SEQ, 3 * D), out(SEQ, D), out(SEQ, D), out(8, D)],
        cost_estimate=cost(1.2e9 * count, 3e6 * count),
    )(bh1, h0, qkv, att, mods, bias, blocks)


def last_gradients(act, bp, att, bb1, noisy, bh0):
    flat = lambda v: v.reshape(-1, v.shape[-1])
    return pl.pallas_call(
        last_kernel,
        name="last_gradients",
        out_shape=(shape((2, 16, LATE, D), BF), shape((PD, D))),
        in_specs=[VM] * 6,
        out_specs=[VM] * 2,
        cost_estimate=cost(1.2e9, 9e6),
    )(*map(flat, (act, bp, att, bb1, noisy, bh0)))


def cond_back(images, class_ids, gm2, gm3, pre, th, cond, features, mod_w, fmod_w, tout_w, sums, patch):
    return pl.pallas_call(
        functools.partial(cond_back_kernel, images),
        name="cond_back",
        out_shape=shape((PAY, D), BF),
        in_specs=[SM] + [VM] * 11,
        out_specs=VM,
        cost_estimate=cost(1e8, 4e6),
    )(class_ids, gm2, gm3, pre, th, cond, features, mod_w, fmod_w, tout_w, sums, patch)


def position_table():
    quarter = D // 4
    frequencies = 1.0 / 10000.0 ** (jnp.arange(quarter, dtype=jnp.float32) / quarter)
    cell_ids = jnp.arange(SEQ, dtype=jnp.int32)
    row_arg = (cell_ids // GRID).astype(jnp.float32)[:, None] * frequencies[None, :]
    col_arg = (cell_ids % GRID).astype(jnp.float32)[:, None] * frequencies[None, :]
    return jnp.concatenate(
        [jnp.sin(col_arg), jnp.cos(col_arg), jnp.sin(row_arg), jnp.cos(row_arg)], axis=1
    )


def time_features(tstep_idx):
    half_freq = FREQ // 2
    frequencies = jnp.exp(-math.log(10000.0) * jnp.arange(half_freq, dtype=jnp.float32) / half_freq)
    angles = (tstep_idx.astype(jnp.float32) + 0.5)[:, None] * frequencies[None, :]
    return jnp.concatenate([jnp.cos(angles), jnp.sin(angles)], axis=1)


def body(
    noisy,
    velocity,
    tstep_idx,
    class_ids,
    time_weight,
    dino,
    owner_map,
    adam_flat,
    adam_m,
    adam_v,
    blocks_w,
    stat_left,
    stat_right,
    root_left,
    root_right,
):
    dp, group = lax.axis_size("dp"), lax.axis_size("shard")
    near = (dp, group) == (8, 4)
    images = noisy.shape[0]
    total_img = images * dp * group
    at = jnp.stack([jnp.asarray(v, jnp.int32) for v in coordinates()])
    flat_w = adam_flat.reshape(-1, 128)
    flat_m = adam_m.reshape(-1, 128)
    flat_v = adam_v.reshape(-1, 128)
    mine = flat_w.astype(BF)
    features = jnp.pad(time_features(tstep_idx), ((0, 4), (0, 0)))
    rows = flat_w.shape[0]
    if near:
        cut = rows // 16 * 8 + 8 if rows // 8 % 2 else rows // 2
        pieces = gather_all(mine, cut)
        places = gather_places(cut)
        blocks = gather_blocks(at, owner_map, blocks_w.astype(BF))
    else:
        pieces = [lax.all_gather(mine, AXES, axis=0, tiled=True)[None]]
        places = [(0, lambda i, at: 0)]
        slot_low = lax.all_gather(blocks_w.astype(BF), "shard", axis=0, tiled=True)
        block_ids = jnp.arange(NBLK, dtype=jnp.int32)
        slot_of = jnp.sum(
            block_ids[:, None] * (owner_map[:, None] == block_ids[None, :]).astype(jnp.int32), axis=0
        )
        blocks = jnp.take(slot_low, slot_of, axis=0)
    (mods, pre, th, cond, mod_w, fmod_w, tout_w, align_low, bias, patch_low, final_low) = conditioning(
        at, class_ids, features, pieces, places, rows)
    h0, qkv, att, bh1, gm2, early, sums = tokens(
        total_img, noisy, velocity, time_weight, dino, mods,
        (bias, patch_low, final_low, align_low), blocks)
    if near:
        early = reduce_units(early)
    half = images // 2
    backs = [
        attention_back(images, first, count, bh1, h0, qkv, att, mods, bias, blocks)
        for first, count in ((0, half), (half, images - half))
    ]
    bb1, bp, act, bh0, gm3 = [jnp.concatenate(pair) for pair in zip(*backs)]
    late, patch = last_gradients(act, bp, att, bb1, noisy, bh0)
    pay = cond_back(images, class_ids, gm2, gm3, pre, th, cond, features, mod_w, fmod_w, tout_w, sums, patch)
    if near:
        late = reduce_units(late)
        grads = gather_owned(late, early[: 4 * UNIT], owner_map)
        parts = gather_all(jnp.concatenate([pay, early[4 * UNIT :]]), PAY_CUT)
        loss, upd, new_m, new_v = adam_near(at, parts, flat_w, flat_m, flat_v)
    else:
        early = early.reshape(2, 16, 5, UNIT, D).transpose(0, 2, 1, 3, 4).reshape(2, 5, D, D)
        late = late.reshape(2, 16, 2, UNIT, D).transpose(0, 2, 1, 3, 4).reshape(4, D, D)
        grad_model = jnp.concatenate([late, early[:, :4].reshape(8, D, D)])
        pays = lax.all_gather(pay, AXES, axis=0, tiled=True).reshape(dp * group, PAY, D)
        align_sum = lax.psum(early[:, 4].astype(F32), AXES)
        loss, upd, new_m, new_v = adam_wide(pays, align_sum, flat_w, flat_m, flat_v)
        slots = jnp.take(grad_model, owner_map, axis=0)
        owned = lax.psum_scatter(slots, "shard", scatter_dimension=0, tiled=True)
        grads = [lax.psum(owned.astype(F32), "dp").astype(BF)]
    block_update, new_left, new_right = shampoo(
        at, grads, blocks_w, stat_left, stat_right, root_left, root_right)
    return (loss, block_update, new_left, new_right,
            upd.reshape(-1), new_m.reshape(-1), new_v.reshape(-1))


def solution(mesh):
    return jax.shard_map(
        body,
        mesh=mesh,
        in_specs=(
            P(("dp", "shard"), None, None),
            P(("dp", "shard"), None, None),
            P(("dp", "shard")),
            P(("dp", "shard")),
            P(("dp", "shard")),
            P(("dp", "shard"), None, None),
            P(),
            P(("dp", "shard")),
            P(("dp", "shard")),
            P(("dp", "shard")),
            P("shard", None, None),
            P("shard", None, None),
            P("shard", None, None),
            P("shard", None, None),
            P("shard", None, None),
        ),
        out_specs=(
            P(),
            P("shard", None, None),
            P("shard", None, None),
            P("shard", None, None),
            P(("dp", "shard")),
            P(("dp", "shard")),
            P(("dp", "shard")),
        ),
        check_vma=False,
    )
```

```python
import functools
import math

import jax
import jax.numpy as jnp
from jax import lax
from jax.experimental import pallas as pl
from jax.experimental.pallas import tpu as pltpu
from jax.sharding import PartitionSpec as P


D = 384
HEADS = 6
HDIM = 64
F = 1536
PD = 16
GRID = 16
SEQ = 256
FREQ = 256
DINO = 768
STEP = 10
NBLK = 12
ADAM_PAD = 2129920

BETA_ONE = 0.9
BETA_TWO = 0.95
ADAM_EPS = 1e-08
ADAM_RATE = 0.01
DECAY_RATE = 0.1
STAT_BETA = 0.9
SHAMPOO_RATE = 0.02
RMS_EPS = 1e-08
REPA_WEIGHT = 0.5
NORM_EPS = 1e-06
QK_SCALE = HDIM ** (-0.5)

AXES = ("dp", "shard")
BF = jnp.bfloat16
F32 = jnp.float32
VM = pl.BlockSpec(memory_space=pltpu.VMEM)
SM = pl.BlockSpec(memory_space=pltpu.SMEM)

FLAT_ROWS = ADAM_PAD // 128
R_PATCH = 0
R_PATCH_B = 48
R_TIME_IN = 51
R_TIME_IN_B = 819
R_TIME_OUT = 822
R_TIME_OUT_B = 1974
R_CLASS = 1977
R_MOD = 4980
R_MOD_B = 11892
R_QUERY_B = 11910
R_VALUE_B = 11913
R_PROJ_B = 11916
R_HIDDEN_B = 11919
R_DOWN_B = 11931
R_FMOD = 11934
R_FMOD_B = 14238
R_FINAL = 14244
R_FINAL_B = 14292
ALIGN_ROWS = 2310

PAY = 64
PLANE_ROWS = FLAT_ROWS // 4


def shape(dims, kind=F32):
    return jax.ShapeDtypeStruct(dims, kind)


def mm(left, right):
    return jnp.dot(left, right, preferred_element_type=F32)


def mm_nt(left, right):
    return lax.dot_general(left, right, (((1,), (1,)), ((), ())), preferred_element_type=F32)


def mm_tn(left, right):
    return lax.dot_general(left, right, (((0,), (0,)), ((), ())), preferred_element_type=F32)


def silu(v):
    return v / (1.0 + jnp.exp(-v))


def silu_slope(v):
    s = 1.0 / (1.0 + jnp.exp(-v))
    return s * (1.0 + v * (1.0 - s))


def split3(v):
    one = v.astype(BF)
    rest = v - one.astype(F32)
    two = rest.astype(BF)
    return one, two, (rest - two.astype(F32)).astype(BF)


def split2(v):
    one = v.astype(BF)
    return one, (v - one.astype(F32)).astype(BF)


def stack3(v):
    one, two, three = split3(v)
    return jnp.concatenate([one.astype(F32), two.astype(F32), three.astype(F32)], axis=0).astype(BF)


def fold3(v):
    third = v.shape[0] // 3
    return v[:third] + v[third : 2 * third] + v[2 * third :]


def place_of(z, x, y, c):
    return ((z * 2 + x) * 2 + y) * 2 + c


def permutation(move):
    pairs = []
    for z in range(4):
        for x in range(2):
            for y in range(2):
                for c in range(2):
                    pairs.append((place_of(z, x, y, c), place_of(*move(z, x, y, c))))
    return pairs


TO_C = permutation(lambda z, x, y, c: (z, x, y, 1 - c))
TO_Y = permutation(lambda z, x, y, c: (z, x, 1 - y, c))
TO_X = permutation(lambda z, x, y, c: (z, 1 - x, y, c))
TO_Z = [permutation(lambda z, x, y, c, d=d: ((z + d) % 4, x, y, c)) for d in range(4)]


def send(value, pairs):
    return lax.ppermute(value, AXES, pairs)


def coordinates():
    dp = lax.axis_index("dp")
    sh = lax.axis_index("shard")
    return dp // 2, dp % 2, sh // 2, sh % 2


def pick(array, start, size):
    return lax.dynamic_slice_in_dim(array, start, size, 0)


TO_XY = permutation(lambda z, x, y, c: (z, 1 - x, 1 - y, c))
TO_CY = permutation(lambda z, x, y, c: (z, x, 1 - y, 1 - c))
TO_PAIR = permutation(lambda z, x, y, c: (z + 1 - 2 * (z % 2), x, y, c))


def spread(first, second):
    first_x = send(first, TO_X)
    second_y = send(second, TO_Y)
    first = jnp.concatenate([first, first_x])
    second = jnp.concatenate([second, second_y])
    return [first, second, send(first, TO_Y), send(second, TO_X)]


def send_plane(value):
    return [send(value, TO_X), send(value, TO_Y), send(value, TO_XY)]


def gather_flat(piece, cut, ready):
    turned = [send(piece, TO_Z[d]) for d in (1, 2, 3)]
    own = [piece] + send_plane(piece)
    turned, ready = lax.optimization_barrier((turned, ready))
    rest = spread(jnp.stack([t[:cut] for t in turned]), jnp.stack([t[cut:] for t in turned]))
    own_c = [send(p, TO_C) for p in own]
    rest_c = [send(p, TO_C) for p in rest]
    return [p[None] for p in own] + rest + [p[None] for p in own_c] + rest_c, ready


def flip(value, bit):
    return 1 - value if bit else value


def flat_places(cut):
    def near(dc, dx, dy):
        return lambda i, at: place_of(at[0], flip(at[1], dx), flip(at[2], dy), flip(at[3], dc))

    def far(dc, kind):
        def entry(i, at):
            z, x, y, c = at
            dz, other = i % 3 + 1, i // 3
            dx, dy = {0: (other, 0), 1: (0, other), 2: (other, 1), 3: (1, other)}[kind]
            return place_of(lax.rem(z + 4 - dz, 4), flip(x, dx), flip(y, dy), flip(c, dc))

        return entry

    places = []
    for dc in (0, 1):
        places += [(0, near(dc, dx, dy)) for dx, dy in ((0, 0), (1, 0), (0, 1), (1, 1))]
        places += [((0, cut, 0, cut)[kind], far(dc, kind)) for kind in range(4)]
    return places


def gather_rows(pay):
    z, _, _, _ = coordinates()
    turned = [send(pick(pay, (z + d) % 4, 1)[0], TO_Z[d]) for d in (1, 2, 3)]
    column = jnp.stack([pick(pay, z, 1)[0]] + turned)
    plane = [column] + send_plane(column)
    return plane + [send(p, TO_C) for p in plane]


def read_coordinates(ref):
    return ref[0], ref[1], ref[2], ref[3]


def cond_kernel(places, rows, at_ref, cls_ref, feat_ref, *refs):
    count = len(places)
    pieces = refs[:count]
    (mods_ref, pre_ref, th_ref, cond_ref, modw_ref, fmodw_ref, tout_ref, align_ref, bias_ref,
     patch_ref, final_ref, flat, rolled) = refs[count:]
    at = read_coordinates(at_ref)
    for ref, (offset, entry) in zip(pieces, places):
        for i in range(ref.shape[0]):
            start = pl.multiple_of(entry(i, at) * rows + offset, 8)
            flat[pl.ds(start, ref.shape[1]), :] = ref[i].astype(F32)

    def row(first, count):
        return jnp.concatenate([flat[first + l : first + l + 1, :] for l in range(count)], axis=1)

    def columns(first, depth, count, which):
        return flat[pl.ds(first + which, depth, stride=count), :].astype(BF)

    def wide(v, first, depth, count, keep=None):
        stacked = stack3(v)
        out = []
        for j in range(count):
            w = columns(first, depth, count, j)
            if keep is not None:
                keep[:, 128 * j : 128 * j + 128] = w
            out.append(fold3(mm(stacked, w)))
        return jnp.concatenate(out, axis=1)

    pre = wide(feat_ref[...], R_TIME_IN, FREQ, 3) + row(R_TIME_IN_B, 3)
    th = silu(pre)
    picked = []
    for m in range(4):
        r = R_CLASS + 3 * cls_ref[m]
        picked.append(jnp.concatenate([flat[pl.ds(r + l, 1), :] for l in range(3)], axis=1))
    picked = jnp.concatenate(picked + [jnp.zeros((4, D), F32)], axis=0)
    cond = wide(th, R_TIME_OUT, D, 3, tout_ref) + row(R_TIME_OUT_B, 3) + picked
    act = silu(cond)
    pre_ref[...] = pre
    th_ref[...] = th
    cond_ref[...] = cond
    mods_ref[:, : 6 * D] = wide(act, R_MOD, D, 18, modw_ref) + row(R_MOD_B, 18)
    mods_ref[:, 6 * D :] = wide(act, R_FMOD, D, 6, fmodw_ref) + row(R_FMOD_B, 6)

    spot = lax.broadcasted_iota(jnp.int32, (ALIGN_ROWS, 128), 1)
    here = pltpu.roll(flat[R_FINAL_B : R_FINAL_B + ALIGN_ROWS, :], 112, 1)
    after = pltpu.roll(flat[R_FINAL_B + 1 : R_FINAL_B + 1 + ALIGN_ROWS, :], 112, 1)
    rolled[...] = jnp.where(spot < 112, here, after)
    for j in range(6):
        align_ref[:, 128 * j : 128 * j + 128] = rolled[pl.ds(j, D, stride=6), :].astype(BF)

    bias_ref[...] = jnp.zeros_like(bias_ref)
    for at_row, first in ((0, R_PATCH_B), (1, R_QUERY_B), (2, R_VALUE_B), (3, R_PROJ_B),
                          (4, R_HIDDEN_B), (5, R_HIDDEN_B + 3), (6, R_HIDDEN_B + 6),
                          (7, R_HIDDEN_B + 9), (8, R_DOWN_B)):
        bias_ref[at_row : at_row + 1, :] = row(first, 3)
    for half in range(2):
        bias_ref[9 + half : 10 + half, :] = jnp.concatenate(
            [rolled[2304 + 3 * half + l : 2305 + 3 * half + l, :] for l in range(3)], axis=1)
    lane = lax.broadcasted_iota(jnp.int32, (1, 128), 1)
    bias_ref[11:12, :128] = jnp.where(lane < PD, flat[R_FINAL_B : R_FINAL_B + 1, :], 0.0)
    patch = [flat[pl.ds(R_PATCH + l, PD, stride=3), :] for l in range(3)]
    patch_ref[...] = jnp.concatenate(patch, axis=1).astype(BF)
    spread = (lax.broadcasted_iota(jnp.int32, (D, 48), 0) // 8
              == lax.broadcasted_iota(jnp.int32, (D, 48), 1)).astype(F32).astype(BF)
    wide_rows = mm(spread, flat[R_FINAL : R_FINAL + 48, :].astype(BF))
    keep = (lax.broadcasted_iota(jnp.int32, (D, 128), 1) // PD
            == lax.broadcasted_iota(jnp.int32, (D, 128), 0) % 8)
    fold = (lax.broadcasted_iota(jnp.int32, (128, 128), 0) % PD
            == lax.broadcasted_iota(jnp.int32, (128, 128), 1)).astype(F32).astype(BF)
    final_ref[...] = mm(jnp.where(keep, wide_rows, 0.0).astype(BF), fold).astype(BF)


def conditioning(at, classes, features, pieces, places, rows):
    kernel = functools.partial(cond_kernel, places, rows)
    return pl.pallas_call(
        kernel,
        name="conditioning",
        out_shape=(shape((8, 8 * D)), shape((8, D)), shape((8, D)), shape((8, D)),
                   shape((D, 6 * D), BF), shape((D, 2 * D), BF), shape((D, D), BF),
                   shape((D, DINO), BF), shape((16, D)), shape((PD, D), BF), shape((D, 128), BF)),
        in_specs=[SM, SM, VM] + [VM] * len(pieces),
        out_specs=[VM] * 11,
        scratch_shapes=[pltpu.VMEM((FLAT_ROWS + 8, 128), F32), pltpu.VMEM((ALIGN_ROWS, 128), F32)],
        cost_estimate=pl.CostEstimate(flops=10**9, bytes_accessed=10**7, transcendentals=0),
    )(at, classes, features, *pieces)


def gather_blocks(mine):
    z, _, _, _ = coordinates()
    half = lax.dynamic_slice_in_dim(mine, 192 * (z % 2), 192, 1)
    near = send(half, TO_Y)
    far = send(near, TO_PAIR)
    return [mine, near, far, send(mine, TO_C), send(near, TO_C), send(far, TO_C)]


def fetch_blocks(at, own_ref, refs, out_ref, sems):
    if len(refs) == 1:
        return [pltpu.make_async_copy(refs[0], out_ref, sems.at[0])]
    z, _, y, c = at
    copies = []
    odd = lax.rem(z, 2)
    for dc in range(2):
        core = flip(c, dc)
        for t in range(3):
            mine, near, far = refs[3 * dc : 3 * dc + 3]
            here = own_ref[3 * (2 * y + core) + t]
            there = own_ref[3 * (2 * (1 - y) + core) + t]
            for source, block, rows in (
                (mine.at[t], here, None),
                (near.at[t], there, pl.ds(pl.multiple_of(192 * odd, 16), 192)),
                (far.at[t], there, pl.ds(pl.multiple_of(192 * (1 - odd), 16), 192)),
            ):
                target = out_ref.at[block] if rows is None else out_ref.at[block, rows]
                copies.append(pltpu.make_async_copy(source, target, sems.at[len(copies)]))
    return copies


UNIT = 24


def unit_of(z, x, y):
    return (2 * x + y) * 4 + z


def reduce_units(units):
    z, x, y, c = coordinates()
    other = pick(units, 1 - c, 1)[0]
    got = send(other, TO_C)
    both = (pick(units, c, 1)[0].astype(F32) + got.astype(F32)).astype(BF)

    def quarter(dx, dy):
        return pick(both, 4 * (2 * flip(x, dx) + flip(y, dy)), 4)

    got = [send(quarter(1, 1), TO_XY), send(quarter(1, 0), TO_X), send(quarter(0, 1), TO_Y)]
    total = quarter(0, 0).astype(F32)
    for g in got:
        total = total + g.astype(F32)
    total = total.astype(BF)
    got = [send(pick(total, (z + d) % 4, 1)[0], TO_Z[d]) for d in (1, 2, 3)]
    total = pick(total, z, 1)[0].astype(F32)
    for g in got:
        total = total + g.astype(F32)
    return total.astype(BF)


def gather_owned(late, early, owner_map):
    _, _, y, c = coordinates()
    mine = jnp.concatenate([late, early]).reshape(6, UNIT, D)
    low = owner_map < 4
    part = jnp.where(low, owner_map // 2, (owner_map - 4) // 4)
    entry = jnp.where(low, owner_map % 2, 2 + (owner_map - 4) % 4)
    slots = jnp.where((part == c)[:, None, None], jnp.take(mine, entry, axis=0), jnp.zeros((), BF))

    def of(dy, dc):
        return pick(slots, 3 * (2 * flip(y, dy) + flip(c, dc)), 3)

    over_c = send(of(1, 1), TO_CY)
    over = send(of(1, 0), TO_Y)
    pair = send(of(0, 1), TO_C)
    both = jnp.stack([of(0, 0) + pair, over + over_c])
    column = [both] + [send(both, TO_Z[d]) for d in (1, 2, 3)]
    return column + [send(v, TO_X) for v in column]


def plane_gradient(plane, pay_ref, flat, rolled, align):
    rows = 8 * pay_ref.shape[0]

    def tile(j):
        return pay_ref[:, 8 * j : 8 * j + 8, :].astype(F32).reshape(rows, D)

    def sums(first, last):
        return jnp.sum(pay_ref[:, first:last, :].astype(F32), axis=0)

    upper = lax.broadcasted_iota(jnp.int32, (rows, 1), 0) % 8 < 4

    def first(v):
        return jnp.where(upper, v, 0.0)

    def second(v):
        return jnp.where(upper, 0.0, v)

    def put_row(v, row):
        for l in range(v.shape[1] // 128):
            flat[row + l : row + l + 1, :] = v[:, 128 * l : 128 * l + 128]

    def put_matrix(v, row, count, which):
        for l in range(v.shape[1] // 128):
            flat[pl.ds(row + which + l, v.shape[0], stride=count), :] = v[:, 128 * l : 128 * l + 128]

    def classes(ids, g_low):
        numbers = (ids[:, 0:1] * 256.0 + ids[:, 1:2]).astype(jnp.int32)
        for part in range(3):
            height = 336 if part < 2 else 329
            marks = lax.broadcasted_iota(jnp.int32, (rows, 336), 1) + 336 * part
            hits = first(jnp.where(marks == numbers, 1.0, 0.0)).astype(BF)
            put_matrix(mm_tn(hits, g_low)[:height], R_CLASS + 3 * 336 * part, 3, 0)

    def modulations(low, bias):
        act = tile(0)[:, low : low + 256]
        halves = (first(act).astype(BF), second(act).astype(BF))
        for t in range(3):
            g = tile(1 + t)
            for half in range(2):
                put_matrix(mm_tn(halves[half], g.astype(BF)), R_MOD + 18 * low, 18, 3 * (t + 3 * half))
                if bias:
                    put_row(column_sum((first, second)[half](g)), R_MOD_B + 3 * (t + 3 * half))

    def finals(which, bias):
        act, g = tile(0), tile(which)
        for half, part in enumerate((first, second)):
            put_matrix(mm_tn(part(act).astype(BF), g.astype(BF)), R_FMOD, 6, 3 * half)
            if bias:
                put_row(column_sum(part(g)), R_FMOD_B + 3 * half)

    if plane == 0:
        left, g = tile(0).astype(BF), tile(1)
        g_cond, g_pre = first(g), second(g)
        put_matrix(mm_tn(left[:, :FREQ], g_pre.astype(BF)), R_TIME_IN, 3, 0)
        put_row(column_sum(g_pre), R_TIME_IN_B)
        put_matrix(mm_tn(left, g_cond.astype(BF)), R_TIME_OUT, 3, 0)
        put_row(column_sum(g_cond), R_TIME_OUT_B)
        classes(tile(2)[:, :128], g.astype(BF))
        total = sums(40, 64)
        for l in range(3):
            flat[pl.ds(R_PATCH + l, PD, stride=3), :] = total[0:16, 128 * l : 128 * l + 128]
        put_row(total[16:17], R_PATCH_B)
    if plane == 1:
        classes(tile(5)[:, :128], tile(4).astype(BF))
        modulations(0, False)
    if plane == 2:
        modulations(128, True)
        finals(4, False)
        total = sums(40, 48)
        for k, row in enumerate((R_QUERY_B, R_VALUE_B, R_PROJ_B, R_HIDDEN_B, R_HIDDEN_B + 3, R_HIDDEN_B + 6,
                                 R_HIDDEN_B + 9, R_DOWN_B)):
            put_row(total[k : k + 1], row)
    if plane == 3:
        finals(1, True)
        total = sums(40, 64)
        for l in range(3):
            flat[R_FINAL + 16 * l : R_FINAL + 16 * l + 16, :] = total[0:16, 128 * l : 128 * l + 128]
        rolled[0:8, :] = jnp.zeros((8, 128), F32)
        rolled[8 + ALIGN_ROWS :, :] = jnp.zeros_like(rolled[8 + ALIGN_ROWS :, :])
        rolled[7:8, :] = pltpu.roll(total[16:17, 0:128], 112, 1)
        for half in range(2):
            for l in range(3):
                lanes = slice(128 * l, 128 * l + 128)
                rolled[pl.ds(8 + 3 * half + l, D, stride=6), :] = align[half, :, lanes].astype(F32)
                r = 8 + 2304 + 3 * half + l
                rolled[r : r + 1, :] = total[17 + half : 18 + half, lanes]
        count = FLAT_ROWS - R_FINAL_B
        spot = lax.broadcasted_iota(jnp.int32, (count, 128), 1)
        here = pltpu.roll(rolled[8 : 8 + count, :], 16, 1)
        before = pltpu.roll(rolled[7 : 7 + count, :], 16, 1)
        flat[R_FINAL_B:FLAT_ROWS, :] = jnp.where(spot < 16, before, here)


def loss_of(pay_ref):
    rows = 8 * pay_ref.shape[0]
    parts = pay_ref[:, PAY - 8 : PAY, 0:128].astype(F32).reshape(rows, 128)
    parts = column_sum(jnp.where(lax.broadcasted_iota(jnp.int32, (rows, 128), 0) % 8 == 7, parts, 0.0))
    return parts[:, 0:1] + parts[:, 1:2] + parts[:, 2:3]


def adam_near_kernel(at_ref, *refs):
    parts = refs[:8]
    w_ref, m_ref, v_ref, loss_ref, upd_ref, new_m_ref, new_v_ref, pay, align, flat, rolled = refs[8:]
    at = read_coordinates(at_ref)
    z, x, y, c = at
    for k, ref in enumerate(parts):
        dc, dy, dx = k // 4, k // 2 % 2, k % 2
        for dz in range(4):
            there = (lax.rem(z + 4 - dz, 4), flip(x, dx), flip(y, dy), flip(c, dc))
            value = ref[dz].astype(F32)
            pay[place_of(*there)] = value
            start = pl.multiple_of(unit_of(*there[:3]) * UNIT, 8)
            align[there[3], pl.ds(start, UNIT), :] = value[16:40]
    loss_ref[...] = loss_of(pay)
    for plane in range(4):
        @pl.when(z == plane)
        def _():
            plane_gradient(plane, pay, flat, rolled, align)
    size = w_ref.shape[0]
    start = pl.multiple_of(place_of(z, x, y, c) * size, 8)
    adam_step(flat[pl.ds(start, size), :], w_ref, m_ref, v_ref, upd_ref, new_m_ref, new_v_ref)


def adam_plane_kernel(plane, pay_ref, align_ref, loss_ref, flat_ref, rolled):
    loss_ref[...] = loss_of(pay_ref)
    plane_gradient(plane, pay_ref, flat_ref, rolled, align_ref)


def adam_step(grad, w_ref, m_ref, v_ref, upd_ref, new_m_ref, new_v_ref):
    new_m = BETA_ONE * m_ref[...] + (1.0 - BETA_ONE) * grad
    new_v = BETA_TWO * v_ref[...] + (1.0 - BETA_TWO) * grad * grad
    new_m_ref[...] = new_m
    new_v_ref[...] = new_v
    right_m = new_m / (1.0 - BETA_ONE**STEP)
    right_v = new_v / (1.0 - BETA_TWO**STEP)
    upd_ref[...] = -ADAM_RATE * (right_m / (jnp.sqrt(right_v) + ADAM_EPS) + DECAY_RATE * w_ref[...])


ROLL_ROWS = 8 + FLAT_ROWS - R_FINAL_B + 8


ROLL_ROWS = 8 + FLAT_ROWS - R_FINAL_B + 8


def adam_near(at, parts, flat_w, m, v):
    size = flat_w.shape
    loss, upd, new_m, new_v = pl.pallas_call(
        adam_near_kernel,
        name="adam",
        out_shape=(shape((1, 1)), shape(size), shape(size), shape(size)),
        in_specs=[SM] + [VM] * 11,
        out_specs=[VM] * 4,
        scratch_shapes=[pltpu.VMEM((32, PAY, D), F32), pltpu.VMEM((2, D, D), F32),
                        pltpu.VMEM((FLAT_ROWS, 128), F32), pltpu.VMEM((ROLL_ROWS, 128), F32)],
        cost_estimate=pl.CostEstimate(flops=10**9, bytes_accessed=10**7, transcendentals=0),
    )(at, *parts, flat_w, m, v)
    return loss[0, 0], upd, new_m, new_v


def adam_wide(pays, align, flat_w, m, v):
    grads = []
    for plane in range(4):
        loss, flat = pl.pallas_call(
            functools.partial(adam_plane_kernel, plane),
            name="adam_gradient",
            out_shape=(shape((1, 1)), shape((FLAT_ROWS, 128))),
            in_specs=[VM] * 2,
            out_specs=[VM] * 2,
            scratch_shapes=[pltpu.VMEM((ROLL_ROWS, 128), F32)],
        )(pays[:, plane], align)
        grads.append(flat[PLANE_ROWS * plane : PLANE_ROWS * (plane + 1)])
    size = flat_w.shape[0]
    place = lax.axis_index("dp") * lax.axis_size("shard") + lax.axis_index("shard")
    grad = lax.dynamic_slice_in_dim(jnp.concatenate(grads), place * size, size, 0)
    upd, new_m, new_v = pl.pallas_call(
        lambda g, *refs: adam_step(g[...], *refs),
        name="adam",
        out_shape=(shape(flat_w.shape),) * 3,
        in_specs=[VM] * 4,
        out_specs=[VM] * 3,
    )(grad, flat_w, m, v)
    return loss[0, 0], upd, new_m, new_v


def shampoo_kernel(near, at_ref, *refs):
    if near:
        parts = refs[:8]
        w_ref, sl_ref, sr_ref, rl_ref, rr_ref, upd_ref, nl_ref, nr_ref, grad = refs[8:]
        z, x, y, _ = read_coordinates(at_ref)
        t = pl.program_id(0)
        for dx in range(2):
            for dz in range(4):
                for dy in range(2):
                    unit = unit_of(lax.rem(z + 4 - dz, 4), flip(x, dx), flip(y, dy))
                    rows = pl.ds(pl.multiple_of(unit * UNIT, 8), UNIT)
                    grad[rows, :] = parts[4 * dx + dz][dy, t].astype(F32)
        g = grad[...].astype(BF)
    else:
        grad_ref, w_ref, sl_ref, sr_ref, rl_ref, rr_ref, upd_ref, nl_ref, nr_ref = refs
        g = grad_ref[0]
    nl_ref[0] = STAT_BETA * sl_ref[0] + (1.0 - STAT_BETA) * mm_nt(g, g)
    nr_ref[0] = STAT_BETA * sr_ref[0] + (1.0 - STAT_BETA) * mm_tn(g, g)
    one, two = split2(rl_ref[0])
    left = mm(one, g) + mm(two, g)
    l_one, l_two = split2(left)
    r_one, r_two = split2(rr_ref[0])
    p = mm(l_one, r_one) + (mm(l_one, r_two) + mm(l_two, r_one))
    mean = jnp.sum(jnp.sum(p * p, axis=1, keepdims=True), axis=0, keepdims=True) * (1.0 / (D * D))
    root = jnp.sqrt(mean)
    upd_ref[0] = -SHAMPOO_RATE * (p / (root + RMS_EPS) + DECAY_RATE * w_ref[0])


def shampoo(at, grads, blocks_w, stat_left, stat_right, root_left, root_right):
    near = len(grads) == 8
    slots = blocks_w.shape[0]
    one = pl.BlockSpec((1, D, D), lambda t: (t, 0, 0))
    return pl.pallas_call(
        functools.partial(shampoo_kernel, near),
        name="shampoo",
        grid=(slots,),
        out_shape=(shape((slots, D, D)),) * 3,
        in_specs=[SM] + ([VM] * 8 if near else [one]) + [one] * 5,
        out_specs=[one] * 3,
        scratch_shapes=[pltpu.VMEM((D, D), F32)] if near else [],
        cost_estimate=pl.CostEstimate(flops=3 * 10**9, bytes_accessed=15 * 10**6, transcendentals=0),
    )(at, *grads, blocks_w, stat_left, stat_right, root_left, root_right)


GELU_C = math.sqrt(2.0 / math.pi)
GELU_D = 0.044715
EARLY = 5 * 24
LATE = 2 * 24
SUMS_MLP = 24


def norm_stats(v):
    centered = v - jnp.sum(v, axis=-1, keepdims=True) * (1.0 / D)
    inv = lax.rsqrt(jnp.sum(centered * centered, axis=-1, keepdims=True) * (1.0 / D) + NORM_EPS)
    return centered * inv, inv


def norm_back(g, normed, inv):
    mean_g = jnp.sum(g, axis=-1, keepdims=True) * (1.0 / D)
    mean_gn = jnp.sum(g * normed, axis=-1, keepdims=True) * (1.0 / D)
    return inv * (g - mean_g - normed * mean_gn)


def column_sum(v):
    return jnp.sum(v, axis=0, keepdims=True)


def head(v, h):
    return v[:, HDIM * h : HDIM * h + HDIM]


def front_kernel(at_ref, own_ref, noisy_ref, mods_ref, bias_ref, patch_ref, pos_ref, *refs):
    h0_ref, qkv_ref, att_ref, h1_ref, all_ref, w_ref, in_sems, out_sem = refs[-8:]
    i = pl.program_id(0)
    fetch = fetch_blocks(read_coordinates(at_ref), own_ref, refs[:-8], w_ref, in_sems)
    keep = pltpu.make_async_copy(w_ref, all_ref, out_sem)

    @pl.when(i == 0)
    def _():
        for copy in fetch:
            copy.start()
        for copy in fetch:
            copy.wait()
        keep.start()

    def mod(t):
        return mods_ref[pl.ds(i, 1), D * t : D * t + D]

    h0 = mm_tn(noisy_ref[0].astype(BF), patch_ref[...]) + bias_ref[0:1, :] + pos_ref[...]
    h0_ref[0] = h0
    normed, _ = norm_stats(h0)
    act = (normed * (1.0 + mod(1)) + mod(0)).astype(BF)
    q = (mm(act, w_ref[0]) + bias_ref[1:2, :]).astype(BF)
    k = mm(act, w_ref[1]).astype(BF)
    v = (mm(act, w_ref[2]) + bias_ref[2:3, :]).astype(BF)
    qkv_ref[0, :, 0:D] = q
    qkv_ref[0, :, D : 2 * D] = k
    qkv_ref[0, :, 2 * D :] = v
    outs = []
    for h in range(HEADS):
        s = mm_nt(head(q, h), head(k, h)) * QK_SCALE
        e = jnp.exp(s - jnp.max(s, axis=-1, keepdims=True))
        p = e * (1.0 / jnp.sum(e, axis=-1, keepdims=True))
        outs.append(mm(p.astype(BF), head(v, h)))
    att = jnp.concatenate(outs, axis=1).astype(BF)
    att_ref[0] = att
    h1_ref[0] = h0 + mod(2) * (mm(att, w_ref[3]) + bias_ref[3:4, :])

    @pl.when(i == pl.num_programs(0) - 1)
    def _():
        keep.wait()


def middle_kernel(images, total_img, tw_ref, h1_ref, vel_ref, dino_ref, mods_ref, bias_ref, w_ref, aw_ref, fw_ref,
                  bh1_ref, gm_ref, units_ref, sums_ref,
                  act2_s, gelu_s, slope_s, bi_s, bb2_s, h1_s, ba_s, act3_s, bo_s):
    i = pl.program_id(0)
    rows = pl.ds(pl.multiple_of(i * SEQ, SEQ), SEQ)

    def mod(t):
        return mods_ref[pl.ds(i, 1), D * t : D * t + D]

    @pl.when(i == 0)
    def _():
        sums_ref[...] = jnp.zeros_like(sums_ref)

    h1 = h1_ref[0]
    n2, inv2 = norm_stats(h1)
    act2 = (n2 * (1.0 + mod(4)) + mod(3)).astype(BF)
    act2_s[rows, :] = act2
    branch = jnp.zeros((SEQ, D), F32) + bias_ref[8:9, :]
    for j in range(4):
        lanes = slice(D * j, D * j + D)
        x = mm(act2, w_ref[4 + j]) + bias_ref[4 + j : 5 + j, :]
        xx = x * x
        t = jnp.tanh(x * (GELU_C + (GELU_C * GELU_D) * xx))
        half = 0.5 + 0.5 * t
        g = (x * half).astype(BF)
        slope_s[:, lanes] = half + (0.5 * x) * (1.0 - t * t) * (GELU_C + (3.0 * GELU_C * GELU_D) * xx)
        gelu_s[rows, lanes] = g
        branch = branch + mm(g, w_ref[8 + j])
    h2 = h1 + mod(5) * branch
    n3, inv3 = norm_stats(h2)
    act3 = (n3 * (1.0 + mod(7)) + mod(6)).astype(BF)
    act3_s[rows, :] = act3
    out = mm(act3, fw_ref[...]) + bias_ref[11:12, 0:128]
    err = out[:, :PD] - vel_ref[0].T
    weight = tw_ref[i]
    loss = jnp.sum(column_sum(err * err), axis=1, keepdims=True) * (weight / (total_img * SEQ * PD))
    bo = jnp.concatenate([err * (2.0 * weight / (total_img * SEQ * PD)), jnp.zeros((SEQ, 128 - PD), F32)],
                         axis=1).astype(BF)
    bo_s[rows, :] = bo

    h1_low = h1.astype(BF)
    h1_s[rows, :] = h1_low
    aligned = mm(h1_low, aw_ref[...]) + jnp.concatenate([bias_ref[9:10, :], bias_ref[10:11, :]], axis=1)
    dino = dino_ref[0].astype(F32)
    dot = jnp.sum(aligned * dino, axis=-1, keepdims=True)
    ra = lax.rsqrt(jnp.sum(aligned * aligned, axis=-1, keepdims=True) + NORM_EPS)
    rd = lax.rsqrt(jnp.sum(dino * dino, axis=-1, keepdims=True) + NORM_EPS)
    scale = REPA_WEIGHT / (total_img * SEQ)
    both = ra * rd
    cosine = dot * both
    loss = loss - column_sum(cosine) * scale
    ba = (dino * (both * -scale) + aligned * (cosine * (ra * ra) * scale)).astype(BF)
    ba_s[rows, :] = ba
    through = mm_nt(ba, aw_ref[...])

    b3 = mm_nt(bo, fw_ref[...])
    bh2 = norm_back(b3 * (1.0 + mod(7)), n3, inv3)
    bb2 = (bh2 * mod(5)).astype(BF)
    bb2_s[rows, :] = bb2
    b2 = jnp.zeros((SEQ, D), F32)
    for j in range(4):
        lanes = slice(D * j, D * j + D)
        bi = (mm_nt(bb2, w_ref[8 + j]) * slope_s[:, lanes]).astype(BF)
        bi_s[rows, lanes] = bi
        sums_ref[16 + j : 17 + j, :] += column_sum(bi.astype(F32))
        b2 = b2 + mm_nt(bi, w_ref[4 + j])
    sums_ref[20:21, :] += column_sum(bb2.astype(F32))
    ba_sum = column_sum(ba.astype(F32))
    sums_ref[21:22, :] += ba_sum[:, :D]
    sums_ref[22:23, :] += ba_sum[:, D:]
    sums_ref[23:24, 0:128] += column_sum(bo.astype(F32))
    bh1_ref[0] = bh2 + norm_back(b2 * (1.0 + mod(4)), n2, inv2) + through
    gm_ref[0, 0:1, :] = column_sum(b2)
    gm_ref[0, 1:2, :] = column_sum(b2 * n2)
    gm_ref[0, 2:3, :] = column_sum(bh2 * branch)
    gm_ref[0, 3:4, :] = column_sum(b3)
    gm_ref[0, 4:5, :] = column_sum(b3 * n3)
    gm_ref[0, 5:6, :] = jnp.broadcast_to(loss, (1, D))
    gm_ref[0, 6:8, :] = jnp.zeros((2, D), F32)

    @pl.when(i == images - 1)
    def _():
        def put(part, j, g):
            g = g.astype(BF)
            for u in range(16):
                units_ref[part, u, 24 * j : 24 * j + 24, :] = g[24 * u : 24 * u + 24, :]

        for j in range(4):
            lanes = slice(D * j, D * j + D)
            put(0, j, mm_tn(act2_s[...], bi_s[:, lanes]))
            put(1, j, mm_tn(gelu_s[:, lanes], bb2_s[...]))
        for p in range(2):
            put(p, 4, mm_tn(h1_s[...], ba_s[:, D * p : D * p + D]))
        g = mm_tn(act3_s[...], bo_s[...]).astype(BF)
        spread = (lax.broadcasted_iota(jnp.int32, (128, 128), 1) % PD
                  == lax.broadcasted_iota(jnp.int32, (128, 128), 0)).astype(F32).astype(BF)
        keep = (lax.broadcasted_iota(jnp.int32, (D, 128), 1) // PD
                == lax.broadcasted_iota(jnp.int32, (D, 128), 0) % 8)
        fold = (lax.broadcasted_iota(jnp.int32, (48, D), 1) // 8
                == lax.broadcasted_iota(jnp.int32, (48, D), 0)).astype(F32).astype(BF)
        flat = mm(fold, jnp.where(keep, mm(g, spread), 0.0).astype(BF))
        for l in range(3):
            sums_ref[0:16, 128 * l : 128 * l + 128] = flat[16 * l : 16 * l + 16, :]


def back_kernel(first, bh1_ref, h0_ref, qkv_ref, att_ref, noisy_ref, mods_ref, bias_ref, w_ref,
                bb1_ref, bp_ref, act_ref, gm_ref, patch_ref):
    i = pl.program_id(0) + first

    def mod(t):
        return mods_ref[pl.ds(i, 1), D * t : D * t + D]

    bh1 = bh1_ref[0]
    att = att_ref[0]
    bb1 = (bh1 * mod(2)).astype(BF)
    bb1_ref[0] = bb1
    gm_ref[0, 2:3, :] = column_sum(bh1 * (mm(att, w_ref[3]) + bias_ref[3:4, :]))
    batt = mm_nt(bb1, w_ref[3]).astype(BF)
    q, k, v = qkv_ref[0, :, 0:D], qkv_ref[0, :, D : 2 * D], qkv_ref[0, :, 2 * D :]
    gq, gk, gv = [], [], []
    for h in range(HEADS):
        qh, kh, vh, bh = head(q, h), head(k, h), head(v, h), head(batt, h)
        s = mm_nt(kh, qh) * QK_SCALE
        e = jnp.exp(s - jnp.max(s, axis=0, keepdims=True))
        p = e * (1.0 / column_sum(e))
        dp = mm_nt(vh, bh)
        ds = (p * (dp - column_sum(dp * p))).astype(BF)
        gv.append(mm(p.astype(BF), bh))
        gk.append(mm(ds, qh))
        gq.append(mm_tn(ds, kh))
    bq = (jnp.concatenate(gq, axis=1) * QK_SCALE).astype(BF)
    bk = (jnp.concatenate(gk, axis=1) * QK_SCALE).astype(BF)
    bv = jnp.concatenate(gv, axis=1).astype(BF)
    bp_ref[0, :, 0:D] = bq
    bp_ref[0, :, D : 2 * D] = bk
    bp_ref[0, :, 2 * D :] = bv
    b1 = mm_nt(bq, w_ref[0]) + mm_nt(bk, w_ref[1]) + mm_nt(bv, w_ref[2])
    n1, inv1 = norm_stats(h0_ref[0])
    act_ref[0] = (n1 * (1.0 + mod(1)) + mod(0)).astype(BF)
    gm_ref[0, 0:1, :] = column_sum(b1)
    gm_ref[0, 1:2, :] = column_sum(b1 * n1)
    bh0 = (bh1 + norm_back(b1 * (1.0 + mod(1)), n1, inv1)).astype(BF)
    patch_ref[0] = mm(noisy_ref[0].astype(BF), bh0)
    gm_ref[0, 3:4, :] = column_sum(bh0.astype(F32))
    gm_ref[0, 4:5, :] = column_sum(bq.astype(F32))
    gm_ref[0, 5:6, :] = column_sum(bv.astype(F32))
    gm_ref[0, 6:7, :] = column_sum(bb1.astype(F32))
    gm_ref[0, 7:8, :] = jnp.zeros((1, D), F32)


def last_kernel(*refs):
    units_ref = refs[-1]
    parts = [refs[4 * k : 4 * k + 4] for k in range(len(refs) // 4)]

    def put(part, j, left, right, lanes):
        g = sum(mm_tn(p[left][...], p[right][:, lanes]) for p in parts).astype(BF)
        for u in range(16):
            units_ref[part, u, 24 * j : 24 * j + 24, :] = g[24 * u : 24 * u + 24, :]

    put(0, 0, 0, 1, slice(0, D))
    put(0, 1, 0, 1, slice(D, 2 * D))
    put(1, 0, 0, 1, slice(2 * D, 3 * D))
    put(1, 1, 2, 3, slice(0, D))


def cond_back_kernel(images, cls_ref, gm2_ref, pre_ref, th_ref, cond_ref, feat_ref, modw_ref, fmodw_ref,
                     tout_ref, sums_ref, align_ref, *refs):
    pay_ref = refs[-1]
    gm3_refs, patch_refs = refs[:-1:2], refs[1:-1:2]
    none = jnp.zeros((4, D), F32)
    gm2 = [gm2_ref[m] for m in range(images)]
    gm3 = [ref[m] for ref in gm3_refs for m in range(ref.shape[0])]
    patch = sum(ref[m] for ref in patch_refs for m in range(ref.shape[0]))

    def rows_of(values, r):
        return jnp.concatenate([v[r : r + 1, :] for v in values] + [none], axis=0)

    tiles = [rows_of(gm3, 0), rows_of(gm3, 1), rows_of(gm3, 2),
             rows_of(gm2, 0), rows_of(gm2, 1), rows_of(gm2, 2)]
    finals = [rows_of(gm2, 3), rows_of(gm2, 4)]
    g_act = jnp.zeros((24, D), F32)
    for t in range(6):
        g_act = g_act + mm_nt(stack3(tiles[t]), modw_ref[:, D * t : D * t + D])
    for t in range(2):
        g_act = g_act + mm_nt(stack3(finals[t]), fmodw_ref[:, D * t : D * t + D])
    cond = cond_ref[...]
    g_cond = fold3(g_act) * silu_slope(cond)
    g_pre = fold3(mm_nt(stack3(g_cond), tout_ref[...])) * silu_slope(pre_ref[...])
    act = silu(cond)
    lane = lax.broadcasted_iota(jnp.int32, (1, 128), 1)
    ids = []
    for m in range(images):
        number = cls_ref[m]
        row = jnp.where(lane == 0, (number // 256).astype(F32), 0.0)
        ids.append(jnp.where(lane == 1, (number % 256).astype(F32), row))
    ids = jnp.concatenate(ids, axis=0)
    loss = sum(v[5:6, 0:128] for v in gm2)
    pieces = [v.astype(F32) for v in split3(loss)]
    loss = jnp.where(lane == 0, pieces[0], jnp.where(lane == 1, pieces[1], jnp.where(lane == 2, pieces[2], 0.0)))
    loss = jnp.concatenate([loss, jnp.zeros((1, D - 128), F32)], axis=1)

    def put(plane, j, upper, lower):
        pay_ref[plane, 8 * j : 8 * j + 8, :] = jnp.concatenate([upper[:4], lower[:4]], axis=0).astype(BF)

    def put_rows(plane, first, v):
        pay_ref[plane, first : first + v.shape[0], :] = v.astype(BF)

    def over(r):
        return sum(v[r : r + 1, :] for v in gm3)

    none = jnp.zeros((8, D), F32)
    row = jnp.zeros((1, D), F32)
    tags = jnp.concatenate([ids, jnp.zeros((4, D - 128), F32)], axis=1)
    pay_ref[...] = jnp.zeros_like(pay_ref)
    put(0, 0, th_ref[...], jnp.concatenate([feat_ref[...], jnp.zeros((8, D - FREQ), F32)], axis=1))
    put(0, 1, g_cond, g_pre)
    put(0, 2, tags, none)
    put_rows(0, 40, patch)
    for plane in (1, 2):
        put(plane, 0, act, act)
        for t in range(3):
            put(plane, 1 + t, tiles[t], tiles[t + 3])
    put(1, 4, g_cond, none)
    put(1, 5, tags, none)
    put(2, 4, finals[0], finals[1])
    sums = sums_ref[...]
    put_rows(2, 40, jnp.concatenate([over(4), over(5), over(6), sums[16:21]], axis=0))
    put(3, 0, act, act)
    put(3, 1, finals[0], finals[1])
    pay_ref[3, 16:40, :] = align_ref[...]
    put_rows(3, 40, sums[0:16])
    last = [[over(3)] + [row] * 6, [row] * 7, [row] * 7, [sums[23:24], sums[21:22], sums[22:23]] + [row] * 4]
    for plane in range(4):
        put_rows(plane, 56, jnp.concatenate(last[plane] + [loss], axis=0))


def cost(flops, moved):
    return pl.CostEstimate(flops=int(flops), bytes_accessed=int(moved), transcendentals=0)


def rows_each(first, *dims):
    return pl.BlockSpec((1,) + dims, lambda i: (i + first,) + (0,) * len(dims))


def front(at, owner_map, noisy, mods, bias, patch_low, pos, pieces):
    images = noisy.shape[0]
    each = functools.partial(rows_each, 0)
    anywhere = pl.BlockSpec(memory_space=pl.ANY)
    return pl.pallas_call(
        front_kernel,
        name="front",
        grid=(images,),
        out_shape=(shape((images, SEQ, D)), shape((images, SEQ, 3 * D), BF),
                   shape((images, SEQ, D), BF), shape((images, SEQ, D)), shape((NBLK, D, D), BF)),
        in_specs=[SM, SM, each(PD, SEQ), VM, VM, VM, VM] + [anywhere] * len(pieces),
        out_specs=[each(SEQ, D), each(SEQ, 3 * D), each(SEQ, D), each(SEQ, D), anywhere],
        scratch_shapes=[pltpu.VMEM((NBLK, D, D), BF), pltpu.SemaphoreType.DMA((18,)), pltpu.SemaphoreType.DMA(())],
        cost_estimate=cost(2.2e9, 1.2e7),
    )(at, owner_map, noisy, mods, bias, patch_low, pos, *pieces)


def middle(total_img, time_weight, h1, velocity, dino, mods, bias, blocks, align_low, final_low):
    images = h1.shape[0]
    each = functools.partial(rows_each, 0)
    full = lambda lanes, kind=BF: pltpu.VMEM((images * SEQ, lanes), kind)
    return pl.pallas_call(
        functools.partial(middle_kernel, images, total_img),
        name="middle",
        grid=(images,),
        out_shape=(shape((images, SEQ, D)), shape((images, 8, D)),
                   shape((2, 16, EARLY, D), BF), shape((SUMS_MLP, D))),
        in_specs=[SM, each(SEQ, D), each(PD, SEQ), each(SEQ, DINO), VM, VM, VM, VM, VM],
        out_specs=[each(SEQ, D), each(8, D), VM, VM],
        scratch_shapes=[full(D), full(F), pltpu.VMEM((SEQ, F), F32), full(F), full(D), full(D),
                        full(DINO), full(D), full(128)],
        cost_estimate=cost(9e9, 1.4e7),
    )(time_weight, h1, velocity, dino, mods, bias, blocks, align_low, final_low)


def attention_back(first, count, bh1, h0, qkv, att, noisy, mods, bias, blocks):
    each = functools.partial(rows_each, first)
    out = functools.partial(rows_each, 0)
    return pl.pallas_call(
        functools.partial(back_kernel, first),
        name="attention_back",
        grid=(count,),
        out_shape=(shape((count, SEQ, D), BF), shape((count, SEQ, 3 * D), BF), shape((count, SEQ, D), BF),
                   shape((count, 8, D)), shape((count, PD, D))),
        in_specs=[each(SEQ, D), each(SEQ, D), each(SEQ, 3 * D), each(SEQ, D), each(PD, SEQ), VM, VM, VM],
        out_specs=[out(SEQ, D), out(SEQ, 3 * D), out(SEQ, D), out(8, D), out(PD, D)],
        cost_estimate=cost(1.2e9 * count, 3e6 * count),
    )(bh1, h0, qkv, att, noisy, mods, bias, blocks)


def last_gradients(parts):
    flat = lambda v: v.reshape(-1, v.shape[-1])
    arrays = [flat(v) for part in parts for v in part]
    return pl.pallas_call(
        last_kernel,
        name="last_gradients",
        out_shape=shape((2, 16, LATE, D), BF),
        in_specs=[VM] * len(arrays),
        out_specs=VM,
        cost_estimate=cost(1.2e9, 9e6),
    )(*arrays)


def cond_back(images, class_ids, gm2, pre, th, cond, features, mod_w, fmod_w, tout_w, sums, align, gm3):
    return pl.pallas_call(
        functools.partial(cond_back_kernel, images),
        name="cond_back",
        out_shape=shape((4, PAY, D), BF),
        in_specs=[SM] + [VM] * (10 + len(gm3)),
        out_specs=VM,
        cost_estimate=cost(1e8, 4e6),
    )(class_ids, gm2, pre, th, cond, features, mod_w, fmod_w, tout_w, sums, align, *gm3)


def position_table():
    quarter = D // 4
    frequencies = 1.0 / 10000.0 ** (jnp.arange(quarter, dtype=jnp.float32) / quarter)
    cell_ids = jnp.arange(SEQ, dtype=jnp.int32)
    row_arg = (cell_ids // GRID).astype(jnp.float32)[:, None] * frequencies[None, :]
    col_arg = (cell_ids % GRID).astype(jnp.float32)[:, None] * frequencies[None, :]
    return jnp.concatenate(
        [jnp.sin(col_arg), jnp.cos(col_arg), jnp.sin(row_arg), jnp.cos(row_arg)], axis=1
    )


def time_features(tstep_idx):
    half_freq = FREQ // 2
    frequencies = jnp.exp(-math.log(10000.0) * jnp.arange(half_freq, dtype=jnp.float32) / half_freq)
    angles = (tstep_idx.astype(jnp.float32) + 0.5)[:, None] * frequencies[None, :]
    return jnp.concatenate([jnp.cos(angles), jnp.sin(angles)], axis=1)


def body(
    noisy,
    velocity,
    tstep_idx,
    class_ids,
    time_weight,
    dino,
    owner_map,
    adam_flat,
    adam_m,
    adam_v,
    blocks_w,
    stat_left,
    stat_right,
    root_left,
    root_right,
):
    dp, group = lax.axis_size("dp"), lax.axis_size("shard")
    near = is_near(dp, group)
    images = noisy.shape[0]
    total_img = images * dp * group
    at = jnp.stack([jnp.asarray(v, jnp.int32) for v in coordinates()])
    flat_w = adam_flat.reshape(-1, 128)
    flat_m = adam_m.reshape(-1, 128)
    flat_v = adam_v.reshape(-1, 128)
    mine = flat_w.astype(BF)
    features = jnp.pad(time_features(tstep_idx), ((0, 4), (0, 0)))
    pos = position_table()
    noisy = jnp.transpose(noisy, (0, 2, 1))
    velocity = jnp.transpose(velocity, (0, 2, 1))
    rows = flat_w.shape[0]
    if near:
        cut = rows // 16 * 8 + 8 if rows // 8 % 2 else rows // 2
        block_parts = gather_blocks(blocks_w.astype(BF))
        pieces, (at, features, pos) = gather_flat(mine, cut, (at, features, pos))
        places = flat_places(cut)
    else:
        pieces = [lax.all_gather(mine, AXES, axis=0, tiled=True)[None]]
        places = [(0, lambda i, at: 0)]
        slot_low = lax.all_gather(blocks_w.astype(BF), "shard", axis=0, tiled=True)
        block_ids = jnp.arange(NBLK, dtype=jnp.int32)
        slot_of = jnp.sum(
            block_ids[:, None] * (owner_map[:, None] == block_ids[None, :]).astype(jnp.int32), axis=0
        )
        block_parts = [jnp.take(slot_low, slot_of, axis=0)]
    (mods, pre, th, cond, mod_w, fmod_w, tout_w, align_low, bias, patch_low, final_low) = conditioning(
        at, class_ids, features, pieces, places, rows)
    h0, qkv, att, h1, blocks = front(at, owner_map, noisy, mods, bias, patch_low, pos, block_parts)
    bh1, gm2, early, sums = middle(
        total_img, time_weight, h1, velocity, dino, mods, bias, blocks, align_low, final_low)
    if near:
        early = reduce_units(early)
    parts, gm3 = [], []
    for first, count in ((0, 1), (1, images - 1)):
        bb1, bp, act, gm, patch = attention_back(first, count, bh1, h0, qkv, att, noisy, mods, bias, blocks)
        parts.append((act, bp, att[first : first + count], bb1))
        gm3 += [gm, patch]
    late = last_gradients(parts)
    align = early[4 * UNIT :] if near else jnp.zeros((UNIT, D), BF)
    pay = cond_back(images, class_ids, gm2, pre, th, cond, features, mod_w, fmod_w, tout_w, sums, align, gm3)
    if near:
        late = reduce_units(late)
        grads = gather_owned(late, early[: 4 * UNIT], owner_map)
        parts = gather_rows(pay)
        loss, upd, new_m, new_v = adam_near(at, parts, flat_w, flat_m, flat_v)
        *grads, loss, upd, new_m, new_v = lax.optimization_barrier((*grads, loss, upd, new_m, new_v))
    else:
        early = early.reshape(2, 16, 5, UNIT, D).transpose(0, 2, 1, 3, 4).reshape(2, 5, D, D)
        late = late.reshape(2, 16, 2, UNIT, D).transpose(0, 2, 1, 3, 4).reshape(4, D, D)
        grad_model = jnp.concatenate([late, early[:, :4].reshape(8, D, D)])
        pays = lax.all_gather(pay, AXES, axis=0, tiled=False)
        align_sum = lax.psum(early[:, 4].astype(F32), AXES)
        loss, upd, new_m, new_v = adam_wide(pays, align_sum, flat_w, flat_m, flat_v)
        slots = jnp.take(grad_model, owner_map, axis=0)
        owned = lax.psum_scatter(slots, "shard", scatter_dimension=0, tiled=True)
        grads = [lax.psum(owned.astype(F32), "dp").astype(BF)]
    block_update, new_left, new_right = shampoo(
        at, grads, blocks_w, stat_left, stat_right, root_left, root_right)
    return (loss, block_update, new_left, new_right,
            upd.reshape(-1), new_m.reshape(-1), new_v.reshape(-1))


def is_near(dp, group):
    return (dp, group) == (8, 4)


def solution(mesh):
    return jax.shard_map(
        body,
        mesh=mesh,
        in_specs=(
            P(("dp", "shard"), None, None),
            P(("dp", "shard"), None, None),
            P(("dp", "shard")),
            P(("dp", "shard")),
            P(("dp", "shard")),
            P(("dp", "shard"), None, None),
            P(),
            P(("dp", "shard")),
            P(("dp", "shard")),
            P(("dp", "shard")),
            P("shard", None, None),
            P("shard", None, None),
            P("shard", None, None),
            P("shard", None, None),
            P("shard", None, None),
        ),
        out_specs=(
            P(),
            P("shard", None, None),
            P("shard", None, None),
            P("shard", None, None),
            P(("dp", "shard")),
            P(("dp", "shard")),
            P(("dp", "shard")),
        ),
        check_vma=False,
    )
```

```python
import functools
import math

import jax
import jax.numpy as jnp
from jax import lax
from jax.experimental import pallas as pl
from jax.experimental.pallas import tpu as pltpu
from jax.sharding import PartitionSpec as P


D = 384
HEADS = 6
HDIM = 64
F = 1536
PD = 16
GRID = 16
SEQ = 256
FREQ = 256
DINO = 768
STEP = 10
NBLK = 12
ADAM_PAD = 2129920

BETA_ONE = 0.9
BETA_TWO = 0.95
ADAM_EPS = 1e-08
ADAM_RATE = 0.01
DECAY_RATE = 0.1
STAT_BETA = 0.9
SHAMPOO_RATE = 0.02
RMS_EPS = 1e-08
REPA_WEIGHT = 0.5
NORM_EPS = 1e-06
QK_SCALE = HDIM ** (-0.5)

AXES = ("dp", "shard")
BF = jnp.bfloat16
F32 = jnp.float32
VM = pl.BlockSpec(memory_space=pltpu.VMEM)
SM = pl.BlockSpec(memory_space=pltpu.SMEM)

FLAT_ROWS = ADAM_PAD // 128
R_PATCH = 0
R_PATCH_B = 48
R_TIME_IN = 51
R_TIME_IN_B = 819
R_TIME_OUT = 822
R_TIME_OUT_B = 1974
R_CLASS = 1977
R_MOD = 4980
R_MOD_B = 11892
R_QUERY_B = 11910
R_VALUE_B = 11913
R_PROJ_B = 11916
R_HIDDEN_B = 11919
R_DOWN_B = 11931
R_FMOD = 11934
R_FMOD_B = 14238
R_FINAL = 14244
R_FINAL_B = 14292
ALIGN_ROWS = 2310

PAY = 64
PLANE_ROWS = FLAT_ROWS // 4


def shape(dims, kind=F32):
    return jax.ShapeDtypeStruct(dims, kind)


def cost(flops, moved):
    return pl.CostEstimate(flops=int(flops), bytes_accessed=int(moved), transcendentals=0)


def room(mib):
    return pltpu.CompilerParams(vmem_limit_bytes=mib * 1024 * 1024)


def mm(left, right):
    return jnp.dot(left, right, preferred_element_type=F32)


def mm_nt(left, right):
    return lax.dot_general(left, right, (((1,), (1,)), ((), ())), preferred_element_type=F32)


def mm_tn(left, right):
    return lax.dot_general(left, right, (((0,), (0,)), ((), ())), preferred_element_type=F32)


def silu(v):
    return v / (1.0 + jnp.exp(-v))


def silu_slope(v):
    s = 1.0 / (1.0 + jnp.exp(-v))
    return s * (1.0 + v * (1.0 - s))


def split3(v):
    one = v.astype(BF)
    rest = v - one.astype(F32)
    two = rest.astype(BF)
    return one, two, (rest - two.astype(F32)).astype(BF)


def split2(v):
    one = v.astype(BF)
    return one, (v - one.astype(F32)).astype(BF)


def stack3(v):
    one, two, three = split3(v)
    return jnp.concatenate([one.astype(F32), two.astype(F32), three.astype(F32)], axis=0).astype(BF)


def fold3(v):
    third = v.shape[0] // 3
    return v[:third] + v[third : 2 * third] + v[2 * third :]


def place_of(z, x, y, c):
    return ((z * 2 + x) * 2 + y) * 2 + c


def permutation(move):
    pairs = []
    for z in range(4):
        for x in range(2):
            for y in range(2):
                for c in range(2):
                    pairs.append((place_of(z, x, y, c), place_of(*move(z, x, y, c))))
    return pairs


TO_C = permutation(lambda z, x, y, c: (z, x, y, 1 - c))
TO_Y = permutation(lambda z, x, y, c: (z, x, 1 - y, c))
TO_X = permutation(lambda z, x, y, c: (z, 1 - x, y, c))
TO_Z = [permutation(lambda z, x, y, c, d=d: ((z + d) % 4, x, y, c)) for d in range(4)]


def send(value, pairs):
    return lax.ppermute(value, AXES, pairs)


def coordinates():
    dp = lax.axis_index("dp")
    sh = lax.axis_index("shard")
    return dp // 2, dp % 2, sh // 2, sh % 2


TO_XY = permutation(lambda z, x, y, c: (z, 1 - x, 1 - y, c))
TO_CY = permutation(lambda z, x, y, c: (z, x, 1 - y, 1 - c))
TO_PAIR = permutation(lambda z, x, y, c: (z + 1 - 2 * (z % 2), x, y, c))


def send_plane(value):
    return [send(value, TO_X), send(value, TO_Y), send(value, TO_XY)]


def gather_flat(piece, cut, ready):
    turned = [send(piece, TO_Z[d]) for d in (1, 2, 3)]
    own_x, own_y = send(piece, TO_X), send(piece, TO_Y)
    first = jnp.stack([t[:cut] for t in turned])
    second = jnp.stack([t[cut:] for t in turned])
    first_x = send(first, TO_X)
    second_y = send(second, TO_Y)
    first_x, second_y, ready = lax.optimization_barrier((first_x, second_y, ready))
    first = jnp.concatenate([own_x[None, :cut], first, first_x])
    second = jnp.concatenate([own_y[None, cut:], second, second_y])
    far = [send(first, TO_Y), send(second, TO_X)]
    own = [piece, own_x[cut:], own_y[:cut]]
    own_c = [send(p, TO_C) for p in own]
    rest_c = [send(p, TO_C) for p in (first, second, *far)]
    return [p[None] for p in own] + [first, second] + far + [p[None] for p in own_c] + rest_c, ready


def flip(value, bit):
    return 1 - value if bit else value


def flat_places(cut):
    def near(dc, dx, dy):
        return lambda i, at: place_of(at[0], flip(at[1], dx), flip(at[2], dy), flip(at[3], dc))

    def far(dc, kind):
        def entry(i, at):
            z, x, y, c = at
            dz, other = (0, 1) if i == 0 else ((i - 1) % 3 + 1, (i - 1) // 3)
            dx, dy = {0: (other, 0), 1: (0, other), 2: (other, 1), 3: (1, other)}[kind]
            return place_of(lax.rem(z + 4 - dz, 4), flip(x, dx), flip(y, dy), flip(c, dc))

        return entry

    places = []
    for dc in (0, 1):
        places += [(0, near(dc, 0, 0)), (cut, near(dc, 1, 0)), (0, near(dc, 0, 1))]
        places += [((0, cut, 0, cut)[kind], far(dc, kind)) for kind in range(4)]
    return places


def gather_rows(keep, away):
    turned = [send(v, TO_Z[d + 1]) for d, v in enumerate(away)]
    column = jnp.stack([keep] + turned)
    plane = [column] + send_plane(column)
    return plane + [send(p, TO_C) for p in plane]


def read_coordinates(ref):
    return ref[0], ref[1], ref[2], ref[3]


def cond_kernel(places, rows, at_ref, cls_ref, feat_ref, *refs):
    count = len(places)
    pieces = refs[:count]
    (mods_ref, pre_ref, th_ref, cond_ref, modw_ref, fmodw_ref, tout_ref, align_ref, bias_ref,
     patch_ref, final_ref, flat, rolled) = refs[count:]
    at = read_coordinates(at_ref)
    for ref, (offset, entry) in zip(pieces, places):
        for i in range(ref.shape[0]):
            start = pl.multiple_of(entry(i, at) * rows + offset, 8)
            flat[pl.ds(start, ref.shape[1]), :] = ref[i].astype(F32)

    def row(first, count):
        return jnp.concatenate([flat[first + l : first + l + 1, :] for l in range(count)], axis=1)

    def columns(first, depth, count, which):
        return flat[pl.ds(first + which, depth, stride=count), :].astype(BF)

    def wide(v, first, depth, count, keep=None):
        stacked = stack3(v)
        out = []
        for j in range(count):
            w = columns(first, depth, count, j)
            if keep is not None:
                keep[:, 128 * j : 128 * j + 128] = w
            out.append(fold3(mm(stacked, w)))
        return jnp.concatenate(out, axis=1)

    pre = wide(feat_ref[...], R_TIME_IN, FREQ, 3) + row(R_TIME_IN_B, 3)
    th = silu(pre)
    picked = []
    for m in range(4):
        r = R_CLASS + 3 * cls_ref[m]
        picked.append(jnp.concatenate([flat[pl.ds(r + l, 1), :] for l in range(3)], axis=1))
    picked = jnp.concatenate(picked + [jnp.zeros((4, D), F32)], axis=0)
    cond = wide(th, R_TIME_OUT, D, 3, tout_ref) + row(R_TIME_OUT_B, 3) + picked
    act = silu(cond)
    pre_ref[...] = pre
    th_ref[...] = th
    cond_ref[...] = cond
    mods_ref[:, : 6 * D] = wide(act, R_MOD, D, 18, modw_ref) + row(R_MOD_B, 18)
    mods_ref[:, 6 * D :] = wide(act, R_FMOD, D, 6, fmodw_ref) + row(R_FMOD_B, 6)

    spot = lax.broadcasted_iota(jnp.int32, (ALIGN_ROWS, 128), 1)
    here = pltpu.roll(flat[R_FINAL_B : R_FINAL_B + ALIGN_ROWS, :], 112, 1)
    after = pltpu.roll(flat[R_FINAL_B + 1 : R_FINAL_B + 1 + ALIGN_ROWS, :], 112, 1)
    rolled[...] = jnp.where(spot < 112, here, after)
    for j in range(6):
        align_ref[:, 128 * j : 128 * j + 128] = rolled[pl.ds(j, D, stride=6), :].astype(BF)

    bias_ref[...] = jnp.zeros_like(bias_ref)
    for at_row, first in ((0, R_PATCH_B), (1, R_QUERY_B), (2, R_VALUE_B), (3, R_PROJ_B),
                          (4, R_HIDDEN_B), (5, R_HIDDEN_B + 3), (6, R_HIDDEN_B + 6),
                          (7, R_HIDDEN_B + 9), (8, R_DOWN_B)):
        bias_ref[at_row : at_row + 1, :] = row(first, 3)
    for half in range(2):
        bias_ref[9 + half : 10 + half, :] = jnp.concatenate(
            [rolled[2304 + 3 * half + l : 2305 + 3 * half + l, :] for l in range(3)], axis=1)
    lane = lax.broadcasted_iota(jnp.int32, (1, 128), 1)
    bias_ref[11:12, :128] = jnp.where(lane < PD, flat[R_FINAL_B : R_FINAL_B + 1, :], 0.0)
    patch = [flat[pl.ds(R_PATCH + l, PD, stride=3), :] for l in range(3)]
    patch_ref[...] = jnp.concatenate(patch, axis=1).astype(BF)
    spread = (lax.broadcasted_iota(jnp.int32, (D, 48), 0) // 8
              == lax.broadcasted_iota(jnp.int32, (D, 48), 1)).astype(F32).astype(BF)
    wide_rows = mm(spread, flat[R_FINAL : R_FINAL + 48, :].astype(BF))
    keep = (lax.broadcasted_iota(jnp.int32, (D, 128), 1) // PD
            == lax.broadcasted_iota(jnp.int32, (D, 128), 0) % 8)
    fold = (lax.broadcasted_iota(jnp.int32, (128, 128), 0) % PD
            == lax.broadcasted_iota(jnp.int32, (128, 128), 1)).astype(F32).astype(BF)
    final_ref[...] = mm(jnp.where(keep, wide_rows, 0.0).astype(BF), fold).astype(BF)


def conditioning(at, classes, features, pieces, places, rows):
    kernel = functools.partial(cond_kernel, places, rows)
    return pl.pallas_call(
        kernel,
        name="conditioning",
        out_shape=(shape((8, 8 * D)), shape((8, D)), shape((8, D)), shape((8, D)),
                   shape((D, 6 * D), BF), shape((D, 2 * D), BF), shape((D, D), BF),
                   shape((D, DINO), BF), shape((16, D)), shape((PD, D), BF), shape((D, 128), BF)),
        in_specs=[SM, SM, VM] + [VM] * len(pieces),
        out_specs=[VM] * 11,
        scratch_shapes=[pltpu.VMEM((FLAT_ROWS + 8, 128), F32), pltpu.VMEM((ALIGN_ROWS, 128), F32)],
        compiler_params=room(28),
        cost_estimate=pl.CostEstimate(flops=10**9, bytes_accessed=10**7, transcendentals=0),
    )(at, classes, features, *pieces)


def gather_blocks(mine):
    z, _, _, _ = coordinates()
    half = lax.dynamic_slice_in_dim(mine, 192 * (z % 2), 192, 1)
    near = send(half, TO_Y)
    far = send(near, TO_PAIR)
    return [mine, near, far, send(mine, TO_C), send(near, TO_C), send(far, TO_C)]


def fetch_blocks(at, own_ref, refs, out_ref, sems):
    if len(refs) == 1:
        return [pltpu.make_async_copy(refs[0], out_ref, sems.at[0])]
    z, _, y, c = at
    copies = []
    odd = lax.rem(z, 2)
    for dc in range(2):
        core = flip(c, dc)
        for t in range(3):
            mine, near, far = refs[3 * dc : 3 * dc + 3]
            here = own_ref[3 * (2 * y + core) + t]
            there = own_ref[3 * (2 * (1 - y) + core) + t]
            for source, block, rows in (
                (mine.at[t], here, None),
                (near.at[t], there, pl.ds(pl.multiple_of(192 * odd, 16), 192)),
                (far.at[t], there, pl.ds(pl.multiple_of(192 * (1 - odd), 16), 192)),
            ):
                target = out_ref.at[block] if rows is None else out_ref.at[block, rows]
                copies.append(pltpu.make_async_copy(source, target, sems.at[len(copies)]))
    return copies


UNIT = 24


def unit_of(z, x, y):
    return (2 * x + y) * 4 + z


def quarter_kernel(at_ref, mine_ref, got_ref, *out_refs):
    _, x, y, _ = read_coordinates(at_ref)
    for out_ref, (dx, dy) in zip(out_refs, ((0, 0), (1, 0), (0, 1), (1, 1))):
        rows = pl.ds(4 * (2 * flip(x, dx) + flip(y, dy)), 4)
        out_ref[...] = (mine_ref[rows].astype(F32) + got_ref[rows].astype(F32)).astype(BF)


def turn_kernel(at_ref, *refs):
    z, _, _, _ = read_coordinates(at_ref)
    for d, out_ref in enumerate(refs[4:]):
        unit = lax.rem(z + d, 4)
        out_ref[...] = sum(ref[unit].astype(F32) for ref in refs[:4]).astype(BF)


def reduce_units(at, mine, other):
    rows = mine.shape[1]
    got = send(other, TO_C)
    own, *away = pl.pallas_call(
        quarter_kernel,
        name="quarter",
        out_shape=(shape((4, rows, D), BF),) * 4,
        in_specs=[SM, VM, VM],
        out_specs=[VM] * 4,
        compiler_params=room(12),
        cost_estimate=cost(1e6, 4e6),
    )(at, mine, got)
    got = [send(v, pairs) for v, pairs in zip(away, (TO_X, TO_Y, TO_XY))]
    own, *away = pl.pallas_call(
        turn_kernel,
        name="turn",
        out_shape=(shape((rows, D), BF),) * 4,
        in_specs=[SM] + [VM] * 4,
        out_specs=[VM] * 4,
        compiler_params=room(8),
        cost_estimate=cost(1e6, 2e6),
    )(at, own, *got)
    return [own] + [send(v, TO_Z[d + 1]) for d, v in enumerate(away)]


def owner_kernel(at_ref, own_ref, *refs):
    late, early = refs[:4], refs[4:8]
    out_refs, total = refs[8:12], refs[12]
    _, _, y, c = read_coordinates(at_ref)
    one = sum(ref[...].astype(F32) for ref in late)
    two = sum(ref[0 : 4 * UNIT, :].astype(F32) for ref in early)
    for k in range(6):
        total[k] = (one[UNIT * k : UNIT * k + UNIT] if k < 2 else two[UNIT * (k - 2) : UNIT * (k - 1)])
    for out_ref, (dy, dc) in zip(out_refs, ((0, 0), (0, 1), (1, 0), (1, 1))):
        first = 3 * (2 * flip(y, dy) + flip(c, dc))
        for t in range(3):
            block = own_ref[first + t]
            low = block < 4
            part = jnp.where(low, lax.div(block, 2), lax.div(block - 4, 4))
            entry = jnp.where(low, lax.rem(block, 2), 2 + lax.rem(jnp.maximum(block - 4, 0), 4))
            out_ref[t] = jnp.where(part == c, total[entry], 0.0).astype(BF)


def join_kernel(own_ref, pair_ref, near_ref, far_ref, out_ref):
    out_ref[0] = own_ref[...] + pair_ref[...]
    out_ref[1] = near_ref[...] + far_ref[...]


def gather_owned(at, late, early, owner_map):
    piece = (3, UNIT, D)
    own, to_c, to_y, to_cy = pl.pallas_call(
        owner_kernel,
        name="owner_rows",
        out_shape=(shape(piece, BF),) * 4,
        in_specs=[SM, SM] + [VM] * 8,
        out_specs=[VM] * 4,
        scratch_shapes=[pltpu.VMEM((6, UNIT, D), F32)],
        compiler_params=room(8),
        cost_estimate=cost(1e6, 1e6),
    )(at, owner_map, *late, *early)
    far, near, pair = send(to_cy, TO_CY), send(to_y, TO_Y), send(to_c, TO_C)
    both = pl.pallas_call(
        join_kernel,
        name="join",
        out_shape=shape((2,) + piece, BF),
        in_specs=[VM] * 4,
        out_specs=VM,
        compiler_params=room(8),
        cost_estimate=cost(1e6, 1e6),
    )(own, pair, near, far)
    column = [both] + [send(both, TO_Z[d]) for d in (1, 2, 3)]
    return column + [send(v, TO_X) for v in column]


def plane_gradient(plane, pay_ref, flat, rolled, align):
    rows = 8 * pay_ref.shape[0]

    def tile(j):
        return pay_ref[:, 8 * j : 8 * j + 8, :].astype(F32).reshape(rows, D)

    def sums(first, last):
        return jnp.sum(pay_ref[:, first:last, :].astype(F32), axis=0)

    upper = lax.broadcasted_iota(jnp.int32, (rows, 1), 0) % 8 < 4

    def first(v):
        return jnp.where(upper, v, 0.0)

    def second(v):
        return jnp.where(upper, 0.0, v)

    def put_row(v, row):
        for l in range(v.shape[1] // 128):
            flat[row + l : row + l + 1, :] = v[:, 128 * l : 128 * l + 128]

    def put_matrix(v, row, count, which):
        for l in range(v.shape[1] // 128):
            flat[pl.ds(row + which + l, v.shape[0], stride=count), :] = v[:, 128 * l : 128 * l + 128]

    def classes(ids, g_low):
        numbers = (ids[:, 0:1] * 256.0 + ids[:, 1:2]).astype(jnp.int32)
        for part in range(3):
            height = 336 if part < 2 else 329
            marks = lax.broadcasted_iota(jnp.int32, (rows, 336), 1) + 336 * part
            hits = first(jnp.where(marks == numbers, 1.0, 0.0)).astype(BF)
            put_matrix(mm_tn(hits, g_low)[:height], R_CLASS + 3 * 336 * part, 3, 0)

    def modulations(low, bias):
        act = tile(0)[:, low : low + 256]
        halves = (first(act).astype(BF), second(act).astype(BF))
        for t in range(3):
            g = tile(1 + t)
            for half in range(2):
                put_matrix(mm_tn(halves[half], g.astype(BF)), R_MOD + 18 * low, 18, 3 * (t + 3 * half))
                if bias:
                    put_row(column_sum((first, second)[half](g)), R_MOD_B + 3 * (t + 3 * half))

    def finals(which, bias):
        act, g = tile(0), tile(which)
        for half, part in enumerate((first, second)):
            put_matrix(mm_tn(part(act).astype(BF), g.astype(BF)), R_FMOD, 6, 3 * half)
            if bias:
                put_row(column_sum(part(g)), R_FMOD_B + 3 * half)

    if plane == 0:
        left, g = tile(0).astype(BF), tile(1)
        g_cond, g_pre = first(g), second(g)
        put_matrix(mm_tn(left[:, :FREQ], g_pre.astype(BF)), R_TIME_IN, 3, 0)
        put_row(column_sum(g_pre), R_TIME_IN_B)
        put_matrix(mm_tn(left, g_cond.astype(BF)), R_TIME_OUT, 3, 0)
        put_row(column_sum(g_cond), R_TIME_OUT_B)
        classes(tile(2)[:, :128], g.astype(BF))
        total = sums(40, 64)
        for l in range(3):
            flat[pl.ds(R_PATCH + l, PD, stride=3), :] = total[0:16, 128 * l : 128 * l + 128]
        put_row(total[16:17], R_PATCH_B)
    if plane == 1:
        classes(tile(5)[:, :128], tile(4).astype(BF))
        modulations(0, False)
    if plane == 2:
        modulations(128, True)
        finals(4, False)
        total = sums(40, 48)
        for k, row in enumerate((R_QUERY_B, R_VALUE_B, R_PROJ_B, R_HIDDEN_B, R_HIDDEN_B + 3, R_HIDDEN_B + 6,
                                 R_HIDDEN_B + 9, R_DOWN_B)):
            put_row(total[k : k + 1], row)
    if plane == 3:
        finals(1, True)
        total = sums(40, 64)
        for l in range(3):
            flat[R_FINAL + 16 * l : R_FINAL + 16 * l + 16, :] = total[0:16, 128 * l : 128 * l + 128]
        rolled[0:8, :] = jnp.zeros((8, 128), F32)
        rolled[8 + ALIGN_ROWS :, :] = jnp.zeros_like(rolled[8 + ALIGN_ROWS :, :])
        rolled[7:8, :] = pltpu.roll(total[16:17, 0:128], 112, 1)
        for half in range(2):
            for l in range(3):
                lanes = slice(128 * l, 128 * l + 128)
                rolled[pl.ds(8 + 3 * half + l, D, stride=6), :] = align[half, :, lanes].astype(F32)
                r = 8 + 2304 + 3 * half + l
                rolled[r : r + 1, :] = total[17 + half : 18 + half, lanes]
        count = FLAT_ROWS - R_FINAL_B
        spot = lax.broadcasted_iota(jnp.int32, (count, 128), 1)
        here = pltpu.roll(rolled[8 : 8 + count, :], 16, 1)
        before = pltpu.roll(rolled[7 : 7 + count, :], 16, 1)
        flat[R_FINAL_B:FLAT_ROWS, :] = jnp.where(spot < 16, before, here)


def loss_of(pay_ref):
    rows = 8 * pay_ref.shape[0]
    parts = pay_ref[:, PAY - 8 : PAY, 0:128].astype(F32).reshape(rows, 128)
    parts = column_sum(jnp.where(lax.broadcasted_iota(jnp.int32, (rows, 128), 0) % 8 == 7, parts, 0.0))
    return parts[:, 0:1] + parts[:, 1:2] + parts[:, 2:3]


def adam_near_kernel(at_ref, *refs):
    parts = refs[:8]
    w_ref, m_ref, v_ref, loss_ref, upd_ref, new_m_ref, new_v_ref, pay, align, flat, rolled = refs[8:]
    at = read_coordinates(at_ref)
    z, x, y, c = at
    for k, ref in enumerate(parts):
        dc, dy, dx = k // 4, k // 2 % 2, k % 2
        for dz in range(4):
            there = (lax.rem(z + 4 - dz, 4), flip(x, dx), flip(y, dy), flip(c, dc))
            value = ref[dz].astype(F32)
            pay[place_of(*there)] = value
            start = pl.multiple_of(unit_of(*there[:3]) * UNIT, 8)
            align[there[3], pl.ds(start, UNIT), :] = value[16:40]
    loss_ref[...] = loss_of(pay)
    for plane in range(4):
        @pl.when(z == plane)
        def _():
            plane_gradient(plane, pay, flat, rolled, align)
    size = w_ref.shape[0]
    start = pl.multiple_of(place_of(z, x, y, c) * size, 8)
    adam_step(flat[pl.ds(start, size), :], w_ref, m_ref, v_ref, upd_ref, new_m_ref, new_v_ref)


def adam_plane_kernel(plane, pay_ref, align_ref, loss_ref, flat_ref, rolled):
    loss_ref[...] = loss_of(pay_ref)
    plane_gradient(plane, pay_ref, flat_ref, rolled, align_ref)


def adam_step(grad, w_ref, m_ref, v_ref, upd_ref, new_m_ref, new_v_ref):
    new_m = BETA_ONE * m_ref[...] + (1.0 - BETA_ONE) * grad
    new_v = BETA_TWO * v_ref[...] + (1.0 - BETA_TWO) * grad * grad
    new_m_ref[...] = new_m
    new_v_ref[...] = new_v
    right_m = new_m / (1.0 - BETA_ONE**STEP)
    right_v = new_v / (1.0 - BETA_TWO**STEP)
    upd_ref[...] = -ADAM_RATE * (right_m / (jnp.sqrt(right_v) + ADAM_EPS) + DECAY_RATE * w_ref[...])


ROLL_ROWS = 8 + FLAT_ROWS - R_FINAL_B + 8


ROLL_ROWS = 8 + FLAT_ROWS - R_FINAL_B + 8


def adam_near(at, parts, flat_w, m, v):
    size = flat_w.shape
    loss, upd, new_m, new_v = pl.pallas_call(
        adam_near_kernel,
        name="adam",
        out_shape=(shape((1, 1)), shape(size), shape(size), shape(size)),
        in_specs=[SM] + [VM] * 11,
        out_specs=[VM] * 4,
        scratch_shapes=[pltpu.VMEM((32, PAY, D), F32), pltpu.VMEM((2, D, D), F32),
                        pltpu.VMEM((FLAT_ROWS, 128), F32), pltpu.VMEM((ROLL_ROWS, 128), F32)],
        compiler_params=room(24),
        cost_estimate=pl.CostEstimate(flops=10**9, bytes_accessed=10**7, transcendentals=0),
    )(at, *parts, flat_w, m, v)
    return loss[0, 0], upd, new_m, new_v


def adam_wide(pays, align, flat_w, m, v):
    grads = []
    for plane in range(4):
        loss, flat = pl.pallas_call(
            functools.partial(adam_plane_kernel, plane),
            name="adam_gradient",
            out_shape=(shape((1, 1)), shape((FLAT_ROWS, 128))),
            in_specs=[VM] * 2,
            out_specs=[VM] * 2,
            scratch_shapes=[pltpu.VMEM((ROLL_ROWS, 128), F32)],
        )(pays[:, plane], align)
        grads.append(flat[PLANE_ROWS * plane : PLANE_ROWS * (plane + 1)])
    size = flat_w.shape[0]
    place = lax.axis_index("dp") * lax.axis_size("shard") + lax.axis_index("shard")
    grad = lax.dynamic_slice_in_dim(jnp.concatenate(grads), place * size, size, 0)
    upd, new_m, new_v = pl.pallas_call(
        lambda g, *refs: adam_step(g[...], *refs),
        name="adam",
        out_shape=(shape(flat_w.shape),) * 3,
        in_specs=[VM] * 4,
        out_specs=[VM] * 3,
    )(grad, flat_w, m, v)
    return loss[0, 0], upd, new_m, new_v


def shampoo_kernel(near, at_ref, *refs):
    t = pl.program_id(0)
    if near:
        parts = refs[:8]
        w_ref, sl_ref, sr_ref, rl_ref, rr_ref, upd_ref, nl_ref, nr_ref, grad = refs[8:]
        z, x, y, _ = read_coordinates(at_ref)
        for dx in range(2):
            for dz in range(4):
                for dy in range(2):
                    unit = unit_of(lax.rem(z + 4 - dz, 4), flip(x, dx), flip(y, dy))
                    rows = pl.ds(pl.multiple_of(unit * UNIT, 8), UNIT)
                    grad[rows, :] = parts[4 * dx + dz][dy, t].astype(F32)
        g = grad[...].astype(BF)
    else:
        grad_ref, w_ref, sl_ref, sr_ref, rl_ref, rr_ref, upd_ref, nl_ref, nr_ref = refs
        g = grad_ref[t]
    nl_ref[0] = STAT_BETA * sl_ref[t] + (1.0 - STAT_BETA) * mm_nt(g, g)
    nr_ref[0] = STAT_BETA * sr_ref[t] + (1.0 - STAT_BETA) * mm_tn(g, g)
    left = mm(jnp.concatenate(split2(rl_ref[t]), axis=1), jnp.concatenate([g, g], axis=0))
    l_one, l_two = split2(left)
    r_one, r_two = split2(rr_ref[t])
    p = mm(jnp.concatenate([l_one, l_two, l_one], axis=1), jnp.concatenate([r_one, r_one, r_two], axis=0))
    mean = jnp.sum(jnp.sum(p * p, axis=1, keepdims=True), axis=0, keepdims=True) * (1.0 / (D * D))
    root = jnp.sqrt(mean)
    upd_ref[0] = -SHAMPOO_RATE * (p / (root + RMS_EPS) + DECAY_RATE * w_ref[t])


def shampoo(at, grads, blocks_w, stat_left, stat_right, root_left, root_right):
    near = len(grads) == 8
    slots = blocks_w.shape[0]
    one = pl.BlockSpec((1, D, D), lambda t: (t, 0, 0))
    return pl.pallas_call(
        functools.partial(shampoo_kernel, near),
        name="shampoo",
        grid=(slots,),
        out_shape=(shape((slots, D, D)),) * 3,
        in_specs=[SM] + [VM] * (len(grads) + 5),
        out_specs=[one] * 3,
        scratch_shapes=[pltpu.VMEM((D, D), F32)] if near else [],
        compiler_params=room(26),
        cost_estimate=pl.CostEstimate(flops=3 * 10**9, bytes_accessed=15 * 10**6, transcendentals=0),
    )(at, *grads, blocks_w, stat_left, stat_right, root_left, root_right)


GELU_C = math.sqrt(2.0 / math.pi)
GELU_D = 0.044715
EARLY = 5 * 24
LATE = 2 * 24
SUMS_MLP = 24


def norm_stats(v):
    centered = v - jnp.sum(v, axis=-1, keepdims=True) * (1.0 / D)
    inv = lax.rsqrt(jnp.sum(centered * centered, axis=-1, keepdims=True) * (1.0 / D) + NORM_EPS)
    return centered * inv, inv


def norm_back(g, normed, inv):
    mean_g = jnp.sum(g, axis=-1, keepdims=True) * (1.0 / D)
    mean_gn = jnp.sum(g * normed, axis=-1, keepdims=True) * (1.0 / D)
    return inv * (g - mean_g - normed * mean_gn)


def column_sum(v):
    return jnp.sum(v, axis=0, keepdims=True)


def head(v, h):
    return v[:, HDIM * h : HDIM * h + HDIM]


def put_pair(core, mine_ref, other_ref, j, zero, one):
    zero, one = zero.astype(BF), one.astype(BF)
    mine, other = jnp.where(core == 0, zero, one), jnp.where(core == 0, one, zero)
    for u in range(16):
        rows = slice(24 * u, 24 * u + 24)
        mine_ref[u, 24 * j : 24 * j + 24, :] = mine[rows]
        other_ref[u, 24 * j : 24 * j + 24, :] = other[rows]


def front_kernel(at_ref, own_ref, noisy_ref, mods_ref, bias_ref, patch_ref, pos_ref, *refs):
    h0_ref, qkv_ref, att_ref, h1_ref, all_ref, w_ref, in_sems, out_sem = refs[-8:]
    i = pl.program_id(0)
    fetch = fetch_blocks(read_coordinates(at_ref), own_ref, refs[:-8], w_ref, in_sems)
    keep = pltpu.make_async_copy(w_ref, all_ref, out_sem)

    @pl.when(i == 0)
    def _():
        for copy in fetch:
            copy.start()
        for copy in fetch:
            copy.wait()
        keep.start()

    def mod(t):
        return mods_ref[pl.ds(i, 1), D * t : D * t + D]

    h0 = mm_tn(noisy_ref[0].astype(BF), patch_ref[...]) + bias_ref[0:1, :] + pos_ref[...]
    h0_ref[0] = h0
    normed, _ = norm_stats(h0)
    act = (normed * (1.0 + mod(1)) + mod(0)).astype(BF)
    q = (mm(act, w_ref[0]) + bias_ref[1:2, :]).astype(BF)
    k = mm(act, w_ref[1]).astype(BF)
    v = (mm(act, w_ref[2]) + bias_ref[2:3, :]).astype(BF)
    qkv_ref[0, :, 0:D] = q
    qkv_ref[0, :, D : 2 * D] = k
    qkv_ref[0, :, 2 * D :] = v
    outs = []
    for h in range(HEADS):
        s = mm_nt(head(q, h), head(k, h)) * QK_SCALE
        e = jnp.exp(s - jnp.max(s, axis=-1, keepdims=True))
        p = e * (1.0 / jnp.sum(e, axis=-1, keepdims=True))
        outs.append(mm(p.astype(BF), head(v, h)))
    att = jnp.concatenate(outs, axis=1).astype(BF)
    att_ref[0] = att
    h1_ref[0] = h0 + mod(2) * (mm(att, w_ref[3]) + bias_ref[3:4, :])

    @pl.when(i == pl.num_programs(0) - 1)
    def _():
        keep.wait()


def middle_kernel(images, total_img, at_ref, tw_ref, h1_ref, vel_ref, dino_ref, mods_ref, bias_ref, w_ref, aw_ref, fw_ref,
                  bh1_ref, gm_ref, mine_ref, other_ref, sums_ref,
                  act2_s, gelu_s, slope_s, bi_s, bb2_s, h1_s, ba_s, act3_s, bo_s):
    i = pl.program_id(0)
    rows = pl.ds(pl.multiple_of(i * SEQ, SEQ), SEQ)

    def mod(t):
        return mods_ref[pl.ds(i, 1), D * t : D * t + D]

    @pl.when(i == 0)
    def _():
        sums_ref[...] = jnp.zeros_like(sums_ref)

    h1 = h1_ref[0]
    n2, inv2 = norm_stats(h1)
    act2 = (n2 * (1.0 + mod(4)) + mod(3)).astype(BF)
    act2_s[rows, :] = act2
    branch = jnp.zeros((SEQ, D), F32) + bias_ref[8:9, :]
    for j in range(4):
        lanes = slice(D * j, D * j + D)
        x = mm(act2, w_ref[4 + j]) + bias_ref[4 + j : 5 + j, :]
        xx = x * x
        t = jnp.tanh(x * (GELU_C + (GELU_C * GELU_D) * xx))
        half = 0.5 + 0.5 * t
        g = (x * half).astype(BF)
        slope_s[:, lanes] = half + (0.5 * x) * (1.0 - t * t) * (GELU_C + (3.0 * GELU_C * GELU_D) * xx)
        gelu_s[rows, lanes] = g
        branch = branch + mm(g, w_ref[8 + j])
    h2 = h1 + mod(5) * branch
    n3, inv3 = norm_stats(h2)
    act3 = (n3 * (1.0 + mod(7)) + mod(6)).astype(BF)
    act3_s[rows, :] = act3
    out = mm(act3, fw_ref[...]) + bias_ref[11:12, 0:128]
    err = out[:, :PD] - vel_ref[0].T
    weight = tw_ref[i]
    loss = jnp.sum(column_sum(err * err), axis=1, keepdims=True) * (weight / (total_img * SEQ * PD))
    bo = jnp.concatenate([err * (2.0 * weight / (total_img * SEQ * PD)), jnp.zeros((SEQ, 128 - PD), F32)],
                         axis=1).astype(BF)
    bo_s[rows, :] = bo

    h1_low = h1.astype(BF)
    h1_s[rows, :] = h1_low
    aligned = mm(h1_low, aw_ref[...]) + jnp.concatenate([bias_ref[9:10, :], bias_ref[10:11, :]], axis=1)
    dino = dino_ref[0].astype(F32)
    dot = jnp.sum(aligned * dino, axis=-1, keepdims=True)
    ra = lax.rsqrt(jnp.sum(aligned * aligned, axis=-1, keepdims=True) + NORM_EPS)
    rd = lax.rsqrt(jnp.sum(dino * dino, axis=-1, keepdims=True) + NORM_EPS)
    scale = REPA_WEIGHT / (total_img * SEQ)
    both = ra * rd
    cosine = dot * both
    loss = loss - column_sum(cosine) * scale
    ba = (dino * (both * -scale) + aligned * (cosine * (ra * ra) * scale)).astype(BF)
    ba_s[rows, :] = ba
    through = mm_nt(ba, aw_ref[...])

    b3 = mm_nt(bo, fw_ref[...])
    bh2 = norm_back(b3 * (1.0 + mod(7)), n3, inv3)
    bb2 = (bh2 * mod(5)).astype(BF)
    bb2_s[rows, :] = bb2
    b2 = jnp.zeros((SEQ, D), F32)
    for j in range(4):
        lanes = slice(D * j, D * j + D)
        bi = (mm_nt(bb2, w_ref[8 + j]) * slope_s[:, lanes]).astype(BF)
        bi_s[rows, lanes] = bi
        sums_ref[16 + j : 17 + j, :] += column_sum(bi.astype(F32))
        b2 = b2 + mm_nt(bi, w_ref[4 + j])
    sums_ref[20:21, :] += column_sum(bb2.astype(F32))
    ba_sum = column_sum(ba.astype(F32))
    sums_ref[21:22, :] += ba_sum[:, :D]
    sums_ref[22:23, :] += ba_sum[:, D:]
    sums_ref[23:24, 0:128] += column_sum(bo.astype(F32))
    bh1_ref[0] = bh2 + norm_back(b2 * (1.0 + mod(4)), n2, inv2) + through
    gm_ref[0, 0:1, :] = column_sum(b2)
    gm_ref[0, 1:2, :] = column_sum(b2 * n2)
    gm_ref[0, 2:3, :] = column_sum(bh2 * branch)
    gm_ref[0, 3:4, :] = column_sum(b3)
    gm_ref[0, 4:5, :] = column_sum(b3 * n3)
    gm_ref[0, 5:6, :] = jnp.broadcast_to(loss, (1, D))
    gm_ref[0, 6:8, :] = jnp.zeros((2, D), F32)

    @pl.when(i == images - 1)
    def _():
        put = functools.partial(put_pair, at_ref[3], mine_ref, other_ref)
        for j in range(4):
            lanes = slice(D * j, D * j + D)
            put(j, mm_tn(act2_s[...], bi_s[:, lanes]), mm_tn(gelu_s[:, lanes], bb2_s[...]))
        put(4, mm_tn(h1_s[...], ba_s[:, 0:D]), mm_tn(h1_s[...], ba_s[:, D:]))
        g = mm_tn(act3_s[...], bo_s[...]).astype(BF)
        spread = (lax.broadcasted_iota(jnp.int32, (128, 128), 1) % PD
                  == lax.broadcasted_iota(jnp.int32, (128, 128), 0)).astype(F32).astype(BF)
        keep = (lax.broadcasted_iota(jnp.int32, (D, 128), 1) // PD
                == lax.broadcasted_iota(jnp.int32, (D, 128), 0) % 8)
        fold = (lax.broadcasted_iota(jnp.int32, (48, D), 1) // 8
                == lax.broadcasted_iota(jnp.int32, (48, D), 0)).astype(F32).astype(BF)
        flat = mm(fold, jnp.where(keep, mm(g, spread), 0.0).astype(BF))
        for l in range(3):
            sums_ref[0:16, 128 * l : 128 * l + 128] = flat[16 * l : 16 * l + 16, :]


def back_kernel(first, bh1_ref, h0_ref, qkv_ref, att_ref, noisy_ref, mods_ref, bias_ref, w_ref,
                bb1_ref, bp_ref, act_ref, gm_ref, patch_ref):
    i = pl.program_id(0) + first

    def mod(t):
        return mods_ref[pl.ds(i, 1), D * t : D * t + D]

    bh1 = bh1_ref[0]
    att = att_ref[0]
    bb1 = (bh1 * mod(2)).astype(BF)
    bb1_ref[0] = bb1
    gm_ref[0, 2:3, :] = column_sum(bh1 * (mm(att, w_ref[3]) + bias_ref[3:4, :]))
    batt = mm_nt(bb1, w_ref[3]).astype(BF)
    q, k, v = qkv_ref[0, :, 0:D], qkv_ref[0, :, D : 2 * D], qkv_ref[0, :, 2 * D :]
    gq, gk, gv = [], [], []
    for h in range(HEADS):
        qh, kh, vh, bh = head(q, h), head(k, h), head(v, h), head(batt, h)
        s = mm_nt(kh, qh) * QK_SCALE
        e = jnp.exp(s - jnp.max(s, axis=0, keepdims=True))
        p = e * (1.0 / column_sum(e))
        dp = mm_nt(vh, bh)
        ds = (p * (dp - column_sum(dp * p))).astype(BF)
        gv.append(mm(p.astype(BF), bh))
        gk.append(mm(ds, qh))
        gq.append(mm_tn(ds, kh))
    bq = (jnp.concatenate(gq, axis=1) * QK_SCALE).astype(BF)
    bk = (jnp.concatenate(gk, axis=1) * QK_SCALE).astype(BF)
    bv = jnp.concatenate(gv, axis=1).astype(BF)
    bp_ref[0, :, 0:D] = bq
    bp_ref[0, :, D : 2 * D] = bk
    bp_ref[0, :, 2 * D :] = bv
    b1 = mm_nt(bq, w_ref[0]) + mm_nt(bk, w_ref[1]) + mm_nt(bv, w_ref[2])
    n1, inv1 = norm_stats(h0_ref[0])
    act_ref[0] = (n1 * (1.0 + mod(1)) + mod(0)).astype(BF)
    gm_ref[0, 0:1, :] = column_sum(b1)
    gm_ref[0, 1:2, :] = column_sum(b1 * n1)
    bh0 = (bh1 + norm_back(b1 * (1.0 + mod(1)), n1, inv1)).astype(BF)
    patch_ref[0] = mm(noisy_ref[0].astype(BF), bh0)
    gm_ref[0, 3:4, :] = column_sum(bh0.astype(F32))
    gm_ref[0, 4:5, :] = column_sum(bq.astype(F32))
    gm_ref[0, 5:6, :] = column_sum(bv.astype(F32))
    gm_ref[0, 6:7, :] = column_sum(bb1.astype(F32))
    gm_ref[0, 7:8, :] = jnp.zeros((1, D), F32)


def last_kernel(counts, at_ref, att_ref, *refs):
    mine_ref, other_ref = refs[-2:]
    put = functools.partial(put_pair, at_ref[3], mine_ref, other_ref)
    parts = []
    first = 0
    for k, count in enumerate(counts):
        act_ref, bp_ref, bb1_ref = refs[3 * k : 3 * k + 3]
        parts.append((act_ref, bp_ref, att_ref, bb1_ref, first))
        first += count * SEQ

    def over(which):
        return sum(which(*p) for p in parts)

    def qkv(j):
        return over(lambda act, bp, att, bb1, first: mm_tn(act[...], bp[:, D * j : D * j + D]))

    put(0, qkv(0), qkv(2))
    put(1, qkv(1), over(lambda act, bp, att, bb1, first: mm_tn(
        att[first : first + bb1.shape[0], :], bb1[...])))


def cond_back_kernel(images, aligns, at_ref, cls_ref, gm2_ref, pre_ref, th_ref, cond_ref, feat_ref, modw_ref, fmodw_ref,
                     tout_ref, sums_ref, *refs):
    align_refs, refs = refs[:aligns], refs[aligns:]
    out_refs, pay_ref, refs = refs[-5:-1], refs[-1], refs[:-5]
    gm3_refs, patch_refs = refs[::2], refs[1::2]
    none = jnp.zeros((4, D), F32)
    gm2 = [gm2_ref[m] for m in range(images)]
    gm3 = [ref[m] for ref in gm3_refs for m in range(ref.shape[0])]
    patch = sum(ref[m] for ref in patch_refs for m in range(ref.shape[0]))

    def rows_of(values, r):
        return jnp.concatenate([v[r : r + 1, :] for v in values] + [none], axis=0)

    tiles = [rows_of(gm3, 0), rows_of(gm3, 1), rows_of(gm3, 2),
             rows_of(gm2, 0), rows_of(gm2, 1), rows_of(gm2, 2)]
    finals = [rows_of(gm2, 3), rows_of(gm2, 4)]
    g_act = jnp.zeros((24, D), F32)
    for t in range(6):
        g_act = g_act + mm_nt(stack3(tiles[t]), modw_ref[:, D * t : D * t + D])
    for t in range(2):
        g_act = g_act + mm_nt(stack3(finals[t]), fmodw_ref[:, D * t : D * t + D])
    cond = cond_ref[...]
    g_cond = fold3(g_act) * silu_slope(cond)
    g_pre = fold3(mm_nt(stack3(g_cond), tout_ref[...])) * silu_slope(pre_ref[...])
    act = silu(cond)
    lane = lax.broadcasted_iota(jnp.int32, (1, 128), 1)
    ids = []
    for m in range(images):
        number = cls_ref[m]
        row = jnp.where(lane == 0, (number // 256).astype(F32), 0.0)
        ids.append(jnp.where(lane == 1, (number % 256).astype(F32), row))
    ids = jnp.concatenate(ids, axis=0)
    loss = sum(v[5:6, 0:128] for v in gm2)
    pieces = [v.astype(F32) for v in split3(loss)]
    loss = jnp.where(lane == 0, pieces[0], jnp.where(lane == 1, pieces[1], jnp.where(lane == 2, pieces[2], 0.0)))
    loss = jnp.concatenate([loss, jnp.zeros((1, D - 128), F32)], axis=1)

    def put(plane, j, upper, lower):
        pay_ref[plane, 8 * j : 8 * j + 8, :] = jnp.concatenate([upper[:4], lower[:4]], axis=0)

    def put_rows(plane, first, v):
        pay_ref[plane, first : first + v.shape[0], :] = v

    def over(r):
        return sum(v[r : r + 1, :] for v in gm3)

    none = jnp.zeros((8, D), F32)
    row = jnp.zeros((1, D), F32)
    tags = jnp.concatenate([ids, jnp.zeros((4, D - 128), F32)], axis=1)
    pay_ref[...] = jnp.zeros_like(pay_ref)
    put(0, 0, th_ref[...], jnp.concatenate([feat_ref[...], jnp.zeros((8, D - FREQ), F32)], axis=1))
    put(0, 1, g_cond, g_pre)
    put(0, 2, tags, none)
    put_rows(0, 40, patch)
    for plane in (1, 2):
        put(plane, 0, act, act)
        for t in range(3):
            put(plane, 1 + t, tiles[t], tiles[t + 3])
    put(1, 4, g_cond, none)
    put(1, 5, tags, none)
    put(2, 4, finals[0], finals[1])
    sums = sums_ref[...]
    put_rows(2, 40, jnp.concatenate([over(4), over(5), over(6), sums[16:21]], axis=0))
    put(3, 0, act, act)
    put(3, 1, finals[0], finals[1])
    put_rows(3, 16, sum(ref[4 * UNIT :, :].astype(F32) for ref in align_refs))
    put_rows(3, 40, sums[0:16])
    last = [[over(3)] + [row] * 6, [row] * 7, [row] * 7, [sums[23:24], sums[21:22], sums[22:23]] + [row] * 4]
    for plane in range(4):
        put_rows(plane, 56, jnp.concatenate(last[plane] + [loss], axis=0))
    for d, out_ref in enumerate(out_refs):
        out_ref[...] = pay_ref[lax.rem(at_ref[0] + d, 4)].astype(BF)


def rows_each(first, *dims):
    return pl.BlockSpec((1,) + dims, lambda i: (i + first,) + (0,) * len(dims))


def front(at, owner_map, noisy, mods, bias, patch_low, pos, pieces):
    images = noisy.shape[0]
    each = functools.partial(rows_each, 0)
    anywhere = pl.BlockSpec(memory_space=pl.ANY)
    return pl.pallas_call(
        front_kernel,
        name="front",
        grid=(images,),
        out_shape=(shape((images, SEQ, D)), shape((images, SEQ, 3 * D), BF),
                   shape((images, SEQ, D), BF), shape((images, SEQ, D)), shape((NBLK, D, D), BF)),
        in_specs=[SM, SM, each(PD, SEQ), VM, VM, VM, VM] + [anywhere] * len(pieces),
        out_specs=[each(SEQ, D), each(SEQ, 3 * D), each(SEQ, D), each(SEQ, D), anywhere],
        scratch_shapes=[pltpu.VMEM((NBLK, D, D), BF), pltpu.SemaphoreType.DMA((18,)), pltpu.SemaphoreType.DMA(())],
        compiler_params=room(24),
        cost_estimate=cost(2.2e9, 1.2e7),
    )(at, owner_map, noisy, mods, bias, patch_low, pos, *pieces)


def middle(total_img, at, time_weight, h1, velocity, dino, mods, bias, blocks, align_low, final_low):
    images = h1.shape[0]
    each = functools.partial(rows_each, 0)
    full = lambda lanes, kind=BF: pltpu.VMEM((images * SEQ, lanes), kind)
    return pl.pallas_call(
        functools.partial(middle_kernel, images, total_img),
        name="middle",
        grid=(images,),
        out_shape=(shape((images, SEQ, D)), shape((images, 8, D)),
                   shape((16, EARLY, D), BF), shape((16, EARLY, D), BF), shape((SUMS_MLP, D))),
        in_specs=[SM, SM, each(SEQ, D), each(PD, SEQ), each(SEQ, DINO), VM, VM, VM, VM, VM],
        out_specs=[each(SEQ, D), each(8, D), VM, VM, VM],
        scratch_shapes=[full(D), full(F), pltpu.VMEM((SEQ, F), F32), full(F), full(D), full(D),
                        full(DINO), full(D), full(128)],
        compiler_params=room(40),
        cost_estimate=cost(9e9, 1.4e7),
    )(at, time_weight, h1, velocity, dino, mods, bias, blocks, align_low, final_low)


def attention_back(first, count, bh1, h0, qkv, att, noisy, mods, bias, blocks):
    each = functools.partial(rows_each, first)
    out = functools.partial(rows_each, 0)
    return pl.pallas_call(
        functools.partial(back_kernel, first),
        name="attention_back",
        grid=(count,),
        out_shape=(shape((count, SEQ, D), BF), shape((count, SEQ, 3 * D), BF), shape((count, SEQ, D), BF),
                   shape((count, 8, D)), shape((count, PD, D))),
        in_specs=[each(SEQ, D), each(SEQ, D), each(SEQ, 3 * D), each(SEQ, D), each(PD, SEQ), VM, VM, VM],
        out_specs=[out(SEQ, D), out(SEQ, 3 * D), out(SEQ, D), out(8, D), out(PD, D)],
        compiler_params=room(24),
        cost_estimate=cost(1.2e9 * count, 3e6 * count),
    )(bh1, h0, qkv, att, noisy, mods, bias, blocks)


def last_gradients(at, att, parts):
    flat = lambda v: v.reshape(-1, v.shape[-1])
    arrays = [flat(v) for part in parts for v in part]
    counts = tuple(part[0].shape[0] for part in parts)
    return pl.pallas_call(
        functools.partial(last_kernel, counts),
        name="last_gradients",
        out_shape=(shape((16, LATE, D), BF),) * 2,
        in_specs=[SM] + [VM] * (len(arrays) + 1),
        out_specs=[VM] * 2,
        compiler_params=room(20),
        cost_estimate=cost(1.2e9, 9e6),
    )(at, flat(att), *arrays)


def cond_back(images, at, class_ids, gm2, pre, th, cond, features, mod_w, fmod_w, tout_w, sums, aligns, gm3):
    return pl.pallas_call(
        functools.partial(cond_back_kernel, images, len(aligns)),
        name="cond_back",
        out_shape=(shape((PAY, D), BF),) * 4,
        in_specs=[SM, SM] + [VM] * (9 + len(aligns) + len(gm3)),
        out_specs=[VM] * 4,
        scratch_shapes=[pltpu.VMEM((4, PAY, D), F32)],
        compiler_params=room(16),
        cost_estimate=cost(1e8, 4e6),
    )(at, class_ids, gm2, pre, th, cond, features, mod_w, fmod_w, tout_w, sums, *aligns, *gm3)


def position_table():
    quarter = D // 4
    frequencies = 1.0 / 10000.0 ** (jnp.arange(quarter, dtype=jnp.float32) / quarter)
    cell_ids = jnp.arange(SEQ, dtype=jnp.int32)
    row_arg = (cell_ids // GRID).astype(jnp.float32)[:, None] * frequencies[None, :]
    col_arg = (cell_ids % GRID).astype(jnp.float32)[:, None] * frequencies[None, :]
    return jnp.concatenate(
        [jnp.sin(col_arg), jnp.cos(col_arg), jnp.sin(row_arg), jnp.cos(row_arg)], axis=1
    )


def time_features(tstep_idx):
    half_freq = FREQ // 2
    frequencies = jnp.exp(-math.log(10000.0) * jnp.arange(half_freq, dtype=jnp.float32) / half_freq)
    angles = (tstep_idx.astype(jnp.float32) + 0.5)[:, None] * frequencies[None, :]
    return jnp.concatenate([jnp.cos(angles), jnp.sin(angles)], axis=1)


def body(
    noisy,
    velocity,
    tstep_idx,
    class_ids,
    time_weight,
    dino,
    owner_map,
    adam_flat,
    adam_m,
    adam_v,
    blocks_w,
    stat_left,
    stat_right,
    root_left,
    root_right,
):
    dp, group = lax.axis_size("dp"), lax.axis_size("shard")
    near = is_near(dp, group)
    images = noisy.shape[0]
    total_img = images * dp * group
    at = jnp.stack([jnp.asarray(v, jnp.int32) for v in coordinates()])
    flat_w = adam_flat.reshape(-1, 128)
    flat_m = adam_m.reshape(-1, 128)
    flat_v = adam_v.reshape(-1, 128)
    mine = flat_w.astype(BF)
    features = jnp.pad(time_features(tstep_idx), ((0, 4), (0, 0)))
    pos = position_table()
    noisy = jnp.transpose(noisy, (0, 2, 1))
    velocity = jnp.transpose(velocity, (0, 2, 1))
    rows = flat_w.shape[0]
    if near:
        cut = rows // 16 * 8 + 8 if rows // 8 % 2 else rows // 2
        block_parts = gather_blocks(blocks_w.astype(BF))
        pieces, (at, features, pos) = gather_flat(mine, cut, (at, features, pos))
        places = flat_places(cut)
    else:
        pieces = [lax.all_gather(mine, AXES, axis=0, tiled=True)[None]]
        places = [(0, lambda i, at: 0)]
        slot_low = lax.all_gather(blocks_w.astype(BF), "shard", axis=0, tiled=True)
        block_ids = jnp.arange(NBLK, dtype=jnp.int32)
        slot_of = jnp.sum(
            block_ids[:, None] * (owner_map[:, None] == block_ids[None, :]).astype(jnp.int32), axis=0
        )
        block_parts = [jnp.take(slot_low, slot_of, axis=0)]
    (mods, pre, th, cond, mod_w, fmod_w, tout_w, align_low, bias, patch_low, final_low) = conditioning(
        at, class_ids, features, pieces, places, rows)
    h0, qkv, att, h1, blocks = front(at, owner_map, noisy, mods, bias, patch_low, pos, block_parts)
    bh1, gm2, mine, other, sums = middle(
        total_img, at, time_weight, h1, velocity, dino, mods, bias, blocks, align_low, final_low)
    if near:
        early = reduce_units(at, mine, other)
    parts, gm3 = [], []
    for first, count in ((0, 1), (1, images - 1)):
        bb1, bp, act, gm, patch = attention_back(first, count, bh1, h0, qkv, att, noisy, mods, bias, blocks)
        parts.append((act, bp, bb1))
        gm3 += [gm, patch]
    late_mine, late_other = last_gradients(at, att, parts)
    aligns = early if near else [jnp.zeros((EARLY, D), BF)]
    keep, *away = cond_back(
        images, at, class_ids, gm2, pre, th, cond, features, mod_w, fmod_w, tout_w, sums, aligns, gm3)
    if near:
        late = reduce_units(at, late_mine, late_other)
        grads = gather_owned(at, late, early, owner_map)
        parts = gather_rows(keep, away)
        loss, upd, new_m, new_v = adam_near(at, parts, flat_w, flat_m, flat_v)
        *grads, loss, upd, new_m, new_v = lax.optimization_barrier((*grads, loss, upd, new_m, new_v))
    else:
        core = at[3]

        def by_part(mine, other):
            pair = jnp.where(core == 0, jnp.stack([mine, other]), jnp.stack([other, mine]))
            count = mine.shape[1] // UNIT
            return pair.reshape(2, 16, count, UNIT, D).transpose(0, 2, 1, 3, 4).reshape(2, count, D, D)

        early, late = by_part(mine, other), by_part(late_mine, late_other)
        late = jnp.stack([late[0, 0], late[0, 1], late[1, 0], late[1, 1]])
        grad_model = jnp.concatenate([late, early[:, :4].reshape(8, D, D)])
        planes = jnp.take(jnp.stack([keep, *away]), (jnp.arange(4) - at[0]) % 4, axis=0)
        pays = lax.all_gather(planes, AXES, axis=0, tiled=False)
        align_sum = lax.psum(early[:, 4].astype(F32), AXES)
        loss, upd, new_m, new_v = adam_wide(pays, align_sum, flat_w, flat_m, flat_v)
        slots = jnp.take(grad_model, owner_map, axis=0)
        owned = lax.psum_scatter(slots, "shard", scatter_dimension=0, tiled=True)
        grads = [lax.psum(owned.astype(F32), "dp").astype(BF)]
    block_update, new_left, new_right = shampoo(
        at, grads, blocks_w, stat_left, stat_right, root_left, root_right)
    return (loss, block_update, new_left, new_right,
            upd.reshape(-1), new_m.reshape(-1), new_v.reshape(-1))


def is_near(dp, group):
    return (dp, group) == (8, 4)


def solution(mesh):
    return jax.shard_map(
        body,
        mesh=mesh,
        in_specs=(
            P(("dp", "shard"), None, None),
            P(("dp", "shard"), None, None),
            P(("dp", "shard")),
            P(("dp", "shard")),
            P(("dp", "shard")),
            P(("dp", "shard"), None, None),
            P(),
            P(("dp", "shard")),
            P(("dp", "shard")),
            P(("dp", "shard")),
            P("shard", None, None),
            P("shard", None, None),
            P("shard", None, None),
            P("shard", None, None),
            P("shard", None, None),
        ),
        out_specs=(
            P(),
            P("shard", None, None),
            P("shard", None, None),
            P("shard", None, None),
            P(("dp", "shard")),
            P(("dp", "shard")),
            P(("dp", "shard")),
        ),
        check_vma=False,
    )
```

```python
import functools
import math

import jax
import jax.numpy as jnp
from jax import lax
from jax.experimental import pallas as pl
from jax.experimental.pallas import tpu as pltpu
from jax.sharding import PartitionSpec as P


D = 384
HEADS = 6
HDIM = 64
F = 1536
PD = 16
GRID = 16
SEQ = 256
FREQ = 256
DINO = 768
STEP = 10
NBLK = 12
ADAM_PAD = 2129920

BETA_ONE = 0.9
BETA_TWO = 0.95
ADAM_EPS = 1e-08
ADAM_RATE = 0.01
DECAY_RATE = 0.1
STAT_BETA = 0.9
SHAMPOO_RATE = 0.02
RMS_EPS = 1e-08
REPA_WEIGHT = 0.5
NORM_EPS = 1e-06
QK_SCALE = HDIM ** (-0.5)

AXES = ("dp", "shard")
BF = jnp.bfloat16
F32 = jnp.float32
VM = pl.BlockSpec(memory_space=pltpu.VMEM)
SM = pl.BlockSpec(memory_space=pltpu.SMEM)

FLAT_ROWS = ADAM_PAD // 128
R_PATCH = 0
R_PATCH_B = 48
R_TIME_IN = 51
R_TIME_IN_B = 819
R_TIME_OUT = 822
R_TIME_OUT_B = 1974
R_CLASS = 1977
R_MOD = 4980
R_MOD_B = 11892
R_QUERY_B = 11910
R_VALUE_B = 11913
R_PROJ_B = 11916
R_HIDDEN_B = 11919
R_DOWN_B = 11931
R_FMOD = 11934
R_FMOD_B = 14238
R_FINAL = 14244
R_FINAL_B = 14292
ALIGN_ROWS = 2310

PAY = 64
PLANE_ROWS = FLAT_ROWS // 4


def shape(dims, kind=F32):
    return jax.ShapeDtypeStruct(dims, kind)


def cost(flops, moved):
    return pl.CostEstimate(flops=int(flops), bytes_accessed=int(moved), transcendentals=0)


def room(mib):
    return pltpu.CompilerParams(vmem_limit_bytes=mib * 1024 * 1024)


def mm(left, right):
    return jnp.dot(left, right, preferred_element_type=F32)


def mm_nt(left, right):
    return lax.dot_general(left, right, (((1,), (1,)), ((), ())), preferred_element_type=F32)


def mm_tn(left, right):
    return lax.dot_general(left, right, (((0,), (0,)), ((), ())), preferred_element_type=F32)


def silu(v):
    return v / (1.0 + jnp.exp(-v))


def silu_slope(v):
    s = 1.0 / (1.0 + jnp.exp(-v))
    return s * (1.0 + v * (1.0 - s))


def split3(v):
    one = v.astype(BF)
    rest = v - one.astype(F32)
    two = rest.astype(BF)
    return one, two, (rest - two.astype(F32)).astype(BF)


def split2(v):
    one = v.astype(BF)
    return one, (v - one.astype(F32)).astype(BF)


def stack3(v):
    one, two, three = split3(v)
    return jnp.concatenate([one.astype(F32), two.astype(F32), three.astype(F32)], axis=0).astype(BF)


def fold3(v):
    third = v.shape[0] // 3
    return v[:third] + v[third : 2 * third] + v[2 * third :]


def place_of(z, x, y, c):
    return ((z * 2 + x) * 2 + y) * 2 + c


def permutation(move):
    pairs = []
    for z in range(4):
        for x in range(2):
            for y in range(2):
                for c in range(2):
                    pairs.append((place_of(z, x, y, c), place_of(*move(z, x, y, c))))
    return pairs


TO_C = permutation(lambda z, x, y, c: (z, x, y, 1 - c))
TO_Y = permutation(lambda z, x, y, c: (z, x, 1 - y, c))
TO_X = permutation(lambda z, x, y, c: (z, 1 - x, y, c))
TO_Z = [permutation(lambda z, x, y, c, d=d: ((z + d) % 4, x, y, c)) for d in range(4)]


def send(value, pairs):
    return lax.ppermute(value, AXES, pairs)


def coordinates():
    dp = lax.axis_index("dp")
    sh = lax.axis_index("shard")
    return dp // 2, dp % 2, sh // 2, sh % 2


TO_XY = permutation(lambda z, x, y, c: (z, 1 - x, 1 - y, c))
TO_CY = permutation(lambda z, x, y, c: (z, x, 1 - y, 1 - c))
TO_PAIR = permutation(lambda z, x, y, c: (z + 1 - 2 * (z % 2), x, y, c))


def send_plane(value):
    return [send(value, TO_X), send(value, TO_Y), send(value, TO_XY)]


def gather_flat(piece, cut, ready):
    turned = [send(piece, TO_Z[d]) for d in (1, 2, 3)]
    own_x, own_y = send(piece, TO_X), send(piece, TO_Y)
    first = jnp.stack([t[:cut] for t in turned])
    second = jnp.stack([t[cut:] for t in turned])
    first_x = send(first, TO_X)
    second_y = send(second, TO_Y)
    second_y, ready = lax.optimization_barrier((second_y, ready))
    first = jnp.concatenate([own_x[None, :cut], first, first_x])
    second = jnp.concatenate([own_y[None, cut:], second, second_y])
    far = [send(first, TO_Y), send(second, TO_X)]
    own = [piece, own_x[cut:], own_y[:cut]]
    own_c = [send(p, TO_C) for p in own]
    rest_c = [send(p, TO_C) for p in (first, second, *far)]
    return [p[None] for p in own] + [first, second] + far + [p[None] for p in own_c] + rest_c, ready


def flip(value, bit):
    return 1 - value if bit else value


def flat_places(cut):
    def near(dc, dx, dy):
        return lambda i, at: place_of(at[0], flip(at[1], dx), flip(at[2], dy), flip(at[3], dc))

    def far(dc, kind):
        def entry(i, at):
            z, x, y, c = at
            dz, other = (0, 1) if i == 0 else ((i - 1) % 3 + 1, (i - 1) // 3)
            dx, dy = {0: (other, 0), 1: (0, other), 2: (other, 1), 3: (1, other)}[kind]
            return place_of(lax.rem(z + 4 - dz, 4), flip(x, dx), flip(y, dy), flip(c, dc))

        return entry

    places = []
    for dc in (0, 1):
        places += [(0, near(dc, 0, 0)), (cut, near(dc, 1, 0)), (0, near(dc, 0, 1))]
        places += [((0, cut, 0, cut)[kind], far(dc, kind)) for kind in range(4)]
    return places


def gather_rows(away, keep, column, finish):
    turned = [send(v, TO_Z[d + 1]) for d, v in enumerate(away)]
    column = column()
    turned, column[1] = lax.optimization_barrier((turned, column[1]))
    plane = jnp.stack([keep] + turned)
    plane = [plane] + send_plane(plane)
    column = finish(column)
    plane, column[4] = lax.optimization_barrier((plane, column[4]))
    return plane + [send(p, TO_C) for p in plane], column


def read_coordinates(ref):
    return ref[0], ref[1], ref[2], ref[3]


def cond_kernel(places, rows, at_ref, cls_ref, feat_ref, *refs):
    count = len(places)
    pieces = refs[:count]
    (mods_ref, pre_ref, th_ref, cond_ref, modw_ref, fmodw_ref, tout_ref, align_ref, bias_ref,
     patch_ref, final_ref, flat, rolled) = refs[count:]
    at = read_coordinates(at_ref)
    for ref, (offset, entry) in zip(pieces, places):
        for i in range(ref.shape[0]):
            start = pl.multiple_of(entry(i, at) * rows + offset, 8)
            flat[pl.ds(start, ref.shape[1]), :] = ref[i].astype(F32)

    def row(first, count):
        return jnp.concatenate([flat[first + l : first + l + 1, :] for l in range(count)], axis=1)

    def columns(first, depth, count, which):
        return flat[pl.ds(first + which, depth, stride=count), :].astype(BF)

    def wide(v, first, depth, count, keep=None):
        stacked = stack3(v)
        out = []
        for j in range(count):
            w = columns(first, depth, count, j)
            if keep is not None:
                keep[:, 128 * j : 128 * j + 128] = w
            out.append(fold3(mm(stacked, w)))
        return jnp.concatenate(out, axis=1)

    pre = wide(feat_ref[...], R_TIME_IN, FREQ, 3) + row(R_TIME_IN_B, 3)
    th = silu(pre)
    picked = []
    for m in range(4):
        r = R_CLASS + 3 * cls_ref[m]
        picked.append(jnp.concatenate([flat[pl.ds(r + l, 1), :] for l in range(3)], axis=1))
    picked = jnp.concatenate(picked + [jnp.zeros((4, D), F32)], axis=0)
    cond = wide(th, R_TIME_OUT, D, 3, tout_ref) + row(R_TIME_OUT_B, 3) + picked
    act = silu(cond)
    pre_ref[...] = pre
    th_ref[...] = th
    cond_ref[...] = cond
    mods_ref[:, : 6 * D] = wide(act, R_MOD, D, 18, modw_ref) + row(R_MOD_B, 18)
    mods_ref[:, 6 * D :] = wide(act, R_FMOD, D, 6, fmodw_ref) + row(R_FMOD_B, 6)

    spot = lax.broadcasted_iota(jnp.int32, (ALIGN_ROWS, 128), 1)
    here = pltpu.roll(flat[R_FINAL_B : R_FINAL_B + ALIGN_ROWS, :], 112, 1)
    after = pltpu.roll(flat[R_FINAL_B + 1 : R_FINAL_B + 1 + ALIGN_ROWS, :], 112, 1)
    rolled[...] = jnp.where(spot < 112, here, after)
    for j in range(6):
        align_ref[:, 128 * j : 128 * j + 128] = rolled[pl.ds(j, D, stride=6), :].astype(BF)

    bias_ref[...] = jnp.zeros_like(bias_ref)
    for at_row, first in ((0, R_PATCH_B), (1, R_QUERY_B), (2, R_VALUE_B), (3, R_PROJ_B),
                          (4, R_HIDDEN_B), (5, R_HIDDEN_B + 3), (6, R_HIDDEN_B + 6),
                          (7, R_HIDDEN_B + 9), (8, R_DOWN_B)):
        bias_ref[at_row : at_row + 1, :] = row(first, 3)
    for half in range(2):
        bias_ref[9 + half : 10 + half, :] = jnp.concatenate(
            [rolled[2304 + 3 * half + l : 2305 + 3 * half + l, :] for l in range(3)], axis=1)
    lane = lax.broadcasted_iota(jnp.int32, (1, 128), 1)
    bias_ref[11:12, :128] = jnp.where(lane < PD, flat[R_FINAL_B : R_FINAL_B + 1, :], 0.0)
    patch = [flat[pl.ds(R_PATCH + l, PD, stride=3), :] for l in range(3)]
    patch_ref[...] = jnp.concatenate(patch, axis=1).astype(BF)
    spread = (lax.broadcasted_iota(jnp.int32, (D, 48), 0) // 8
              == lax.broadcasted_iota(jnp.int32, (D, 48), 1)).astype(F32).astype(BF)
    wide_rows = mm(spread, flat[R_FINAL : R_FINAL + 48, :].astype(BF))
    keep = (lax.broadcasted_iota(jnp.int32, (D, 128), 1) // PD
            == lax.broadcasted_iota(jnp.int32, (D, 128), 0) % 8)
    fold = (lax.broadcasted_iota(jnp.int32, (128, 128), 0) % PD
            == lax.broadcasted_iota(jnp.int32, (128, 128), 1)).astype(F32).astype(BF)
    final_ref[...] = mm(jnp.where(keep, wide_rows, 0.0).astype(BF), fold).astype(BF)


def conditioning(at, classes, features, pieces, places, rows):
    kernel = functools.partial(cond_kernel, places, rows)
    return pl.pallas_call(
        kernel,
        name="conditioning",
        out_shape=(shape((8, 8 * D)), shape((8, D)), shape((8, D)), shape((8, D)),
                   shape((D, 6 * D), BF), shape((D, 2 * D), BF), shape((D, D), BF),
                   shape((D, DINO), BF), shape((16, D)), shape((PD, D), BF), shape((D, 128), BF)),
        in_specs=[SM, SM, VM] + [VM] * len(pieces),
        out_specs=[VM] * 11,
        scratch_shapes=[pltpu.VMEM((FLAT_ROWS + 8, 128), F32), pltpu.VMEM((ALIGN_ROWS, 128), F32)],
        compiler_params=room(28),
        cost_estimate=pl.CostEstimate(flops=10**9, bytes_accessed=10**7, transcendentals=0),
    )(at, classes, features, *pieces)


def gather_blocks(mine):
    z, _, _, _ = coordinates()
    half = lax.dynamic_slice_in_dim(mine, 192 * (z % 2), 192, 1)
    near = send(half, TO_Y)
    far = send(near, TO_PAIR)
    return [mine, near, far, send(mine, TO_C), send(near, TO_C), send(far, TO_C)]


def place_blocks_kernel(at_ref, own_ref, mine_ref, near_ref, far_ref, mine_c_ref, near_c_ref, far_c_ref, out_ref):
    z, _, y, c = read_coordinates(at_ref)
    for core, mine, near, far in ((c, mine_ref, near_ref, far_ref), (1 - c, mine_c_ref, near_c_ref, far_c_ref)):
        for t in range(3):
            out_ref[own_ref[3 * (2 * y + core) + t]] = mine[t]
            there = own_ref[3 * (2 * (1 - y) + core) + t]
            odd = pl.multiple_of(192 * lax.rem(z, 2), 16)
            even = pl.multiple_of(192 * (1 - lax.rem(z, 2)), 16)
            out_ref[there, pl.ds(odd, 192), :] = near[t]
            out_ref[there, pl.ds(even, 192), :] = far[t]


def place_blocks(at, owner_map, parts):
    return pl.pallas_call(
        place_blocks_kernel,
        name="place_blocks",
        out_shape=shape((NBLK, D, D), BF),
        in_specs=[SM, SM] + [VM] * 6,
        out_specs=VM,
        compiler_params=room(12),
        cost_estimate=cost(1e6, 7e6),
    )(at, owner_map, *parts)


UNIT = 24


def unit_of(z, x, y):
    return (2 * x + y) * 4 + z


def quarter_kernel(at_ref, mine_ref, got_ref, *out_refs):
    _, x, y, _ = read_coordinates(at_ref)
    for out_ref, (dx, dy) in zip(out_refs, ((0, 0), (1, 0), (0, 1), (1, 1))):
        rows = pl.ds(4 * (2 * flip(x, dx) + flip(y, dy)), 4)
        out_ref[...] = (mine_ref[rows].astype(F32) + got_ref[rows].astype(F32)).astype(BF)


def turn_kernel(at_ref, *refs):
    z, _, _, _ = read_coordinates(at_ref)
    for d, out_ref in enumerate(refs[4:]):
        unit = lax.rem(z + d, 4)
        out_ref[...] = sum(ref[unit].astype(F32) for ref in refs[:4]).astype(BF)


def reduce_units(at, mine, other):
    rows = mine.shape[1]
    got = send(other, TO_C)
    own, *away = pl.pallas_call(
        quarter_kernel,
        name="quarter",
        out_shape=(shape((4, rows, D), BF),) * 4,
        in_specs=[SM, VM, VM],
        out_specs=[VM] * 4,
        compiler_params=room(12),
        cost_estimate=cost(1e6, 4e6),
    )(at, mine, got)
    got = [send(v, pairs) for v, pairs in zip(away, (TO_X, TO_Y, TO_XY))]
    own, *away = pl.pallas_call(
        turn_kernel,
        name="turn",
        out_shape=(shape((rows, D), BF),) * 4,
        in_specs=[SM] + [VM] * 4,
        out_specs=[VM] * 4,
        compiler_params=room(8),
        cost_estimate=cost(1e6, 2e6),
    )(at, own, *got)
    return [own] + [send(v, TO_Z[d + 1]) for d, v in enumerate(away)]


def owner_kernel(at_ref, own_ref, *refs):
    late, early = refs[:4], refs[4:8]
    out_refs, total = refs[8:12], refs[12]
    _, _, y, c = read_coordinates(at_ref)
    one = sum(ref[...].astype(F32) for ref in late)
    two = sum(ref[0 : 4 * UNIT, :].astype(F32) for ref in early)
    for k in range(6):
        total[k] = (one[UNIT * k : UNIT * k + UNIT] if k < 2 else two[UNIT * (k - 2) : UNIT * (k - 1)])
    for out_ref, (dy, dc) in zip(out_refs, ((0, 0), (0, 1), (1, 0), (1, 1))):
        first = 3 * (2 * flip(y, dy) + flip(c, dc))
        for t in range(3):
            block = own_ref[first + t]
            low = block < 4
            part = jnp.where(low, lax.div(block, 2), lax.div(block - 4, 4))
            entry = jnp.where(low, lax.rem(block, 2), 2 + lax.rem(jnp.maximum(block - 4, 0), 4))
            out_ref[t] = jnp.where(part == c, total[entry], 0.0).astype(BF)


def join_kernel(own_ref, pair_ref, near_ref, far_ref, out_ref):
    out_ref[0] = own_ref[...] + pair_ref[...]
    out_ref[1] = near_ref[...] + far_ref[...]


def turn_owned(at, late, early, owner_map):
    piece = (3, UNIT, D)
    own, to_c, to_y, to_cy = pl.pallas_call(
        owner_kernel,
        name="owner_rows",
        out_shape=(shape(piece, BF),) * 4,
        in_specs=[SM, SM] + [VM] * 8,
        out_specs=[VM] * 4,
        scratch_shapes=[pltpu.VMEM((6, UNIT, D), F32)],
        compiler_params=room(8),
        cost_estimate=cost(1e6, 1e6),
    )(at, owner_map, *late, *early)
    far, near, pair = send(to_cy, TO_CY), send(to_y, TO_Y), send(to_c, TO_C)
    both = pl.pallas_call(
        join_kernel,
        name="join",
        out_shape=shape((2,) + piece, BF),
        in_specs=[VM] * 4,
        out_specs=VM,
        compiler_params=room(8),
        cost_estimate=cost(1e6, 1e6),
    )(own, pair, near, far)
    return [both] + [send(both, TO_Z[d]) for d in (1, 2, 3)]


def cross_owned(column):
    return column + [send(v, TO_X) for v in column]


def plane_gradient(plane, pay_ref, flat, rolled, align):
    rows = 8 * pay_ref.shape[0]

    def tile(j):
        return pay_ref[:, 8 * j : 8 * j + 8, :].astype(F32).reshape(rows, D)

    def sums(first, last):
        return jnp.sum(pay_ref[:, first:last, :].astype(F32), axis=0)

    upper = lax.broadcasted_iota(jnp.int32, (rows, 1), 0) % 8 < 4

    def first(v):
        return jnp.where(upper, v, 0.0)

    def second(v):
        return jnp.where(upper, 0.0, v)

    def put_row(v, row):
        for l in range(v.shape[1] // 128):
            flat[row + l : row + l + 1, :] = v[:, 128 * l : 128 * l + 128]

    def put_matrix(v, row, count, which):
        for l in range(v.shape[1] // 128):
            flat[pl.ds(row + which + l, v.shape[0], stride=count), :] = v[:, 128 * l : 128 * l + 128]

    def classes(ids, g_low):
        numbers = (ids[:, 0:1] * 256.0 + ids[:, 1:2]).astype(jnp.int32)
        for part in range(3):
            height = 336 if part < 2 else 329
            marks = lax.broadcasted_iota(jnp.int32, (rows, 336), 1) + 336 * part
            hits = first(jnp.where(marks == numbers, 1.0, 0.0)).astype(BF)
            put_matrix(mm_tn(hits, g_low)[:height], R_CLASS + 3 * 336 * part, 3, 0)

    def modulations(low, bias):
        act = tile(0)[:, low : low + 256]
        halves = (first(act).astype(BF), second(act).astype(BF))
        for t in range(3):
            g = tile(1 + t)
            for half in range(2):
                put_matrix(mm_tn(halves[half], g.astype(BF)), R_MOD + 18 * low, 18, 3 * (t + 3 * half))
                if bias:
                    put_row(column_sum((first, second)[half](g)), R_MOD_B + 3 * (t + 3 * half))

    def finals(which, bias):
        act, g = tile(0), tile(which)
        for half, part in enumerate((first, second)):
            put_matrix(mm_tn(part(act).astype(BF), g.astype(BF)), R_FMOD, 6, 3 * half)
            if bias:
                put_row(column_sum(part(g)), R_FMOD_B + 3 * half)

    if plane == 0:
        left, g = tile(0).astype(BF), tile(1)
        g_cond, g_pre = first(g), second(g)
        put_matrix(mm_tn(left[:, :FREQ], g_pre.astype(BF)), R_TIME_IN, 3, 0)
        put_row(column_sum(g_pre), R_TIME_IN_B)
        put_matrix(mm_tn(left, g_cond.astype(BF)), R_TIME_OUT, 3, 0)
        put_row(column_sum(g_cond), R_TIME_OUT_B)
        classes(tile(2)[:, :128], g.astype(BF))
        total = sums(40, 64)
        for l in range(3):
            flat[pl.ds(R_PATCH + l, PD, stride=3), :] = total[0:16, 128 * l : 128 * l + 128]
        put_row(total[16:17], R_PATCH_B)
    if plane == 1:
        classes(tile(5)[:, :128], tile(4).astype(BF))
        modulations(0, False)
    if plane == 2:
        modulations(128, True)
        finals(4, False)
        total = sums(40, 48)
        for k, row in enumerate((R_QUERY_B, R_VALUE_B, R_PROJ_B, R_HIDDEN_B, R_HIDDEN_B + 3, R_HIDDEN_B + 6,
                                 R_HIDDEN_B + 9, R_DOWN_B)):
            put_row(total[k : k + 1], row)
    if plane == 3:
        finals(1, True)
        total = sums(40, 64)
        for l in range(3):
            flat[R_FINAL + 16 * l : R_FINAL + 16 * l + 16, :] = total[0:16, 128 * l : 128 * l + 128]
        rolled[0:8, :] = jnp.zeros((8, 128), F32)
        rolled[8 + ALIGN_ROWS :, :] = jnp.zeros_like(rolled[8 + ALIGN_ROWS :, :])
        rolled[7:8, :] = pltpu.roll(total[16:17, 0:128], 112, 1)
        for half in range(2):
            for l in range(3):
                lanes = slice(128 * l, 128 * l + 128)
                rolled[pl.ds(8 + 3 * half + l, D, stride=6), :] = align[half, :, lanes].astype(F32)
                r = 8 + 2304 + 3 * half + l
                rolled[r : r + 1, :] = total[17 + half : 18 + half, lanes]
        count = FLAT_ROWS - R_FINAL_B
        spot = lax.broadcasted_iota(jnp.int32, (count, 128), 1)
        here = pltpu.roll(rolled[8 : 8 + count, :], 16, 1)
        before = pltpu.roll(rolled[7 : 7 + count, :], 16, 1)
        flat[R_FINAL_B:FLAT_ROWS, :] = jnp.where(spot < 16, before, here)


def loss_of(pay_ref):
    rows = 8 * pay_ref.shape[0]
    parts = pay_ref[:, PAY - 8 : PAY, 0:128].astype(F32).reshape(rows, 128)
    parts = column_sum(jnp.where(lax.broadcasted_iota(jnp.int32, (rows, 128), 0) % 8 == 7, parts, 0.0))
    return parts[:, 0:1] + parts[:, 1:2] + parts[:, 2:3]


def adam_near_kernel(at_ref, *refs):
    parts = refs[:8]
    w_ref, m_ref, v_ref, loss_ref, upd_ref, new_m_ref, new_v_ref, pay, align, flat, rolled = refs[8:]
    at = read_coordinates(at_ref)
    z, x, y, c = at
    for k, ref in enumerate(parts):
        dc, dy, dx = k // 4, k // 2 % 2, k % 2
        for dz in range(4):
            there = (lax.rem(z + 4 - dz, 4), flip(x, dx), flip(y, dy), flip(c, dc))
            value = ref[dz].astype(F32)
            pay[place_of(*there)] = value
            start = pl.multiple_of(unit_of(*there[:3]) * UNIT, 8)
            align[there[3], pl.ds(start, UNIT), :] = value[16:40]
    loss_ref[...] = loss_of(pay)
    for plane in range(4):
        @pl.when(z == plane)
        def _():
            plane_gradient(plane, pay, flat, rolled, align)
    size = w_ref.shape[0]
    start = pl.multiple_of(place_of(z, x, y, c) * size, 8)
    adam_step(flat[pl.ds(start, size), :], w_ref, m_ref, v_ref, upd_ref, new_m_ref, new_v_ref)


def adam_plane_kernel(plane, pay_ref, align_ref, loss_ref, flat_ref, rolled):
    loss_ref[...] = loss_of(pay_ref)
    plane_gradient(plane, pay_ref, flat_ref, rolled, align_ref)


def adam_step(grad, w_ref, m_ref, v_ref, upd_ref, new_m_ref, new_v_ref):
    new_m = BETA_ONE * m_ref[...] + (1.0 - BETA_ONE) * grad
    new_v = BETA_TWO * v_ref[...] + (1.0 - BETA_TWO) * grad * grad
    new_m_ref[...] = new_m
    new_v_ref[...] = new_v
    right_m = new_m / (1.0 - BETA_ONE**STEP)
    right_v = new_v / (1.0 - BETA_TWO**STEP)
    upd_ref[...] = -ADAM_RATE * (right_m / (jnp.sqrt(right_v) + ADAM_EPS) + DECAY_RATE * w_ref[...])


ROLL_ROWS = 8 + FLAT_ROWS - R_FINAL_B + 8


ROLL_ROWS = 8 + FLAT_ROWS - R_FINAL_B + 8


def adam_near(at, parts, flat_w, m, v):
    size = flat_w.shape
    loss, upd, new_m, new_v = pl.pallas_call(
        adam_near_kernel,
        name="adam",
        out_shape=(shape((1, 1)), shape(size), shape(size), shape(size)),
        in_specs=[SM] + [VM] * 11,
        out_specs=[VM] * 4,
        scratch_shapes=[pltpu.VMEM((32, PAY, D), F32), pltpu.VMEM((2, D, D), F32),
                        pltpu.VMEM((FLAT_ROWS, 128), F32), pltpu.VMEM((ROLL_ROWS, 128), F32)],
        compiler_params=room(24),
        cost_estimate=pl.CostEstimate(flops=10**9, bytes_accessed=10**7, transcendentals=0),
    )(at, *parts, flat_w, m, v)
    return loss[0, 0], upd, new_m, new_v


def adam_wide(pays, align, flat_w, m, v):
    grads = []
    for plane in range(4):
        loss, flat = pl.pallas_call(
            functools.partial(adam_plane_kernel, plane),
            name="adam_gradient",
            out_shape=(shape((1, 1)), shape((FLAT_ROWS, 128))),
            in_specs=[VM] * 2,
            out_specs=[VM] * 2,
            scratch_shapes=[pltpu.VMEM((ROLL_ROWS, 128), F32)],
        )(pays[:, plane], align)
        grads.append(flat[PLANE_ROWS * plane : PLANE_ROWS * (plane + 1)])
    size = flat_w.shape[0]
    place = lax.axis_index("dp") * lax.axis_size("shard") + lax.axis_index("shard")
    grad = lax.dynamic_slice_in_dim(jnp.concatenate(grads), place * size, size, 0)
    upd, new_m, new_v = pl.pallas_call(
        lambda g, *refs: adam_step(g[...], *refs),
        name="adam",
        out_shape=(shape(flat_w.shape),) * 3,
        in_specs=[VM] * 4,
        out_specs=[VM] * 3,
    )(grad, flat_w, m, v)
    return loss[0, 0], upd, new_m, new_v


def shampoo_kernel(near, at_ref, *refs):
    t = pl.program_id(0)
    if near:
        parts = refs[:8]
        w_ref, sl_ref, sr_ref, rl_ref, rr_ref, upd_ref, nl_ref, nr_ref, grad = refs[8:]
        z, x, y, _ = read_coordinates(at_ref)
        for dx in range(2):
            for dz in range(4):
                for dy in range(2):
                    unit = unit_of(lax.rem(z + 4 - dz, 4), flip(x, dx), flip(y, dy))
                    rows = pl.ds(pl.multiple_of(unit * UNIT, 8), UNIT)
                    grad[rows, :] = parts[4 * dx + dz][dy, t].astype(F32)
        g = grad[...].astype(BF)
    else:
        grad_ref, w_ref, sl_ref, sr_ref, rl_ref, rr_ref, upd_ref, nl_ref, nr_ref = refs
        g = grad_ref[t]
    nl_ref[0] = STAT_BETA * sl_ref[t] + (1.0 - STAT_BETA) * mm_nt(g, g)
    nr_ref[0] = STAT_BETA * sr_ref[t] + (1.0 - STAT_BETA) * mm_tn(g, g)
    left = mm(jnp.concatenate(split2(rl_ref[t]), axis=1), jnp.concatenate([g, g], axis=0))
    l_one, l_two = split2(left)
    r_one, r_two = split2(rr_ref[t])
    p = mm(jnp.concatenate([l_one, l_two, l_one], axis=1), jnp.concatenate([r_one, r_one, r_two], axis=0))
    mean = jnp.sum(jnp.sum(p * p, axis=1, keepdims=True), axis=0, keepdims=True) * (1.0 / (D * D))
    root = jnp.sqrt(mean)
    upd_ref[0] = -SHAMPOO_RATE * (p / (root + RMS_EPS) + DECAY_RATE * w_ref[t])


def shampoo(at, grads, blocks_w, stat_left, stat_right, root_left, root_right):
    near = len(grads) == 8
    slots = blocks_w.shape[0]
    one = pl.BlockSpec((1, D, D), lambda t: (t, 0, 0))
    return pl.pallas_call(
        functools.partial(shampoo_kernel, near),
        name="shampoo",
        grid=(slots,),
        out_shape=(shape((slots, D, D)),) * 3,
        in_specs=[SM] + [VM] * (len(grads) + 5),
        out_specs=[one] * 3,
        scratch_shapes=[pltpu.VMEM((D, D), F32)] if near else [],
        compiler_params=room(26),
        cost_estimate=pl.CostEstimate(flops=3 * 10**9, bytes_accessed=15 * 10**6, transcendentals=0),
    )(at, *grads, blocks_w, stat_left, stat_right, root_left, root_right)


GELU_C = math.sqrt(2.0 / math.pi)
GELU_D = 0.044715
EARLY = 5 * 24
LATE = 2 * 24
SUMS_MLP = 24


def norm_stats(v):
    centered = v - jnp.sum(v, axis=-1, keepdims=True) * (1.0 / D)
    inv = lax.rsqrt(jnp.sum(centered * centered, axis=-1, keepdims=True) * (1.0 / D) + NORM_EPS)
    return centered * inv, inv


def norm_back(g, normed, inv):
    mean_g = jnp.sum(g, axis=-1, keepdims=True) * (1.0 / D)
    mean_gn = jnp.sum(g * normed, axis=-1, keepdims=True) * (1.0 / D)
    return inv * (g - mean_g - normed * mean_gn)


def column_sum(v):
    return jnp.sum(v, axis=0, keepdims=True)


def head(v, h):
    return v[:, HDIM * h : HDIM * h + HDIM]


def put_pair(core, mine_ref, other_ref, j, zero, one):
    zero, one = zero.astype(BF), one.astype(BF)
    mine, other = jnp.where(core == 0, zero, one), jnp.where(core == 0, one, zero)
    for u in range(16):
        rows = slice(24 * u, 24 * u + 24)
        mine_ref[u, 24 * j : 24 * j + 24, :] = mine[rows]
        other_ref[u, 24 * j : 24 * j + 24, :] = other[rows]


def front_kernel(noisy_ref, mods_ref, bias_ref, patch_ref, pos_ref, w_ref,
                 h0_ref, qkv_ref, att_ref, h1_ref):
    i = pl.program_id(0)

    def mod(t):
        return mods_ref[pl.ds(i, 1), D * t : D * t + D]

    h0 = mm_tn(noisy_ref[0].astype(BF), patch_ref[...]) + bias_ref[0:1, :] + pos_ref[...]
    h0_ref[0] = h0
    normed, _ = norm_stats(h0)
    act = (normed * (1.0 + mod(1)) + mod(0)).astype(BF)
    q = (mm(act, w_ref[0]) + bias_ref[1:2, :]).astype(BF)
    k = mm(act, w_ref[1]).astype(BF)
    v = (mm(act, w_ref[2]) + bias_ref[2:3, :]).astype(BF)
    qkv_ref[0, :, 0:D] = q
    qkv_ref[0, :, D : 2 * D] = k
    qkv_ref[0, :, 2 * D :] = v
    scores, probs, outs = [], [], []
    for h in range(HEADS + 2):
        if h < HEADS:
            scores.append(mm_nt(head(q, h), head(k, h)))
        if 1 <= h <= HEADS:
            s = scores[h - 1] * QK_SCALE
            e = jnp.exp(s - jnp.max(s, axis=-1, keepdims=True))
            probs.append((e * (1.0 / jnp.sum(e, axis=-1, keepdims=True))).astype(BF))
        if h >= 2:
            outs.append(mm(probs[h - 2], head(v, h - 2)))
    att = jnp.concatenate(outs, axis=1).astype(BF)
    att_ref[0] = att
    h1_ref[0] = h0 + mod(2) * (mm(att, w_ref[3]) + bias_ref[3:4, :])


def middle_kernel(images, total_img, at_ref, tw_ref, h1_ref, vel_ref, dino_ref, mods_ref, bias_ref, w_ref, aw_ref, fw_ref,
                  bh1_ref, gm_ref, mine_ref, other_ref, sums_ref,
                  act2_s, gelu_s, slope_s, bi_s, bb2_s, h1_s, ba_s, act3_s, bo_s, up_s):
    i = pl.program_id(0)
    rows = pl.ds(pl.multiple_of(i * SEQ, SEQ), SEQ)

    def mod(t):
        return mods_ref[pl.ds(i, 1), D * t : D * t + D]

    @pl.when(i == 0)
    def _():
        sums_ref[...] = jnp.zeros_like(sums_ref)
        for j in range(4):
            up_s[:, D * j : D * j + D] = w_ref[4 + j]

    h1 = h1_ref[0]
    n2, inv2 = norm_stats(h1)
    act2 = (n2 * (1.0 + mod(4)) + mod(3)).astype(BF)
    act2_s[rows, :] = act2
    branch = jnp.zeros((SEQ, D), F32) + bias_ref[8:9, :]
    for j in range(2):
        lanes = slice(2 * D * j, 2 * D * j + 2 * D)
        bias = jnp.concatenate([bias_ref[4 + 2 * j : 5 + 2 * j, :], bias_ref[5 + 2 * j : 6 + 2 * j, :]], axis=1)
        x = mm(act2, up_s[:, lanes]) + bias
        xx = x * x
        t = jnp.tanh(x * (GELU_C + (GELU_C * GELU_D) * xx))
        half = 0.5 + 0.5 * t
        g = (x * half).astype(BF)
        slope_s[:, lanes] = half + (0.5 * x) * (1.0 - t * t) * (GELU_C + (3.0 * GELU_C * GELU_D) * xx)
        gelu_s[rows, lanes] = g
        branch = branch + mm(g, w_ref[8 + 2 * j : 10 + 2 * j].reshape(2 * D, D))
    h2 = h1 + mod(5) * branch
    n3, inv3 = norm_stats(h2)
    act3 = (n3 * (1.0 + mod(7)) + mod(6)).astype(BF)
    act3_s[rows, :] = act3
    out = mm(act3, fw_ref[...]) + bias_ref[11:12, 0:128]
    err = out[:, :PD] - vel_ref[0].T
    weight = tw_ref[i]
    loss = jnp.sum(column_sum(err * err), axis=1, keepdims=True) * (weight / (total_img * SEQ * PD))
    bo = jnp.concatenate([err * (2.0 * weight / (total_img * SEQ * PD)), jnp.zeros((SEQ, 128 - PD), F32)],
                         axis=1).astype(BF)
    bo_s[rows, :] = bo

    h1_low = h1.astype(BF)
    h1_s[rows, :] = h1_low
    aligned = mm(h1_low, aw_ref[...]) + jnp.concatenate([bias_ref[9:10, :], bias_ref[10:11, :]], axis=1)
    dino = dino_ref[0].astype(F32)
    dot = jnp.sum(aligned * dino, axis=-1, keepdims=True)
    ra = lax.rsqrt(jnp.sum(aligned * aligned, axis=-1, keepdims=True) + NORM_EPS)
    rd = lax.rsqrt(jnp.sum(dino * dino, axis=-1, keepdims=True) + NORM_EPS)
    scale = REPA_WEIGHT / (total_img * SEQ)
    both = ra * rd
    cosine = dot * both
    loss = loss - column_sum(cosine) * scale
    ba = (dino * (both * -scale) + aligned * (cosine * (ra * ra) * scale)).astype(BF)
    ba_s[rows, :] = ba
    through = mm_nt(ba, aw_ref[...])

    b3 = mm_nt(bo, fw_ref[...])
    bh2 = norm_back(b3 * (1.0 + mod(7)), n3, inv3)
    bb2 = (bh2 * mod(5)).astype(BF)
    bb2_s[rows, :] = bb2
    b2 = jnp.zeros((SEQ, D), F32)
    for j in range(2):
        lanes = slice(2 * D * j, 2 * D * j + 2 * D)
        bi = (mm_nt(bb2, w_ref[8 + 2 * j : 10 + 2 * j].reshape(2 * D, D)) * slope_s[:, lanes]).astype(BF)
        bi_s[rows, lanes] = bi
        bi_sum = column_sum(bi.astype(F32))
        sums_ref[16 + 2 * j : 17 + 2 * j, :] += bi_sum[:, :D]
        sums_ref[17 + 2 * j : 18 + 2 * j, :] += bi_sum[:, D:]
        b2 = b2 + mm_nt(bi, up_s[:, lanes])
    sums_ref[20:21, :] += column_sum(bb2.astype(F32))
    ba_sum = column_sum(ba.astype(F32))
    sums_ref[21:22, :] += ba_sum[:, :D]
    sums_ref[22:23, :] += ba_sum[:, D:]
    sums_ref[23:24, 0:128] += column_sum(bo.astype(F32))
    bh1_ref[0] = bh2 + norm_back(b2 * (1.0 + mod(4)), n2, inv2) + through
    gm_ref[0, 0:1, :] = column_sum(b2)
    gm_ref[0, 1:2, :] = column_sum(b2 * n2)
    gm_ref[0, 2:3, :] = column_sum(bh2 * branch)
    gm_ref[0, 3:4, :] = column_sum(b3)
    gm_ref[0, 4:5, :] = column_sum(b3 * n3)
    gm_ref[0, 5:6, :] = jnp.broadcast_to(loss, (1, D))
    gm_ref[0, 6:8, :] = jnp.zeros((2, D), F32)

    @pl.when(i == images - 1)
    def _():
        put = functools.partial(put_pair, at_ref[3], mine_ref, other_ref)
        for j in range(2):
            lanes = slice(2 * D * j, 2 * D * j + 2 * D)
            up = mm_tn(act2_s[...], bi_s[:, lanes]).astype(BF)
            down = mm_tn(bb2_s[...], gelu_s[:, lanes]).astype(BF)
            put(2 * j, up[:, :D], down[:, :D].T)
            put(2 * j + 1, up[:, D:], down[:, D:].T)
        align = mm_tn(h1_s[...], ba_s[...])
        put(4, align[:, :D], align[:, D:])
        g = mm_tn(act3_s[...], bo_s[...]).astype(BF)
        spread = (lax.broadcasted_iota(jnp.int32, (128, 128), 1) % PD
                  == lax.broadcasted_iota(jnp.int32, (128, 128), 0)).astype(F32).astype(BF)
        keep = (lax.broadcasted_iota(jnp.int32, (D, 128), 1) // PD
                == lax.broadcasted_iota(jnp.int32, (D, 128), 0) % 8)
        fold = (lax.broadcasted_iota(jnp.int32, (48, D), 1) // 8
                == lax.broadcasted_iota(jnp.int32, (48, D), 0)).astype(F32).astype(BF)
        flat = mm(fold, jnp.where(keep, mm(g, spread), 0.0).astype(BF))
        for l in range(3):
            sums_ref[0:16, 128 * l : 128 * l + 128] = flat[16 * l : 16 * l + 16, :]


def back_kernel(first, bh1_ref, h0_ref, qkv_ref, att_ref, noisy_ref, mods_ref, bias_ref, w_ref,
                bb1_ref, bp_ref, act_ref, gm_ref, patch_ref):
    i = pl.program_id(0) + first

    def mod(t):
        return mods_ref[pl.ds(i, 1), D * t : D * t + D]

    bh1 = bh1_ref[0]
    att = att_ref[0]
    bb1 = (bh1 * mod(2)).astype(BF)
    bb1_ref[0] = bb1
    gm_ref[0, 2:3, :] = column_sum(bh1 * (mm(att, w_ref[3]) + bias_ref[3:4, :]))
    batt = mm_nt(bb1, w_ref[3]).astype(BF)
    q, k, v = qkv_ref[0, :, 0:D], qkv_ref[0, :, D : 2 * D], qkv_ref[0, :, 2 * D :]
    ready, halves, gq, gk, gv = [], [], [], [], []
    for h in range(HEADS + 2):
        if h < HEADS:
            ready.append((mm_nt(head(k, h), head(q, h)), mm_nt(head(v, h), head(batt, h))))
        if 1 <= h <= HEADS:
            s, dp = ready[h - 1]
            s = s * QK_SCALE
            e = jnp.exp(s - jnp.max(s, axis=0, keepdims=True))
            p = e * (1.0 / column_sum(e))
            halves.append((p.astype(BF), (p * (dp - column_sum(dp * p))).astype(BF)))
        if h >= 2:
            p, ds = halves[h - 2]
            gv.append(mm(p, head(batt, h - 2)))
            gk.append(mm(ds, head(q, h - 2)))
            gq.append(mm_tn(ds, head(k, h - 2)))
    bq = (jnp.concatenate(gq, axis=1) * QK_SCALE).astype(BF)
    bk = (jnp.concatenate(gk, axis=1) * QK_SCALE).astype(BF)
    bv = jnp.concatenate(gv, axis=1).astype(BF)
    bp_ref[0, :, 0:D] = bq
    bp_ref[0, :, D : 2 * D] = bk
    bp_ref[0, :, 2 * D :] = bv
    b1 = mm_nt(bq, w_ref[0]) + mm_nt(bk, w_ref[1]) + mm_nt(bv, w_ref[2])
    n1, inv1 = norm_stats(h0_ref[0])
    act_ref[0] = (n1 * (1.0 + mod(1)) + mod(0)).astype(BF)
    gm_ref[0, 0:1, :] = column_sum(b1)
    gm_ref[0, 1:2, :] = column_sum(b1 * n1)
    bh0 = (bh1 + norm_back(b1 * (1.0 + mod(1)), n1, inv1)).astype(BF)
    patch_ref[0] = mm(noisy_ref[0].astype(BF), bh0)
    gm_ref[0, 3:4, :] = column_sum(bh0.astype(F32))
    gm_ref[0, 4:5, :] = column_sum(bq.astype(F32))
    gm_ref[0, 5:6, :] = column_sum(bv.astype(F32))
    gm_ref[0, 6:7, :] = column_sum(bb1.astype(F32))
    gm_ref[0, 7:8, :] = jnp.zeros((1, D), F32)


def last_kernel(counts, at_ref, att_ref, *refs):
    mine_ref, other_ref = refs[-2:]
    put = functools.partial(put_pair, at_ref[3], mine_ref, other_ref)
    parts = []
    first = 0
    for k, count in enumerate(counts):
        act_ref, bp_ref, bb1_ref = refs[3 * k : 3 * k + 3]
        parts.append((act_ref, bp_ref, att_ref, bb1_ref, first))
        first += count * SEQ

    def over(which):
        return sum(which(*p) for p in parts)

    def qkv(j):
        return over(lambda act, bp, att, bb1, first: mm_tn(act[...], bp[:, D * j : D * j + D]))

    put(0, qkv(0), qkv(2))
    put(1, qkv(1), over(lambda act, bp, att, bb1, first: mm_tn(
        att[first : first + bb1.shape[0], :], bb1[...])))


def cond_back_kernel(images, aligns, at_ref, cls_ref, gm2_ref, pre_ref, th_ref, cond_ref, feat_ref, modw_ref, fmodw_ref,
                     tout_ref, sums_ref, *refs):
    align_refs, refs = refs[:aligns], refs[aligns:]
    out_refs, pay_ref, refs = refs[-5:-1], refs[-1], refs[:-5]
    gm3_refs, patch_refs = refs[::2], refs[1::2]
    none = jnp.zeros((4, D), F32)
    gm2 = [gm2_ref[m] for m in range(images)]
    gm3 = [ref[m] for ref in gm3_refs for m in range(ref.shape[0])]
    patch = sum(ref[m] for ref in patch_refs for m in range(ref.shape[0]))

    def rows_of(values, r):
        return jnp.concatenate([v[r : r + 1, :] for v in values] + [none], axis=0)

    tiles = [rows_of(gm3, 0), rows_of(gm3, 1), rows_of(gm3, 2),
             rows_of(gm2, 0), rows_of(gm2, 1), rows_of(gm2, 2)]
    finals = [rows_of(gm2, 3), rows_of(gm2, 4)]
    g_act = jnp.zeros((24, D), F32)
    for t in range(6):
        g_act = g_act + mm_nt(stack3(tiles[t]), modw_ref[:, D * t : D * t + D])
    for t in range(2):
        g_act = g_act + mm_nt(stack3(finals[t]), fmodw_ref[:, D * t : D * t + D])
    cond = cond_ref[...]
    g_cond = fold3(g_act) * silu_slope(cond)
    g_pre = fold3(mm_nt(stack3(g_cond), tout_ref[...])) * silu_slope(pre_ref[...])
    act = silu(cond)
    lane = lax.broadcasted_iota(jnp.int32, (1, 128), 1)
    ids = []
    for m in range(images):
        number = cls_ref[m]
        row = jnp.where(lane == 0, (number // 256).astype(F32), 0.0)
        ids.append(jnp.where(lane == 1, (number % 256).astype(F32), row))
    ids = jnp.concatenate(ids, axis=0)
    loss = sum(v[5:6, 0:128] for v in gm2)
    pieces = [v.astype(F32) for v in split3(loss)]
    loss = jnp.where(lane == 0, pieces[0], jnp.where(lane == 1, pieces[1], jnp.where(lane == 2, pieces[2], 0.0)))
    loss = jnp.concatenate([loss, jnp.zeros((1, D - 128), F32)], axis=1)

    def put(plane, j, upper, lower):
        pay_ref[plane, 8 * j : 8 * j + 8, :] = jnp.concatenate([upper[:4], lower[:4]], axis=0)

    def put_rows(plane, first, v):
        pay_ref[plane, first : first + v.shape[0], :] = v

    def over(r):
        return sum(v[r : r + 1, :] for v in gm3)

    none = jnp.zeros((8, D), F32)
    row = jnp.zeros((1, D), F32)
    tags = jnp.concatenate([ids, jnp.zeros((4, D - 128), F32)], axis=1)
    pay_ref[...] = jnp.zeros_like(pay_ref)
    put(0, 0, th_ref[...], jnp.concatenate([feat_ref[...], jnp.zeros((8, D - FREQ), F32)], axis=1))
    put(0, 1, g_cond, g_pre)
    put(0, 2, tags, none)
    put_rows(0, 40, patch)
    for plane in (1, 2):
        put(plane, 0, act, act)
        for t in range(3):
            put(plane, 1 + t, tiles[t], tiles[t + 3])
    put(1, 4, g_cond, none)
    put(1, 5, tags, none)
    put(2, 4, finals[0], finals[1])
    sums = sums_ref[...]
    put_rows(2, 40, jnp.concatenate([over(4), over(5), over(6), sums[16:21]], axis=0))
    put(3, 0, act, act)
    put(3, 1, finals[0], finals[1])
    put_rows(3, 16, sum(ref[4 * UNIT :, :].astype(F32) for ref in align_refs))
    put_rows(3, 40, sums[0:16])
    last = [[over(3)] + [row] * 6, [row] * 7, [row] * 7, [sums[23:24], sums[21:22], sums[22:23]] + [row] * 4]
    for plane in range(4):
        put_rows(plane, 56, jnp.concatenate(last[plane] + [loss], axis=0))
    for d, out_ref in enumerate(out_refs):
        out_ref[...] = pay_ref[lax.rem(at_ref[0] + d, 4)].astype(BF)


def rows_each(first, *dims):
    return pl.BlockSpec((1,) + dims, lambda i: (i + first,) + (0,) * len(dims))


def front(noisy, mods, bias, patch_low, pos, blocks):
    images = noisy.shape[0]
    each = functools.partial(rows_each, 0)
    return pl.pallas_call(
        front_kernel,
        name="front",
        grid=(images,),
        out_shape=(shape((images, SEQ, D)), shape((images, SEQ, 3 * D), BF),
                   shape((images, SEQ, D), BF), shape((images, SEQ, D))),
        in_specs=[each(PD, SEQ), VM, VM, VM, VM, VM],
        out_specs=[each(SEQ, D), each(SEQ, 3 * D), each(SEQ, D), each(SEQ, D)],
        compiler_params=room(24),
        cost_estimate=cost(2.2e9, 1.2e7),
    )(noisy, mods, bias, patch_low, pos, blocks)


def middle(total_img, at, time_weight, h1, velocity, dino, mods, bias, blocks, align_low, final_low):
    images = h1.shape[0]
    each = functools.partial(rows_each, 0)
    full = lambda lanes, kind=BF: pltpu.VMEM((images * SEQ, lanes), kind)
    return pl.pallas_call(
        functools.partial(middle_kernel, images, total_img),
        name="middle",
        grid=(images,),
        out_shape=(shape((images, SEQ, D)), shape((images, 8, D)),
                   shape((16, EARLY, D), BF), shape((16, EARLY, D), BF), shape((SUMS_MLP, D))),
        in_specs=[SM, SM, each(SEQ, D), each(PD, SEQ), each(SEQ, DINO), VM, VM, VM, VM, VM],
        out_specs=[each(SEQ, D), each(8, D), VM, VM, VM],
        scratch_shapes=[full(D), full(F), pltpu.VMEM((SEQ, F), F32), full(F), full(D), full(D),
                        full(DINO), full(D), full(128), pltpu.VMEM((D, F), BF)],
        compiler_params=room(40),
        cost_estimate=cost(9e9, 1.4e7),
    )(at, time_weight, h1, velocity, dino, mods, bias, blocks, align_low, final_low)


def attention_back(first, count, bh1, h0, qkv, att, noisy, mods, bias, blocks):
    each = functools.partial(rows_each, first)
    out = functools.partial(rows_each, 0)
    return pl.pallas_call(
        functools.partial(back_kernel, first),
        name="attention_back",
        grid=(count,),
        out_shape=(shape((count, SEQ, D), BF), shape((count, SEQ, 3 * D), BF), shape((count, SEQ, D), BF),
                   shape((count, 8, D)), shape((count, PD, D))),
        in_specs=[each(SEQ, D), each(SEQ, D), each(SEQ, 3 * D), each(SEQ, D), each(PD, SEQ), VM, VM, VM],
        out_specs=[out(SEQ, D), out(SEQ, 3 * D), out(SEQ, D), out(8, D), out(PD, D)],
        compiler_params=room(24),
        cost_estimate=cost(1.2e9 * count, 3e6 * count),
    )(bh1, h0, qkv, att, noisy, mods, bias, blocks)


def last_gradients(at, att, parts):
    flat = lambda v: v.reshape(-1, v.shape[-1])
    arrays = [flat(v) for part in parts for v in part]
    counts = tuple(part[0].shape[0] for part in parts)
    return pl.pallas_call(
        functools.partial(last_kernel, counts),
        name="last_gradients",
        out_shape=(shape((16, LATE, D), BF),) * 2,
        in_specs=[SM] + [VM] * (len(arrays) + 1),
        out_specs=[VM] * 2,
        compiler_params=room(20),
        cost_estimate=cost(1.2e9, 9e6),
    )(at, flat(att), *arrays)


def cond_back(images, at, class_ids, gm2, pre, th, cond, features, mod_w, fmod_w, tout_w, sums, aligns, gm3):
    return pl.pallas_call(
        functools.partial(cond_back_kernel, images, len(aligns)),
        name="cond_back",
        out_shape=(shape((PAY, D), BF),) * 4,
        in_specs=[SM, SM] + [VM] * (9 + len(aligns) + len(gm3)),
        out_specs=[VM] * 4,
        scratch_shapes=[pltpu.VMEM((4, PAY, D), F32)],
        compiler_params=room(16),
        cost_estimate=cost(1e8, 4e6),
    )(at, class_ids, gm2, pre, th, cond, features, mod_w, fmod_w, tout_w, sums, *aligns, *gm3)


def position_table():
    quarter = D // 4
    frequencies = 1.0 / 10000.0 ** (jnp.arange(quarter, dtype=jnp.float32) / quarter)
    cell_ids = jnp.arange(SEQ, dtype=jnp.int32)
    row_arg = (cell_ids // GRID).astype(jnp.float32)[:, None] * frequencies[None, :]
    col_arg = (cell_ids % GRID).astype(jnp.float32)[:, None] * frequencies[None, :]
    return jnp.concatenate(
        [jnp.sin(col_arg), jnp.cos(col_arg), jnp.sin(row_arg), jnp.cos(row_arg)], axis=1
    )


def time_features(tstep_idx):
    half_freq = FREQ // 2
    frequencies = jnp.exp(-math.log(10000.0) * jnp.arange(half_freq, dtype=jnp.float32) / half_freq)
    angles = (tstep_idx.astype(jnp.float32) + 0.5)[:, None] * frequencies[None, :]
    return jnp.concatenate([jnp.cos(angles), jnp.sin(angles)], axis=1)


def body(
    noisy,
    velocity,
    tstep_idx,
    class_ids,
    time_weight,
    dino,
    owner_map,
    adam_flat,
    adam_m,
    adam_v,
    blocks_w,
    stat_left,
    stat_right,
    root_left,
    root_right,
):
    dp, group = lax.axis_size("dp"), lax.axis_size("shard")
    near = is_near(dp, group)
    images = noisy.shape[0]
    total_img = images * dp * group
    at = jnp.stack([jnp.asarray(v, jnp.int32) for v in coordinates()])
    flat_w = adam_flat.reshape(-1, 128)
    flat_m = adam_m.reshape(-1, 128)
    flat_v = adam_v.reshape(-1, 128)
    mine = flat_w.astype(BF)
    features = jnp.pad(time_features(tstep_idx), ((0, 4), (0, 0)))
    pos = position_table()
    noisy = jnp.transpose(noisy, (0, 2, 1))
    velocity = jnp.transpose(velocity, (0, 2, 1))
    rows = flat_w.shape[0]
    if near:
        cut = rows // 16 * 8 + 8 if rows // 8 % 2 else rows // 2
        block_parts = gather_blocks(blocks_w.astype(BF))
        pieces, (at, features, pos) = gather_flat(mine, cut, (at, features, pos))
        places = flat_places(cut)
        blocks = place_blocks(at, owner_map, block_parts)
    else:
        pieces = [lax.all_gather(mine, AXES, axis=0, tiled=True)[None]]
        places = [(0, lambda i, at: 0)]
        slot_low = lax.all_gather(blocks_w.astype(BF), "shard", axis=0, tiled=True)
        block_ids = jnp.arange(NBLK, dtype=jnp.int32)
        slot_of = jnp.sum(
            block_ids[:, None] * (owner_map[:, None] == block_ids[None, :]).astype(jnp.int32), axis=0
        )
        blocks = jnp.take(slot_low, slot_of, axis=0)
    (mods, pre, th, cond, mod_w, fmod_w, tout_w, align_low, bias, patch_low, final_low) = conditioning(
        at, class_ids, features, pieces, places, rows)
    h0, qkv, att, h1 = front(noisy, mods, bias, patch_low, pos, blocks)
    bh1, gm2, mine, other, sums = middle(
        total_img, at, time_weight, h1, velocity, dino, mods, bias, blocks, align_low, final_low)
    if near:
        early = reduce_units(at, mine, other)
    parts, gm3 = [], []
    for first, count in ((0, 1), (1, images - 1)):
        bb1, bp, act, gm, patch = attention_back(first, count, bh1, h0, qkv, att, noisy, mods, bias, blocks)
        parts.append((act, bp, bb1))
        gm3 += [gm, patch]
    late_mine, late_other = last_gradients(at, att, parts)
    aligns = early if near else [jnp.zeros((EARLY, D), BF)]
    keep, *away = cond_back(
        images, at, class_ids, gm2, pre, th, cond, features, mod_w, fmod_w, tout_w, sums, aligns, gm3)
    if near:
        late = reduce_units(at, late_mine, late_other)
        parts, grads = gather_rows(
            away, keep, lambda: turn_owned(at, late, early, owner_map), cross_owned)
        loss, upd, new_m, new_v = adam_near(at, parts, flat_w, flat_m, flat_v)
        *grads, loss, upd, new_m, new_v = lax.optimization_barrier((*grads, loss, upd, new_m, new_v))
    else:
        core = at[3]

        def by_part(mine, other):
            pair = jnp.where(core == 0, jnp.stack([mine, other]), jnp.stack([other, mine]))
            count = mine.shape[1] // UNIT
            return pair.reshape(2, 16, count, UNIT, D).transpose(0, 2, 1, 3, 4).reshape(2, count, D, D)

        early, late = by_part(mine, other), by_part(late_mine, late_other)
        late = jnp.stack([late[0, 0], late[0, 1], late[1, 0], late[1, 1]])
        grad_model = jnp.concatenate([late, early[:, :4].reshape(8, D, D)])
        planes = jnp.take(jnp.stack([keep, *away]), (jnp.arange(4) - at[0]) % 4, axis=0)
        pays = lax.all_gather(planes, AXES, axis=0, tiled=False)
        align_sum = lax.psum(early[:, 4].astype(F32), AXES)
        loss, upd, new_m, new_v = adam_wide(pays, align_sum, flat_w, flat_m, flat_v)
        slots = jnp.take(grad_model, owner_map, axis=0)
        owned = lax.psum_scatter(slots, "shard", scatter_dimension=0, tiled=True)
        grads = [lax.psum(owned.astype(F32), "dp").astype(BF)]
    block_update, new_left, new_right = shampoo(
        at, grads, blocks_w, stat_left, stat_right, root_left, root_right)
    return (loss, block_update, new_left, new_right,
            upd.reshape(-1), new_m.reshape(-1), new_v.reshape(-1))


def is_near(dp, group):
    return (dp, group) == (8, 4)


def solution(mesh):
    return jax.shard_map(
        body,
        mesh=mesh,
        in_specs=(
            P(("dp", "shard"), None, None),
            P(("dp", "shard"), None, None),
            P(("dp", "shard")),
            P(("dp", "shard")),
            P(("dp", "shard")),
            P(("dp", "shard"), None, None),
            P(),
            P(("dp", "shard")),
            P(("dp", "shard")),
            P(("dp", "shard")),
            P("shard", None, None),
            P("shard", None, None),
            P("shard", None, None),
            P("shard", None, None),
            P("shard", None, None),
        ),
        out_specs=(
            P(),
            P("shard", None, None),
            P("shard", None, None),
            P("shard", None, None),
            P(("dp", "shard")),
            P(("dp", "shard")),
            P(("dp", "shard")),
        ),
        check_vma=False,
    )
```

```python
import functools
import math

import jax
import jax.numpy as jnp
from jax import lax
from jax.experimental import pallas as pl
from jax.experimental.pallas import tpu as pltpu
from jax.sharding import PartitionSpec as P


D = 384
HEADS = 6
HDIM = 64
F = 1536
PD = 16
GRID = 16
SEQ = 256
FREQ = 256
DINO = 768
STEP = 10
NBLK = 12
ADAM_PAD = 2129920

BETA_ONE = 0.9
BETA_TWO = 0.95
ADAM_EPS = 1e-08
ADAM_RATE = 0.01
DECAY_RATE = 0.1
STAT_BETA = 0.9
SHAMPOO_RATE = 0.02
RMS_EPS = 1e-08
REPA_WEIGHT = 0.5
NORM_EPS = 1e-06
QK_SCALE = HDIM ** (-0.5)

AXES = ("dp", "shard")
BF = jnp.bfloat16
F32 = jnp.float32
VM = pl.BlockSpec(memory_space=pltpu.VMEM)
SM = pl.BlockSpec(memory_space=pltpu.SMEM)

FLAT_ROWS = ADAM_PAD // 128
R_PATCH = 0
R_PATCH_B = 48
R_TIME_IN = 51
R_TIME_IN_B = 819
R_TIME_OUT = 822
R_TIME_OUT_B = 1974
R_CLASS = 1977
R_MOD = 4980
R_MOD_B = 11892
R_QUERY_B = 11910
R_VALUE_B = 11913
R_PROJ_B = 11916
R_HIDDEN_B = 11919
R_DOWN_B = 11931
R_FMOD = 11934
R_FMOD_B = 14238
R_FINAL = 14244
R_FINAL_B = 14292
ALIGN_ROWS = 2310

PAY = 64
PLANE_ROWS = FLAT_ROWS // 4


def shape(dims, kind=F32):
    return jax.ShapeDtypeStruct(dims, kind)


def cost(flops, moved):
    return pl.CostEstimate(flops=int(flops), bytes_accessed=int(moved), transcendentals=0)


def room(mib):
    return pltpu.CompilerParams(vmem_limit_bytes=mib * 1024 * 1024)


def mm(left, right):
    return jnp.dot(left, right, preferred_element_type=F32)


def mm_nt(left, right):
    return lax.dot_general(left, right, (((1,), (1,)), ((), ())), preferred_element_type=F32)


def mm_tn(left, right):
    return lax.dot_general(left, right, (((0,), (0,)), ((), ())), preferred_element_type=F32)


def silu(v):
    return v / (1.0 + jnp.exp(-v))


def silu_slope(v):
    s = 1.0 / (1.0 + jnp.exp(-v))
    return s * (1.0 + v * (1.0 - s))


def split3(v):
    one = v.astype(BF)
    rest = v - one.astype(F32)
    two = rest.astype(BF)
    return one, two, (rest - two.astype(F32)).astype(BF)


def split2(v):
    one = v.astype(BF)
    return one, (v - one.astype(F32)).astype(BF)


def stack3(v):
    one, two, three = split3(v)
    return jnp.concatenate([one.astype(F32), two.astype(F32), three.astype(F32)], axis=0).astype(BF)


def fold3(v):
    third = v.shape[0] // 3
    return v[:third] + v[third : 2 * third] + v[2 * third :]


def place_of(z, x, y, c):
    return ((z * 2 + x) * 2 + y) * 2 + c


def permutation(move):
    pairs = []
    for z in range(4):
        for x in range(2):
            for y in range(2):
                for c in range(2):
                    pairs.append((place_of(z, x, y, c), place_of(*move(z, x, y, c))))
    return pairs


TO_C = permutation(lambda z, x, y, c: (z, x, y, 1 - c))
TO_Y = permutation(lambda z, x, y, c: (z, x, 1 - y, c))
TO_X = permutation(lambda z, x, y, c: (z, 1 - x, y, c))
TO_Z = [permutation(lambda z, x, y, c, d=d: (z ^ d, x, y, c)) for d in range(4)]


def send(value, pairs):
    return lax.ppermute(value, AXES, pairs)


def coordinates():
    dp = lax.axis_index("dp")
    sh = lax.axis_index("shard")
    return dp // 2, dp % 2, sh // 2, sh % 2


TO_XY = permutation(lambda z, x, y, c: (z, 1 - x, 1 - y, c))
TO_CY = permutation(lambda z, x, y, c: (z, x, 1 - y, 1 - c))
TO_PAIR = permutation(lambda z, x, y, c: (z + 1 - 2 * (z % 2), x, y, c))


def gather_flat(piece, cut, ready):
    turned = [send(piece, TO_Z[d]) for d in (1, 2, 3)]
    own_x, own_y = send(piece, TO_X), send(piece, TO_Y)
    first = jnp.stack([t[:cut] for t in turned])
    second = jnp.stack([t[cut:] for t in turned])
    first_x = send(first, TO_X)
    second_y = send(second, TO_Y)
    second_y, ready = lax.optimization_barrier((second_y, ready))
    first = jnp.concatenate([own_x[None, :cut], first, first_x])
    second = jnp.concatenate([own_y[None, cut:], second, second_y])
    far = [send(first, TO_Y), send(second, TO_X)]
    own = [piece, own_x[cut:], own_y[:cut]]
    own_c = [send(p, TO_C) for p in own]
    rest_c = [send(p, TO_C) for p in (first, second, *far)]
    return [p[None] for p in own] + [first, second] + far + [p[None] for p in own_c] + rest_c, ready


def flip(value, bit):
    return 1 - value if bit else value


def flat_places(cut):
    def near(dc, dx, dy):
        return lambda i, at: place_of(at[0], flip(at[1], dx), flip(at[2], dy), flip(at[3], dc))

    def far(dc, kind):
        def entry(i, at):
            z, x, y, c = at
            dz, other = (0, 1) if i == 0 else ((i - 1) % 3 + 1, (i - 1) // 3)
            dx, dy = {0: (other, 0), 1: (0, other), 2: (other, 1), 3: (1, other)}[kind]
            return place_of(z ^ dz, flip(x, dx), flip(y, dy), flip(c, dc))

        return entry

    places = []
    for dc in (0, 1):
        places += [(0, near(dc, 0, 0)), (cut, near(dc, 1, 0)), (0, near(dc, 0, 1))]
        places += [((0, cut, 0, cut)[kind], far(dc, kind)) for kind in range(4)]
    return places


def read_coordinates(ref):
    return ref[0], ref[1], ref[2], ref[3]


def cond_kernel(places, rows, at_ref, cls_ref, feat_ref, *refs):
    count = len(places)
    pieces = refs[:count]
    (mods_ref, pre_ref, th_ref, cond_ref, modw_ref, fmodw_ref, tout_ref, align_ref, bias_ref,
     patch_ref, final_ref, flat, rolled) = refs[count:]
    at = read_coordinates(at_ref)
    for ref, (offset, entry) in zip(pieces, places):
        for i in range(ref.shape[0]):
            start = pl.multiple_of(entry(i, at) * rows + offset, 8)
            flat[pl.ds(start, ref.shape[1]), :] = ref[i].astype(F32)

    def row(first, count):
        return jnp.concatenate([flat[first + l : first + l + 1, :] for l in range(count)], axis=1)

    def columns(first, depth, count, which):
        return flat[pl.ds(first + which, depth, stride=count), :].astype(BF)

    def wide(v, first, depth, count, keep=None):
        stacked = stack3(v)
        out = []
        for j in range(count):
            w = columns(first, depth, count, j)
            if keep is not None:
                keep[:, 128 * j : 128 * j + 128] = w
            out.append(fold3(mm(stacked, w)))
        return jnp.concatenate(out, axis=1)

    pre = wide(feat_ref[...], R_TIME_IN, FREQ, 3) + row(R_TIME_IN_B, 3)
    th = silu(pre)
    picked = []
    for m in range(4):
        r = R_CLASS + 3 * cls_ref[m]
        picked.append(jnp.concatenate([flat[pl.ds(r + l, 1), :] for l in range(3)], axis=1))
    picked = jnp.concatenate(picked + [jnp.zeros((4, D), F32)], axis=0)
    cond = wide(th, R_TIME_OUT, D, 3, tout_ref) + row(R_TIME_OUT_B, 3) + picked
    act = silu(cond)
    pre_ref[...] = pre
    th_ref[...] = th
    cond_ref[...] = cond
    mods_ref[:, : 6 * D] = wide(act, R_MOD, D, 18, modw_ref) + row(R_MOD_B, 18)
    mods_ref[:, 6 * D :] = wide(act, R_FMOD, D, 6, fmodw_ref) + row(R_FMOD_B, 6)

    spot = lax.broadcasted_iota(jnp.int32, (ALIGN_ROWS, 128), 1)
    here = pltpu.roll(flat[R_FINAL_B : R_FINAL_B + ALIGN_ROWS, :], 112, 1)
    after = pltpu.roll(flat[R_FINAL_B + 1 : R_FINAL_B + 1 + ALIGN_ROWS, :], 112, 1)
    rolled[...] = jnp.where(spot < 112, here, after)
    for j in range(6):
        align_ref[:, 128 * j : 128 * j + 128] = rolled[pl.ds(j, D, stride=6), :].astype(BF)

    bias_ref[...] = jnp.zeros_like(bias_ref)
    for at_row, first in ((0, R_PATCH_B), (1, R_QUERY_B), (2, R_VALUE_B), (3, R_PROJ_B),
                          (4, R_HIDDEN_B), (5, R_HIDDEN_B + 3), (6, R_HIDDEN_B + 6),
                          (7, R_HIDDEN_B + 9), (8, R_DOWN_B)):
        bias_ref[at_row : at_row + 1, :] = row(first, 3)
    for half in range(2):
        bias_ref[9 + half : 10 + half, :] = jnp.concatenate(
            [rolled[2304 + 3 * half + l : 2305 + 3 * half + l, :] for l in range(3)], axis=1)
    lane = lax.broadcasted_iota(jnp.int32, (1, 128), 1)
    bias_ref[11:12, :128] = jnp.where(lane < PD, flat[R_FINAL_B : R_FINAL_B + 1, :], 0.0)
    patch = [flat[pl.ds(R_PATCH + l, PD, stride=3), :] for l in range(3)]
    patch_ref[...] = jnp.concatenate(patch, axis=1).astype(BF)
    spread = (lax.broadcasted_iota(jnp.int32, (D, 48), 0) // 8
              == lax.broadcasted_iota(jnp.int32, (D, 48), 1)).astype(F32).astype(BF)
    wide_rows = mm(spread, flat[R_FINAL : R_FINAL + 48, :].astype(BF))
    keep = (lax.broadcasted_iota(jnp.int32, (D, 128), 1) // PD
            == lax.broadcasted_iota(jnp.int32, (D, 128), 0) % 8)
    fold = (lax.broadcasted_iota(jnp.int32, (128, 128), 0) % PD
            == lax.broadcasted_iota(jnp.int32, (128, 128), 1)).astype(F32).astype(BF)
    final_ref[...] = mm(jnp.where(keep, wide_rows, 0.0).astype(BF), fold).astype(BF)


def conditioning(at, classes, features, pieces, places, rows):
    kernel = functools.partial(cond_kernel, places, rows)
    return pl.pallas_call(
        kernel,
        name="conditioning",
        out_shape=(shape((8, 8 * D)), shape((8, D)), shape((8, D)), shape((8, D)),
                   shape((D, 6 * D), BF), shape((D, 2 * D), BF), shape((D, D), BF),
                   shape((D, DINO), BF), shape((16, D)), shape((PD, D), BF), shape((D, 128), BF)),
        in_specs=[SM, SM, VM] + [VM] * len(pieces),
        out_specs=[VM] * 11,
        scratch_shapes=[pltpu.VMEM((FLAT_ROWS + 8, 128), F32), pltpu.VMEM((ALIGN_ROWS, 128), F32)],
        compiler_params=room(28),
        cost_estimate=pl.CostEstimate(flops=10**9, bytes_accessed=10**7, transcendentals=0),
    )(at, classes, features, *pieces)


def gather_blocks(mine):
    z, _, _, _ = coordinates()
    half = lax.dynamic_slice_in_dim(mine, 192 * (z % 2), 192, 1)
    near = send(half, TO_Y)
    far = send(near, TO_PAIR)
    return [mine, near, far, send(mine, TO_C), send(near, TO_C), send(far, TO_C)]


def place_blocks_kernel(at_ref, own_ref, mine_ref, near_ref, far_ref, mine_c_ref, near_c_ref, far_c_ref, out_ref):
    z, _, y, c = read_coordinates(at_ref)
    for core, mine, near, far in ((c, mine_ref, near_ref, far_ref), (1 - c, mine_c_ref, near_c_ref, far_c_ref)):
        for t in range(3):
            out_ref[own_ref[3 * (2 * y + core) + t]] = mine[t]
            there = own_ref[3 * (2 * (1 - y) + core) + t]
            odd = pl.multiple_of(192 * lax.rem(z, 2), 16)
            even = pl.multiple_of(192 * (1 - lax.rem(z, 2)), 16)
            out_ref[there, pl.ds(odd, 192), :] = near[t]
            out_ref[there, pl.ds(even, 192), :] = far[t]


def place_blocks(at, owner_map, parts):
    return pl.pallas_call(
        place_blocks_kernel,
        name="place_blocks",
        out_shape=shape((NBLK, D, D), BF),
        in_specs=[SM, SM] + [VM] * 6,
        out_specs=VM,
        compiler_params=room(12),
        cost_estimate=cost(1e6, 7e6),
    )(at, owner_map, *parts)


UNIT = 24


def unit_of(z, x, y):
    return (2 * x + y) * 4 + z


def quarter_kernel(at_ref, mine_ref, got_ref, *out_refs):
    _, x, y, _ = read_coordinates(at_ref)
    for out_ref, (dx, dy) in zip(out_refs, ((0, 0), (1, 0), (0, 1), (1, 1))):
        rows = pl.ds(4 * (2 * flip(x, dx) + flip(y, dy)), 4)
        out_ref[...] = (mine_ref[rows].astype(F32) + got_ref[rows].astype(F32)).astype(BF)


def turn_kernel(at_ref, *refs):
    z, _, _, _ = read_coordinates(at_ref)
    for d, out_ref in enumerate(refs[4:]):
        unit = z ^ d
        out_ref[...] = sum(ref[unit].astype(F32) for ref in refs[:4]).astype(BF)


def reduce_units(at, mine, other):
    rows = mine.shape[1]
    got = send(other, TO_C)
    own, *away = pl.pallas_call(
        quarter_kernel,
        name="quarter",
        out_shape=(shape((4, rows, D), BF),) * 4,
        in_specs=[SM, VM, VM],
        out_specs=[VM] * 4,
        compiler_params=room(12),
        cost_estimate=cost(1e6, 4e6),
    )(at, mine, got)
    got = [send(v, pairs) for v, pairs in zip(away, (TO_X, TO_Y, TO_XY))]
    own, *away = pl.pallas_call(
        turn_kernel,
        name="turn",
        out_shape=(shape((rows, D), BF),) * 4,
        in_specs=[SM] + [VM] * 4,
        out_specs=[VM] * 4,
        compiler_params=room(8),
        cost_estimate=cost(1e6, 2e6),
    )(at, own, *got)
    return [own] + [send(v, TO_Z[d + 1]) for d, v in enumerate(away)]


def rows_kernel(at_ref, pay_ref, *refs):
    early, out_refs, total_ref = refs[:4], refs[4:8], refs[8]
    total = sum(ref[...].astype(F32) for ref in early).astype(BF)
    total_ref[...] = total
    for d, out_ref in enumerate(out_refs):
        plane = at_ref[0] ^ d
        out_ref[...] = pay_ref[plane]

        @pl.when(plane == 3)
        def _():
            out_ref[16:40, :] = total[4 * UNIT :]


def owner_kernel(at_ref, own_ref, *refs):
    late, early = refs[:4], refs[4]
    out_refs, total = refs[5:9], refs[9]
    _, _, y, c = read_coordinates(at_ref)
    one = sum(ref[...].astype(F32) for ref in late)
    two = early[...].astype(F32)
    for k in range(6):
        total[k] = (one[UNIT * k : UNIT * k + UNIT] if k < 2 else two[UNIT * (k - 2) : UNIT * (k - 1)])
    for out_ref, (dy, dc) in zip(out_refs, ((0, 0), (0, 1), (1, 0), (1, 1))):
        first = 3 * (2 * flip(y, dy) + flip(c, dc))
        for t in range(3):
            block = own_ref[first + t]
            low = block < 4
            part = jnp.where(low, lax.div(block, 2), lax.div(block - 4, 4))
            entry = jnp.where(low, lax.rem(block, 2), 2 + lax.rem(jnp.maximum(block - 4, 0), 4))
            out_ref[t] = jnp.where(part == c, total[entry], 0.0).astype(BF)


def join_kernel(own_ref, pair_ref, near_ref, far_ref, out_ref):
    out_ref[0] = own_ref[...] + pair_ref[...]
    out_ref[1] = near_ref[...] + far_ref[...]


def exchange_gradients(at, owner_map, pay, late, early):
    piece = (3, UNIT, D)
    keep, *away, early = pl.pallas_call(
        rows_kernel,
        name="pay_rows",
        out_shape=(shape((PAY, D), BF),) * 4 + (shape((EARLY, D), BF),),
        in_specs=[SM] + [VM] * 5,
        out_specs=[VM] * 5,
        compiler_params=room(8),
        cost_estimate=cost(1e6, 1e6),
    )(at, pay, *early)
    turned = [send(v, TO_Z[d + 1]) for d, v in enumerate(away)]
    own, to_c, to_y, to_cy = pl.pallas_call(
        owner_kernel,
        name="owner_rows",
        out_shape=(shape(piece, BF),) * 4,
        in_specs=[SM, SM] + [VM] * 5,
        out_specs=[VM] * 4,
        scratch_shapes=[pltpu.VMEM((6, UNIT, D), F32)],
        compiler_params=room(8),
        cost_estimate=cost(1e6, 1e6),
    )(at, owner_map, *late, early)
    far, near, pair = send(to_cy, TO_CY), send(to_y, TO_Y), send(to_c, TO_C)
    turned, pair = lax.optimization_barrier((turned, pair))
    rows = jnp.stack([keep] + turned)
    plane = [rows, send(rows, TO_X), send(rows, TO_Y)]
    both = pl.pallas_call(
        join_kernel,
        name="join",
        out_shape=shape((2,) + piece, BF),
        in_specs=[VM] * 4,
        out_specs=VM,
        compiler_params=room(8),
        cost_estimate=cost(1e6, 1e6),
    )(own, pair, near, far)
    column = [both] + [send(both, TO_Z[d]) for d in (1, 2, 3)]
    crossed = [send(both, TO_X)]
    plane[1], column[1] = lax.optimization_barrier((plane[1], column[1]))
    plane.append(send(plane[1], TO_Y))
    slots = column + crossed + [send(v, TO_X) for v in column[1:]]
    return slots, plane + [send(p, TO_C) for p in plane]


def plane_gradient(plane, pay_ref, flat, rolled, align):
    rows = 8 * pay_ref.shape[0]

    def tile(j):
        return pay_ref[:, 8 * j : 8 * j + 8, :].astype(F32).reshape(rows, D)

    def sums(first, last):
        return jnp.sum(pay_ref[:, first:last, :].astype(F32), axis=0)

    upper = lax.broadcasted_iota(jnp.int32, (rows, 1), 0) % 8 < 4

    def first(v):
        return jnp.where(upper, v, 0.0)

    def second(v):
        return jnp.where(upper, 0.0, v)

    def put_row(v, row):
        for l in range(v.shape[1] // 128):
            flat[row + l : row + l + 1, :] = v[:, 128 * l : 128 * l + 128]

    def put_matrix(v, row, count, which):
        for l in range(v.shape[1] // 128):
            flat[pl.ds(row + which + l, v.shape[0], stride=count), :] = v[:, 128 * l : 128 * l + 128]

    def classes(ids, g_low):
        numbers = (ids[:, 0:1] * 256.0 + ids[:, 1:2]).astype(jnp.int32)
        for part in range(3):
            height = 336 if part < 2 else 329
            marks = lax.broadcasted_iota(jnp.int32, (rows, 336), 1) + 336 * part
            hits = first(jnp.where(marks == numbers, 1.0, 0.0)).astype(BF)
            put_matrix(mm_tn(hits, g_low)[:height], R_CLASS + 3 * 336 * part, 3, 0)

    def modulations(low, bias):
        act = tile(0)[:, low : low + 256]
        halves = (first(act).astype(BF), second(act).astype(BF))
        for t in range(3):
            g = tile(1 + t)
            for half in range(2):
                put_matrix(mm_tn(halves[half], g.astype(BF)), R_MOD + 18 * low, 18, 3 * (t + 3 * half))
                if bias:
                    put_row(column_sum((first, second)[half](g)), R_MOD_B + 3 * (t + 3 * half))

    def finals(which, bias):
        act, g = tile(0), tile(which)
        for half, part in enumerate((first, second)):
            put_matrix(mm_tn(part(act).astype(BF), g.astype(BF)), R_FMOD, 6, 3 * half)
            if bias:
                put_row(column_sum(part(g)), R_FMOD_B + 3 * half)

    if plane == 0:
        left, g = tile(0).astype(BF), tile(1)
        g_cond, g_pre = first(g), second(g)
        put_matrix(mm_tn(left[:, :FREQ], g_pre.astype(BF)), R_TIME_IN, 3, 0)
        put_row(column_sum(g_pre), R_TIME_IN_B)
        put_matrix(mm_tn(left, g_cond.astype(BF)), R_TIME_OUT, 3, 0)
        put_row(column_sum(g_cond), R_TIME_OUT_B)
        classes(tile(2)[:, :128], g.astype(BF))
        total = sums(40, 64)
        for l in range(3):
            flat[pl.ds(R_PATCH + l, PD, stride=3), :] = total[0:16, 128 * l : 128 * l + 128]
        put_row(total[16:17], R_PATCH_B)
    if plane == 1:
        classes(tile(5)[:, :128], tile(4).astype(BF))
        modulations(0, False)
    if plane == 2:
        modulations(128, True)
        finals(4, False)
        total = sums(40, 48)
        for k, row in enumerate((R_QUERY_B, R_VALUE_B, R_PROJ_B, R_HIDDEN_B, R_HIDDEN_B + 3, R_HIDDEN_B + 6,
                                 R_HIDDEN_B + 9, R_DOWN_B)):
            put_row(total[k : k + 1], row)
    if plane == 3:
        finals(1, True)
        total = sums(40, 64)
        for l in range(3):
            flat[R_FINAL + 16 * l : R_FINAL + 16 * l + 16, :] = total[0:16, 128 * l : 128 * l + 128]
        rolled[0:8, :] = jnp.zeros((8, 128), F32)
        rolled[8 + ALIGN_ROWS :, :] = jnp.zeros_like(rolled[8 + ALIGN_ROWS :, :])
        rolled[7:8, :] = pltpu.roll(total[16:17, 0:128], 112, 1)
        for half in range(2):
            for l in range(3):
                lanes = slice(128 * l, 128 * l + 128)
                rolled[pl.ds(8 + 3 * half + l, D, stride=6), :] = align[half, :, lanes].astype(F32)
                r = 8 + 2304 + 3 * half + l
                rolled[r : r + 1, :] = total[17 + half : 18 + half, lanes]
        count = FLAT_ROWS - R_FINAL_B
        spot = lax.broadcasted_iota(jnp.int32, (count, 128), 1)
        here = pltpu.roll(rolled[8 : 8 + count, :], 16, 1)
        before = pltpu.roll(rolled[7 : 7 + count, :], 16, 1)
        flat[R_FINAL_B:FLAT_ROWS, :] = jnp.where(spot < 16, before, here)


def loss_of(pay_ref):
    rows = 8 * pay_ref.shape[0]
    parts = pay_ref[:, PAY - 8 : PAY, 0:128].astype(F32).reshape(rows, 128)
    parts = column_sum(jnp.where(lax.broadcasted_iota(jnp.int32, (rows, 128), 0) % 8 == 7, parts, 0.0))
    return parts[:, 0:1] + parts[:, 1:2] + parts[:, 2:3]


def adam_near_kernel(at_ref, *refs):
    parts = refs[:8]
    w_ref, m_ref, v_ref, loss_ref, upd_ref, new_m_ref, new_v_ref, pay, align, flat, rolled = refs[8:]
    at = read_coordinates(at_ref)
    z, x, y, c = at
    for k, ref in enumerate(parts):
        dc, dy, dx = k // 4, k // 2 % 2, k % 2
        for dz in range(4):
            there = (z ^ dz, flip(x, dx), flip(y, dy), flip(c, dc))
            value = ref[dz].astype(F32)
            pay[place_of(*there)] = value
            start = pl.multiple_of(unit_of(*there[:3]) * UNIT, 8)
            align[there[3], pl.ds(start, UNIT), :] = value[16:40]
    loss_ref[...] = loss_of(pay)
    for plane in range(4):
        @pl.when(z == plane)
        def _():
            plane_gradient(plane, pay, flat, rolled, align)
    size = w_ref.shape[0]
    start = pl.multiple_of(place_of(z, x, y, c) * size, 8)
    adam_step(flat[pl.ds(start, size), :], w_ref, m_ref, v_ref, upd_ref, new_m_ref, new_v_ref)


def adam_plane_kernel(plane, pay_ref, align_ref, loss_ref, flat_ref, rolled):
    loss_ref[...] = loss_of(pay_ref)
    plane_gradient(plane, pay_ref, flat_ref, rolled, align_ref)


def adam_step(grad, w_ref, m_ref, v_ref, upd_ref, new_m_ref, new_v_ref):
    new_m = BETA_ONE * m_ref[...] + (1.0 - BETA_ONE) * grad
    new_v = BETA_TWO * v_ref[...] + (1.0 - BETA_TWO) * grad * grad
    new_m_ref[...] = new_m
    new_v_ref[...] = new_v
    right_m = new_m / (1.0 - BETA_ONE**STEP)
    right_v = new_v / (1.0 - BETA_TWO**STEP)
    upd_ref[...] = -ADAM_RATE * (right_m / (jnp.sqrt(right_v) + ADAM_EPS) + DECAY_RATE * w_ref[...])


ROLL_ROWS = 8 + FLAT_ROWS - R_FINAL_B + 8


ROLL_ROWS = 8 + FLAT_ROWS - R_FINAL_B + 8


def adam_near(at, parts, flat_w, m, v):
    size = flat_w.shape
    loss, upd, new_m, new_v = pl.pallas_call(
        adam_near_kernel,
        name="adam",
        out_shape=(shape((1, 1)), shape(size), shape(size), shape(size)),
        in_specs=[SM] + [VM] * 11,
        out_specs=[VM] * 4,
        scratch_shapes=[pltpu.VMEM((32, PAY, D), F32), pltpu.VMEM((2, D, D), F32),
                        pltpu.VMEM((FLAT_ROWS, 128), F32), pltpu.VMEM((ROLL_ROWS, 128), F32)],
        compiler_params=room(24),
        cost_estimate=pl.CostEstimate(flops=10**9, bytes_accessed=10**7, transcendentals=0),
    )(at, *parts, flat_w, m, v)
    return loss[0, 0], upd, new_m, new_v


def adam_wide(pays, align, flat_w, m, v):
    grads = []
    for plane in range(4):
        loss, flat = pl.pallas_call(
            functools.partial(adam_plane_kernel, plane),
            name="adam_gradient",
            out_shape=(shape((1, 1)), shape((FLAT_ROWS, 128))),
            in_specs=[VM] * 2,
            out_specs=[VM] * 2,
            scratch_shapes=[pltpu.VMEM((ROLL_ROWS, 128), F32)],
        )(pays[:, plane], align)
        grads.append(flat[PLANE_ROWS * plane : PLANE_ROWS * (plane + 1)])
    size = flat_w.shape[0]
    place = lax.axis_index("dp") * lax.axis_size("shard") + lax.axis_index("shard")
    grad = lax.dynamic_slice_in_dim(jnp.concatenate(grads), place * size, size, 0)
    upd, new_m, new_v = pl.pallas_call(
        lambda g, *refs: adam_step(g[...], *refs),
        name="adam",
        out_shape=(shape(flat_w.shape),) * 3,
        in_specs=[VM] * 4,
        out_specs=[VM] * 3,
    )(grad, flat_w, m, v)
    return loss[0, 0], upd, new_m, new_v


def shampoo_kernel(near, at_ref, *refs):
    t = pl.program_id(0)
    if near:
        parts = refs[:8]
        w_ref, sl_ref, sr_ref, rl_ref, rr_ref, upd_ref, nl_ref, nr_ref, grad = refs[8:]
        z, x, y, _ = read_coordinates(at_ref)
        for dx in range(2):
            for dz in range(4):
                for dy in range(2):
                    unit = unit_of(z ^ dz, flip(x, dx), flip(y, dy))
                    rows = pl.ds(pl.multiple_of(unit * UNIT, 8), UNIT)
                    grad[rows, :] = parts[4 * dx + dz][dy, t].astype(F32)
        g = grad[...].astype(BF)
    else:
        grad_ref, w_ref, sl_ref, sr_ref, rl_ref, rr_ref, upd_ref, nl_ref, nr_ref = refs
        g = grad_ref[t]
    nl_ref[0] = STAT_BETA * sl_ref[t] + (1.0 - STAT_BETA) * mm_nt(g, g)
    nr_ref[0] = STAT_BETA * sr_ref[t] + (1.0 - STAT_BETA) * mm_tn(g, g)
    left = mm(jnp.concatenate(split2(rl_ref[t]), axis=1), jnp.concatenate([g, g], axis=0))
    l_one, l_two = split2(left)
    r_one, r_two = split2(rr_ref[t])
    p = mm(jnp.concatenate([l_one, l_two, l_one], axis=1), jnp.concatenate([r_one, r_one, r_two], axis=0))
    mean = jnp.sum(jnp.sum(p * p, axis=1, keepdims=True), axis=0, keepdims=True) * (1.0 / (D * D))
    root = jnp.sqrt(mean)
    upd_ref[0] = -SHAMPOO_RATE * (p / (root + RMS_EPS) + DECAY_RATE * w_ref[t])


def shampoo(at, grads, blocks_w, stat_left, stat_right, root_left, root_right):
    near = len(grads) == 8
    slots = blocks_w.shape[0]
    one = pl.BlockSpec((1, D, D), lambda t: (t, 0, 0))
    return pl.pallas_call(
        functools.partial(shampoo_kernel, near),
        name="shampoo",
        grid=(slots,),
        out_shape=(shape((slots, D, D)),) * 3,
        in_specs=[SM] + [VM] * (len(grads) + 5),
        out_specs=[one] * 3,
        scratch_shapes=[pltpu.VMEM((D, D), F32)] if near else [],
        compiler_params=room(26),
        cost_estimate=pl.CostEstimate(flops=3 * 10**9, bytes_accessed=15 * 10**6, transcendentals=0),
    )(at, *grads, blocks_w, stat_left, stat_right, root_left, root_right)


GELU_C = math.sqrt(2.0 / math.pi)
GELU_D = 0.044715
EARLY = 5 * 24
LATE = 2 * 24
SUMS_MLP = 24


def norm_stats(v):
    centered = v - jnp.sum(v, axis=-1, keepdims=True) * (1.0 / D)
    inv = lax.rsqrt(jnp.sum(centered * centered, axis=-1, keepdims=True) * (1.0 / D) + NORM_EPS)
    return centered * inv, inv


def norm_back(g, normed, inv):
    mean_g = jnp.sum(g, axis=-1, keepdims=True) * (1.0 / D)
    mean_gn = jnp.sum(g * normed, axis=-1, keepdims=True) * (1.0 / D)
    return inv * (g - mean_g - normed * mean_gn)


def column_sum(v):
    return jnp.sum(v, axis=0, keepdims=True)


def head(v, h):
    return v[:, HDIM * h : HDIM * h + HDIM]


def put_pair(core, mine_ref, other_ref, j, zero, one):
    zero, one = zero.astype(BF), one.astype(BF)
    mine, other = jnp.where(core == 0, zero, one), jnp.where(core == 0, one, zero)
    for u in range(16):
        rows = slice(24 * u, 24 * u + 24)
        mine_ref[u, 24 * j : 24 * j + 24, :] = mine[rows]
        other_ref[u, 24 * j : 24 * j + 24, :] = other[rows]


def front_kernel(noisy_ref, mods_ref, bias_ref, patch_ref, pos_ref, w_ref,
                 h0_ref, qkv_ref, att_ref, h1_ref):
    i = pl.program_id(0)

    def mod(t):
        return mods_ref[pl.ds(i, 1), D * t : D * t + D]

    h0 = mm_tn(noisy_ref[0].astype(BF), patch_ref[...]) + bias_ref[0:1, :] + pos_ref[...]
    h0_ref[0] = h0
    normed, _ = norm_stats(h0)
    act = (normed * (1.0 + mod(1)) + mod(0)).astype(BF)
    q = (mm(act, w_ref[0]) + bias_ref[1:2, :]).astype(BF)
    k = mm(act, w_ref[1]).astype(BF)
    v = (mm(act, w_ref[2]) + bias_ref[2:3, :]).astype(BF)
    qkv_ref[0, :, 0:D] = q
    qkv_ref[0, :, D : 2 * D] = k
    qkv_ref[0, :, 2 * D :] = v
    scores, probs, outs = [], [], []
    for h in range(HEADS + 2):
        if h < HEADS:
            scores.append(mm_nt(head(q, h), head(k, h)))
        if 1 <= h <= HEADS:
            s = scores[h - 1] * QK_SCALE
            e = jnp.exp(s - jnp.max(s, axis=-1, keepdims=True))
            probs.append((e * (1.0 / jnp.sum(e, axis=-1, keepdims=True))).astype(BF))
        if h >= 2:
            outs.append(mm(probs[h - 2], head(v, h - 2)))
    att = jnp.concatenate(outs, axis=1).astype(BF)
    att_ref[0] = att
    h1_ref[0] = h0 + mod(2) * (mm(att, w_ref[3]) + bias_ref[3:4, :])


def middle_kernel(images, total_img, at_ref, tw_ref, h1_ref, vel_ref, dino_ref, mods_ref, bias_ref, w_ref, aw_ref, fw_ref,
                  bh1_ref, gm_ref, mine_ref, other_ref, sums_ref,
                  act2_s, gelu_s, slope_s, bi_s, bb2_s, h1_s, ba_s, act3_s, bo_s, up_s):
    i = pl.program_id(0)
    rows = pl.ds(pl.multiple_of(i * SEQ, SEQ), SEQ)

    def mod(t):
        return mods_ref[pl.ds(i, 1), D * t : D * t + D]

    @pl.when(i == 0)
    def _():
        sums_ref[...] = jnp.zeros_like(sums_ref)
        for j in range(4):
            up_s[:, D * j : D * j + D] = w_ref[4 + j]

    h1 = h1_ref[0]
    h1_low = h1.astype(BF)
    h1_s[rows, :] = h1_low
    aligned = mm(h1_low, aw_ref[...])
    n2, inv2 = norm_stats(h1)
    act2 = (n2 * (1.0 + mod(4)) + mod(3)).astype(BF)
    act2_s[rows, :] = act2

    def lanes_of(j):
        return slice(2 * D * j, 2 * D * j + 2 * D)

    def pair_row(j):
        return jnp.concatenate([bias_ref[j : j + 1, :], bias_ref[j + 1 : j + 2, :]], axis=1)

    def expand(j):
        return mm(act2, up_s[:, lanes_of(j)])

    def activate(j, x):
        x = x + pair_row(4 + 2 * j)
        xx = x * x
        t = jnp.tanh(x * (GELU_C + (GELU_C * GELU_D) * xx))
        half = 0.5 + 0.5 * t
        slope_s[:, lanes_of(j)] = half + (0.5 * x) * (1.0 - t * t) * (GELU_C + (3.0 * GELU_C * GELU_D) * xx)
        g = (x * half).astype(BF)
        gelu_s[rows, lanes_of(j)] = g
        return g

    def contract(j, g):
        return mm(g, w_ref[8 + 2 * j : 10 + 2 * j].reshape(2 * D, D))

    x_one = expand(0)
    aligned = aligned + pair_row(9)
    dino = dino_ref[0].astype(F32)
    dot = jnp.sum(aligned * dino, axis=-1, keepdims=True)
    ra = lax.rsqrt(jnp.sum(aligned * aligned, axis=-1, keepdims=True) + NORM_EPS)
    rd = lax.rsqrt(jnp.sum(dino * dino, axis=-1, keepdims=True) + NORM_EPS)
    x_two = expand(1)
    g_one = activate(0, x_one)
    scale = REPA_WEIGHT / (total_img * SEQ)
    both = ra * rd
    cosine = dot * both
    ba = (dino * (both * -scale) + aligned * (cosine * (ra * ra) * scale)).astype(BF)
    ba_s[rows, :] = ba
    branch = contract(0, g_one)
    g_two = activate(1, x_two)
    through = mm_nt(ba, aw_ref[...])
    branch = branch + contract(1, g_two) + bias_ref[8:9, :]
    ba_sum = column_sum(ba.astype(F32))
    h2 = h1 + mod(5) * branch
    n3, inv3 = norm_stats(h2)
    act3 = (n3 * (1.0 + mod(7)) + mod(6)).astype(BF)
    act3_s[rows, :] = act3
    out = mm(act3, fw_ref[...]) + bias_ref[11:12, 0:128]
    err = out[:, :PD] - vel_ref[0].T
    weight = tw_ref[i]
    loss = jnp.sum(column_sum(err * err), axis=1, keepdims=True) * (weight / (total_img * SEQ * PD))
    loss = loss - column_sum(cosine) * scale
    bo = jnp.concatenate([err * (2.0 * weight / (total_img * SEQ * PD)), jnp.zeros((SEQ, 128 - PD), F32)],
                         axis=1).astype(BF)
    bo_s[rows, :] = bo

    b3 = mm_nt(bo, fw_ref[...])
    bh2 = norm_back(b3 * (1.0 + mod(7)), n3, inv3)
    bb2 = (bh2 * mod(5)).astype(BF)
    bb2_s[rows, :] = bb2
    b2 = jnp.zeros((SEQ, D), F32)
    for j in range(2):
        lanes = slice(2 * D * j, 2 * D * j + 2 * D)
        bi = (mm_nt(bb2, w_ref[8 + 2 * j : 10 + 2 * j].reshape(2 * D, D)) * slope_s[:, lanes]).astype(BF)
        bi_s[rows, lanes] = bi
        bi_sum = column_sum(bi.astype(F32))
        sums_ref[16 + 2 * j : 17 + 2 * j, :] += bi_sum[:, :D]
        sums_ref[17 + 2 * j : 18 + 2 * j, :] += bi_sum[:, D:]
        b2 = b2 + mm_nt(bi, up_s[:, lanes])
    sums_ref[20:21, :] += column_sum(bb2.astype(F32))
    sums_ref[21:22, :] += ba_sum[:, :D]
    sums_ref[22:23, :] += ba_sum[:, D:]
    sums_ref[23:24, 0:128] += column_sum(bo.astype(F32))
    bh1_ref[0] = bh2 + norm_back(b2 * (1.0 + mod(4)), n2, inv2) + through
    gm_ref[0, 0:1, :] = column_sum(b2)
    gm_ref[0, 1:2, :] = column_sum(b2 * n2)
    gm_ref[0, 2:3, :] = column_sum(bh2 * branch)
    gm_ref[0, 3:4, :] = column_sum(b3)
    gm_ref[0, 4:5, :] = column_sum(b3 * n3)
    gm_ref[0, 5:6, :] = jnp.broadcast_to(loss, (1, D))
    gm_ref[0, 6:8, :] = jnp.zeros((2, D), F32)

    @pl.when(i == images - 1)
    def _():
        put = functools.partial(put_pair, at_ref[3], mine_ref, other_ref)
        for j in range(2):
            lanes = slice(2 * D * j, 2 * D * j + 2 * D)
            up = mm_tn(act2_s[...], bi_s[:, lanes]).astype(BF)
            down = mm_tn(bb2_s[...], gelu_s[:, lanes]).astype(BF)
            put(2 * j, up[:, :D], down[:, :D].T)
            put(2 * j + 1, up[:, D:], down[:, D:].T)
        align = mm_tn(h1_s[...], ba_s[...])
        put(4, align[:, :D], align[:, D:])
        g = mm_tn(act3_s[...], bo_s[...]).astype(BF)
        spread = (lax.broadcasted_iota(jnp.int32, (128, 128), 1) % PD
                  == lax.broadcasted_iota(jnp.int32, (128, 128), 0)).astype(F32).astype(BF)
        keep = (lax.broadcasted_iota(jnp.int32, (D, 128), 1) // PD
                == lax.broadcasted_iota(jnp.int32, (D, 128), 0) % 8)
        fold = (lax.broadcasted_iota(jnp.int32, (48, D), 1) // 8
                == lax.broadcasted_iota(jnp.int32, (48, D), 0)).astype(F32).astype(BF)
        flat = mm(fold, jnp.where(keep, mm(g, spread), 0.0).astype(BF))
        for l in range(3):
            sums_ref[0:16, 128 * l : 128 * l + 128] = flat[16 * l : 16 * l + 16, :]


def back_kernel(first, bh1_ref, h0_ref, qkv_ref, att_ref, noisy_ref, mods_ref, bias_ref, w_ref,
                bb1_ref, bp_ref, act_ref, gm_ref, patch_ref):
    i = pl.program_id(0) + first

    def mod(t):
        return mods_ref[pl.ds(i, 1), D * t : D * t + D]

    bh1 = bh1_ref[0]
    att = att_ref[0]
    bb1 = (bh1 * mod(2)).astype(BF)
    bb1_ref[0] = bb1
    gm_ref[0, 2:3, :] = column_sum(bh1 * (mm(att, w_ref[3]) + bias_ref[3:4, :]))
    batt = mm_nt(bb1, w_ref[3]).astype(BF)
    q, k, v = qkv_ref[0, :, 0:D], qkv_ref[0, :, D : 2 * D], qkv_ref[0, :, 2 * D :]
    ready, halves, gq, gk, gv = [], [], [], [], []
    for h in range(HEADS + 2):
        if h < HEADS:
            ready.append((mm_nt(head(k, h), head(q, h)), mm_nt(head(v, h), head(batt, h))))
        if 1 <= h <= HEADS:
            s, dp = ready[h - 1]
            s = s * QK_SCALE
            e = jnp.exp(s - jnp.max(s, axis=0, keepdims=True))
            p = e * (1.0 / column_sum(e))
            halves.append((p.astype(BF), (p * (dp - column_sum(dp * p))).astype(BF)))
        if h >= 2:
            p, ds = halves[h - 2]
            gv.append(mm(p, head(batt, h - 2)))
            gk.append(mm(ds, head(q, h - 2)))
            gq.append(mm_tn(ds, head(k, h - 2)))
    bq = (jnp.concatenate(gq, axis=1) * QK_SCALE).astype(BF)
    bk = (jnp.concatenate(gk, axis=1) * QK_SCALE).astype(BF)
    bv = jnp.concatenate(gv, axis=1).astype(BF)
    bp_ref[0, :, 0:D] = bq
    bp_ref[0, :, D : 2 * D] = bk
    bp_ref[0, :, 2 * D :] = bv
    b1 = mm_nt(bq, w_ref[0]) + mm_nt(bk, w_ref[1]) + mm_nt(bv, w_ref[2])
    n1, inv1 = norm_stats(h0_ref[0])
    act_ref[0] = (n1 * (1.0 + mod(1)) + mod(0)).astype(BF)
    gm_ref[0, 0:1, :] = column_sum(b1)
    gm_ref[0, 1:2, :] = column_sum(b1 * n1)
    bh0 = (bh1 + norm_back(b1 * (1.0 + mod(1)), n1, inv1)).astype(BF)
    patch_ref[0] = mm(noisy_ref[0].astype(BF), bh0)
    gm_ref[0, 3:4, :] = column_sum(bh0.astype(F32))
    gm_ref[0, 4:5, :] = column_sum(bq.astype(F32))
    gm_ref[0, 5:6, :] = column_sum(bv.astype(F32))
    gm_ref[0, 6:7, :] = column_sum(bb1.astype(F32))
    gm_ref[0, 7:8, :] = jnp.zeros((1, D), F32)


def last_kernel(counts, at_ref, att_ref, *refs):
    mine_ref, other_ref = refs[-2:]
    put = functools.partial(put_pair, at_ref[3], mine_ref, other_ref)
    parts = []
    first = 0
    for k, count in enumerate(counts):
        act_ref, bp_ref, bb1_ref = refs[3 * k : 3 * k + 3]
        parts.append((act_ref, bp_ref, att_ref, bb1_ref, first))
        first += count * SEQ

    def over(which):
        return sum(which(*p) for p in parts)

    def qkv(j):
        return over(lambda act, bp, att, bb1, first: mm_tn(act[...], bp[:, D * j : D * j + D]))

    put(0, qkv(0), qkv(2))
    put(1, qkv(1), over(lambda act, bp, att, bb1, first: mm_tn(
        att[first : first + bb1.shape[0], :], bb1[...])))


def cond_back_kernel(images, cls_ref, gm2_ref, pre_ref, th_ref, cond_ref, feat_ref, modw_ref, fmodw_ref,
                     tout_ref, sums_ref, *refs):
    out_ref, pay_ref, refs = refs[-2], refs[-1], refs[:-2]
    gm3_refs, patch_refs = refs[::2], refs[1::2]
    none = jnp.zeros((4, D), F32)
    gm2 = [gm2_ref[m] for m in range(images)]
    gm3 = [ref[m] for ref in gm3_refs for m in range(ref.shape[0])]
    patch = sum(ref[m] for ref in patch_refs for m in range(ref.shape[0]))

    def rows_of(values, r):
        return jnp.concatenate([v[r : r + 1, :] for v in values] + [none], axis=0)

    tiles = [rows_of(gm3, 0), rows_of(gm3, 1), rows_of(gm3, 2),
             rows_of(gm2, 0), rows_of(gm2, 1), rows_of(gm2, 2)]
    finals = [rows_of(gm2, 3), rows_of(gm2, 4)]
    g_act = jnp.zeros((24, D), F32)
    for t in range(6):
        g_act = g_act + mm_nt(stack3(tiles[t]), modw_ref[:, D * t : D * t + D])
    for t in range(2):
        g_act = g_act + mm_nt(stack3(finals[t]), fmodw_ref[:, D * t : D * t + D])
    cond = cond_ref[...]
    g_cond = fold3(g_act) * silu_slope(cond)
    g_pre = fold3(mm_nt(stack3(g_cond), tout_ref[...])) * silu_slope(pre_ref[...])
    act = silu(cond)
    lane = lax.broadcasted_iota(jnp.int32, (1, 128), 1)
    ids = []
    for m in range(images):
        number = cls_ref[m]
        row = jnp.where(lane == 0, (number // 256).astype(F32), 0.0)
        ids.append(jnp.where(lane == 1, (number % 256).astype(F32), row))
    ids = jnp.concatenate(ids, axis=0)
    loss = sum(v[5:6, 0:128] for v in gm2)
    pieces = [v.astype(F32) for v in split3(loss)]
    loss = jnp.where(lane == 0, pieces[0], jnp.where(lane == 1, pieces[1], jnp.where(lane == 2, pieces[2], 0.0)))
    loss = jnp.concatenate([loss, jnp.zeros((1, D - 128), F32)], axis=1)

    def put(plane, j, upper, lower):
        pay_ref[plane, 8 * j : 8 * j + 8, :] = jnp.concatenate([upper[:4], lower[:4]], axis=0)

    def put_rows(plane, first, v):
        pay_ref[plane, first : first + v.shape[0], :] = v

    def over(r):
        return sum(v[r : r + 1, :] for v in gm3)

    none = jnp.zeros((8, D), F32)
    row = jnp.zeros((1, D), F32)
    tags = jnp.concatenate([ids, jnp.zeros((4, D - 128), F32)], axis=1)
    pay_ref[...] = jnp.zeros_like(pay_ref)
    put(0, 0, th_ref[...], jnp.concatenate([feat_ref[...], jnp.zeros((8, D - FREQ), F32)], axis=1))
    put(0, 1, g_cond, g_pre)
    put(0, 2, tags, none)
    put_rows(0, 40, patch)
    for plane in (1, 2):
        put(plane, 0, act, act)
        for t in range(3):
            put(plane, 1 + t, tiles[t], tiles[t + 3])
    put(1, 4, g_cond, none)
    put(1, 5, tags, none)
    put(2, 4, finals[0], finals[1])
    sums = sums_ref[...]
    put_rows(2, 40, jnp.concatenate([over(4), over(5), over(6), sums[16:21]], axis=0))
    put(3, 0, act, act)
    put(3, 1, finals[0], finals[1])
    put_rows(3, 40, sums[0:16])
    last = [[over(3)] + [row] * 6, [row] * 7, [row] * 7, [sums[23:24], sums[21:22], sums[22:23]] + [row] * 4]
    for plane in range(4):
        put_rows(plane, 56, jnp.concatenate(last[plane] + [loss], axis=0))
    out_ref[...] = pay_ref[...].astype(BF)


def rows_each(first, *dims):
    return pl.BlockSpec((1,) + dims, lambda i: (i + first,) + (0,) * len(dims))


def front(noisy, mods, bias, patch_low, pos, blocks):
    images = noisy.shape[0]
    each = functools.partial(rows_each, 0)
    return pl.pallas_call(
        front_kernel,
        name="front",
        grid=(images,),
        out_shape=(shape((images, SEQ, D)), shape((images, SEQ, 3 * D), BF),
                   shape((images, SEQ, D), BF), shape((images, SEQ, D))),
        in_specs=[each(PD, SEQ), VM, VM, VM, VM, VM],
        out_specs=[each(SEQ, D), each(SEQ, 3 * D), each(SEQ, D), each(SEQ, D)],
        compiler_params=room(24),
        cost_estimate=cost(2.2e9, 1.2e7),
    )(noisy, mods, bias, patch_low, pos, blocks)


def middle(total_img, at, time_weight, h1, velocity, dino, mods, bias, blocks, align_low, final_low):
    images = h1.shape[0]
    each = functools.partial(rows_each, 0)
    full = lambda lanes, kind=BF: pltpu.VMEM((images * SEQ, lanes), kind)
    return pl.pallas_call(
        functools.partial(middle_kernel, images, total_img),
        name="middle",
        grid=(images,),
        out_shape=(shape((images, SEQ, D)), shape((images, 8, D)),
                   shape((16, EARLY, D), BF), shape((16, EARLY, D), BF), shape((SUMS_MLP, D))),
        in_specs=[SM, SM, each(SEQ, D), each(PD, SEQ), each(SEQ, DINO), VM, VM, VM, VM, VM],
        out_specs=[each(SEQ, D), each(8, D), VM, VM, VM],
        scratch_shapes=[full(D), full(F), pltpu.VMEM((SEQ, F), F32), full(F), full(D), full(D),
                        full(DINO), full(D), full(128), pltpu.VMEM((D, F), BF)],
        compiler_params=room(40),
        cost_estimate=cost(9e9, 1.4e7),
    )(at, time_weight, h1, velocity, dino, mods, bias, blocks, align_low, final_low)


def attention_back(first, count, bh1, h0, qkv, att, noisy, mods, bias, blocks):
    each = functools.partial(rows_each, first)
    out = functools.partial(rows_each, 0)
    return pl.pallas_call(
        functools.partial(back_kernel, first),
        name="attention_back",
        grid=(count,),
        out_shape=(shape((count, SEQ, D), BF), shape((count, SEQ, 3 * D), BF), shape((count, SEQ, D), BF),
                   shape((count, 8, D)), shape((count, PD, D))),
        in_specs=[each(SEQ, D), each(SEQ, D), each(SEQ, 3 * D), each(SEQ, D), each(PD, SEQ), VM, VM, VM],
        out_specs=[out(SEQ, D), out(SEQ, 3 * D), out(SEQ, D), out(8, D), out(PD, D)],
        compiler_params=room(24),
        cost_estimate=cost(1.2e9 * count, 3e6 * count),
    )(bh1, h0, qkv, att, noisy, mods, bias, blocks)


def last_gradients(at, att, parts):
    flat = lambda v: v.reshape(-1, v.shape[-1])
    arrays = [flat(v) for part in parts for v in part]
    counts = tuple(part[0].shape[0] for part in parts)
    return pl.pallas_call(
        functools.partial(last_kernel, counts),
        name="last_gradients",
        out_shape=(shape((16, LATE, D), BF),) * 2,
        in_specs=[SM] + [VM] * (len(arrays) + 1),
        out_specs=[VM] * 2,
        compiler_params=room(20),
        cost_estimate=cost(1.2e9, 9e6),
    )(at, flat(att), *arrays)


def cond_back(images, class_ids, gm2, pre, th, cond, features, mod_w, fmod_w, tout_w, sums, gm3):
    return pl.pallas_call(
        functools.partial(cond_back_kernel, images),
        name="cond_back",
        out_shape=shape((4, PAY, D), BF),
        in_specs=[SM] + [VM] * (9 + len(gm3)),
        out_specs=VM,
        scratch_shapes=[pltpu.VMEM((4, PAY, D), F32)],
        compiler_params=room(16),
        cost_estimate=cost(1e8, 4e6),
    )(class_ids, gm2, pre, th, cond, features, mod_w, fmod_w, tout_w, sums, *gm3)


def position_table():
    quarter = D // 4
    frequencies = 1.0 / 10000.0 ** (jnp.arange(quarter, dtype=jnp.float32) / quarter)
    cell_ids = jnp.arange(SEQ, dtype=jnp.int32)
    row_arg = (cell_ids // GRID).astype(jnp.float32)[:, None] * frequencies[None, :]
    col_arg = (cell_ids % GRID).astype(jnp.float32)[:, None] * frequencies[None, :]
    return jnp.concatenate(
        [jnp.sin(col_arg), jnp.cos(col_arg), jnp.sin(row_arg), jnp.cos(row_arg)], axis=1
    )


def time_features(tstep_idx):
    half_freq = FREQ // 2
    frequencies = jnp.exp(-math.log(10000.0) * jnp.arange(half_freq, dtype=jnp.float32) / half_freq)
    angles = (tstep_idx.astype(jnp.float32) + 0.5)[:, None] * frequencies[None, :]
    return jnp.concatenate([jnp.cos(angles), jnp.sin(angles)], axis=1)


def body(
    noisy,
    velocity,
    tstep_idx,
    class_ids,
    time_weight,
    dino,
    owner_map,
    adam_flat,
    adam_m,
    adam_v,
    blocks_w,
    stat_left,
    stat_right,
    root_left,
    root_right,
):
    dp, group = lax.axis_size("dp"), lax.axis_size("shard")
    near = is_near(dp, group)
    images = noisy.shape[0]
    total_img = images * dp * group
    at = jnp.stack([jnp.asarray(v, jnp.int32) for v in coordinates()])
    flat_w = adam_flat.reshape(-1, 128)
    flat_m = adam_m.reshape(-1, 128)
    flat_v = adam_v.reshape(-1, 128)
    mine = flat_w.astype(BF)
    features = jnp.pad(time_features(tstep_idx), ((0, 4), (0, 0)))
    pos = position_table()
    noisy = jnp.transpose(noisy, (0, 2, 1))
    velocity = jnp.transpose(velocity, (0, 2, 1))
    rows = flat_w.shape[0]
    if near:
        cut = rows // 16 * 8 + 8 if rows // 8 % 2 else rows // 2
        block_parts = gather_blocks(blocks_w.astype(BF))
        pieces, (at, features, pos) = gather_flat(mine, cut, (at, features, pos))
        places = flat_places(cut)
        blocks = place_blocks(at, owner_map, block_parts)
    else:
        pieces = [lax.all_gather(mine, AXES, axis=0, tiled=True)[None]]
        places = [(0, lambda i, at: 0)]
        slot_low = lax.all_gather(blocks_w.astype(BF), "shard", axis=0, tiled=True)
        block_ids = jnp.arange(NBLK, dtype=jnp.int32)
        slot_of = jnp.sum(
            block_ids[:, None] * (owner_map[:, None] == block_ids[None, :]).astype(jnp.int32), axis=0
        )
        blocks = jnp.take(slot_low, slot_of, axis=0)
    (mods, pre, th, cond, mod_w, fmod_w, tout_w, align_low, bias, patch_low, final_low) = conditioning(
        at, class_ids, features, pieces, places, rows)
    h0, qkv, att, h1 = front(noisy, mods, bias, patch_low, pos, blocks)
    bh1, gm2, mine, other, sums = middle(
        total_img, at, time_weight, h1, velocity, dino, mods, bias, blocks, align_low, final_low)
    if near:
        early = reduce_units(at, mine, other)
    parts, gm3 = [], []
    for first, count in ((0, 1), (1, images - 1)):
        bb1, bp, act, gm, patch = attention_back(first, count, bh1, h0, qkv, att, noisy, mods, bias, blocks)
        parts.append((act, bp, bb1))
        gm3 += [gm, patch]
    late_mine, late_other = last_gradients(at, att, parts)
    pay = cond_back(images, class_ids, gm2, pre, th, cond, features, mod_w, fmod_w, tout_w, sums, gm3)
    if near:
        late = reduce_units(at, late_mine, late_other)
        grads, parts = exchange_gradients(at, owner_map, pay, late, early)
        loss, upd, new_m, new_v = adam_near(at, parts, flat_w, flat_m, flat_v)
        *grads, loss, upd, new_m, new_v = lax.optimization_barrier((*grads, loss, upd, new_m, new_v))
        updates = shampoo(at, grads, blocks_w, stat_left, stat_right, root_left, root_right)
    else:
        core = at[3]

        def by_part(mine, other):
            pair = jnp.where(core == 0, jnp.stack([mine, other]), jnp.stack([other, mine]))
            count = mine.shape[1] // UNIT
            return pair.reshape(2, 16, count, UNIT, D).transpose(0, 2, 1, 3, 4).reshape(2, count, D, D)

        early, late = by_part(mine, other), by_part(late_mine, late_other)
        late = jnp.stack([late[0, 0], late[0, 1], late[1, 0], late[1, 1]])
        grad_model = jnp.concatenate([late, early[:, :4].reshape(8, D, D)])
        pays = lax.all_gather(pay, AXES, axis=0, tiled=False)
        align_sum = lax.psum(early[:, 4].astype(F32), AXES)
        loss, upd, new_m, new_v = adam_wide(pays, align_sum, flat_w, flat_m, flat_v)
        slots = jnp.take(grad_model, owner_map, axis=0)
        owned = lax.psum_scatter(slots, "shard", scatter_dimension=0, tiled=True)
        grads = [lax.psum(owned.astype(F32), "dp").astype(BF)]
        updates = shampoo(at, grads, blocks_w, stat_left, stat_right, root_left, root_right)
    return (loss, *updates,
            upd.reshape(-1), new_m.reshape(-1), new_v.reshape(-1))


def is_near(dp, group):
    return (dp, group) == (8, 4)


def solution(mesh):
    return jax.shard_map(
        body,
        mesh=mesh,
        in_specs=(
            P(("dp", "shard"), None, None),
            P(("dp", "shard"), None, None),
            P(("dp", "shard")),
            P(("dp", "shard")),
            P(("dp", "shard")),
            P(("dp", "shard"), None, None),
            P(),
            P(("dp", "shard")),
            P(("dp", "shard")),
            P(("dp", "shard")),
            P("shard", None, None),
            P("shard", None, None),
            P("shard", None, None),
            P("shard", None, None),
            P("shard", None, None),
        ),
        out_specs=(
            P(),
            P("shard", None, None),
            P("shard", None, None),
            P("shard", None, None),
            P(("dp", "shard")),
            P(("dp", "shard")),
            P(("dp", "shard")),
        ),
        check_vma=False,
    )
```

```python
import functools
import math

import jax
import jax.numpy as jnp
from jax import lax
from jax.experimental import pallas as pl
from jax.experimental.pallas import tpu as pltpu
from jax.sharding import PartitionSpec as P


D = 384
HEADS = 6
HDIM = 64
F = 1536
PD = 16
GRID = 16
SEQ = 256
FREQ = 256
DINO = 768
STEP = 10
NBLK = 12
ADAM_PAD = 2129920

BETA_ONE = 0.9
BETA_TWO = 0.95
ADAM_EPS = 1e-08
ADAM_RATE = 0.01
DECAY_RATE = 0.1
STAT_BETA = 0.9
SHAMPOO_RATE = 0.02
RMS_EPS = 1e-08
REPA_WEIGHT = 0.5
NORM_EPS = 1e-06
QK_SCALE = HDIM ** (-0.5)

AXES = ("dp", "shard")
BF = jnp.bfloat16
F32 = jnp.float32
VM = pl.BlockSpec(memory_space=pltpu.VMEM)
SM = pl.BlockSpec(memory_space=pltpu.SMEM)

FLAT_ROWS = ADAM_PAD // 128
R_PATCH = 0
R_PATCH_B = 48
R_TIME_IN = 51
R_TIME_IN_B = 819
R_TIME_OUT = 822
R_TIME_OUT_B = 1974
R_CLASS = 1977
R_MOD = 4980
R_MOD_B = 11892
R_QUERY_B = 11910
R_VALUE_B = 11913
R_PROJ_B = 11916
R_HIDDEN_B = 11919
R_DOWN_B = 11931
R_FMOD = 11934
R_FMOD_B = 14238
R_FINAL = 14244
R_FINAL_B = 14292
ALIGN_ROWS = 2310

PAY = 64
PLANE_ROWS = FLAT_ROWS // 4


def shape(dims, kind=F32):
    return jax.ShapeDtypeStruct(dims, kind)


def cost(flops, moved):
    return pl.CostEstimate(flops=int(flops), bytes_accessed=int(moved), transcendentals=0)


def room(mib):
    return pltpu.CompilerParams(vmem_limit_bytes=mib * 1024 * 1024)


def mm(left, right):
    return jnp.dot(left, right, preferred_element_type=F32)


def mm_nt(left, right):
    return lax.dot_general(left, right, (((1,), (1,)), ((), ())), preferred_element_type=F32)


def mm_tn(left, right):
    return lax.dot_general(left, right, (((0,), (0,)), ((), ())), preferred_element_type=F32)


def silu(v):
    return v / (1.0 + jnp.exp(-v))


def silu_slope(v):
    s = 1.0 / (1.0 + jnp.exp(-v))
    return s * (1.0 + v * (1.0 - s))


def split3(v):
    one = v.astype(BF)
    rest = v - one.astype(F32)
    two = rest.astype(BF)
    return one, two, (rest - two.astype(F32)).astype(BF)


def split2(v):
    one = v.astype(BF)
    return one, (v - one.astype(F32)).astype(BF)


def stack3(v):
    one, two, three = split3(v)
    return jnp.concatenate([one.astype(F32), two.astype(F32), three.astype(F32)], axis=0).astype(BF)


def fold3(v):
    third = v.shape[0] // 3
    return v[:third] + v[third : 2 * third] + v[2 * third :]


def place_of(z, x, y, c):
    return ((z * 2 + x) * 2 + y) * 2 + c


def permutation(move):
    pairs = []
    for z in range(4):
        for x in range(2):
            for y in range(2):
                for c in range(2):
                    pairs.append((place_of(z, x, y, c), place_of(*move(z, x, y, c))))
    return pairs


TO_C = permutation(lambda z, x, y, c: (z, x, y, 1 - c))
TO_Y = permutation(lambda z, x, y, c: (z, x, 1 - y, c))
TO_X = permutation(lambda z, x, y, c: (z, 1 - x, y, c))
TO_Z = [permutation(lambda z, x, y, c, d=d: (z ^ d, x, y, c)) for d in range(4)]


def send(value, pairs):
    return lax.ppermute(value, AXES, pairs)


def coordinates():
    dp = lax.axis_index("dp")
    sh = lax.axis_index("shard")
    return dp // 2, dp % 2, sh // 2, sh % 2


TO_XY = permutation(lambda z, x, y, c: (z, 1 - x, 1 - y, c))
TO_CY = permutation(lambda z, x, y, c: (z, x, 1 - y, 1 - c))
TO_PAIR = permutation(lambda z, x, y, c: (z + 1 - 2 * (z % 2), x, y, c))


def gather_flat(piece, cut, ready):
    turned = [send(piece, TO_Z[d]) for d in (1, 2, 3)]
    own_x, own_y = send(piece, TO_X), send(piece, TO_Y)
    first = jnp.stack([t[:cut] for t in turned])
    second = jnp.stack([t[cut:] for t in turned])
    first_x = send(first, TO_X)
    second_y = send(second, TO_Y)
    second_y, ready = lax.optimization_barrier((second_y, ready))
    first = jnp.concatenate([own_x[None, :cut], first, first_x])
    second = jnp.concatenate([own_y[None, cut:], second, second_y])
    far = [send(first, TO_Y), send(second, TO_X)]
    own = [piece, own_x[cut:], own_y[:cut]]
    own_c = [send(p, TO_C) for p in own]
    rest_c = [send(p, TO_C) for p in (first, second, *far)]
    return [p[None] for p in own] + [first, second] + far + [p[None] for p in own_c] + rest_c, ready


def flip(value, bit):
    return 1 - value if bit else value


def flat_places(cut):
    def near(dc, dx, dy):
        return lambda i, at: place_of(at[0], flip(at[1], dx), flip(at[2], dy), flip(at[3], dc))

    def far(dc, kind):
        def entry(i, at):
            z, x, y, c = at
            dz, other = (0, 1) if i == 0 else ((i - 1) % 3 + 1, (i - 1) // 3)
            dx, dy = {0: (other, 0), 1: (0, other), 2: (other, 1), 3: (1, other)}[kind]
            return place_of(z ^ dz, flip(x, dx), flip(y, dy), flip(c, dc))

        return entry

    places = []
    for dc in (0, 1):
        places += [(0, near(dc, 0, 0)), (cut, near(dc, 1, 0)), (0, near(dc, 0, 1))]
        places += [((0, cut, 0, cut)[kind], far(dc, kind)) for kind in range(4)]
    return places


def read_coordinates(ref):
    return ref[0], ref[1], ref[2], ref[3]


def cond_kernel(places, rows, at_ref, cls_ref, feat_ref, *refs):
    count = len(places)
    pieces = refs[:count]
    (mods_ref, pre_ref, th_ref, cond_ref, modw_ref, fmodw_ref, tout_ref, align_ref, bias_ref,
     patch_ref, final_ref, flat, rolled) = refs[count:]
    at = read_coordinates(at_ref)
    for ref, (offset, entry) in zip(pieces, places):
        for i in range(ref.shape[0]):
            start = pl.multiple_of(entry(i, at) * rows + offset, 8)
            flat[pl.ds(start, ref.shape[1]), :] = ref[i].astype(F32)

    def row(first, count):
        return jnp.concatenate([flat[first + l : first + l + 1, :] for l in range(count)], axis=1)

    def columns(first, depth, count, which):
        return flat[pl.ds(first + which, depth, stride=count), :].astype(BF)

    def wide(v, first, depth, count, keep=None):
        stacked = stack3(v)
        out = []
        for j in range(count):
            w = columns(first, depth, count, j)
            if keep is not None:
                keep[:, 128 * j : 128 * j + 128] = w
            out.append(fold3(mm(stacked, w)))
        return jnp.concatenate(out, axis=1)

    pre = wide(feat_ref[...], R_TIME_IN, FREQ, 3) + row(R_TIME_IN_B, 3)
    th = silu(pre)
    picked = []
    for m in range(4):
        r = R_CLASS + 3 * cls_ref[m]
        picked.append(jnp.concatenate([flat[pl.ds(r + l, 1), :] for l in range(3)], axis=1))
    picked = jnp.concatenate(picked + [jnp.zeros((4, D), F32)], axis=0)
    cond = wide(th, R_TIME_OUT, D, 3, tout_ref) + row(R_TIME_OUT_B, 3) + picked
    act = silu(cond)
    pre_ref[...] = pre
    th_ref[...] = th
    cond_ref[...] = cond
    mods_ref[:, : 6 * D] = wide(act, R_MOD, D, 18, modw_ref) + row(R_MOD_B, 18)
    mods_ref[:, 6 * D :] = wide(act, R_FMOD, D, 6, fmodw_ref) + row(R_FMOD_B, 6)

    spot = lax.broadcasted_iota(jnp.int32, (ALIGN_ROWS, 128), 1)
    here = pltpu.roll(flat[R_FINAL_B : R_FINAL_B + ALIGN_ROWS, :], 112, 1)
    after = pltpu.roll(flat[R_FINAL_B + 1 : R_FINAL_B + 1 + ALIGN_ROWS, :], 112, 1)
    rolled[...] = jnp.where(spot < 112, here, after)
    for j in range(6):
        align_ref[:, 128 * j : 128 * j + 128] = rolled[pl.ds(j, D, stride=6), :].astype(BF)

    bias_ref[...] = jnp.zeros_like(bias_ref)
    for at_row, first in ((0, R_PATCH_B), (1, R_QUERY_B), (2, R_VALUE_B), (3, R_PROJ_B),
                          (4, R_HIDDEN_B), (5, R_HIDDEN_B + 3), (6, R_HIDDEN_B + 6),
                          (7, R_HIDDEN_B + 9), (8, R_DOWN_B)):
        bias_ref[at_row : at_row + 1, :] = row(first, 3)
    for half in range(2):
        bias_ref[9 + half : 10 + half, :] = jnp.concatenate(
            [rolled[2304 + 3 * half + l : 2305 + 3 * half + l, :] for l in range(3)], axis=1)
    lane = lax.broadcasted_iota(jnp.int32, (1, 128), 1)
    bias_ref[11:12, :128] = jnp.where(lane < PD, flat[R_FINAL_B : R_FINAL_B + 1, :], 0.0)
    patch = [flat[pl.ds(R_PATCH + l, PD, stride=3), :] for l in range(3)]
    patch_ref[...] = jnp.concatenate(patch, axis=1).astype(BF)
    spread = (lax.broadcasted_iota(jnp.int32, (D, 48), 0) // 8
              == lax.broadcasted_iota(jnp.int32, (D, 48), 1)).astype(F32).astype(BF)
    wide_rows = mm(spread, flat[R_FINAL : R_FINAL + 48, :].astype(BF))
    keep = (lax.broadcasted_iota(jnp.int32, (D, 128), 1) // PD
            == lax.broadcasted_iota(jnp.int32, (D, 128), 0) % 8)
    fold = (lax.broadcasted_iota(jnp.int32, (128, 128), 0) % PD
            == lax.broadcasted_iota(jnp.int32, (128, 128), 1)).astype(F32).astype(BF)
    final_ref[...] = mm(jnp.where(keep, wide_rows, 0.0).astype(BF), fold).astype(BF)


def conditioning(at, classes, features, pieces, places, rows):
    kernel = functools.partial(cond_kernel, places, rows)
    return pl.pallas_call(
        kernel,
        name="conditioning",
        out_shape=(shape((8, 8 * D)), shape((8, D)), shape((8, D)), shape((8, D)),
                   shape((D, 6 * D), BF), shape((D, 2 * D), BF), shape((D, D), BF),
                   shape((D, DINO), BF), shape((16, D)), shape((PD, D), BF), shape((D, 128), BF)),
        in_specs=[SM, SM, VM] + [VM] * len(pieces),
        out_specs=[VM] * 11,
        scratch_shapes=[pltpu.VMEM((FLAT_ROWS + 8, 128), F32), pltpu.VMEM((ALIGN_ROWS, 128), F32)],
        compiler_params=room(28),
        cost_estimate=pl.CostEstimate(flops=10**9, bytes_accessed=10**7, transcendentals=0),
    )(at, classes, features, *pieces)


def gather_blocks(mine):
    z, _, _, _ = coordinates()
    half = lax.dynamic_slice_in_dim(mine, 192 * (z % 2), 192, 1)
    near = send(half, TO_Y)
    far = send(near, TO_PAIR)
    return [mine, near, far, send(mine, TO_C), send(near, TO_C), send(far, TO_C)]


def place_blocks_kernel(at_ref, own_ref, mine_ref, near_ref, far_ref, mine_c_ref, near_c_ref, far_c_ref, out_ref):
    z, _, y, c = read_coordinates(at_ref)
    for core, mine, near, far in ((c, mine_ref, near_ref, far_ref), (1 - c, mine_c_ref, near_c_ref, far_c_ref)):
        for t in range(3):
            out_ref[own_ref[3 * (2 * y + core) + t]] = mine[t]
            there = own_ref[3 * (2 * (1 - y) + core) + t]
            odd = pl.multiple_of(192 * lax.rem(z, 2), 16)
            even = pl.multiple_of(192 * (1 - lax.rem(z, 2)), 16)
            out_ref[there, pl.ds(odd, 192), :] = near[t]
            out_ref[there, pl.ds(even, 192), :] = far[t]


def place_blocks(at, owner_map, parts):
    return pl.pallas_call(
        place_blocks_kernel,
        name="place_blocks",
        out_shape=shape((NBLK, D, D), BF),
        in_specs=[SM, SM] + [VM] * 6,
        out_specs=VM,
        compiler_params=room(12),
        cost_estimate=cost(1e6, 7e6),
    )(at, owner_map, *parts)


UNIT = 24


def unit_of(z, x, y):
    return (2 * x + y) * 4 + z


def quarter_kernel(at_ref, mine_ref, got_ref, *out_refs):
    _, x, y, _ = read_coordinates(at_ref)
    for out_ref, (dx, dy) in zip(out_refs, ((0, 0), (1, 0), (0, 1), (1, 1))):
        rows = pl.ds(4 * (2 * flip(x, dx) + flip(y, dy)), 4)
        out_ref[...] = (mine_ref[rows].astype(F32) + got_ref[rows].astype(F32)).astype(BF)


def turn_kernel(at_ref, *refs):
    z, _, _, _ = read_coordinates(at_ref)
    for d, out_ref in enumerate(refs[4:]):
        unit = z ^ d
        out_ref[...] = sum(ref[unit].astype(F32) for ref in refs[:4]).astype(BF)


def reduce_units(at, mine, other):
    rows = mine.shape[1]
    got = send(other, TO_C)
    own, *away = pl.pallas_call(
        quarter_kernel,
        name="quarter",
        out_shape=(shape((4, rows, D), BF),) * 4,
        in_specs=[SM, VM, VM],
        out_specs=[VM] * 4,
        compiler_params=room(12),
        cost_estimate=cost(1e6, 4e6),
    )(at, mine, got)
    got = [send(v, pairs) for v, pairs in zip(away, (TO_X, TO_Y, TO_XY))]
    own, *away = pl.pallas_call(
        turn_kernel,
        name="turn",
        out_shape=(shape((rows, D), BF),) * 4,
        in_specs=[SM] + [VM] * 4,
        out_specs=[VM] * 4,
        compiler_params=room(8),
        cost_estimate=cost(1e6, 2e6),
    )(at, own, *got)
    return [own] + [send(v, TO_Z[d + 1]) for d, v in enumerate(away)]


def rows_kernel(at_ref, pay_ref, *refs):
    early, out_refs, total_ref = refs[:4], refs[4:8], refs[8]
    total = sum(ref[...].astype(F32) for ref in early).astype(BF)
    total_ref[...] = total
    for d, out_ref in enumerate(out_refs):
        plane = at_ref[0] ^ d
        out_ref[...] = pay_ref[plane]

        @pl.when(plane == 3)
        def _():
            out_ref[16:40, :] = total[4 * UNIT :]


def owner_kernel(at_ref, own_ref, *refs):
    late, early = refs[:4], refs[4]
    out_refs, total = refs[5:9], refs[9]
    _, _, y, c = read_coordinates(at_ref)
    one = sum(ref[...].astype(F32) for ref in late)
    two = early[...].astype(F32)
    for k in range(6):
        total[k] = (one[UNIT * k : UNIT * k + UNIT] if k < 2 else two[UNIT * (k - 2) : UNIT * (k - 1)])
    for out_ref, (dy, dc) in zip(out_refs, ((0, 0), (0, 1), (1, 0), (1, 1))):
        first = 3 * (2 * flip(y, dy) + flip(c, dc))
        for t in range(3):
            block = own_ref[first + t]
            low = block < 4
            part = jnp.where(low, lax.div(block, 2), lax.div(block - 4, 4))
            entry = jnp.where(low, lax.rem(block, 2), 2 + lax.rem(jnp.maximum(block - 4, 0), 4))
            out_ref[t] = jnp.where(part == c, total[entry], 0.0).astype(BF)


def join_kernel(own_ref, pair_ref, near_ref, far_ref, out_ref):
    out_ref[0] = own_ref[...] + pair_ref[...]
    out_ref[1] = near_ref[...] + far_ref[...]


def exchange_gradients(at, owner_map, pay, late, early):
    piece = (3, UNIT, D)
    keep, *away, early = pl.pallas_call(
        rows_kernel,
        name="pay_rows",
        out_shape=(shape((PAY, D), BF),) * 4 + (shape((EARLY, D), BF),),
        in_specs=[SM] + [VM] * 5,
        out_specs=[VM] * 5,
        compiler_params=room(8),
        cost_estimate=cost(1e6, 1e6),
    )(at, pay, *early)
    turned = [send(v, TO_Z[d + 1]) for d, v in enumerate(away)]
    own, to_c, to_y, to_cy = pl.pallas_call(
        owner_kernel,
        name="owner_rows",
        out_shape=(shape(piece, BF),) * 4,
        in_specs=[SM, SM] + [VM] * 5,
        out_specs=[VM] * 4,
        scratch_shapes=[pltpu.VMEM((6, UNIT, D), F32)],
        compiler_params=room(8),
        cost_estimate=cost(1e6, 1e6),
    )(at, owner_map, *late, early)
    far, near, pair = send(to_cy, TO_CY), send(to_y, TO_Y), send(to_c, TO_C)
    turned, pair = lax.optimization_barrier((turned, pair))
    rows = jnp.stack([keep] + turned)
    plane = [rows, send(rows, TO_X), send(rows, TO_Y)]
    both = pl.pallas_call(
        join_kernel,
        name="join",
        out_shape=shape((2,) + piece, BF),
        in_specs=[VM] * 4,
        out_specs=VM,
        compiler_params=room(8),
        cost_estimate=cost(1e6, 1e6),
    )(own, pair, near, far)
    column = [both] + [send(both, TO_Z[d]) for d in (1, 2, 3)]
    crossed = [send(both, TO_X)]
    plane[1], column[1] = lax.optimization_barrier((plane[1], column[1]))
    plane.append(send(plane[1], TO_Y))
    crossed.append(send(column[1], TO_X))
    crossed[1], column[2], column[3] = lax.optimization_barrier((crossed[1], column[2], column[3]))
    slots = column + crossed + [send(v, TO_X) for v in column[2:]]
    return slots, plane + [send(p, TO_C) for p in plane]


def plane_gradient(plane, pay_ref, flat, rolled, align):
    rows = 8 * pay_ref.shape[0]

    def tile(j):
        return pay_ref[:, 8 * j : 8 * j + 8, :].astype(F32).reshape(rows, D)

    def sums(first, last):
        return jnp.sum(pay_ref[:, first:last, :].astype(F32), axis=0)

    upper = lax.broadcasted_iota(jnp.int32, (rows, 1), 0) % 8 < 4

    def first(v):
        return jnp.where(upper, v, 0.0)

    def second(v):
        return jnp.where(upper, 0.0, v)

    def put_row(v, row):
        for l in range(v.shape[1] // 128):
            flat[row + l : row + l + 1, :] = v[:, 128 * l : 128 * l + 128]

    def put_matrix(v, row, count, which):
        for l in range(v.shape[1] // 128):
            flat[pl.ds(row + which + l, v.shape[0], stride=count), :] = v[:, 128 * l : 128 * l + 128]

    def classes(ids, g_low):
        numbers = (ids[:, 0:1] * 256.0 + ids[:, 1:2]).astype(jnp.int32)
        for part in range(3):
            height = 336 if part < 2 else 329
            marks = lax.broadcasted_iota(jnp.int32, (rows, 336), 1) + 336 * part
            hits = first(jnp.where(marks == numbers, 1.0, 0.0)).astype(BF)
            put_matrix(mm_tn(hits, g_low)[:height], R_CLASS + 3 * 336 * part, 3, 0)

    def modulations(low, bias):
        act = tile(0)[:, low : low + 256]
        halves = (first(act).astype(BF), second(act).astype(BF))
        for t in range(3):
            g = tile(1 + t)
            for half in range(2):
                put_matrix(mm_tn(halves[half], g.astype(BF)), R_MOD + 18 * low, 18, 3 * (t + 3 * half))
                if bias:
                    put_row(column_sum((first, second)[half](g)), R_MOD_B + 3 * (t + 3 * half))

    def finals(which, bias):
        act, g = tile(0), tile(which)
        for half, part in enumerate((first, second)):
            put_matrix(mm_tn(part(act).astype(BF), g.astype(BF)), R_FMOD, 6, 3 * half)
            if bias:
                put_row(column_sum(part(g)), R_FMOD_B + 3 * half)

    if plane == 0:
        left, g = tile(0).astype(BF), tile(1)
        g_cond, g_pre = first(g), second(g)
        put_matrix(mm_tn(left[:, :FREQ], g_pre.astype(BF)), R_TIME_IN, 3, 0)
        put_row(column_sum(g_pre), R_TIME_IN_B)
        put_matrix(mm_tn(left, g_cond.astype(BF)), R_TIME_OUT, 3, 0)
        put_row(column_sum(g_cond), R_TIME_OUT_B)
        classes(tile(2)[:, :128], g.astype(BF))
        total = sums(40, 64)
        for l in range(3):
            flat[pl.ds(R_PATCH + l, PD, stride=3), :] = total[0:16, 128 * l : 128 * l + 128]
        put_row(total[16:17], R_PATCH_B)
    if plane == 1:
        classes(tile(5)[:, :128], tile(4).astype(BF))
        modulations(0, False)
    if plane == 2:
        modulations(128, True)
        finals(4, False)
        total = sums(40, 48)
        for k, row in enumerate((R_QUERY_B, R_VALUE_B, R_PROJ_B, R_HIDDEN_B, R_HIDDEN_B + 3, R_HIDDEN_B + 6,
                                 R_HIDDEN_B + 9, R_DOWN_B)):
            put_row(total[k : k + 1], row)
    if plane == 3:
        finals(1, True)
        total = sums(40, 64)
        for l in range(3):
            flat[R_FINAL + 16 * l : R_FINAL + 16 * l + 16, :] = total[0:16, 128 * l : 128 * l + 128]
        rolled[0:8, :] = jnp.zeros((8, 128), F32)
        rolled[8 + ALIGN_ROWS :, :] = jnp.zeros_like(rolled[8 + ALIGN_ROWS :, :])
        rolled[7:8, :] = pltpu.roll(total[16:17, 0:128], 112, 1)
        for half in range(2):
            for l in range(3):
                lanes = slice(128 * l, 128 * l + 128)
                rolled[pl.ds(8 + 3 * half + l, D, stride=6), :] = align[half, :, lanes].astype(F32)
                r = 8 + 2304 + 3 * half + l
                rolled[r : r + 1, :] = total[17 + half : 18 + half, lanes]
        count = FLAT_ROWS - R_FINAL_B
        spot = lax.broadcasted_iota(jnp.int32, (count, 128), 1)
        here = pltpu.roll(rolled[8 : 8 + count, :], 16, 1)
        before = pltpu.roll(rolled[7 : 7 + count, :], 16, 1)
        flat[R_FINAL_B:FLAT_ROWS, :] = jnp.where(spot < 16, before, here)


def loss_of(pay_ref):
    rows = 8 * pay_ref.shape[0]
    parts = pay_ref[:, PAY - 8 : PAY, 0:128].astype(F32).reshape(rows, 128)
    parts = column_sum(jnp.where(lax.broadcasted_iota(jnp.int32, (rows, 128), 0) % 8 == 7, parts, 0.0))
    return parts[:, 0:1] + parts[:, 1:2] + parts[:, 2:3]


def adam_near_kernel(at_ref, *refs):
    parts = refs[:8]
    w_ref, m_ref, v_ref, loss_ref, upd_ref, new_m_ref, new_v_ref, pay, align, flat, rolled = refs[8:]
    at = read_coordinates(at_ref)
    z, x, y, c = at
    for k, ref in enumerate(parts):
        dc, dy, dx = k // 4, k // 2 % 2, k % 2
        for dz in range(4):
            there = (z ^ dz, flip(x, dx), flip(y, dy), flip(c, dc))
            value = ref[dz].astype(F32)
            pay[place_of(*there)] = value
            start = pl.multiple_of(unit_of(*there[:3]) * UNIT, 8)
            align[there[3], pl.ds(start, UNIT), :] = value[16:40]
    loss_ref[...] = loss_of(pay)
    for plane in range(4):
        @pl.when(z == plane)
        def _():
            plane_gradient(plane, pay, flat, rolled, align)
    size = w_ref.shape[0]
    start = pl.multiple_of(place_of(z, x, y, c) * size, 8)
    adam_step(flat[pl.ds(start, size), :], w_ref, m_ref, v_ref, upd_ref, new_m_ref, new_v_ref)


def adam_plane_kernel(plane, pay_ref, align_ref, loss_ref, flat_ref, rolled):
    loss_ref[...] = loss_of(pay_ref)
    plane_gradient(plane, pay_ref, flat_ref, rolled, align_ref)


def adam_step(grad, w_ref, m_ref, v_ref, upd_ref, new_m_ref, new_v_ref):
    new_m = BETA_ONE * m_ref[...] + (1.0 - BETA_ONE) * grad
    new_v = BETA_TWO * v_ref[...] + (1.0 - BETA_TWO) * grad * grad
    new_m_ref[...] = new_m
    new_v_ref[...] = new_v
    right_m = new_m / (1.0 - BETA_ONE**STEP)
    right_v = new_v / (1.0 - BETA_TWO**STEP)
    upd_ref[...] = -ADAM_RATE * (right_m / (jnp.sqrt(right_v) + ADAM_EPS) + DECAY_RATE * w_ref[...])


ROLL_ROWS = 8 + FLAT_ROWS - R_FINAL_B + 8


ROLL_ROWS = 8 + FLAT_ROWS - R_FINAL_B + 8


def adam_near(at, parts, flat_w, m, v):
    size = flat_w.shape
    loss, upd, new_m, new_v = pl.pallas_call(
        adam_near_kernel,
        name="adam",
        out_shape=(shape((1, 1)), shape(size), shape(size), shape(size)),
        in_specs=[SM] + [VM] * 11,
        out_specs=[VM] * 4,
        scratch_shapes=[pltpu.VMEM((32, PAY, D), F32), pltpu.VMEM((2, D, D), F32),
                        pltpu.VMEM((FLAT_ROWS, 128), F32), pltpu.VMEM((ROLL_ROWS, 128), F32)],
        compiler_params=room(24),
        cost_estimate=pl.CostEstimate(flops=10**9, bytes_accessed=10**7, transcendentals=0),
    )(at, *parts, flat_w, m, v)
    return loss[0, 0], upd, new_m, new_v


def adam_wide(pays, align, flat_w, m, v):
    grads = []
    for plane in range(4):
        loss, flat = pl.pallas_call(
            functools.partial(adam_plane_kernel, plane),
            name="adam_gradient",
            out_shape=(shape((1, 1)), shape((FLAT_ROWS, 128))),
            in_specs=[VM] * 2,
            out_specs=[VM] * 2,
            scratch_shapes=[pltpu.VMEM((ROLL_ROWS, 128), F32)],
        )(pays[:, plane], align)
        grads.append(flat[PLANE_ROWS * plane : PLANE_ROWS * (plane + 1)])
    size = flat_w.shape[0]
    place = lax.axis_index("dp") * lax.axis_size("shard") + lax.axis_index("shard")
    grad = lax.dynamic_slice_in_dim(jnp.concatenate(grads), place * size, size, 0)
    upd, new_m, new_v = pl.pallas_call(
        lambda g, *refs: adam_step(g[...], *refs),
        name="adam",
        out_shape=(shape(flat_w.shape),) * 3,
        in_specs=[VM] * 4,
        out_specs=[VM] * 3,
    )(grad, flat_w, m, v)
    return loss[0, 0], upd, new_m, new_v


def shampoo_kernel(near, at_ref, *refs):
    t = pl.program_id(0)
    if near:
        parts = refs[:8]
        w_ref, sl_ref, sr_ref, rl_ref, rr_ref, upd_ref, nl_ref, nr_ref, grad = refs[8:]
        z, x, y, _ = read_coordinates(at_ref)
        for dx in range(2):
            for dz in range(4):
                for dy in range(2):
                    unit = unit_of(z ^ dz, flip(x, dx), flip(y, dy))
                    rows = pl.ds(pl.multiple_of(unit * UNIT, 8), UNIT)
                    grad[rows, :] = parts[4 * dx + dz][dy, t].astype(F32)
        g = grad[...].astype(BF)
    else:
        grad_ref, w_ref, sl_ref, sr_ref, rl_ref, rr_ref, upd_ref, nl_ref, nr_ref = refs
        g = grad_ref[t]
    nl_ref[0] = STAT_BETA * sl_ref[t] + (1.0 - STAT_BETA) * mm_nt(g, g)
    nr_ref[0] = STAT_BETA * sr_ref[t] + (1.0 - STAT_BETA) * mm_tn(g, g)
    left = mm(jnp.concatenate(split2(rl_ref[t]), axis=1), jnp.concatenate([g, g], axis=0))
    left = left.astype(BF)
    p = mm(jnp.concatenate([left, left], axis=1), jnp.concatenate(split2(rr_ref[t]), axis=0))
    mean = jnp.sum(jnp.sum(p * p, axis=1, keepdims=True), axis=0, keepdims=True) * (1.0 / (D * D))
    root = jnp.sqrt(mean)
    upd_ref[0] = -SHAMPOO_RATE * (p / (root + RMS_EPS) + DECAY_RATE * w_ref[t])


def shampoo(at, grads, blocks_w, stat_left, stat_right, root_left, root_right):
    near = len(grads) == 8
    slots = blocks_w.shape[0]
    one = pl.BlockSpec((1, D, D), lambda t: (t, 0, 0))
    return pl.pallas_call(
        functools.partial(shampoo_kernel, near),
        name="shampoo",
        grid=(slots,),
        out_shape=(shape((slots, D, D)),) * 3,
        in_specs=[SM] + [VM] * (len(grads) + 5),
        out_specs=[one] * 3,
        scratch_shapes=[pltpu.VMEM((D, D), F32)] if near else [],
        compiler_params=room(26),
        cost_estimate=pl.CostEstimate(flops=3 * 10**9, bytes_accessed=15 * 10**6, transcendentals=0),
    )(at, *grads, blocks_w, stat_left, stat_right, root_left, root_right)


GELU_C = math.sqrt(2.0 / math.pi)
GELU_D = 0.044715
EARLY = 5 * 24
LATE = 2 * 24
SUMS_MLP = 24


def norm_stats(v):
    centered = v - jnp.sum(v, axis=-1, keepdims=True) * (1.0 / D)
    inv = lax.rsqrt(jnp.sum(centered * centered, axis=-1, keepdims=True) * (1.0 / D) + NORM_EPS)
    return centered * inv, inv


def norm_back(g, normed, inv):
    mean_g = jnp.sum(g, axis=-1, keepdims=True) * (1.0 / D)
    mean_gn = jnp.sum(g * normed, axis=-1, keepdims=True) * (1.0 / D)
    return inv * (g - mean_g - normed * mean_gn)


def column_sum(v):
    return jnp.sum(v, axis=0, keepdims=True)


def head(v, h):
    return v[:, HDIM * h : HDIM * h + HDIM]


def put_pair(core, mine_ref, other_ref, j, zero, one):
    zero, one = zero.astype(BF), one.astype(BF)
    mine, other = jnp.where(core == 0, zero, one), jnp.where(core == 0, one, zero)
    for u in range(16):
        rows = slice(24 * u, 24 * u + 24)
        mine_ref[u, 24 * j : 24 * j + 24, :] = mine[rows]
        other_ref[u, 24 * j : 24 * j + 24, :] = other[rows]


def front_kernel(noisy_ref, mods_ref, bias_ref, patch_ref, pos_ref, w_ref,
                 h0_ref, qkv_ref, att_ref, h1_ref):
    i = pl.program_id(0)

    def mod(t):
        return mods_ref[pl.ds(i, 1), D * t : D * t + D]

    h0 = mm_tn(noisy_ref[0].astype(BF), patch_ref[...]) + bias_ref[0:1, :] + pos_ref[...]
    h0_ref[0] = h0
    normed, _ = norm_stats(h0)
    act = (normed * (1.0 + mod(1)) + mod(0)).astype(BF)
    q = (mm(act, w_ref[0]) + bias_ref[1:2, :]).astype(BF)
    k = mm(act, w_ref[1]).astype(BF)
    v = (mm(act, w_ref[2]) + bias_ref[2:3, :]).astype(BF)
    qkv_ref[0, :, 0:D] = q
    qkv_ref[0, :, D : 2 * D] = k
    qkv_ref[0, :, 2 * D :] = v
    scores, probs, outs = [], [], []
    for h in range(HEADS + 2):
        if h < HEADS:
            scores.append(mm_nt(head(q, h), head(k, h)))
        if 1 <= h <= HEADS:
            s = scores[h - 1] * QK_SCALE
            e = jnp.exp(s - jnp.max(s, axis=-1, keepdims=True))
            probs.append((e * (1.0 / jnp.sum(e, axis=-1, keepdims=True))).astype(BF))
        if h >= 2:
            outs.append(mm(probs[h - 2], head(v, h - 2)))
    att = jnp.concatenate(outs, axis=1).astype(BF)
    att_ref[0] = att
    h1_ref[0] = h0 + mod(2) * (mm(att, w_ref[3]) + bias_ref[3:4, :])


def middle_kernel(images, total_img, at_ref, tw_ref, h1_ref, vel_ref, dino_ref, mods_ref, bias_ref, w_ref, aw_ref, fw_ref,
                  bh1_ref, gm_ref, mine_ref, other_ref, sums_ref,
                  act2_s, gelu_s, slope_s, bi_s, bb2_s, h1_s, ba_s, act3_s, bo_s, up_s):
    i = pl.program_id(0)
    rows = pl.ds(pl.multiple_of(i * SEQ, SEQ), SEQ)

    def mod(t):
        return mods_ref[pl.ds(i, 1), D * t : D * t + D]

    @pl.when(i == 0)
    def _():
        sums_ref[...] = jnp.zeros_like(sums_ref)
        for j in range(4):
            up_s[:, D * j : D * j + D] = w_ref[4 + j]

    h1 = h1_ref[0]
    h1_low = h1.astype(BF)
    h1_s[rows, :] = h1_low
    aligned = mm(h1_low, aw_ref[...])
    n2, inv2 = norm_stats(h1)
    act2 = (n2 * (1.0 + mod(4)) + mod(3)).astype(BF)
    act2_s[rows, :] = act2

    def lanes_of(j):
        return slice(2 * D * j, 2 * D * j + 2 * D)

    def pair_row(j):
        return jnp.concatenate([bias_ref[j : j + 1, :], bias_ref[j + 1 : j + 2, :]], axis=1)

    def expand(j):
        return mm(act2, up_s[:, lanes_of(j)])

    def activate(j, x):
        x = x + pair_row(4 + 2 * j)
        xx = x * x
        t = jnp.tanh(x * (GELU_C + (GELU_C * GELU_D) * xx))
        half = 0.5 + 0.5 * t
        slope_s[:, lanes_of(j)] = half + (0.5 * x) * (1.0 - t * t) * (GELU_C + (3.0 * GELU_C * GELU_D) * xx)
        g = (x * half).astype(BF)
        gelu_s[rows, lanes_of(j)] = g
        return g

    def contract(j, g):
        return mm(g, w_ref[8 + 2 * j : 10 + 2 * j].reshape(2 * D, D))

    x_one = expand(0)
    aligned = aligned + pair_row(9)
    dino = dino_ref[0].astype(F32)
    dot = jnp.sum(aligned * dino, axis=-1, keepdims=True)
    ra = lax.rsqrt(jnp.sum(aligned * aligned, axis=-1, keepdims=True) + NORM_EPS)
    rd = lax.rsqrt(jnp.sum(dino * dino, axis=-1, keepdims=True) + NORM_EPS)
    x_two = expand(1)
    g_one = activate(0, x_one)
    scale = REPA_WEIGHT / (total_img * SEQ)
    both = ra * rd
    cosine = dot * both
    ba = dino * (both * -scale) + aligned * (cosine * (ra * ra) * scale)
    ba_sum = column_sum(ba)
    ba = ba.astype(BF)
    ba_s[rows, :] = ba
    branch = contract(0, g_one)
    g_two = activate(1, x_two)
    through = mm_nt(ba, aw_ref[...])
    branch = branch + contract(1, g_two) + bias_ref[8:9, :]
    h2 = h1 + mod(5) * branch
    n3, inv3 = norm_stats(h2)
    act3 = (n3 * (1.0 + mod(7)) + mod(6)).astype(BF)
    act3_s[rows, :] = act3
    out = mm(act3, fw_ref[...]) + bias_ref[11:12, 0:128]
    err = out[:, :PD] - vel_ref[0].T
    weight = tw_ref[i]
    loss = jnp.sum(column_sum(err * err), axis=1, keepdims=True) * (weight / (total_img * SEQ * PD))
    loss = loss - column_sum(cosine) * scale
    bo = jnp.concatenate([err * (2.0 * weight / (total_img * SEQ * PD)), jnp.zeros((SEQ, 128 - PD), F32)],
                         axis=1).astype(BF)
    bo_s[rows, :] = bo

    b3 = mm_nt(bo, fw_ref[...])
    bh2 = norm_back(b3 * (1.0 + mod(7)), n3, inv3)
    bb2 = (bh2 * mod(5)).astype(BF)
    bb2_s[rows, :] = bb2
    b2 = jnp.zeros((SEQ, D), F32)
    for j in range(2):
        lanes = slice(2 * D * j, 2 * D * j + 2 * D)
        bi = mm_nt(bb2, w_ref[8 + 2 * j : 10 + 2 * j].reshape(2 * D, D)) * slope_s[:, lanes]
        bi_sum = column_sum(bi)
        bi = bi.astype(BF)
        bi_s[rows, lanes] = bi
        sums_ref[16 + 2 * j : 17 + 2 * j, :] += bi_sum[:, :D]
        sums_ref[17 + 2 * j : 18 + 2 * j, :] += bi_sum[:, D:]
        b2 = b2 + mm_nt(bi, up_s[:, lanes])
    sums_ref[20:21, :] += column_sum(bb2.astype(F32))
    sums_ref[21:22, :] += ba_sum[:, :D]
    sums_ref[22:23, :] += ba_sum[:, D:]
    sums_ref[23:24, 0:128] += column_sum(bo.astype(F32))
    bh1_ref[0] = bh2 + norm_back(b2 * (1.0 + mod(4)), n2, inv2) + through
    gm_ref[0, 0:1, :] = column_sum(b2)
    gm_ref[0, 1:2, :] = column_sum(b2 * n2)
    gm_ref[0, 2:3, :] = column_sum(bh2 * branch)
    gm_ref[0, 3:4, :] = column_sum(b3)
    gm_ref[0, 4:5, :] = column_sum(b3 * n3)
    gm_ref[0, 5:6, :] = jnp.broadcast_to(loss, (1, D))
    gm_ref[0, 6:8, :] = jnp.zeros((2, D), F32)

    @pl.when(i == images - 1)
    def _():
        put = functools.partial(put_pair, at_ref[3], mine_ref, other_ref)
        for j in range(2):
            lanes = slice(2 * D * j, 2 * D * j + 2 * D)
            up = mm_tn(act2_s[...], bi_s[:, lanes]).astype(BF)
            down = mm_tn(bb2_s[...], gelu_s[:, lanes]).astype(BF)
            put(2 * j, up[:, :D], down[:, :D].T)
            put(2 * j + 1, up[:, D:], down[:, D:].T)
        align = mm_tn(h1_s[...], ba_s[...])
        put(4, align[:, :D], align[:, D:])
        g = mm_tn(act3_s[...], bo_s[...]).astype(BF)
        spread = (lax.broadcasted_iota(jnp.int32, (128, 128), 1) % PD
                  == lax.broadcasted_iota(jnp.int32, (128, 128), 0)).astype(F32).astype(BF)
        keep = (lax.broadcasted_iota(jnp.int32, (D, 128), 1) // PD
                == lax.broadcasted_iota(jnp.int32, (D, 128), 0) % 8)
        fold = (lax.broadcasted_iota(jnp.int32, (48, D), 1) // 8
                == lax.broadcasted_iota(jnp.int32, (48, D), 0)).astype(F32).astype(BF)
        flat = mm(fold, jnp.where(keep, mm(g, spread), 0.0).astype(BF))
        for l in range(3):
            sums_ref[0:16, 128 * l : 128 * l + 128] = flat[16 * l : 16 * l + 16, :]


def back_kernel(first, bh1_ref, h0_ref, qkv_ref, att_ref, noisy_ref, mods_ref, bias_ref, w_ref,
                bb1_ref, bp_ref, act_ref, gm_ref, patch_ref):
    i = pl.program_id(0) + first

    def mod(t):
        return mods_ref[pl.ds(i, 1), D * t : D * t + D]

    bh1 = bh1_ref[0]
    att = att_ref[0]
    bb1 = (bh1 * mod(2)).astype(BF)
    bb1_ref[0] = bb1
    gm_ref[0, 2:3, :] = column_sum(bh1 * (mm(att, w_ref[3]) + bias_ref[3:4, :]))
    batt = mm_nt(bb1, w_ref[3]).astype(BF)
    q, k, v = qkv_ref[0, :, 0:D], qkv_ref[0, :, D : 2 * D], qkv_ref[0, :, 2 * D :]
    ready, halves, gq, gk, gv = [], [], [], [], []
    for h in range(HEADS + 2):
        if h < HEADS:
            ready.append((mm_nt(head(k, h), head(q, h)), mm_nt(head(v, h), head(batt, h))))
        if 1 <= h <= HEADS:
            s, dp = ready[h - 1]
            s = s * QK_SCALE
            e = jnp.exp(s - jnp.max(s, axis=0, keepdims=True))
            p = e * (1.0 / column_sum(e))
            halves.append((p.astype(BF), (p * (dp - column_sum(dp * p))).astype(BF)))
        if h >= 2:
            p, ds = halves[h - 2]
            gv.append(mm(p, head(batt, h - 2)))
            gk.append(mm(ds, head(q, h - 2)))
            gq.append(mm_tn(ds, head(k, h - 2)))
    bq = (jnp.concatenate(gq, axis=1) * QK_SCALE).astype(BF)
    bk = (jnp.concatenate(gk, axis=1) * QK_SCALE).astype(BF)
    bv = jnp.concatenate(gv, axis=1).astype(BF)
    bp_ref[0, :, 0:D] = bq
    bp_ref[0, :, D : 2 * D] = bk
    bp_ref[0, :, 2 * D :] = bv
    b1 = mm_nt(bq, w_ref[0]) + mm_nt(bk, w_ref[1]) + mm_nt(bv, w_ref[2])
    n1, inv1 = norm_stats(h0_ref[0])
    act_ref[0] = (n1 * (1.0 + mod(1)) + mod(0)).astype(BF)
    gm_ref[0, 0:1, :] = column_sum(b1)
    gm_ref[0, 1:2, :] = column_sum(b1 * n1)
    bh0 = (bh1 + norm_back(b1 * (1.0 + mod(1)), n1, inv1)).astype(BF)
    patch_ref[0] = mm(noisy_ref[0].astype(BF), bh0)
    gm_ref[0, 3:4, :] = column_sum(bh0.astype(F32))
    gm_ref[0, 4:5, :] = column_sum(bq.astype(F32))
    gm_ref[0, 5:6, :] = column_sum(bv.astype(F32))
    gm_ref[0, 6:7, :] = column_sum(bb1.astype(F32))
    gm_ref[0, 7:8, :] = jnp.zeros((1, D), F32)


def last_kernel(counts, at_ref, att_ref, *refs):
    mine_ref, other_ref = refs[-2:]
    put = functools.partial(put_pair, at_ref[3], mine_ref, other_ref)
    parts = []
    first = 0
    for k, count in enumerate(counts):
        act_ref, bp_ref, bb1_ref = refs[3 * k : 3 * k + 3]
        parts.append((act_ref, bp_ref, att_ref, bb1_ref, first))
        first += count * SEQ

    def over(which):
        return sum(which(*p) for p in parts)

    def qkv(j):
        return over(lambda act, bp, att, bb1, first: mm_tn(act[...], bp[:, D * j : D * j + D]))

    put(0, qkv(0), qkv(2))
    put(1, qkv(1), over(lambda act, bp, att, bb1, first: mm_tn(
        att[first : first + bb1.shape[0], :], bb1[...])))


def cond_back_kernel(images, cls_ref, gm2_ref, pre_ref, th_ref, cond_ref, feat_ref, modw_ref, fmodw_ref,
                     tout_ref, sums_ref, *refs):
    out_ref, pay_ref, refs = refs[-2], refs[-1], refs[:-2]
    gm3_refs, patch_refs = refs[::2], refs[1::2]
    none = jnp.zeros((4, D), F32)
    gm2 = [gm2_ref[m] for m in range(images)]
    gm3 = [ref[m] for ref in gm3_refs for m in range(ref.shape[0])]
    patch = sum(ref[m] for ref in patch_refs for m in range(ref.shape[0]))

    def rows_of(values, r):
        return jnp.concatenate([v[r : r + 1, :] for v in values] + [none], axis=0)

    tiles = [rows_of(gm3, 0), rows_of(gm3, 1), rows_of(gm3, 2),
             rows_of(gm2, 0), rows_of(gm2, 1), rows_of(gm2, 2)]
    finals = [rows_of(gm2, 3), rows_of(gm2, 4)]
    g_act = jnp.zeros((24, D), F32)
    for t in range(6):
        g_act = g_act + mm_nt(stack3(tiles[t]), modw_ref[:, D * t : D * t + D])
    for t in range(2):
        g_act = g_act + mm_nt(stack3(finals[t]), fmodw_ref[:, D * t : D * t + D])
    cond = cond_ref[...]
    g_cond = fold3(g_act) * silu_slope(cond)
    g_pre = fold3(mm_nt(stack3(g_cond), tout_ref[...])) * silu_slope(pre_ref[...])
    act = silu(cond)
    lane = lax.broadcasted_iota(jnp.int32, (1, 128), 1)
    ids = []
    for m in range(images):
        number = cls_ref[m]
        row = jnp.where(lane == 0, (number // 256).astype(F32), 0.0)
        ids.append(jnp.where(lane == 1, (number % 256).astype(F32), row))
    ids = jnp.concatenate(ids, axis=0)
    loss = sum(v[5:6, 0:128] for v in gm2)
    pieces = [v.astype(F32) for v in split3(loss)]
    loss = jnp.where(lane == 0, pieces[0], jnp.where(lane == 1, pieces[1], jnp.where(lane == 2, pieces[2], 0.0)))
    loss = jnp.concatenate([loss, jnp.zeros((1, D - 128), F32)], axis=1)

    def put(plane, j, upper, lower):
        pay_ref[plane, 8 * j : 8 * j + 8, :] = jnp.concatenate([upper[:4], lower[:4]], axis=0)

    def put_rows(plane, first, v):
        pay_ref[plane, first : first + v.shape[0], :] = v

    def over(r):
        return sum(v[r : r + 1, :] for v in gm3)

    none = jnp.zeros((8, D), F32)
    row = jnp.zeros((1, D), F32)
    tags = jnp.concatenate([ids, jnp.zeros((4, D - 128), F32)], axis=1)
    pay_ref[...] = jnp.zeros_like(pay_ref)
    put(0, 0, th_ref[...], jnp.concatenate([feat_ref[...], jnp.zeros((8, D - FREQ), F32)], axis=1))
    put(0, 1, g_cond, g_pre)
    put(0, 2, tags, none)
    put_rows(0, 40, patch)
    for plane in (1, 2):
        put(plane, 0, act, act)
        for t in range(3):
            put(plane, 1 + t, tiles[t], tiles[t + 3])
    put(1, 4, g_cond, none)
    put(1, 5, tags, none)
    put(2, 4, finals[0], finals[1])
    sums = sums_ref[...]
    put_rows(2, 40, jnp.concatenate([over(4), over(5), over(6), sums[16:21]], axis=0))
    put(3, 0, act, act)
    put(3, 1, finals[0], finals[1])
    put_rows(3, 40, sums[0:16])
    last = [[over(3)] + [row] * 6, [row] * 7, [row] * 7, [sums[23:24], sums[21:22], sums[22:23]] + [row] * 4]
    for plane in range(4):
        put_rows(plane, 56, jnp.concatenate(last[plane] + [loss], axis=0))
    out_ref[...] = pay_ref[...].astype(BF)


def rows_each(first, *dims):
    return pl.BlockSpec((1,) + dims, lambda i: (i + first,) + (0,) * len(dims))


def front(noisy, mods, bias, patch_low, pos, blocks):
    images = noisy.shape[0]
    each = functools.partial(rows_each, 0)
    return pl.pallas_call(
        front_kernel,
        name="front",
        grid=(images,),
        out_shape=(shape((images, SEQ, D)), shape((images, SEQ, 3 * D), BF),
                   shape((images, SEQ, D), BF), shape((images, SEQ, D))),
        in_specs=[each(PD, SEQ), VM, VM, VM, VM, VM],
        out_specs=[each(SEQ, D), each(SEQ, 3 * D), each(SEQ, D), each(SEQ, D)],
        compiler_params=room(24),
        cost_estimate=cost(2.2e9, 1.2e7),
    )(noisy, mods, bias, patch_low, pos, blocks)


def middle(total_img, at, time_weight, h1, velocity, dino, mods, bias, blocks, align_low, final_low):
    images = h1.shape[0]
    each = functools.partial(rows_each, 0)
    full = lambda lanes, kind=BF: pltpu.VMEM((images * SEQ, lanes), kind)
    return pl.pallas_call(
        functools.partial(middle_kernel, images, total_img),
        name="middle",
        grid=(images,),
        out_shape=(shape((images, SEQ, D)), shape((images, 8, D)),
                   shape((16, EARLY, D), BF), shape((16, EARLY, D), BF), shape((SUMS_MLP, D))),
        in_specs=[SM, SM, each(SEQ, D), each(PD, SEQ), each(SEQ, DINO), VM, VM, VM, VM, VM],
        out_specs=[each(SEQ, D), each(8, D), VM, VM, VM],
        scratch_shapes=[full(D), full(F), pltpu.VMEM((SEQ, F), F32), full(F), full(D), full(D),
                        full(DINO), full(D), full(128), pltpu.VMEM((D, F), BF)],
        compiler_params=room(40),
        cost_estimate=cost(9e9, 1.4e7),
    )(at, time_weight, h1, velocity, dino, mods, bias, blocks, align_low, final_low)


def attention_back(first, count, bh1, h0, qkv, att, noisy, mods, bias, blocks):
    each = functools.partial(rows_each, first)
    out = functools.partial(rows_each, 0)
    return pl.pallas_call(
        functools.partial(back_kernel, first),
        name="attention_back",
        grid=(count,),
        out_shape=(shape((count, SEQ, D), BF), shape((count, SEQ, 3 * D), BF), shape((count, SEQ, D), BF),
                   shape((count, 8, D)), shape((count, PD, D))),
        in_specs=[each(SEQ, D), each(SEQ, D), each(SEQ, 3 * D), each(SEQ, D), each(PD, SEQ), VM, VM, VM],
        out_specs=[out(SEQ, D), out(SEQ, 3 * D), out(SEQ, D), out(8, D), out(PD, D)],
        compiler_params=room(24),
        cost_estimate=cost(1.2e9 * count, 3e6 * count),
    )(bh1, h0, qkv, att, noisy, mods, bias, blocks)


def last_gradients(at, att, parts):
    flat = lambda v: v.reshape(-1, v.shape[-1])
    arrays = [flat(v) for part in parts for v in part]
    counts = tuple(part[0].shape[0] for part in parts)
    return pl.pallas_call(
        functools.partial(last_kernel, counts),
        name="last_gradients",
        out_shape=(shape((16, LATE, D), BF),) * 2,
        in_specs=[SM] + [VM] * (len(arrays) + 1),
        out_specs=[VM] * 2,
        compiler_params=room(20),
        cost_estimate=cost(1.2e9, 9e6),
    )(at, flat(att), *arrays)


def cond_back(images, class_ids, gm2, pre, th, cond, features, mod_w, fmod_w, tout_w, sums, gm3):
    return pl.pallas_call(
        functools.partial(cond_back_kernel, images),
        name="cond_back",
        out_shape=shape((4, PAY, D), BF),
        in_specs=[SM] + [VM] * (9 + len(gm3)),
        out_specs=VM,
        scratch_shapes=[pltpu.VMEM((4, PAY, D), F32)],
        compiler_params=room(16),
        cost_estimate=cost(1e8, 4e6),
    )(class_ids, gm2, pre, th, cond, features, mod_w, fmod_w, tout_w, sums, *gm3)


def position_table():
    quarter = D // 4
    frequencies = 1.0 / 10000.0 ** (jnp.arange(quarter, dtype=jnp.float32) / quarter)
    cell_ids = jnp.arange(SEQ, dtype=jnp.int32)
    row_arg = (cell_ids // GRID).astype(jnp.float32)[:, None] * frequencies[None, :]
    col_arg = (cell_ids % GRID).astype(jnp.float32)[:, None] * frequencies[None, :]
    return jnp.concatenate(
        [jnp.sin(col_arg), jnp.cos(col_arg), jnp.sin(row_arg), jnp.cos(row_arg)], axis=1
    )


def time_features(tstep_idx):
    half_freq = FREQ // 2
    frequencies = jnp.exp(-math.log(10000.0) * jnp.arange(half_freq, dtype=jnp.float32) / half_freq)
    angles = (tstep_idx.astype(jnp.float32) + 0.5)[:, None] * frequencies[None, :]
    return jnp.concatenate([jnp.cos(angles), jnp.sin(angles)], axis=1)


def body(
    noisy,
    velocity,
    tstep_idx,
    class_ids,
    time_weight,
    dino,
    owner_map,
    adam_flat,
    adam_m,
    adam_v,
    blocks_w,
    stat_left,
    stat_right,
    root_left,
    root_right,
):
    dp, group = lax.axis_size("dp"), lax.axis_size("shard")
    near = is_near(dp, group)
    images = noisy.shape[0]
    total_img = images * dp * group
    at = jnp.stack([jnp.asarray(v, jnp.int32) for v in coordinates()])
    flat_w = adam_flat.reshape(-1, 128)
    flat_m = adam_m.reshape(-1, 128)
    flat_v = adam_v.reshape(-1, 128)
    mine = flat_w.astype(BF)
    features = jnp.pad(time_features(tstep_idx), ((0, 4), (0, 0)))
    pos = position_table()
    noisy = jnp.transpose(noisy, (0, 2, 1))
    velocity = jnp.transpose(velocity, (0, 2, 1))
    rows = flat_w.shape[0]
    if near:
        cut = rows // 16 * 8 + 8 if rows // 8 % 2 else rows // 2
        block_parts = gather_blocks(blocks_w.astype(BF))
        pieces, (at, features, pos) = gather_flat(mine, cut, (at, features, pos))
        places = flat_places(cut)
        blocks = place_blocks(at, owner_map, block_parts)
    else:
        pieces = [lax.all_gather(mine, AXES, axis=0, tiled=True)[None]]
        places = [(0, lambda i, at: 0)]
        slot_low = lax.all_gather(blocks_w.astype(BF), "shard", axis=0, tiled=True)
        block_ids = jnp.arange(NBLK, dtype=jnp.int32)
        slot_of = jnp.sum(
            block_ids[:, None] * (owner_map[:, None] == block_ids[None, :]).astype(jnp.int32), axis=0
        )
        blocks = jnp.take(slot_low, slot_of, axis=0)
    (mods, pre, th, cond, mod_w, fmod_w, tout_w, align_low, bias, patch_low, final_low) = conditioning(
        at, class_ids, features, pieces, places, rows)
    h0, qkv, att, h1 = front(noisy, mods, bias, patch_low, pos, blocks)
    bh1, gm2, mine, other, sums = middle(
        total_img, at, time_weight, h1, velocity, dino, mods, bias, blocks, align_low, final_low)
    if near:
        early = reduce_units(at, mine, other)
    parts, gm3 = [], []
    for first, count in ((0, 1), (1, images - 1)):
        bb1, bp, act, gm, patch = attention_back(first, count, bh1, h0, qkv, att, noisy, mods, bias, blocks)
        parts.append((act, bp, bb1))
        gm3 += [gm, patch]
    late_mine, late_other = last_gradients(at, att, parts)
    pay = cond_back(images, class_ids, gm2, pre, th, cond, features, mod_w, fmod_w, tout_w, sums, gm3)
    if near:
        late = reduce_units(at, late_mine, late_other)
        grads, parts = exchange_gradients(at, owner_map, pay, late, early)
        loss, upd, new_m, new_v = adam_near(at, parts, flat_w, flat_m, flat_v)
        *grads, loss, upd, new_m, new_v = lax.optimization_barrier((*grads, loss, upd, new_m, new_v))
        updates = shampoo(at, grads, blocks_w, stat_left, stat_right, root_left, root_right)
    else:
        core = at[3]

        def by_part(mine, other):
            pair = jnp.where(core == 0, jnp.stack([mine, other]), jnp.stack([other, mine]))
            count = mine.shape[1] // UNIT
            return pair.reshape(2, 16, count, UNIT, D).transpose(0, 2, 1, 3, 4).reshape(2, count, D, D)

        early, late = by_part(mine, other), by_part(late_mine, late_other)
        late = jnp.stack([late[0, 0], late[0, 1], late[1, 0], late[1, 1]])
        grad_model = jnp.concatenate([late, early[:, :4].reshape(8, D, D)])
        pays = lax.all_gather(pay, AXES, axis=0, tiled=False)
        align_sum = lax.psum(early[:, 4].astype(F32), AXES)
        loss, upd, new_m, new_v = adam_wide(pays, align_sum, flat_w, flat_m, flat_v)
        slots = jnp.take(grad_model, owner_map, axis=0)
        owned = lax.psum_scatter(slots, "shard", scatter_dimension=0, tiled=True)
        grads = [lax.psum(owned.astype(F32), "dp").astype(BF)]
        updates = shampoo(at, grads, blocks_w, stat_left, stat_right, root_left, root_right)
    return (loss, *updates,
            upd.reshape(-1), new_m.reshape(-1), new_v.reshape(-1))


def is_near(dp, group):
    return (dp, group) == (8, 4)


def solution(mesh):
    return jax.shard_map(
        body,
        mesh=mesh,
        in_specs=(
            P(("dp", "shard"), None, None),
            P(("dp", "shard"), None, None),
            P(("dp", "shard")),
            P(("dp", "shard")),
            P(("dp", "shard")),
            P(("dp", "shard"), None, None),
            P(),
            P(("dp", "shard")),
            P(("dp", "shard")),
            P(("dp", "shard")),
            P("shard", None, None),
            P("shard", None, None),
            P("shard", None, None),
            P("shard", None, None),
            P("shard", None, None),
        ),
        out_specs=(
            P(),
            P("shard", None, None),
            P("shard", None, None),
            P("shard", None, None),
            P(("dp", "shard")),
            P(("dp", "shard")),
            P(("dp", "shard")),
        ),
        check_vma=False,
    )
```

```python
import functools
import math

import jax
import jax.numpy as jnp
from jax import lax
from jax.experimental import pallas as pl
from jax.experimental.pallas import tpu as pltpu
from jax.sharding import PartitionSpec as P


D = 384
HEADS = 6
HDIM = 64
F = 1536
PD = 16
GRID = 16
SEQ = 256
FREQ = 256
DINO = 768
STEP = 10
NBLK = 12
ADAM_PAD = 2129920

BETA_ONE = 0.9
BETA_TWO = 0.95
ADAM_EPS = 1e-08
ADAM_RATE = 0.01
DECAY_RATE = 0.1
STAT_BETA = 0.9
SHAMPOO_RATE = 0.02
RMS_EPS = 1e-08
REPA_WEIGHT = 0.5
NORM_EPS = 1e-06
QK_SCALE = HDIM ** (-0.5)

AXES = ("dp", "shard")
BF = jnp.bfloat16
F32 = jnp.float32
VM = pl.BlockSpec(memory_space=pltpu.VMEM)
SM = pl.BlockSpec(memory_space=pltpu.SMEM)

FLAT_ROWS = ADAM_PAD // 128
R_PATCH = 0
R_PATCH_B = 48
R_TIME_IN = 51
R_TIME_IN_B = 819
R_TIME_OUT = 822
R_TIME_OUT_B = 1974
R_CLASS = 1977
R_MOD = 4980
R_MOD_B = 11892
R_QUERY_B = 11910
R_VALUE_B = 11913
R_PROJ_B = 11916
R_HIDDEN_B = 11919
R_DOWN_B = 11931
R_FMOD = 11934
R_FMOD_B = 14238
R_FINAL = 14244
R_FINAL_B = 14292
ALIGN_ROWS = 2310

PAY = 64
PLANE_ROWS = FLAT_ROWS // 4


def shape(dims, kind=F32):
    return jax.ShapeDtypeStruct(dims, kind)


def cost(flops, moved):
    return pl.CostEstimate(flops=int(flops), bytes_accessed=int(moved), transcendentals=0)


def room(mib):
    return pltpu.CompilerParams(vmem_limit_bytes=mib * 1024 * 1024)


def mm(left, right):
    return jnp.dot(left, right, preferred_element_type=F32)


def mm_nt(left, right):
    return lax.dot_general(left, right, (((1,), (1,)), ((), ())), preferred_element_type=F32)


def mm_tn(left, right):
    return lax.dot_general(left, right, (((0,), (0,)), ((), ())), preferred_element_type=F32)


def silu(v):
    return v / (1.0 + jnp.exp(-v))


def silu_slope(v):
    s = 1.0 / (1.0 + jnp.exp(-v))
    return s * (1.0 + v * (1.0 - s))


def split3(v):
    one = v.astype(BF)
    rest = v - one.astype(F32)
    two = rest.astype(BF)
    return one, two, (rest - two.astype(F32)).astype(BF)


def split2(v):
    one = v.astype(BF)
    return one, (v - one.astype(F32)).astype(BF)


def stack3(v):
    one, two, three = split3(v)
    return jnp.concatenate([one.astype(F32), two.astype(F32), three.astype(F32)], axis=0).astype(BF)


def fold3(v):
    third = v.shape[0] // 3
    return v[:third] + v[third : 2 * third] + v[2 * third :]


def place_of(z, x, y, c):
    return ((z * 2 + x) * 2 + y) * 2 + c


def permutation(move):
    pairs = []
    for z in range(4):
        for x in range(2):
            for y in range(2):
                for c in range(2):
                    pairs.append((place_of(z, x, y, c), place_of(*move(z, x, y, c))))
    return pairs


TO_C = permutation(lambda z, x, y, c: (z, x, y, 1 - c))
TO_Y = permutation(lambda z, x, y, c: (z, x, 1 - y, c))
TO_X = permutation(lambda z, x, y, c: (z, 1 - x, y, c))
TO_Z = [permutation(lambda z, x, y, c, d=d: (z ^ d, x, y, c)) for d in range(4)]


def send(value, pairs):
    return lax.ppermute(value, AXES, pairs)


def coordinates():
    dp = lax.axis_index("dp")
    sh = lax.axis_index("shard")
    return dp // 2, dp % 2, sh // 2, sh % 2


TO_XY = permutation(lambda z, x, y, c: (z, 1 - x, 1 - y, c))
TO_CY = permutation(lambda z, x, y, c: (z, x, 1 - y, 1 - c))
TO_PAIR = permutation(lambda z, x, y, c: (z + 1 - 2 * (z % 2), x, y, c))


def gather_flat(piece, cut, ready):
    turned = [send(piece, TO_Z[d]) for d in (1, 2, 3)]
    own_x, own_y = send(piece, TO_X), send(piece, TO_Y)
    first = jnp.stack([t[:cut] for t in turned])
    second = jnp.stack([t[cut:] for t in turned])
    first_x = send(first, TO_X)
    second_y = send(second, TO_Y)
    second_y, ready = lax.optimization_barrier((second_y, ready))
    first = jnp.concatenate([own_x[None, :cut], first, first_x])
    second = jnp.concatenate([own_y[None, cut:], second, second_y])
    far = [send(first, TO_Y), send(second, TO_X)]
    own = [piece, own_x[cut:], own_y[:cut]]
    own_c = [send(p, TO_C) for p in own]
    rest_c = [send(p, TO_C) for p in (first, second, *far)]
    return [p[None] for p in own] + [first, second] + far + [p[None] for p in own_c] + rest_c, ready


def flip(value, bit):
    return 1 - value if bit else value


def flat_places(cut):
    def near(dc, dx, dy):
        return lambda i, at: place_of(at[0], flip(at[1], dx), flip(at[2], dy), flip(at[3], dc))

    def far(dc, kind):
        def entry(i, at):
            z, x, y, c = at
            dz, other = (0, 1) if i == 0 else ((i - 1) % 3 + 1, (i - 1) // 3)
            dx, dy = {0: (other, 0), 1: (0, other), 2: (other, 1), 3: (1, other)}[kind]
            return place_of(z ^ dz, flip(x, dx), flip(y, dy), flip(c, dc))

        return entry

    places = []
    for dc in (0, 1):
        places += [(0, near(dc, 0, 0)), (cut, near(dc, 1, 0)), (0, near(dc, 0, 1))]
        places += [((0, cut, 0, cut)[kind], far(dc, kind)) for kind in range(4)]
    return places


def read_coordinates(ref):
    return ref[0], ref[1], ref[2], ref[3]


def cond_kernel(places, rows, at_ref, cls_ref, feat_ref, *refs):
    count = len(places)
    pieces = refs[:count]
    (mods_ref, pre_ref, th_ref, cond_ref, modw_ref, fmodw_ref, tout_ref, align_ref, bias_ref,
     patch_ref, final_ref, flat, rolled) = refs[count:]
    at = read_coordinates(at_ref)
    for ref, (offset, entry) in zip(pieces, places):
        for i in range(ref.shape[0]):
            start = pl.multiple_of(entry(i, at) * rows + offset, 8)
            flat[pl.ds(start, ref.shape[1]), :] = ref[i].astype(F32)

    def row(first, count):
        return jnp.concatenate([flat[first + l : first + l + 1, :] for l in range(count)], axis=1)

    def columns(first, depth, count, which):
        return flat[pl.ds(first + which, depth, stride=count), :].astype(BF)

    def wide(v, first, depth, count, keep=None):
        stacked = stack3(v)
        out = []
        for j in range(count):
            w = columns(first, depth, count, j)
            if keep is not None:
                keep[:, 128 * j : 128 * j + 128] = w
            out.append(fold3(mm(stacked, w)))
        return jnp.concatenate(out, axis=1)

    pre = wide(feat_ref[...], R_TIME_IN, FREQ, 3) + row(R_TIME_IN_B, 3)
    th = silu(pre)
    picked = []
    for m in range(4):
        r = R_CLASS + 3 * cls_ref[m]
        picked.append(jnp.concatenate([flat[pl.ds(r + l, 1), :] for l in range(3)], axis=1))
    picked = jnp.concatenate(picked + [jnp.zeros((4, D), F32)], axis=0)
    cond = wide(th, R_TIME_OUT, D, 3, tout_ref) + row(R_TIME_OUT_B, 3) + picked
    act = silu(cond)
    pre_ref[...] = pre
    th_ref[...] = th
    cond_ref[...] = cond
    mods_ref[:, : 6 * D] = wide(act, R_MOD, D, 18, modw_ref) + row(R_MOD_B, 18)
    mods_ref[:, 6 * D :] = wide(act, R_FMOD, D, 6, fmodw_ref) + row(R_FMOD_B, 6)

    spot = lax.broadcasted_iota(jnp.int32, (ALIGN_ROWS, 128), 1)
    here = pltpu.roll(flat[R_FINAL_B : R_FINAL_B + ALIGN_ROWS, :], 112, 1)
    after = pltpu.roll(flat[R_FINAL_B + 1 : R_FINAL_B + 1 + ALIGN_ROWS, :], 112, 1)
    rolled[...] = jnp.where(spot < 112, here, after)
    for j in range(6):
        align_ref[:, 128 * j : 128 * j + 128] = rolled[pl.ds(j, D, stride=6), :].astype(BF)

    bias_ref[...] = jnp.zeros_like(bias_ref)
    for at_row, first in ((0, R_PATCH_B), (1, R_QUERY_B), (2, R_VALUE_B), (3, R_PROJ_B),
                          (4, R_HIDDEN_B), (5, R_HIDDEN_B + 3), (6, R_HIDDEN_B + 6),
                          (7, R_HIDDEN_B + 9), (8, R_DOWN_B)):
        bias_ref[at_row : at_row + 1, :] = row(first, 3)
    for half in range(2):
        bias_ref[9 + half : 10 + half, :] = jnp.concatenate(
            [rolled[2304 + 3 * half + l : 2305 + 3 * half + l, :] for l in range(3)], axis=1)
    lane = lax.broadcasted_iota(jnp.int32, (1, 128), 1)
    bias_ref[11:12, :128] = jnp.where(lane < PD, flat[R_FINAL_B : R_FINAL_B + 1, :], 0.0)
    patch = [flat[pl.ds(R_PATCH + l, PD, stride=3), :] for l in range(3)]
    patch_ref[...] = jnp.concatenate(patch, axis=1).astype(BF)
    spread = (lax.broadcasted_iota(jnp.int32, (D, 48), 0) // 8
              == lax.broadcasted_iota(jnp.int32, (D, 48), 1)).astype(F32).astype(BF)
    wide_rows = mm(spread, flat[R_FINAL : R_FINAL + 48, :].astype(BF))
    keep = (lax.broadcasted_iota(jnp.int32, (D, 128), 1) // PD
            == lax.broadcasted_iota(jnp.int32, (D, 128), 0) % 8)
    fold = (lax.broadcasted_iota(jnp.int32, (128, 128), 0) % PD
            == lax.broadcasted_iota(jnp.int32, (128, 128), 1)).astype(F32).astype(BF)
    final_ref[...] = mm(jnp.where(keep, wide_rows, 0.0).astype(BF), fold).astype(BF)


def conditioning(at, classes, features, pieces, places, rows):
    kernel = functools.partial(cond_kernel, places, rows)
    return pl.pallas_call(
        kernel,
        name="conditioning",
        out_shape=(shape((8, 8 * D)), shape((8, D)), shape((8, D)), shape((8, D)),
                   shape((D, 6 * D), BF), shape((D, 2 * D), BF), shape((D, D), BF),
                   shape((D, DINO), BF), shape((16, D)), shape((PD, D), BF), shape((D, 128), BF)),
        in_specs=[SM, SM, VM] + [VM] * len(pieces),
        out_specs=[VM] * 11,
        scratch_shapes=[pltpu.VMEM((FLAT_ROWS + 8, 128), F32), pltpu.VMEM((ALIGN_ROWS, 128), F32)],
        compiler_params=room(28),
        cost_estimate=pl.CostEstimate(flops=10**9, bytes_accessed=10**7, transcendentals=0),
    )(at, classes, features, *pieces)


def gather_blocks(mine):
    z, _, _, _ = coordinates()
    half = lax.dynamic_slice_in_dim(mine, 192 * (z % 2), 192, 1)
    near = send(half, TO_Y)
    far = send(near, TO_PAIR)
    return [mine, near, far, send(mine, TO_C), send(near, TO_C), send(far, TO_C)]


def place_blocks_kernel(at_ref, own_ref, mine_ref, near_ref, far_ref, mine_c_ref, near_c_ref, far_c_ref, out_ref):
    z, _, y, c = read_coordinates(at_ref)
    for core, mine, near, far in ((c, mine_ref, near_ref, far_ref), (1 - c, mine_c_ref, near_c_ref, far_c_ref)):
        for t in range(3):
            out_ref[own_ref[3 * (2 * y + core) + t]] = mine[t]
            there = own_ref[3 * (2 * (1 - y) + core) + t]
            odd = pl.multiple_of(192 * lax.rem(z, 2), 16)
            even = pl.multiple_of(192 * (1 - lax.rem(z, 2)), 16)
            out_ref[there, pl.ds(odd, 192), :] = near[t]
            out_ref[there, pl.ds(even, 192), :] = far[t]


def place_blocks(at, owner_map, parts):
    return pl.pallas_call(
        place_blocks_kernel,
        name="place_blocks",
        out_shape=shape((NBLK, D, D), BF),
        in_specs=[SM, SM] + [VM] * 6,
        out_specs=VM,
        compiler_params=room(12),
        cost_estimate=cost(1e6, 7e6),
    )(at, owner_map, *parts)


UNIT = 24


def unit_of(z, x, y):
    return (2 * x + y) * 4 + z


def quarter_kernel(at_ref, mine_ref, got_ref, *out_refs):
    _, x, y, _ = read_coordinates(at_ref)
    for out_ref, (dx, dy) in zip(out_refs, ((0, 0), (1, 0), (0, 1), (1, 1))):
        rows = pl.ds(4 * (2 * flip(x, dx) + flip(y, dy)), 4)
        out_ref[...] = (mine_ref[rows].astype(F32) + got_ref[rows].astype(F32)).astype(BF)


def turn_kernel(at_ref, *refs):
    z, _, _, _ = read_coordinates(at_ref)
    for d, out_ref in enumerate(refs[4:]):
        unit = z ^ d
        out_ref[...] = sum(ref[unit].astype(F32) for ref in refs[:4]).astype(BF)


def reduce_units(at, mine, other):
    rows = mine.shape[1]
    got = send(other, TO_C)
    own, *away = pl.pallas_call(
        quarter_kernel,
        name="quarter",
        out_shape=(shape((4, rows, D), BF),) * 4,
        in_specs=[SM, VM, VM],
        out_specs=[VM] * 4,
        compiler_params=room(12),
        cost_estimate=cost(1e6, 4e6),
    )(at, mine, got)
    got = [send(v, pairs) for v, pairs in zip(away, (TO_X, TO_Y, TO_XY))]
    own, *away = pl.pallas_call(
        turn_kernel,
        name="turn",
        out_shape=(shape((rows, D), BF),) * 4,
        in_specs=[SM] + [VM] * 4,
        out_specs=[VM] * 4,
        compiler_params=room(8),
        cost_estimate=cost(1e6, 2e6),
    )(at, own, *got)
    return [own] + [send(v, TO_Z[d + 1]) for d, v in enumerate(away)]


def rows_kernel(at_ref, pay_ref, *refs):
    early, out_refs, total_ref = refs[:4], refs[4:8], refs[8]
    total = sum(ref[...].astype(F32) for ref in early).astype(BF)
    total_ref[...] = total
    for d, out_ref in enumerate(out_refs):
        plane = at_ref[0] ^ d
        out_ref[...] = pay_ref[plane]

        @pl.when(plane == 3)
        def _():
            out_ref[16:40, :] = total[4 * UNIT :]


def owner_kernel(at_ref, own_ref, *refs):
    late, early = refs[:4], refs[4]
    out_refs, total = refs[5:9], refs[9]
    _, _, y, c = read_coordinates(at_ref)
    one = sum(ref[...].astype(F32) for ref in late)
    two = early[...].astype(F32)
    for k in range(6):
        total[k] = (one[UNIT * k : UNIT * k + UNIT] if k < 2 else two[UNIT * (k - 2) : UNIT * (k - 1)])
    for out_ref, (dy, dc) in zip(out_refs, ((0, 0), (0, 1), (1, 0), (1, 1))):
        first = 3 * (2 * flip(y, dy) + flip(c, dc))
        for t in range(3):
            block = own_ref[first + t]
            low = block < 4
            part = jnp.where(low, lax.div(block, 2), lax.div(block - 4, 4))
            entry = jnp.where(low, lax.rem(block, 2), 2 + lax.rem(jnp.maximum(block - 4, 0), 4))
            out_ref[t] = jnp.where(part == c, total[entry], 0.0).astype(BF)


def join_kernel(own_ref, pair_ref, near_ref, far_ref, out_ref):
    out_ref[0] = own_ref[...] + pair_ref[...]
    out_ref[1] = near_ref[...] + far_ref[...]


def exchange_gradients(at, owner_map, pay, late, early):
    piece = (3, UNIT, D)
    keep, *away, early = pl.pallas_call(
        rows_kernel,
        name="pay_rows",
        out_shape=(shape((PAY, D), BF),) * 4 + (shape((EARLY, D), BF),),
        in_specs=[SM] + [VM] * 5,
        out_specs=[VM] * 5,
        compiler_params=room(8),
        cost_estimate=cost(1e6, 1e6),
    )(at, pay, *early)
    turned = [send(v, TO_Z[d + 1]) for d, v in enumerate(away)]
    own, to_c, to_y, to_cy = pl.pallas_call(
        owner_kernel,
        name="owner_rows",
        out_shape=(shape(piece, BF),) * 4,
        in_specs=[SM, SM] + [VM] * 5,
        out_specs=[VM] * 4,
        scratch_shapes=[pltpu.VMEM((6, UNIT, D), F32)],
        compiler_params=room(8),
        cost_estimate=cost(1e6, 1e6),
    )(at, owner_map, *late, early)
    far, near, pair = send(to_cy, TO_CY), send(to_y, TO_Y), send(to_c, TO_C)
    turned, pair = lax.optimization_barrier((turned, pair))
    rows = jnp.stack([keep] + turned)
    plane = [rows, send(rows, TO_X), send(rows, TO_Y)]
    both = pl.pallas_call(
        join_kernel,
        name="join",
        out_shape=shape((2,) + piece, BF),
        in_specs=[VM] * 4,
        out_specs=VM,
        compiler_params=room(8),
        cost_estimate=cost(1e6, 1e6),
    )(own, pair, near, far)
    column = [both] + [send(both, TO_Z[d]) for d in (1, 2, 3)]
    crossed = [send(both, TO_X)]
    plane[1], column[1] = lax.optimization_barrier((plane[1], column[1]))
    plane.append(send(plane[1], TO_Y))
    crossed.append(send(column[1], TO_X))
    pairs = [send(p, TO_C) for p in plane[:3]]
    slots = column + crossed + [send(v, TO_X) for v in column[2:]]
    return slots, plane + pairs + [send(plane[3], TO_C)]


def plane_gradient(plane, pay_ref, flat, rolled, align):
    rows = 8 * pay_ref.shape[0]

    def tile(j):
        return pay_ref[:, 8 * j : 8 * j + 8, :].astype(F32).reshape(rows, D)

    def sums(first, last):
        return jnp.sum(pay_ref[:, first:last, :].astype(F32), axis=0)

    upper = lax.broadcasted_iota(jnp.int32, (rows, 1), 0) % 8 < 4

    def first(v):
        return jnp.where(upper, v, 0.0)

    def second(v):
        return jnp.where(upper, 0.0, v)

    def put_row(v, row):
        for l in range(v.shape[1] // 128):
            flat[row + l : row + l + 1, :] = v[:, 128 * l : 128 * l + 128]

    def put_matrix(v, row, count, which):
        for l in range(v.shape[1] // 128):
            flat[pl.ds(row + which + l, v.shape[0], stride=count), :] = v[:, 128 * l : 128 * l + 128]

    def classes(ids, g_low):
        numbers = (ids[:, 0:1] * 256.0 + ids[:, 1:2]).astype(jnp.int32)
        for part in range(3):
            height = 336 if part < 2 else 329
            marks = lax.broadcasted_iota(jnp.int32, (rows, 336), 1) + 336 * part
            hits = first(jnp.where(marks == numbers, 1.0, 0.0)).astype(BF)
            put_matrix(mm_tn(hits, g_low)[:height], R_CLASS + 3 * 336 * part, 3, 0)

    def modulations(low, bias):
        act = tile(0)[:, low : low + 256]
        halves = (first(act).astype(BF), second(act).astype(BF))
        for t in range(3):
            g = tile(1 + t)
            for half in range(2):
                put_matrix(mm_tn(halves[half], g.astype(BF)), R_MOD + 18 * low, 18, 3 * (t + 3 * half))
                if bias:
                    put_row(column_sum((first, second)[half](g)), R_MOD_B + 3 * (t + 3 * half))

    def finals(which, bias):
        act, g = tile(0), tile(which)
        for half, part in enumerate((first, second)):
            put_matrix(mm_tn(part(act).astype(BF), g.astype(BF)), R_FMOD, 6, 3 * half)
            if bias:
                put_row(column_sum(part(g)), R_FMOD_B + 3 * half)

    if plane == 0:
        left, g = tile(0).astype(BF), tile(1)
        g_cond, g_pre = first(g), second(g)
        put_matrix(mm_tn(left[:, :FREQ], g_pre.astype(BF)), R_TIME_IN, 3, 0)
        put_row(column_sum(g_pre), R_TIME_IN_B)
        put_matrix(mm_tn(left, g_cond.astype(BF)), R_TIME_OUT, 3, 0)
        put_row(column_sum(g_cond), R_TIME_OUT_B)
        classes(tile(2)[:, :128], g.astype(BF))
        total = sums(40, 64)
        for l in range(3):
            flat[pl.ds(R_PATCH + l, PD, stride=3), :] = total[0:16, 128 * l : 128 * l + 128]
        put_row(total[16:17], R_PATCH_B)
    if plane == 1:
        classes(tile(5)[:, :128], tile(4).astype(BF))
        modulations(0, False)
    if plane == 2:
        modulations(128, True)
        finals(4, False)
        total = sums(40, 48)
        for k, row in enumerate((R_QUERY_B, R_VALUE_B, R_PROJ_B, R_HIDDEN_B, R_HIDDEN_B + 3, R_HIDDEN_B + 6,
                                 R_HIDDEN_B + 9, R_DOWN_B)):
            put_row(total[k : k + 1], row)
    if plane == 3:
        finals(1, True)
        total = sums(40, 64)
        for l in range(3):
            flat[R_FINAL + 16 * l : R_FINAL + 16 * l + 16, :] = total[0:16, 128 * l : 128 * l + 128]
        rolled[0:8, :] = jnp.zeros((8, 128), F32)
        rolled[8 + ALIGN_ROWS :, :] = jnp.zeros_like(rolled[8 + ALIGN_ROWS :, :])
        rolled[7:8, :] = pltpu.roll(total[16:17, 0:128], 112, 1)
        for half in range(2):
            for l in range(3):
                lanes = slice(128 * l, 128 * l + 128)
                rolled[pl.ds(8 + 3 * half + l, D, stride=6), :] = align[half, :, lanes].astype(F32)
                r = 8 + 2304 + 3 * half + l
                rolled[r : r + 1, :] = total[17 + half : 18 + half, lanes]
        count = FLAT_ROWS - R_FINAL_B
        spot = lax.broadcasted_iota(jnp.int32, (count, 128), 1)
        here = pltpu.roll(rolled[8 : 8 + count, :], 16, 1)
        before = pltpu.roll(rolled[7 : 7 + count, :], 16, 1)
        flat[R_FINAL_B:FLAT_ROWS, :] = jnp.where(spot < 16, before, here)


def loss_of(pay_ref):
    rows = 8 * pay_ref.shape[0]
    parts = pay_ref[:, PAY - 8 : PAY, 0:128].astype(F32).reshape(rows, 128)
    parts = column_sum(jnp.where(lax.broadcasted_iota(jnp.int32, (rows, 128), 0) % 8 == 7, parts, 0.0))
    return parts[:, 0:1] + parts[:, 1:2] + parts[:, 2:3]


def adam_near_kernel(at_ref, *refs):
    parts = refs[:8]
    w_ref, m_ref, v_ref, loss_ref, upd_ref, new_m_ref, new_v_ref, pay, align, flat, rolled = refs[8:]
    at = read_coordinates(at_ref)
    z, x, y, c = at
    for k, ref in enumerate(parts):
        dc, dy, dx = k // 4, k // 2 % 2, k % 2
        for dz in range(4):
            there = (z ^ dz, flip(x, dx), flip(y, dy), flip(c, dc))
            value = ref[dz].astype(F32)
            pay[place_of(*there)] = value
            start = pl.multiple_of(unit_of(*there[:3]) * UNIT, 8)
            align[there[3], pl.ds(start, UNIT), :] = value[16:40]
    loss_ref[...] = loss_of(pay)
    for plane in range(4):
        @pl.when(z == plane)
        def _():
            plane_gradient(plane, pay, flat, rolled, align)
    size = w_ref.shape[0]
    start = pl.multiple_of(place_of(z, x, y, c) * size, 8)
    adam_step(flat[pl.ds(start, size), :], w_ref, m_ref, v_ref, upd_ref, new_m_ref, new_v_ref)


def adam_plane_kernel(plane, pay_ref, align_ref, loss_ref, flat_ref, rolled):
    loss_ref[...] = loss_of(pay_ref)
    plane_gradient(plane, pay_ref, flat_ref, rolled, align_ref)


def adam_step(grad, w_ref, m_ref, v_ref, upd_ref, new_m_ref, new_v_ref):
    new_m = BETA_ONE * m_ref[...] + (1.0 - BETA_ONE) * grad
    new_v = BETA_TWO * v_ref[...] + (1.0 - BETA_TWO) * grad * grad
    new_m_ref[...] = new_m
    new_v_ref[...] = new_v
    right_m = new_m / (1.0 - BETA_ONE**STEP)
    right_v = new_v / (1.0 - BETA_TWO**STEP)
    upd_ref[...] = -ADAM_RATE * (right_m / (jnp.sqrt(right_v) + ADAM_EPS) + DECAY_RATE * w_ref[...])


ROLL_ROWS = 8 + FLAT_ROWS - R_FINAL_B + 8


ROLL_ROWS = 8 + FLAT_ROWS - R_FINAL_B + 8


def adam_near(at, parts, flat_w, m, v):
    size = flat_w.shape
    loss, upd, new_m, new_v = pl.pallas_call(
        adam_near_kernel,
        name="adam",
        out_shape=(shape((1, 1)), shape(size), shape(size), shape(size)),
        in_specs=[SM] + [VM] * 11,
        out_specs=[VM] * 4,
        scratch_shapes=[pltpu.VMEM((32, PAY, D), F32), pltpu.VMEM((2, D, D), F32),
                        pltpu.VMEM((FLAT_ROWS, 128), F32), pltpu.VMEM((ROLL_ROWS, 128), F32)],
        compiler_params=room(24),
        cost_estimate=pl.CostEstimate(flops=10**9, bytes_accessed=10**7, transcendentals=0),
    )(at, *parts, flat_w, m, v)
    return loss[0, 0], upd, new_m, new_v


def adam_wide(pays, align, flat_w, m, v):
    grads = []
    for plane in range(4):
        loss, flat = pl.pallas_call(
            functools.partial(adam_plane_kernel, plane),
            name="adam_gradient",
            out_shape=(shape((1, 1)), shape((FLAT_ROWS, 128))),
            in_specs=[VM] * 2,
            out_specs=[VM] * 2,
            scratch_shapes=[pltpu.VMEM((ROLL_ROWS, 128), F32)],
        )(pays[:, plane], align)
        grads.append(flat[PLANE_ROWS * plane : PLANE_ROWS * (plane + 1)])
    size = flat_w.shape[0]
    place = lax.axis_index("dp") * lax.axis_size("shard") + lax.axis_index("shard")
    grad = lax.dynamic_slice_in_dim(jnp.concatenate(grads), place * size, size, 0)
    upd, new_m, new_v = pl.pallas_call(
        lambda g, *refs: adam_step(g[...], *refs),
        name="adam",
        out_shape=(shape(flat_w.shape),) * 3,
        in_specs=[VM] * 4,
        out_specs=[VM] * 3,
    )(grad, flat_w, m, v)
    return loss[0, 0], upd, new_m, new_v


def shampoo_kernel(near, at_ref, *refs):
    t = pl.program_id(0)
    if near:
        parts = refs[:8]
        w_ref, sl_ref, sr_ref, rl_ref, rr_ref, upd_ref, nl_ref, nr_ref, grad = refs[8:]
        z, x, y, _ = read_coordinates(at_ref)
        for dx in range(2):
            for dz in range(4):
                for dy in range(2):
                    unit = unit_of(z ^ dz, flip(x, dx), flip(y, dy))
                    rows = pl.ds(pl.multiple_of(unit * UNIT, 8), UNIT)
                    grad[rows, :] = parts[4 * dx + dz][dy, t].astype(F32)
        g = grad[...].astype(BF)
    else:
        grad_ref, w_ref, sl_ref, sr_ref, rl_ref, rr_ref, upd_ref, nl_ref, nr_ref = refs
        g = grad_ref[t]
    nl_ref[0] = STAT_BETA * sl_ref[t] + (1.0 - STAT_BETA) * mm_nt(g, g)
    nr_ref[0] = STAT_BETA * sr_ref[t] + (1.0 - STAT_BETA) * mm_tn(g, g)
    left = mm(jnp.concatenate(split2(rl_ref[t]), axis=1), jnp.concatenate([g, g], axis=0))
    left = left.astype(BF)
    p = mm(jnp.concatenate([left, left], axis=1), jnp.concatenate(split2(rr_ref[t]), axis=0))
    mean = jnp.sum(jnp.sum(p * p, axis=1, keepdims=True), axis=0, keepdims=True) * (1.0 / (D * D))
    root = jnp.sqrt(mean)
    upd_ref[0] = -SHAMPOO_RATE * (p / (root + RMS_EPS) + DECAY_RATE * w_ref[t])


def shampoo(at, grads, blocks_w, stat_left, stat_right, root_left, root_right):
    near = len(grads) == 8
    slots = blocks_w.shape[0]
    one = pl.BlockSpec((1, D, D), lambda t: (t, 0, 0))
    return pl.pallas_call(
        functools.partial(shampoo_kernel, near),
        name="shampoo",
        grid=(slots,),
        out_shape=(shape((slots, D, D)),) * 3,
        in_specs=[SM] + [VM] * (len(grads) + 5),
        out_specs=[one] * 3,
        scratch_shapes=[pltpu.VMEM((D, D), F32)] if near else [],
        compiler_params=room(26),
        cost_estimate=pl.CostEstimate(flops=3 * 10**9, bytes_accessed=15 * 10**6, transcendentals=0),
    )(at, *grads, blocks_w, stat_left, stat_right, root_left, root_right)


GELU_C = math.sqrt(2.0 / math.pi)
GELU_D = 0.044715
EARLY = 5 * 24
LATE = 2 * 24
SUMS_MLP = 24


def norm_stats(v):
    centered = v - jnp.sum(v, axis=-1, keepdims=True) * (1.0 / D)
    inv = lax.rsqrt(jnp.sum(centered * centered, axis=-1, keepdims=True) * (1.0 / D) + NORM_EPS)
    return centered * inv, inv


def norm_back(g, normed, inv):
    mean_g = jnp.sum(g, axis=-1, keepdims=True) * (1.0 / D)
    mean_gn = jnp.sum(g * normed, axis=-1, keepdims=True) * (1.0 / D)
    return inv * (g - mean_g - normed * mean_gn)


def column_sum(v):
    return jnp.sum(v, axis=0, keepdims=True)


def head(v, h):
    return v[:, HDIM * h : HDIM * h + HDIM]


def put_pair(core, mine_ref, other_ref, j, zero, one):
    zero, one = zero.astype(BF), one.astype(BF)
    mine, other = jnp.where(core == 0, zero, one), jnp.where(core == 0, one, zero)
    for u in range(16):
        rows = slice(24 * u, 24 * u + 24)
        mine_ref[u, 24 * j : 24 * j + 24, :] = mine[rows]
        other_ref[u, 24 * j : 24 * j + 24, :] = other[rows]


def front_kernel(noisy_ref, mods_ref, bias_ref, patch_ref, pos_ref, w_ref,
                 h0_ref, qkv_ref, att_ref, h1_ref):
    i = pl.program_id(0)

    def mod(t):
        return mods_ref[pl.ds(i, 1), D * t : D * t + D]

    h0 = mm_tn(noisy_ref[0].astype(BF), patch_ref[...]) + bias_ref[0:1, :] + pos_ref[...]
    h0_ref[0] = h0
    normed, _ = norm_stats(h0)
    act = (normed * (1.0 + mod(1)) + mod(0)).astype(BF)
    q = (mm(act, w_ref[0]) + bias_ref[1:2, :]).astype(BF)
    k = mm(act, w_ref[1]).astype(BF)
    v = (mm(act, w_ref[2]) + bias_ref[2:3, :]).astype(BF)
    qkv_ref[0, :, 0:D] = q
    qkv_ref[0, :, D : 2 * D] = k
    qkv_ref[0, :, 2 * D :] = v
    v_t = v.T
    scores, probs, outs = [], [], []
    for h in range(HEADS + 2):
        if h < HEADS:
            scores.append(mm_nt(head(k, h), head(q, h)))
        if 1 <= h <= HEADS:
            s = scores[h - 1] * QK_SCALE
            e = jnp.exp(s - jnp.max(s, axis=0, keepdims=True))
            probs.append((e * (1.0 / column_sum(e))).astype(BF))
        if h >= 2:
            outs.append(mm(v_t[HDIM * (h - 2) : HDIM * (h - 1), :], probs[h - 2]))
    att = jnp.concatenate(outs, axis=0).astype(BF).T
    att_ref[0] = att
    h1_ref[0] = h0 + mod(2) * (mm(att, w_ref[3]) + bias_ref[3:4, :])


def encoder_kernel(dino_ref, out_ref):
    dino = dino_ref[0].astype(F32)
    out_ref[0] = lax.rsqrt(jnp.sum(dino * dino, axis=-1, keepdims=True) + NORM_EPS)


def encoder_norms(dino):
    images = dino.shape[0]
    each = functools.partial(rows_each, 0)
    return pl.pallas_call(
        encoder_kernel,
        name="encoder_norms",
        grid=(images,),
        out_shape=shape((images, SEQ, 1)),
        in_specs=[each(SEQ, DINO)],
        out_specs=each(SEQ, 1),
        compiler_params=room(8),
        cost_estimate=cost(1e6, 2e6),
    )(dino)


def middle_kernel(images, total_img, at_ref, tw_ref, h1_ref, vel_ref, dino_ref, rd_ref, mods_ref, bias_ref, w_ref, aw_ref, fw_ref,
                  bh1_ref, gm_ref, mine_ref, other_ref, sums_ref,
                  act2_s, gelu_s, slope_s, bi_s, bb2_s, h1_s, ba_s, act3_s, bo_s, up_s):
    i = pl.program_id(0)
    rows = pl.ds(pl.multiple_of(i * SEQ, SEQ), SEQ)

    def mod(t):
        return mods_ref[pl.ds(i, 1), D * t : D * t + D]

    @pl.when(i == 0)
    def _():
        sums_ref[...] = jnp.zeros_like(sums_ref)
        for j in range(4):
            up_s[:, D * j : D * j + D] = w_ref[4 + j]

    h1 = h1_ref[0]
    h1_low = h1.astype(BF)
    h1_s[rows, :] = h1_low
    aligned = mm(h1_low, aw_ref[...])
    n2, inv2 = norm_stats(h1)
    act2 = (n2 * (1.0 + mod(4)) + mod(3)).astype(BF)
    act2_s[rows, :] = act2

    def lanes_of(j):
        return slice(2 * D * j, 2 * D * j + 2 * D)

    def pair_row(j):
        return jnp.concatenate([bias_ref[j : j + 1, :], bias_ref[j + 1 : j + 2, :]], axis=1)

    def expand(j):
        return mm(act2, up_s[:, lanes_of(j)])

    def activate(j, x):
        x = x + pair_row(4 + 2 * j)
        xx = x * x
        t = jnp.tanh(x * (GELU_C + (GELU_C * GELU_D) * xx))
        half = 0.5 + 0.5 * t
        slope_s[:, lanes_of(j)] = half + (0.5 * x) * (1.0 - t * t) * (GELU_C + (3.0 * GELU_C * GELU_D) * xx)
        g = (x * half).astype(BF)
        gelu_s[rows, lanes_of(j)] = g
        return g

    def contract(j, g):
        return mm(g, w_ref[8 + 2 * j : 10 + 2 * j].reshape(2 * D, D))

    x_one = expand(0)
    aligned = aligned + pair_row(9)
    dino = dino_ref[0].astype(F32)
    dot = jnp.sum(aligned * dino, axis=-1, keepdims=True)
    ra = lax.rsqrt(jnp.sum(aligned * aligned, axis=-1, keepdims=True) + NORM_EPS)
    rd = rd_ref[0]
    x_two = expand(1)
    g_one = activate(0, x_one)
    scale = REPA_WEIGHT / (total_img * SEQ)
    both = ra * rd
    cosine = dot * both
    ba = dino * (both * -scale) + aligned * (cosine * (ra * ra) * scale)
    ba_sum = column_sum(ba)
    ba = ba.astype(BF)
    ba_s[rows, :] = ba
    branch = contract(0, g_one)
    g_two = activate(1, x_two)
    through = mm_nt(ba, aw_ref[...])
    branch = branch + contract(1, g_two) + bias_ref[8:9, :]
    h2 = h1 + mod(5) * branch
    n3, inv3 = norm_stats(h2)
    act3 = (n3 * (1.0 + mod(7)) + mod(6)).astype(BF)
    act3_s[rows, :] = act3
    out = mm(act3, fw_ref[...]) + bias_ref[11:12, 0:128]
    err = out[:, :PD] - vel_ref[0].T
    weight = tw_ref[i]
    loss = jnp.sum(column_sum(err * err), axis=1, keepdims=True) * (weight / (total_img * SEQ * PD))
    loss = loss - column_sum(cosine) * scale
    bo = jnp.concatenate([err * (2.0 * weight / (total_img * SEQ * PD)), jnp.zeros((SEQ, 128 - PD), F32)],
                         axis=1).astype(BF)
    bo_s[rows, :] = bo

    b3 = mm_nt(bo, fw_ref[...])
    bh2 = norm_back(b3 * (1.0 + mod(7)), n3, inv3)
    bb2 = bh2 * mod(5)
    bb2_sum = column_sum(bb2)
    bb2 = bb2.astype(BF)
    bb2_s[rows, :] = bb2
    b2 = jnp.zeros((SEQ, D), F32)
    for j in range(2):
        lanes = slice(2 * D * j, 2 * D * j + 2 * D)
        bi = mm_nt(bb2, w_ref[8 + 2 * j : 10 + 2 * j].reshape(2 * D, D)) * slope_s[:, lanes]
        bi_sum = column_sum(bi)
        bi = bi.astype(BF)
        bi_s[rows, lanes] = bi
        sums_ref[16 + 2 * j : 17 + 2 * j, :] += bi_sum[:, :D]
        sums_ref[17 + 2 * j : 18 + 2 * j, :] += bi_sum[:, D:]
        b2 = b2 + mm_nt(bi, up_s[:, lanes])
    sums_ref[20:21, :] += bb2_sum
    sums_ref[21:22, :] += ba_sum[:, :D]
    sums_ref[22:23, :] += ba_sum[:, D:]
    sums_ref[23:24, 0:128] += column_sum(bo.astype(F32))
    bh1_ref[0] = bh2 + norm_back(b2 * (1.0 + mod(4)), n2, inv2) + through
    gm_ref[0, 0:1, :] = column_sum(b2)
    gm_ref[0, 1:2, :] = column_sum(b2 * n2)
    gm_ref[0, 2:3, :] = column_sum(bh2 * branch)
    gm_ref[0, 3:4, :] = column_sum(b3)
    gm_ref[0, 4:5, :] = column_sum(b3 * n3)
    gm_ref[0, 5:6, :] = jnp.broadcast_to(loss, (1, D))
    gm_ref[0, 6:8, :] = jnp.zeros((2, D), F32)

    @pl.when(i == images - 1)
    def _():
        put = functools.partial(put_pair, at_ref[3], mine_ref, other_ref)
        for j in range(2):
            lanes = slice(2 * D * j, 2 * D * j + 2 * D)
            up = mm_tn(act2_s[...], bi_s[:, lanes]).astype(BF)
            down = mm_tn(bb2_s[...], gelu_s[:, lanes]).astype(BF)
            put(2 * j, up[:, :D], down[:, :D].T)
            put(2 * j + 1, up[:, D:], down[:, D:].T)
        align = mm_tn(h1_s[...], ba_s[...])
        put(4, align[:, :D], align[:, D:])
        g = mm_tn(act3_s[...], bo_s[...]).astype(BF)
        spread = (lax.broadcasted_iota(jnp.int32, (128, 128), 1) % PD
                  == lax.broadcasted_iota(jnp.int32, (128, 128), 0)).astype(F32).astype(BF)
        keep = (lax.broadcasted_iota(jnp.int32, (D, 128), 1) // PD
                == lax.broadcasted_iota(jnp.int32, (D, 128), 0) % 8)
        fold = (lax.broadcasted_iota(jnp.int32, (48, D), 1) // 8
                == lax.broadcasted_iota(jnp.int32, (48, D), 0)).astype(F32).astype(BF)
        flat = mm(fold, jnp.where(keep, mm(g, spread), 0.0).astype(BF))
        for l in range(3):
            sums_ref[0:16, 128 * l : 128 * l + 128] = flat[16 * l : 16 * l + 16, :]


def back_kernel(first, bh1_ref, h0_ref, qkv_ref, att_ref, noisy_ref, mods_ref, bias_ref, w_ref,
                bb1_ref, bp_ref, act_ref, gm_ref, patch_ref):
    i = pl.program_id(0) + first

    def mod(t):
        return mods_ref[pl.ds(i, 1), D * t : D * t + D]

    bh1 = bh1_ref[0]
    att = att_ref[0]
    bb1 = (bh1 * mod(2)).astype(BF)
    bb1_ref[0] = bb1
    gm_ref[0, 2:3, :] = column_sum(bh1 * (mm(att, w_ref[3]) + bias_ref[3:4, :]))
    batt = mm_nt(bb1, w_ref[3]).astype(BF)
    q, k, v = qkv_ref[0, :, 0:D], qkv_ref[0, :, D : 2 * D], qkv_ref[0, :, 2 * D :]
    k_t = k.T
    ready, halves, gq, gk, gv = [], [], [], [], []
    for h in range(HEADS + 2):
        if h < HEADS:
            ready.append((mm_nt(head(k, h), head(q, h)), mm_nt(head(v, h), head(batt, h))))
        if 1 <= h <= HEADS:
            s, dp = ready[h - 1]
            s = s * QK_SCALE
            e = jnp.exp(s - jnp.max(s, axis=0, keepdims=True))
            p = e * (1.0 / column_sum(e))
            halves.append((p.astype(BF), (p * (dp - column_sum(dp * p))).astype(BF)))
        if h >= 2:
            p, ds = halves[h - 2]
            gv.append(mm(p, head(batt, h - 2)))
            gk.append(mm(ds, head(q, h - 2)))
            gq.append(mm(k_t[HDIM * (h - 2) : HDIM * (h - 1), :], ds))
    bq = (jnp.concatenate(gq, axis=0) * QK_SCALE).astype(BF).T
    bk = (jnp.concatenate(gk, axis=1) * QK_SCALE).astype(BF)
    bv = jnp.concatenate(gv, axis=1).astype(BF)
    bp_ref[0, :, 0:D] = bq
    bp_ref[0, :, D : 2 * D] = bk
    bp_ref[0, :, 2 * D :] = bv
    b1 = mm_nt(bq, w_ref[0]) + mm_nt(bk, w_ref[1]) + mm_nt(bv, w_ref[2])
    n1, inv1 = norm_stats(h0_ref[0])
    act_ref[0] = (n1 * (1.0 + mod(1)) + mod(0)).astype(BF)
    gm_ref[0, 0:1, :] = column_sum(b1)
    gm_ref[0, 1:2, :] = column_sum(b1 * n1)
    bh0 = (bh1 + norm_back(b1 * (1.0 + mod(1)), n1, inv1)).astype(BF)
    patch_ref[0] = mm(noisy_ref[0].astype(BF), bh0)
    gm_ref[0, 3:4, :] = column_sum(bh0.astype(F32))
    gm_ref[0, 4:5, :] = column_sum(bq.astype(F32))
    gm_ref[0, 5:6, :] = column_sum(bv.astype(F32))
    gm_ref[0, 6:7, :] = column_sum(bb1.astype(F32))
    gm_ref[0, 7:8, :] = jnp.zeros((1, D), F32)


def last_kernel(counts, at_ref, att_ref, *refs):
    mine_ref, other_ref = refs[-2:]
    put = functools.partial(put_pair, at_ref[3], mine_ref, other_ref)
    parts = []
    first = 0
    for k, count in enumerate(counts):
        act_ref, bp_ref, bb1_ref = refs[3 * k : 3 * k + 3]
        parts.append((act_ref, bp_ref, att_ref, bb1_ref, first))
        first += count * SEQ

    def over(which):
        return sum(which(*p) for p in parts)

    def qkv(j):
        return over(lambda act, bp, att, bb1, first: mm_tn(act[...], bp[:, D * j : D * j + D]))

    put(0, qkv(0), qkv(2))
    put(1, qkv(1), over(lambda act, bp, att, bb1, first: mm_tn(
        att[first : first + bb1.shape[0], :], bb1[...])))


def cond_back_kernel(images, cls_ref, gm2_ref, pre_ref, th_ref, cond_ref, feat_ref, modw_ref, fmodw_ref,
                     tout_ref, sums_ref, *refs):
    out_ref, pay_ref, refs = refs[-2], refs[-1], refs[:-2]
    gm3_refs, patch_refs = refs[::2], refs[1::2]
    none = jnp.zeros((4, D), F32)
    gm2 = [gm2_ref[m] for m in range(images)]
    gm3 = [ref[m] for ref in gm3_refs for m in range(ref.shape[0])]
    patch = sum(ref[m] for ref in patch_refs for m in range(ref.shape[0]))

    def rows_of(values, r):
        return jnp.concatenate([v[r : r + 1, :] for v in values] + [none], axis=0)

    tiles = [rows_of(gm3, 0), rows_of(gm3, 1), rows_of(gm3, 2),
             rows_of(gm2, 0), rows_of(gm2, 1), rows_of(gm2, 2)]
    finals = [rows_of(gm2, 3), rows_of(gm2, 4)]
    g_act = jnp.zeros((24, D), F32)
    for t in range(6):
        g_act = g_act + mm_nt(stack3(tiles[t]), modw_ref[:, D * t : D * t + D])
    for t in range(2):
        g_act = g_act + mm_nt(stack3(finals[t]), fmodw_ref[:, D * t : D * t + D])
    cond = cond_ref[...]
    g_cond = fold3(g_act) * silu_slope(cond)
    g_pre = fold3(mm_nt(stack3(g_cond), tout_ref[...])) * silu_slope(pre_ref[...])
    act = silu(cond)
    lane = lax.broadcasted_iota(jnp.int32, (1, 128), 1)
    ids = []
    for m in range(images):
        number = cls_ref[m]
        row = jnp.where(lane == 0, (number // 256).astype(F32), 0.0)
        ids.append(jnp.where(lane == 1, (number % 256).astype(F32), row))
    ids = jnp.concatenate(ids, axis=0)
    loss = sum(v[5:6, 0:128] for v in gm2)
    pieces = [v.astype(F32) for v in split3(loss)]
    loss = jnp.where(lane == 0, pieces[0], jnp.where(lane == 1, pieces[1], jnp.where(lane == 2, pieces[2], 0.0)))
    loss = jnp.concatenate([loss, jnp.zeros((1, D - 128), F32)], axis=1)

    def put(plane, j, upper, lower):
        pay_ref[plane, 8 * j : 8 * j + 8, :] = jnp.concatenate([upper[:4], lower[:4]], axis=0)

    def put_rows(plane, first, v):
        pay_ref[plane, first : first + v.shape[0], :] = v

    def over(r):
        return sum(v[r : r + 1, :] for v in gm3)

    none = jnp.zeros((8, D), F32)
    row = jnp.zeros((1, D), F32)
    tags = jnp.concatenate([ids, jnp.zeros((4, D - 128), F32)], axis=1)
    pay_ref[...] = jnp.zeros_like(pay_ref)
    put(0, 0, th_ref[...], jnp.concatenate([feat_ref[...], jnp.zeros((8, D - FREQ), F32)], axis=1))
    put(0, 1, g_cond, g_pre)
    put(0, 2, tags, none)
    put_rows(0, 40, patch)
    for plane in (1, 2):
        put(plane, 0, act, act)
        for t in range(3):
            put(plane, 1 + t, tiles[t], tiles[t + 3])
    put(1, 4, g_cond, none)
    put(1, 5, tags, none)
    put(2, 4, finals[0], finals[1])
    sums = sums_ref[...]
    put_rows(2, 40, jnp.concatenate([over(4), over(5), over(6), sums[16:21]], axis=0))
    put(3, 0, act, act)
    put(3, 1, finals[0], finals[1])
    put_rows(3, 40, sums[0:16])
    last = [[over(3)] + [row] * 6, [row] * 7, [row] * 7, [sums[23:24], sums[21:22], sums[22:23]] + [row] * 4]
    for plane in range(4):
        put_rows(plane, 56, jnp.concatenate(last[plane] + [loss], axis=0))
    out_ref[...] = pay_ref[...].astype(BF)


def rows_each(first, *dims):
    return pl.BlockSpec((1,) + dims, lambda i: (i + first,) + (0,) * len(dims))


def front(noisy, mods, bias, patch_low, pos, blocks):
    images = noisy.shape[0]
    each = functools.partial(rows_each, 0)
    return pl.pallas_call(
        front_kernel,
        name="front",
        grid=(images,),
        out_shape=(shape((images, SEQ, D)), shape((images, SEQ, 3 * D), BF),
                   shape((images, SEQ, D), BF), shape((images, SEQ, D))),
        in_specs=[each(PD, SEQ), VM, VM, VM, VM, VM],
        out_specs=[each(SEQ, D), each(SEQ, 3 * D), each(SEQ, D), each(SEQ, D)],
        compiler_params=room(24),
        cost_estimate=cost(2.2e9, 1.2e7),
    )(noisy, mods, bias, patch_low, pos, blocks)


def middle(total_img, at, time_weight, h1, velocity, dino, dino_rd, mods, bias, blocks, align_low, final_low):
    images = h1.shape[0]
    each = functools.partial(rows_each, 0)
    full = lambda lanes, kind=BF: pltpu.VMEM((images * SEQ, lanes), kind)
    return pl.pallas_call(
        functools.partial(middle_kernel, images, total_img),
        name="middle",
        grid=(images,),
        out_shape=(shape((images, SEQ, D)), shape((images, 8, D)),
                   shape((16, EARLY, D), BF), shape((16, EARLY, D), BF), shape((SUMS_MLP, D))),
        in_specs=[SM, SM, each(SEQ, D), each(PD, SEQ), each(SEQ, DINO), each(SEQ, 1), VM, VM, VM, VM, VM],
        out_specs=[each(SEQ, D), each(8, D), VM, VM, VM],
        scratch_shapes=[full(D), full(F), pltpu.VMEM((SEQ, F), F32), full(F), full(D), full(D),
                        full(DINO), full(D), full(128), pltpu.VMEM((D, F), BF)],
        compiler_params=room(40),
        cost_estimate=cost(9e9, 1.4e7),
    )(at, time_weight, h1, velocity, dino, dino_rd, mods, bias, blocks, align_low, final_low)


def attention_back(first, count, bh1, h0, qkv, att, noisy, mods, bias, blocks):
    each = functools.partial(rows_each, first)
    out = functools.partial(rows_each, 0)
    return pl.pallas_call(
        functools.partial(back_kernel, first),
        name="attention_back",
        grid=(count,),
        out_shape=(shape((count, SEQ, D), BF), shape((count, SEQ, 3 * D), BF), shape((count, SEQ, D), BF),
                   shape((count, 8, D)), shape((count, PD, D))),
        in_specs=[each(SEQ, D), each(SEQ, D), each(SEQ, 3 * D), each(SEQ, D), each(PD, SEQ), VM, VM, VM],
        out_specs=[out(SEQ, D), out(SEQ, 3 * D), out(SEQ, D), out(8, D), out(PD, D)],
        compiler_params=room(24),
        cost_estimate=cost(1.2e9 * count, 3e6 * count),
    )(bh1, h0, qkv, att, noisy, mods, bias, blocks)


def last_gradients(at, att, parts):
    flat = lambda v: v.reshape(-1, v.shape[-1])
    arrays = [flat(v) for part in parts for v in part]
    counts = tuple(part[0].shape[0] for part in parts)
    return pl.pallas_call(
        functools.partial(last_kernel, counts),
        name="last_gradients",
        out_shape=(shape((16, LATE, D), BF),) * 2,
        in_specs=[SM] + [VM] * (len(arrays) + 1),
        out_specs=[VM] * 2,
        compiler_params=room(20),
        cost_estimate=cost(1.2e9, 9e6),
    )(at, flat(att), *arrays)


def cond_back(images, class_ids, gm2, pre, th, cond, features, mod_w, fmod_w, tout_w, sums, gm3):
    return pl.pallas_call(
        functools.partial(cond_back_kernel, images),
        name="cond_back",
        out_shape=shape((4, PAY, D), BF),
        in_specs=[SM] + [VM] * (9 + len(gm3)),
        out_specs=VM,
        scratch_shapes=[pltpu.VMEM((4, PAY, D), F32)],
        compiler_params=room(16),
        cost_estimate=cost(1e8, 4e6),
    )(class_ids, gm2, pre, th, cond, features, mod_w, fmod_w, tout_w, sums, *gm3)


def position_table():
    quarter = D // 4
    frequencies = 1.0 / 10000.0 ** (jnp.arange(quarter, dtype=jnp.float32) / quarter)
    cell_ids = jnp.arange(SEQ, dtype=jnp.int32)
    row_arg = (cell_ids // GRID).astype(jnp.float32)[:, None] * frequencies[None, :]
    col_arg = (cell_ids % GRID).astype(jnp.float32)[:, None] * frequencies[None, :]
    return jnp.concatenate(
        [jnp.sin(col_arg), jnp.cos(col_arg), jnp.sin(row_arg), jnp.cos(row_arg)], axis=1
    )


def time_features(tstep_idx):
    half_freq = FREQ // 2
    frequencies = jnp.exp(-math.log(10000.0) * jnp.arange(half_freq, dtype=jnp.float32) / half_freq)
    angles = (tstep_idx.astype(jnp.float32) + 0.5)[:, None] * frequencies[None, :]
    return jnp.concatenate([jnp.cos(angles), jnp.sin(angles)], axis=1)


def body(
    noisy,
    velocity,
    tstep_idx,
    class_ids,
    time_weight,
    dino,
    owner_map,
    adam_flat,
    adam_m,
    adam_v,
    blocks_w,
    stat_left,
    stat_right,
    root_left,
    root_right,
):
    dp, group = lax.axis_size("dp"), lax.axis_size("shard")
    near = is_near(dp, group)
    images = noisy.shape[0]
    total_img = images * dp * group
    at = jnp.stack([jnp.asarray(v, jnp.int32) for v in coordinates()])
    flat_w = adam_flat.reshape(-1, 128)
    flat_m = adam_m.reshape(-1, 128)
    flat_v = adam_v.reshape(-1, 128)
    mine = flat_w.astype(BF)
    features = jnp.pad(time_features(tstep_idx), ((0, 4), (0, 0)))
    pos = position_table()
    dino_rd = encoder_norms(dino)
    noisy = jnp.transpose(noisy, (0, 2, 1))
    velocity = jnp.transpose(velocity, (0, 2, 1))
    rows = flat_w.shape[0]
    if near:
        cut = rows // 16 * 8 + 8 if rows // 8 % 2 else rows // 2
        block_parts = gather_blocks(blocks_w.astype(BF))
        pieces, (at, features, pos) = gather_flat(mine, cut, (at, features, pos))
        places = flat_places(cut)
        blocks = place_blocks(at, owner_map, block_parts)
    else:
        pieces = [lax.all_gather(mine, AXES, axis=0, tiled=True)[None]]
        places = [(0, lambda i, at: 0)]
        slot_low = lax.all_gather(blocks_w.astype(BF), "shard", axis=0, tiled=True)
        block_ids = jnp.arange(NBLK, dtype=jnp.int32)
        slot_of = jnp.sum(
            block_ids[:, None] * (owner_map[:, None] == block_ids[None, :]).astype(jnp.int32), axis=0
        )
        blocks = jnp.take(slot_low, slot_of, axis=0)
    (mods, pre, th, cond, mod_w, fmod_w, tout_w, align_low, bias, patch_low, final_low) = conditioning(
        at, class_ids, features, pieces, places, rows)
    h0, qkv, att, h1 = front(noisy, mods, bias, patch_low, pos, blocks)
    bh1, gm2, mine, other, sums = middle(
        total_img, at, time_weight, h1, velocity, dino, dino_rd, mods, bias, blocks, align_low, final_low)
    if near:
        early = reduce_units(at, mine, other)
    parts, gm3 = [], []
    for first, count in ((0, 1), (1, images - 1)):
        bb1, bp, act, gm, patch = attention_back(first, count, bh1, h0, qkv, att, noisy, mods, bias, blocks)
        parts.append((act, bp, bb1))
        gm3 += [gm, patch]
    late_mine, late_other = last_gradients(at, att, parts)
    pay = cond_back(images, class_ids, gm2, pre, th, cond, features, mod_w, fmod_w, tout_w, sums, gm3)
    if near:
        late = reduce_units(at, late_mine, late_other)
        grads, parts = exchange_gradients(at, owner_map, pay, late, early)
        loss, upd, new_m, new_v = adam_near(at, parts, flat_w, flat_m, flat_v)
        *grads, loss, upd, new_m, new_v = lax.optimization_barrier((*grads, loss, upd, new_m, new_v))
        updates = shampoo(at, grads, blocks_w, stat_left, stat_right, root_left, root_right)
    else:
        core = at[3]

        def by_part(mine, other):
            pair = jnp.where(core == 0, jnp.stack([mine, other]), jnp.stack([other, mine]))
            count = mine.shape[1] // UNIT
            return pair.reshape(2, 16, count, UNIT, D).transpose(0, 2, 1, 3, 4).reshape(2, count, D, D)

        early, late = by_part(mine, other), by_part(late_mine, late_other)
        late = jnp.stack([late[0, 0], late[0, 1], late[1, 0], late[1, 1]])
        grad_model = jnp.concatenate([late, early[:, :4].reshape(8, D, D)])
        pays = lax.all_gather(pay, AXES, axis=0, tiled=False)
        align_sum = lax.psum(early[:, 4].astype(F32), AXES)
        loss, upd, new_m, new_v = adam_wide(pays, align_sum, flat_w, flat_m, flat_v)
        slots = jnp.take(grad_model, owner_map, axis=0)
        owned = lax.psum_scatter(slots, "shard", scatter_dimension=0, tiled=True)
        grads = [lax.psum(owned.astype(F32), "dp").astype(BF)]
        updates = shampoo(at, grads, blocks_w, stat_left, stat_right, root_left, root_right)
    return (loss, *updates,
            upd.reshape(-1), new_m.reshape(-1), new_v.reshape(-1))


def is_near(dp, group):
    return (dp, group) == (8, 4)


def solution(mesh):
    return jax.shard_map(
        body,
        mesh=mesh,
        in_specs=(
            P(("dp", "shard"), None, None),
            P(("dp", "shard"), None, None),
            P(("dp", "shard")),
            P(("dp", "shard")),
            P(("dp", "shard")),
            P(("dp", "shard"), None, None),
            P(),
            P(("dp", "shard")),
            P(("dp", "shard")),
            P(("dp", "shard")),
            P("shard", None, None),
            P("shard", None, None),
            P("shard", None, None),
            P("shard", None, None),
            P("shard", None, None),
        ),
        out_specs=(
            P(),
            P("shard", None, None),
            P("shard", None, None),
            P("shard", None, None),
            P(("dp", "shard")),
            P(("dp", "shard")),
            P(("dp", "shard")),
        ),
        check_vma=False,
    )
```
